32 devices in a mesh: dp: 4 (over y, x), expert: 8 (over z, core).
Axes of the slice: x: 2, y: 2, z: 4, core: 2. Of those that a mesh axis runs over, the one named last changes fastest.
Arguments:
- tokens: bfloat16 [32768, 768], P(('dp', 'expert')), may hold values from -6 to 6
- gain_one: float32 [768], replicated, may hold values from 0.25 to 1.75
- query_w: bfloat16 [768, 768], replicated, may hold values from -0.109375 to 0.109375
- key_w: bfloat16 [768, 768], replicated, may hold values from -0.109375 to 0.109375
- value_w: bfloat16 [768, 768], replicated, may hold values from -0.21875 to 0.21875
- out_w: bfloat16 [768, 768], replicated, may hold values from -0.625 to 0.625
- rel_table: float32 [32, 12], replicated, may hold values from -4 to 4
- gain_two: float32 [768], replicated, may hold values from 0.25 to 1.75
- router_w: bfloat16 [768, 8], replicated, may hold values from -0.15625 to 0.15625
- expert_in: bfloat16 [8, 768, 3072], P('expert'), may hold values from -0.21875 to 0.21875
- expert_out: bfloat16 [8, 3072, 768], P('expert'), may hold values from -0.875 to 0.875
- routes: int32 [32768, 1], P(('dp', 'expert')), may hold values from 0 to 7
- buckets: int32 [2047], replicated, may hold values from 0 to 31, as said below
- cotangent: bfloat16 [32768, 768], P(('dp', 'expert')), may hold values from -6 to 6
Outputs:
- output: bfloat16 [32768, 768], P(('dp', 'expert'))
- input_grad: float32 [32768, 768], P(('dp', 'expert'))
- query_grad: float32 [768, 768], replicated
- key_grad: float32 [768, 768], replicated
- value_grad: float32 [768, 768], replicated
- out_grad: float32 [768, 768], replicated
- rel_grad: float32 [32, 12], replicated
- gain_one_grad: float32 [768], replicated
- gain_two_grad: float32 [768], replicated
- router_grad: float32 [768, 8], replicated
- expert_in_grad: float32 [8, 768, 3072], P('expert', 'dp')
- expert_out_grad: float32 [8, 3072, 768], P('expert', None, 'dp')
The draws below stay inside these ranges and needn't reach their ends.
Inputs may be any that keep to these rules, and one draw needn't show every extreme that they name: buckets depends only on the distance |j - i| and on the sign of j - i, never falls as the distance grows on either side, is below 16 for j - i <= 0 and 16 or more for j - i > 0.
All inputs are finite; a program needn't handle non-finite values.
Results may differ from the reference program's by a relative error of at most 0.015.
The reference program's roundings to bfloat16 on the way count: a program that leaves them out, or rounds other values in their place, can miss the bound.
Values may be sent and summed in bfloat16 or wider, within the bound.
A program may use at most 448 MiB of HBM per device.

```python
import math
import jax
import jax.numpy as jnp
from jax import lax

D = 768
HEADS = 12
HEAD_DIM = 64
FF = 3072
BUCKETS = 32
SEQ = 1024
EXPERTS = 8
CAP = 160
TOKENS = 32768
DEVICES = 32


def draw_buckets(key, part):
    increments = 1 + jax.random.randint(key, (7,), 0, 2 ** jnp.arange(1, 8, dtype=jnp.int32)) * SEQ // 1024
    bounds = 8 + jnp.cumsum(increments)
    offsets = jnp.arange(2 * SEQ - 1, dtype=jnp.int32) - (SEQ - 1)
    distance = jnp.abs(offsets)
    far_bucket = 8 + jnp.sum((bounds[None, :] <= distance[:, None]).astype(jnp.int32), axis=1)
    magnitude = jnp.where(distance < 8, distance, far_bucket)
    return (magnitude + 16 * (offsets > 0).astype(jnp.int32)).astype(jnp.int32)


def block_scale(own_key, dims, split, least, high):
    gain = 1.0
    for dim, blocks in split:
        heights = jax.random.uniform(jax.random.fold_in(jax.random.fold_in(own_key, 6), dim), (blocks,), jnp.float32, least / len(split), high / len(split))
        gain = gain * jnp.repeat(jnp.exp(heights), dims[dim] // blocks).reshape((-1,) + (1,) * (len(dims) - 1 - dim))
    return gain


def choose_distinct(stream_key, rows, amount, top, lift):
    order = jax.random.permutation(jax.random.fold_in(stream_key, 1), amount)
    favour = order
    for power in range(3):
        favour = favour * favour // amount
    favour = favour * lift // amount
    tickets = jax.random.randint(jax.random.fold_in(stream_key, 2), (rows, amount), 0, 4096) + favour
    holders = jax.random.permutation(jax.random.fold_in(stream_key, 3), rows)[jnp.arange(amount) % rows]
    tickets = jnp.where(jnp.arange(rows)[:, None] == holders[None, :], 1 << 14, tickets)
    merit = tickets * amount + jnp.arange(amount)
    return lax.top_k(merit.astype(jnp.int32), top)[1].astype(jnp.int32)


def bell_draw(stream_key, extent, deviation, limit, pieces=(), kind=jnp.bfloat16):
    drawn = jax.random.normal(stream_key, extent, jnp.float32) * deviation
    if len(pieces) > 0:
        drawn = block_scale(stream_key, extent, pieces, -0.22, 0.18) * drawn
    return jnp.clip(drawn, min=-limit, max=limit).astype(kind)


def setup_inputs(seed: int = 0) -> dict:
    streams_of = jax.random.split(jax.random.key(seed), 15)
    tokens = bell_draw(streams_of[0], (TOKENS, D), 1.0, 6.0, ((0, 32),))
    gain_one = jnp.clip(1.0 + 0.15 * jax.random.normal(streams_of[1], (D,), jnp.float32), 0.25, 1.75)
    query_w = bell_draw(streams_of[2], (D, D), (4 * D) ** -0.5, 0.109375)
    key_w = bell_draw(streams_of[3], (D, D), (4 * D) ** -0.5, 0.109375)
    value_w = bell_draw(streams_of[4], (D, D), D ** -0.5, 0.21875)
    out_w = bell_draw(streams_of[5], (D, D), (D // 8) ** -0.5, 0.625)
    rel_table = bell_draw(streams_of[6], (BUCKETS, HEADS), 1.0, 4.0, (), jnp.float32)
    gain_two = jnp.clip(1.0 + 0.15 * jax.random.normal(streams_of[7], (D,), jnp.float32), 0.25, 1.75)
    router_w = bell_draw(streams_of[8], (D, EXPERTS), (2 * D) ** -0.5, 0.15625)
    expert_in = bell_draw(streams_of[9], (EXPERTS, D, FF), D ** -0.5, 0.21875, ((0, 8),))
    expert_out = bell_draw(streams_of[10], (EXPERTS, FF, D), (max(1, FF // (EXPERTS * EXPERTS))) ** -0.5, 0.875, ((0, 8),))
    routes = choose_distinct(streams_of[11], TOKENS, EXPERTS, 1, 1024)
    buckets = draw_buckets(jax.random.fold_in(streams_of[14], 71), 0)
    cotangent = bell_draw(streams_of[13], (TOKENS, D), 1.0, 6.0, ((0, 32),))
    return {"tokens": tokens, "gain_one": gain_one, "query_w": query_w, "key_w": key_w, "value_w": value_w, "out_w": out_w, "rel_table": rel_table, "gain_two": gain_two, "router_w": router_w, "expert_in": expert_in, "expert_out": expert_out, "routes": routes, "buckets": buckets, "cotangent": cotangent}


epsilon = 1e-06
highest = lax.Precision.HIGHEST

@jax.custom_vjp
def low(v):
    return lax.optimization_barrier(v.astype(jnp.bfloat16)).astype(jnp.float32)

@jax.custom_vjp
def low_back(v):
    return v

def low_keep(v):
    return (low(v), None)

def low_pass(kept, grad):
    return (grad,)

def back_keep(v):
    return (v, None)

def back_low(kept, grad):
    return (low(grad),)
low.defvjp(low_keep, low_pass)
low_back.defvjp(back_keep, back_low)

def matmul(left, right):
    return jnp.dot(left, right, precision=highest)

def rms_norm(values, gain_vec):
    return values * lax.rsqrt(lax.optimization_barrier(jnp.mean(values * values, axis=-1, keepdims=True)) + epsilon) * gain_vec

def reference(tokens, gain_one, query_w, key_w, value_w, out_w, rel_table, gain_two, router_w, expert_in, expert_out, routes, buckets, cotangent):
    group_seqs = math.gcd(DEVICES, max(1, 4096 // SEQ))
    group_count = DEVICES // group_seqs
    group_rows = group_seqs * SEQ
    route_ids = routes[:, 0].astype(jnp.int32)
    one_hot_int = (route_ids[:, None] == jnp.arange(EXPERTS, dtype=jnp.int32)[None, :]).astype(jnp.int32)
    per_device = one_hot_int.reshape(DEVICES, SEQ, EXPERTS)
    position = lax.optimization_barrier(jnp.sum((jnp.cumsum(per_device, axis=1) - 1) * per_device, axis=2))
    kept_mask = position < CAP
    local_slot = jnp.where(kept_mask, route_ids.reshape(DEVICES, SEQ) * CAP + position, EXPERTS * CAP)
    slot_index = (local_slot + jnp.arange(DEVICES, dtype=jnp.int32)[:, None] * (EXPERTS * CAP + 1)).reshape(TOKENS).astype(jnp.int32)
    row_source = jnp.full((DEVICES * (EXPERTS * CAP + 1),), TOKENS, jnp.int32).at[slot_index].set(jnp.arange(TOKENS, dtype=jnp.int32))
    row_source = row_source.reshape(DEVICES, EXPERTS * CAP + 1)[:, :EXPERTS * CAP]
    row_source = row_source.reshape(DEVICES, EXPERTS, CAP).transpose(1, 0, 2).reshape(EXPERTS, DEVICES * CAP).astype(jnp.int32)
    route_mask = one_hot_int.astype(jnp.float32).reshape(group_count, group_rows, EXPERTS)
    offsets = jnp.arange(SEQ, dtype=jnp.int32)[None, :] - jnp.arange(SEQ, dtype=jnp.int32)[:, None] + (SEQ - 1)
    bucket_grid = buckets[offsets]

    def forward(tokens_f, gain_a, query_f, key_f, value_f, out_f, rel_f, gain_b, router_f, expert_in_f, expert_out_f):
        bias_full = jnp.transpose(rel_f[bucket_grid], (2, 0, 1))

        def attend(operands):
            query_seq, key_seq, value_seq = operands
            logits = low_back(jnp.einsum('qhd,khd->hqk', query_seq, key_seq, precision=highest)) + bias_full
            att_weights = low(jax.nn.softmax(logits, axis=-1))
            return jnp.einsum('hqk,khd->qhd', att_weights, value_seq, precision=highest)

        def shaped(matrix):
            return matrix.reshape(group_seqs, SEQ, HEADS, HEAD_DIM)

        def dense_group(operands):
            tokens_g, mask_g = operands
            normed = low(rms_norm(tokens_g, gain_a))
            queries = low(low_back(matmul(normed, query_f)))
            key_rows = low(low_back(matmul(normed, key_f)))
            value_rows = low(low_back(matmul(normed, value_f)))
            context = lax.map(jax.checkpoint(attend), (shaped(queries), shaped(key_rows), shaped(value_rows)))
            context = low(low_back(context.reshape(group_rows, D)))
            branch = low_back(matmul(context, out_f))
            hidden = tokens_g + branch
            normed_two = low(rms_norm(hidden, gain_b))
            router_logits = low_back(matmul(normed_two, router_f))
            gate_value = lax.optimization_barrier(jnp.sum(jax.nn.softmax(router_logits, axis=-1) * mask_g, axis=-1))
            return (hidden, normed_two, gate_value)
        hidden, normed_two, gate_value = lax.map(jax.checkpoint(dense_group), (tokens_f.reshape(group_count, group_rows, D), route_mask))
        hidden = hidden.reshape(TOKENS, D)
        gate_value = gate_value.reshape(TOKENS)
        dispatch_rows = low_back(normed_two.reshape(TOKENS, D))
        source_rows = jnp.concatenate([dispatch_rows, jnp.zeros((1, D), jnp.float32)], axis=0)

        def expert_pass(operands):
            row_ids, weight_in, weight_out = operands
            rows_in = source_rows[row_ids]
            preact = low_back(matmul(rows_in, weight_in))
            active = low(jax.nn.gelu(preact, approximate=True))
            return low(low_back(matmul(active, weight_out)))
        returned = lax.map(jax.checkpoint(expert_pass), (row_source, expert_in_f, expert_out_f))
        returned = returned.reshape(EXPERTS, DEVICES, CAP, D).transpose(1, 0, 2, 3).reshape(DEVICES, EXPERTS * CAP, D)
        returned = jnp.concatenate([returned, jnp.zeros((DEVICES, 1, D), jnp.float32)], axis=1)
        gathered = returned.reshape(DEVICES * (EXPERTS * CAP + 1), D)[slot_index]
        return hidden + gate_value[:, None] * gathered
    primals = (tokens.astype(jnp.float32), gain_one, query_w.astype(jnp.float32), key_w.astype(jnp.float32), value_w.astype(jnp.float32), out_w.astype(jnp.float32), rel_table, gain_two, router_w.astype(jnp.float32), expert_in.astype(jnp.float32), expert_out.astype(jnp.float32))
    output, pullback = jax.vjp(forward, *primals)
    gradients = pullback(cotangent.astype(jnp.float32))
    return (output.astype(jnp.bfloat16), gradients[0], gradients[2], gradients[3], gradients[4], gradients[5], gradients[6], gradients[1], gradients[7], gradients[8], gradients[9], gradients[10])
```

```python
import jax
import jax.numpy as jnp
from jax import lax
from jax.experimental import pallas as pl
from jax.experimental.pallas import tpu as pltpu
from jax.sharding import PartitionSpec as P

bf16 = jnp.bfloat16
f32 = jnp.float32
epsilon = 1e-06
highest = lax.Precision.HIGHEST

def dot_f32(left, right):
    return lax.dot_general(left, right, (((1,), (0,)), ((), ())), preferred_element_type=f32)


def fill_toeplitz(base_ref, head, row):
    rows, width = base_ref.shape[1:]
    spread = jnp.broadcast_to(row, (8, width))
    eight = pltpu.roll(spread, 0, 1, stride=1, stride_axis=0)
    for group in range(rows // 8):
        base_ref[head, 8 * group : 8 * group + 8, :] = (
            eight if group == 0 else pltpu.roll(eight, 8 * group, 1)
        )


def attend_kernel(q_ref, k_ref, v_ref, u_ref, ctx_ref, ctxt_ref, lse_ref, base, qt, vt, s_scr, p_scr):
    seq = q_ref.shape[0]
    span = 256
    half = seq
    qt[...] = q_ref[...].T
    vt[...] = v_ref[...].T
    for head in range(2):
        fill_toeplitz(base, head, u_ref[0, head : head + 1, :])
    zeros = jnp.zeros((64, span), bf16)

    def step(idx, carry):
        cols = pl.ds(pl.multiple_of(idx * span, span), span)
        outs = []
        for head in range(2):
            part = qt[64 * head : 64 * head + 64, cols]
            rhs = jnp.concatenate([part, zeros] if head == 0 else [zeros, part], axis=0)
            peak = None
            for kb in range(seq // 128):
                rows = slice(128 * kb, 128 * kb + 128)
                offs = pl.multiple_of(half + span * idx - 128 * kb, 128)
                s = dot_f32(k_ref[rows, :], rhs) + base[head, :, pl.ds(offs, span)]
                s_scr[head, rows, :] = s
                now = jnp.max(s.reshape(16, 8, span), axis=0)
                peak = now if peak is None else jnp.maximum(peak, now)
            peak = jnp.max(peak, axis=0, keepdims=True)
            total = None
            for kb in range(seq // 128):
                rows = slice(128 * kb, 128 * kb + 128)
                e = jnp.exp(s_scr[head, rows, :] - peak)
                s_scr[head, rows, :] = e
                now = jnp.sum(e.reshape(16, 8, span), axis=0)
                total = now if total is None else total + now
            total = jnp.sum(total, axis=0, keepdims=True)
            inv = 1.0 / total
            for kb in range(seq // 128):
                rows = slice(128 * kb, 128 * kb + 128)
                p_scr[head, rows, :] = (s_scr[head, rows, :] * inv).astype(bf16)
            lse_ref[0, head : head + 1, cols] = peak + jnp.log(total)
            outs.append(dot_f32(vt[64 * head : 64 * head + 64, :], p_scr[head]))
        both = jnp.concatenate(outs, axis=0)
        ctxt_ref[:, cols] = both
        ctx_ref[cols, :] = both.T.astype(bf16)
        return carry

    lax.fori_loop(0, seq // span, step, 0)


def attend(q, k, v, u):
    seq, width = q.shape
    pairs = width // 128
    blk = pl.BlockSpec((seq, 128), lambda p: (0, p))
    return pl.pallas_call(
        attend_kernel,
        grid=(pairs,),
        in_specs=[blk, blk, blk, pl.BlockSpec((1, 2, 2 * seq), lambda p: (p, 0, 0))],
        out_specs=[
            blk,
            pl.BlockSpec((128, seq), lambda p: (p, 0)),
            pl.BlockSpec((1, 8, seq), lambda p: (p, 0, 0)),
        ],
        out_shape=[
            jax.ShapeDtypeStruct((seq, width), bf16),
            jax.ShapeDtypeStruct((width, seq), f32),
            jax.ShapeDtypeStruct((pairs, 8, seq), f32),
        ],
        scratch_shapes=[
            pltpu.VMEM((2, 128, 2 * seq), f32),
            pltpu.VMEM((128, seq), bf16),
            pltpu.VMEM((128, seq), bf16),
            pltpu.VMEM((2, seq, 256), f32),
            pltpu.VMEM((2, seq, 256), bf16),
        ],
        compiler_params=pltpu.CompilerParams(vmem_limit_bytes=48 << 20),
        cost_estimate=pl.CostEstimate(
            flops=16 * seq * seq * width, bytes_accessed=20 * seq * width, transcendentals=seq * seq * 12
        ),
        name="attend",
    )(q, k, v, u)


def split_rows(row):
    hi = row.astype(bf16).astype(f32)
    mid = (row - hi).astype(bf16).astype(f32)
    low = row - hi - mid
    idx = lax.broadcasted_iota(jnp.int32, (16, row.shape[1]), 0)
    return jnp.where(idx == 0, hi, jnp.where(idx == 1, mid, jnp.where(idx == 2, low, 0.0))).astype(bf16)


def attend_back_kernel(
    q_ref, k_ref, v_ref, g_ref, u_ref, ctxt_ref, lse_ref,
    dq_ref, dk_ref, dv_ref, diag_ref,
    base, acc, kaug, vaug, qaug, gaug, qz, gz, kt, dqt,
):
    seq = q_ref.shape[0]
    span = 256
    lane = lax.broadcasted_iota(jnp.int32, (seq, 128), 1)
    gt = g_ref[...].T
    qtv = q_ref[...].T
    kt[...] = k_ref[...].T
    gtf = gt.astype(f32)
    pad = jnp.zeros((48, seq), bf16)
    one = jnp.ones((seq, 128), bf16)
    nil = jnp.zeros((seq, 128), bf16)
    acc[...] = jnp.zeros_like(acc)
    for head in range(2):
        fill_toeplitz(base, head, u_ref[0, head : head + 1, :])
        own = (lane < 64) if head == 0 else (lane >= 64)
        origin = 64 if head == 0 else 0
        extra = jnp.where((lane >= origin) & (lane < origin + 3), one, nil)
        kaug[head] = jnp.where(own, k_ref[...], extra)
        vaug[head] = jnp.where(own, v_ref[...], extra)
        qz[head] = jnp.where(own, q_ref[...], nil)
        gz[head] = jnp.where(own, g_ref[...], nil)
        rows = slice(64 * head, 64 * head + 64)
        lse = split_rows(-lse_ref[0, head : head + 1, :])
        dsum = split_rows(-jnp.sum(gtf[rows] * ctxt_ref[rows, :], axis=0, keepdims=True))
        for dst, src, aug in ((qaug, qtv, lse), (gaug, gt, dsum)):
            dst[head, rows, :] = src[rows]
            dst[head, origin : origin + 16, :] = aug
            dst[head, origin + 16 : origin + 64, :] = pad

    dqt[...] = jnp.zeros_like(dqt)

    def step(idx, carry):
        rows = pl.ds(pl.multiple_of(idx * span, span), span)
        dv = None
        dk = None
        for head in range(2):
            s = dot_f32(kaug[head, rows, :], qaug[head])
            dp = dot_f32(vaug[head, rows, :], gaug[head])
            tops = []
            grads = []
            for part in range(2):
                offs = pl.ds(pl.multiple_of(seq - span * idx - 128 * part, 128), seq)
                p = jnp.exp(s[128 * part : 128 * part + 128] + base[head, :, offs])
                ds_ = p * dp[128 * part : 128 * part + 128]
                acc[head, :, offs] += ds_
                tops.append(p.astype(bf16))
                grads.append(ds_.astype(bf16))
            p = jnp.concatenate(tops, axis=0)
            ds_ = jnp.concatenate(grads, axis=0)
            now = dot_f32(p, gz[head])
            dv = now if dv is None else dv + now
            now = dot_f32(ds_, qz[head])
            dk = now if dk is None else dk + now
            dqt[64 * head : 64 * head + 64, :] += dot_f32(kt[64 * head : 64 * head + 64, rows], ds_)
        dv_ref[rows, :] = dv.astype(bf16)
        dk_ref[rows, :] = dk.astype(bf16)
        return carry

    lax.fori_loop(0, seq // span, step, 0)
    dq_ref[...] = dqt[...].T.astype(bf16)
    width = 2 * seq
    for head in range(2):
        total = acc[head, 0:8, :]
        for group in range(1, 16):
            total = total + pltpu.roll(acc[head, 8 * group : 8 * group + 8, :], width - 8 * group, 1)
        sub = lax.broadcasted_iota(jnp.int32, (8, width), 0)
        for bit in (1, 2, 4):
            total = jnp.where((sub & bit) != 0, pltpu.roll(total, width - bit, 1), total)
        diag_ref[0, head : head + 1, :] = jnp.sum(total, axis=0, keepdims=True)


def attend_back(q, k, v, g, u, ctxt, lse):
    seq, width = q.shape
    pairs = width // 128
    blk = pl.BlockSpec((seq, 128), lambda p: (0, p))
    return pl.pallas_call(
        attend_back_kernel,
        grid=(pairs,),
        in_specs=[
            blk, blk, blk, blk,
            pl.BlockSpec((1, 2, 2 * seq), lambda p: (p, 0, 0)),
            pl.BlockSpec((128, seq), lambda p: (p, 0)),
            pl.BlockSpec((1, 8, seq), lambda p: (p, 0, 0)),
        ],
        out_specs=[blk, blk, blk, pl.BlockSpec((1, 8, 2 * seq), lambda p: (p, 0, 0))],
        out_shape=[jax.ShapeDtypeStruct((seq, width), bf16)] * 3
        + [jax.ShapeDtypeStruct((pairs, 8, 2 * seq), f32)],
        scratch_shapes=[
            pltpu.VMEM((2, 128, 2 * seq), f32),
            pltpu.VMEM((2, 128, 2 * seq), f32),
            pltpu.VMEM((2, seq, 128), bf16),
            pltpu.VMEM((2, seq, 128), bf16),
            pltpu.VMEM((2, 128, seq), bf16),
            pltpu.VMEM((2, 128, seq), bf16),
            pltpu.VMEM((2, seq, 128), bf16),
            pltpu.VMEM((2, seq, 128), bf16),
            pltpu.VMEM((128, seq), bf16),
            pltpu.VMEM((128, seq), f32),
        ],
        compiler_params=pltpu.CompilerParams(vmem_limit_bytes=56 << 20),
        cost_estimate=pl.CostEstimate(
            flops=40 * seq * seq * width, bytes_accessed=20 * seq * width, transcendentals=seq * seq * 12
        ),
        name="attend_back",
    )(q, k, v, g, u, ctxt, lse)


def rms_backward(grad_norm, values, row_scale, gain_vec):
    weighted = grad_norm * gain_vec
    gain_grad = jnp.sum(grad_norm * values * row_scale, axis=0)
    grad_in = row_scale * weighted - values * row_scale**3 * jnp.mean(
        weighted * values, axis=-1, keepdims=True
    )
    return grad_in, gain_grad


def rms_forward(values, gain_vec):
    row_scale = lax.rsqrt(jnp.mean(values * values, axis=-1, keepdims=True) + epsilon)
    return values * row_scale * gain_vec, row_scale


def gelu_tanh(values):
    return jax.nn.gelu(values, approximate=True)


def contract(left, right, dims):
    return lax.dot_general(left, right, (((dims[0],), (dims[1],)), ((), ())), preferred_element_type=f32)


def on_device(
    tokens, gain_one, query_w, key_w, value_w, out_w, rel_table, gain_two, router_w,
    expert_in, expert_out, routes, buckets, cotangent,
):
    seq_len, width = tokens.shape
    heads = rel_table.shape[1]
    experts = lax.axis_size("expert")
    capacity = (5 * seq_len + 4 * experts - 1) // (4 * experts)
    slots = experts * capacity
    weight_in = expert_in[0]
    weight_out = expert_out[0]

    route_ids = routes[:, 0]
    route_hot = route_ids[:, None] == jnp.arange(experts, dtype=jnp.int32)[None, :]
    route_int = route_hot.astype(jnp.int32)
    route_float = route_hot.astype(f32)
    position = jnp.sum((jnp.cumsum(route_int, axis=0) - 1) * route_int, axis=1)
    slot_index = jnp.where(position < capacity, route_ids * capacity + position, slots)
    pick = (jnp.arange(slots, dtype=jnp.int32)[:, None] == slot_index[None, :]).astype(bf16)

    def exchange(rows):
        rows = rows.reshape(experts, capacity, width)
        return lax.all_to_all(rows, "expert", split_axis=0, concat_axis=0, tiled=True).reshape(slots, width)

    def scatter_rows(rows):
        return contract(pick, rows, (1, 0)).astype(bf16)

    def gather_rows(rows):
        return contract(pick, rows, (0, 0))

    grad_recv = exchange(scatter_rows(cotangent))

    tokens_f = tokens.astype(f32)
    normed, scale_one = rms_forward(tokens_f, gain_one)
    normed_low = normed.astype(bf16)
    queries = contract(normed_low, query_w, (1, 0)).astype(bf16)
    key_rows = contract(normed_low, key_w, (1, 0)).astype(bf16)
    value_rows = contract(normed_low, value_w, (1, 0)).astype(bf16)
    reach = jnp.concatenate([buckets, jnp.full((1,), -1, jnp.int32)])[::-1]
    bucket_hot = (jnp.arange(rel_table.shape[0], dtype=jnp.int32)[:, None] == reach[None, :]).astype(f32)
    spread = jnp.einsum("bh,bx->hx", rel_table, bucket_hot, precision=highest)
    spread = spread.reshape(heads // 2, 2, 2 * seq_len)
    context, context_t, logsum = attend(queries, key_rows, value_rows, spread)
    hidden = tokens_f + contract(context, out_w, (1, 0))
    normed_two, scale_two = rms_forward(hidden, gain_two)
    normed_two_low = normed_two.astype(bf16)

    received = exchange(scatter_rows(normed_two_low))
    own = lax.axis_index("expert")
    own_hot = (jnp.arange(experts, dtype=jnp.int32) == own).astype(f32)[None, :]
    probs_recv = jax.nn.softmax(contract(received, router_w, (1, 0)), axis=-1)
    gate_recv = jnp.sum(probs_recv * own_hot, axis=-1, keepdims=True)
    grad_recv_f = grad_recv.astype(f32)
    grad_produced = (grad_recv_f * gate_recv).astype(bf16)
    preact = contract(received, weight_in, (1, 0))
    gelu_values, gelu_pullback = jax.vjp(gelu_tanh, preact)
    active = gelu_values.astype(bf16)
    produced = contract(active, weight_out, (1, 0)).astype(bf16)
    gate_grad = jnp.sum(grad_recv_f * produced.astype(f32), axis=-1, keepdims=True)
    logit_low = (gate_grad * gate_recv * (own_hot - probs_recv)).astype(bf16)
    grad_active = contract(grad_produced, weight_out, (1, 1))
    grad_preact = gelu_pullback(grad_active)[0].astype(bf16)
    grad_received = contract(grad_preact, weight_in, (1, 1)) + contract(logit_low, router_w, (1, 1))
    grad_rows = exchange(grad_received.astype(bf16))
    returned = exchange(produced)
    in_grad = contract(received, grad_preact, (0, 0)).astype(bf16)
    out_grad_local = contract(active, grad_produced, (0, 0)).astype(bf16)
    router_grad = contract(received, logit_low, (0, 0))
    in_share = lax.psum_scatter(in_grad, "dp", scatter_dimension=0, tiled=True).astype(f32)
    out_share = lax.psum_scatter(out_grad_local, "dp", scatter_dimension=1, tiled=True).astype(f32)

    router_probs = jax.nn.softmax(contract(normed_two_low, router_w, (1, 0)), axis=-1)
    gate_value = jnp.sum(router_probs * route_float, axis=-1, keepdims=True)
    output = (hidden + gate_value * gather_rows(returned)).astype(bf16)

    grad_out = cotangent.astype(f32)
    grad_normed_two = gather_rows(grad_rows)
    grad_hidden_norm, gain_two_grad = rms_backward(grad_normed_two, hidden, scale_two, gain_two)
    grad_hidden = grad_out + grad_hidden_norm
    branch_low = grad_hidden.astype(bf16)
    out_w_grad = contract(context, branch_low, (0, 0))
    grad_context = contract(branch_low, out_w, (1, 1)).astype(bf16)
    out_w_grad = lax.psum(out_w_grad, ("dp", "expert"))
    query_grad, key_grad, value_grad, diagonals = attend_back(
        queries, key_rows, value_rows, grad_context, spread, context_t, logsum
    )
    query_w_grad = contract(normed_low, query_grad, (0, 0))
    key_w_grad = contract(normed_low, key_grad, (0, 0))
    value_w_grad = contract(normed_low, value_grad, (0, 0))
    grad_normed = (
        contract(query_grad, query_w, (1, 1))
        + contract(key_grad, key_w, (1, 1))
        + contract(value_grad, value_w, (1, 1))
    )
    grad_tokens_norm, gain_one_grad = rms_backward(grad_normed, tokens_f, scale_one, gain_one)
    input_grad = grad_hidden + grad_tokens_norm
    diagonals = diagonals[:, :2].reshape(heads, 2 * seq_len)
    rel_grad = jnp.einsum("bx,hx->bh", bucket_hot, diagonals, precision=highest)
    query_w_grad, key_w_grad, value_w_grad, rel_grad, gain_one_grad, gain_two_grad, router_grad = lax.psum(
        (query_w_grad, key_w_grad, value_w_grad, rel_grad, gain_one_grad, gain_two_grad, router_grad),
        ("dp", "expert"),
    )
    return (
        output, input_grad, query_w_grad, key_w_grad, value_w_grad, out_w_grad, rel_grad,
        gain_one_grad, gain_two_grad, router_grad, in_share[None], out_share[None],
    )


def solution(mesh):
    rows = P(("dp", "expert"), None)
    whole = P()
    split = P("expert", None, None)
    return jax.shard_map(
        on_device,
        mesh=mesh,
        in_specs=(
            rows, whole, whole, whole, whole, whole, whole, whole, whole, split, split, rows, whole, rows,
        ),
        out_specs=(
            rows, rows, whole, whole, whole, whole, whole, whole, whole, whole,
            P("expert", "dp", None), P("expert", None, "dp"),
        ),
        check_vma=False,
    )
```

```python
import functools

import jax
import jax.numpy as jnp
from jax import lax
from jax.experimental import pallas as pl
from jax.experimental.pallas import tpu as pltpu
from jax.sharding import PartitionSpec as P

bf16 = jnp.bfloat16
f32 = jnp.float32
epsilon = 1e-06
highest = lax.Precision.HIGHEST

def dot_f32(left, right):
    return lax.dot_general(left, right, (((1,), (0,)), ((), ())), preferred_element_type=f32)


def dot_nt(left, right):
    return lax.dot_general(left, right, (((1,), (1,)), ((), ())), preferred_element_type=f32)


def fill_toeplitz(base_ref, head, row):
    rows, width = base_ref.shape[1:]
    spread = jnp.broadcast_to(row, (8, width))
    eight = pltpu.roll(spread, 0, 1, stride=1, stride_axis=0)
    for group in range(rows // 8):
        base_ref[head, 8 * group : 8 * group + 8, :] = (
            eight if group == 0 else pltpu.roll(eight, 8 * group, 1)
        )


def attend_kernel(q_ref, k_ref, v_ref, u_ref, ctx_ref, ctxt_ref, lse_ref, base, qt, vt, s_scr, p_scr):
    seq = q_ref.shape[0]
    span = 256
    half = seq
    qt[...] = q_ref[...].T
    vt[...] = v_ref[...].T
    for head in range(2):
        fill_toeplitz(base, head, u_ref[0, head : head + 1, :])
    zeros = jnp.zeros((64, span), bf16)

    def step(idx, carry):
        cols = pl.ds(pl.multiple_of(idx * span, span), span)
        outs = []
        for head in range(2):
            part = qt[64 * head : 64 * head + 64, cols]
            rhs = jnp.concatenate([part, zeros] if head == 0 else [zeros, part], axis=0)
            peak = None
            for kb in range(seq // 128):
                rows = slice(128 * kb, 128 * kb + 128)
                offs = pl.multiple_of(half + span * idx - 128 * kb, 128)
                s = dot_f32(k_ref[rows, :], rhs) + base[head, :, pl.ds(offs, span)]
                s_scr[head, rows, :] = s
                now = jnp.max(s.reshape(16, 8, span), axis=0)
                peak = now if peak is None else jnp.maximum(peak, now)
            peak = jnp.max(peak, axis=0, keepdims=True)
            total = None
            for kb in range(seq // 128):
                rows = slice(128 * kb, 128 * kb + 128)
                e = jnp.exp(s_scr[head, rows, :] - peak)
                s_scr[head, rows, :] = e
                now = jnp.sum(e.reshape(16, 8, span), axis=0)
                total = now if total is None else total + now
            total = jnp.sum(total, axis=0, keepdims=True)
            inv = 1.0 / total
            for kb in range(seq // 128):
                rows = slice(128 * kb, 128 * kb + 128)
                p_scr[head, rows, :] = (s_scr[head, rows, :] * inv).astype(bf16)
            lse_ref[0, head : head + 1, cols] = peak + jnp.log(total)
            outs.append(dot_f32(vt[64 * head : 64 * head + 64, :], p_scr[head]))
        both = jnp.concatenate(outs, axis=0)
        ctxt_ref[:, cols] = both
        ctx_ref[cols, :] = both.T.astype(bf16)
        return carry

    lax.fori_loop(0, seq // span, step, 0)


def attend(q, k, v, u):
    seq, width = q.shape
    pairs = width // 128
    blk = pl.BlockSpec((seq, 128), lambda p: (0, p))
    return pl.pallas_call(
        attend_kernel,
        grid=(pairs,),
        in_specs=[blk, blk, blk, pl.BlockSpec((1, 2, 2 * seq), lambda p: (p, 0, 0))],
        out_specs=[
            blk,
            pl.BlockSpec((128, seq), lambda p: (p, 0)),
            pl.BlockSpec((1, 8, seq), lambda p: (p, 0, 0)),
        ],
        out_shape=[
            jax.ShapeDtypeStruct((seq, width), bf16),
            jax.ShapeDtypeStruct((width, seq), f32),
            jax.ShapeDtypeStruct((pairs, 8, seq), f32),
        ],
        scratch_shapes=[
            pltpu.VMEM((2, 128, 2 * seq), f32),
            pltpu.VMEM((128, seq), bf16),
            pltpu.VMEM((128, seq), bf16),
            pltpu.VMEM((2, seq, 256), f32),
            pltpu.VMEM((2, seq, 256), bf16),
        ],
        compiler_params=pltpu.CompilerParams(vmem_limit_bytes=48 << 20),
        cost_estimate=pl.CostEstimate(
            flops=16 * seq * seq * width, bytes_accessed=20 * seq * width, transcendentals=seq * seq * 12
        ),
        name="attend",
    )(q, k, v, u)


def split_rows(row):
    hi = row.astype(bf16).astype(f32)
    mid = (row - hi).astype(bf16).astype(f32)
    low = row - hi - mid
    idx = lax.broadcasted_iota(jnp.int32, (16, row.shape[1]), 0)
    return jnp.where(idx == 0, hi, jnp.where(idx == 1, mid, jnp.where(idx == 2, low, 0.0))).astype(bf16)


def attend_back_kernel(
    q_ref, k_ref, v_ref, g_ref, u_ref, ctxt_ref, lse_ref,
    dq_ref, dk_ref, dv_ref, diag_ref,
    base, acc, kaug, vaug, qaug, gaug, qz, gz, kt, dqt,
):
    seq = q_ref.shape[0]
    span = 256
    lane = lax.broadcasted_iota(jnp.int32, (seq, 128), 1)
    gt = g_ref[...].T
    qtv = q_ref[...].T
    kt[...] = k_ref[...].T
    gtf = gt.astype(f32)
    pad = jnp.zeros((48, seq), bf16)
    one = jnp.ones((seq, 128), bf16)
    nil = jnp.zeros((seq, 128), bf16)
    acc[...] = jnp.zeros_like(acc)
    for head in range(2):
        fill_toeplitz(base, head, u_ref[0, head : head + 1, :])
        own = (lane < 64) if head == 0 else (lane >= 64)
        origin = 64 if head == 0 else 0
        extra = jnp.where((lane >= origin) & (lane < origin + 3), one, nil)
        kaug[head] = jnp.where(own, k_ref[...], extra)
        vaug[head] = jnp.where(own, v_ref[...], extra)
        qz[head] = jnp.where(own, q_ref[...], nil)
        gz[head] = jnp.where(own, g_ref[...], nil)
        rows = slice(64 * head, 64 * head + 64)
        lse = split_rows(-lse_ref[0, head : head + 1, :])
        dsum = split_rows(-jnp.sum(gtf[rows] * ctxt_ref[rows, :], axis=0, keepdims=True))
        for dst, src, aug in ((qaug, qtv, lse), (gaug, gt, dsum)):
            dst[head, rows, :] = src[rows]
            dst[head, origin : origin + 16, :] = aug
            dst[head, origin + 16 : origin + 64, :] = pad

    dqt[...] = jnp.zeros_like(dqt)

    def step(idx, carry):
        rows = pl.ds(pl.multiple_of(idx * span, span), span)
        dv = None
        dk = None
        for head in range(2):
            s = dot_f32(kaug[head, rows, :], qaug[head])
            dp = dot_f32(vaug[head, rows, :], gaug[head])
            tops = []
            grads = []
            for part in range(2):
                offs = pl.ds(pl.multiple_of(seq - span * idx - 128 * part, 128), seq)
                p = jnp.exp(s[128 * part : 128 * part + 128] + base[head, :, offs])
                ds_ = p * dp[128 * part : 128 * part + 128]
                acc[head, :, offs] += ds_
                tops.append(p.astype(bf16))
                grads.append(ds_.astype(bf16))
            p = jnp.concatenate(tops, axis=0)
            ds_ = jnp.concatenate(grads, axis=0)
            now = dot_f32(p, gz[head])
            dv = now if dv is None else dv + now
            now = dot_f32(ds_, qz[head])
            dk = now if dk is None else dk + now
            dqt[64 * head : 64 * head + 64, :] += dot_f32(kt[64 * head : 64 * head + 64, rows], ds_)
        dv_ref[rows, :] = dv.astype(bf16)
        dk_ref[rows, :] = dk.astype(bf16)
        return carry

    lax.fori_loop(0, seq // span, step, 0)
    dq_ref[...] = dqt[...].T.astype(bf16)
    width = 2 * seq
    for head in range(2):
        total = acc[head, 0:8, :]
        for group in range(1, 16):
            total = total + pltpu.roll(acc[head, 8 * group : 8 * group + 8, :], width - 8 * group, 1)
        sub = lax.broadcasted_iota(jnp.int32, (8, width), 0)
        for bit in (1, 2, 4):
            total = jnp.where((sub & bit) != 0, pltpu.roll(total, width - bit, 1), total)
        diag_ref[0, head : head + 1, :] = jnp.sum(total, axis=0, keepdims=True)


def attend_back(q, k, v, g, u, ctxt, lse):
    seq, width = q.shape
    pairs = width // 128
    blk = pl.BlockSpec((seq, 128), lambda p: (0, p))
    return pl.pallas_call(
        attend_back_kernel,
        grid=(pairs,),
        in_specs=[
            blk, blk, blk, blk,
            pl.BlockSpec((1, 2, 2 * seq), lambda p: (p, 0, 0)),
            pl.BlockSpec((128, seq), lambda p: (p, 0)),
            pl.BlockSpec((1, 8, seq), lambda p: (p, 0, 0)),
        ],
        out_specs=[blk, blk, blk, pl.BlockSpec((1, 8, 2 * seq), lambda p: (p, 0, 0))],
        out_shape=[jax.ShapeDtypeStruct((seq, width), bf16)] * 3
        + [jax.ShapeDtypeStruct((pairs, 8, 2 * seq), f32)],
        scratch_shapes=[
            pltpu.VMEM((2, 128, 2 * seq), f32),
            pltpu.VMEM((2, 128, 2 * seq), f32),
            pltpu.VMEM((2, seq, 128), bf16),
            pltpu.VMEM((2, seq, 128), bf16),
            pltpu.VMEM((2, 128, seq), bf16),
            pltpu.VMEM((2, 128, seq), bf16),
            pltpu.VMEM((2, seq, 128), bf16),
            pltpu.VMEM((2, seq, 128), bf16),
            pltpu.VMEM((128, seq), bf16),
            pltpu.VMEM((128, seq), f32),
        ],
        compiler_params=pltpu.CompilerParams(vmem_limit_bytes=56 << 20),
        cost_estimate=pl.CostEstimate(
            flops=40 * seq * seq * width, bytes_accessed=20 * seq * width, transcendentals=seq * seq * 12
        ),
        name="attend_back",
    )(q, k, v, g, u, ctxt, lse)


def gelu_both(v):
    scale = 0.7978845608028654
    square = v * v
    t = jnp.tanh(scale * v * (1.0 + 0.044715 * square))
    half = 0.5 * (1.0 + t)
    slope = half + 0.5 * v * (1.0 - t * t) * (scale * (1.0 + 3 * 0.044715 * square))
    return v * half, slope


def expert_kernel(
    experts, capacity, tile,
    xs, gr_h, win_h, wout_h, rw,
    gback_o, prod_o, dwin_o, dwout_o, drw_o,
    xall, gr, gp, win, wout, act, gpre, gback, gsend, prod, logit, acc_p, acc_g, xt, gpt, stage,
    send_x, recv_x, send_g, recv_g, local, out_sem,
):
    me = lax.axis_index("expert")
    place = me // 2
    chips = experts // 2
    span = 2 * capacity
    width = xall.shape[1]
    hidden = win.shape[1]
    barrier = pltpu.get_barrier_semaphore()
    for k in range(1, experts):
        pl.semaphore_signal(barrier, inc=1, device_id={"expert": lax.rem(me + k, experts)})
    loads = [
        pltpu.make_async_copy(win_h, win, local.at[0]),
        pltpu.make_async_copy(wout_h, wout, local.at[1]),
        pltpu.make_async_copy(gr_h, gr, local.at[2]),
    ]
    rows_of = lambda who: pl.ds(pl.multiple_of(who * capacity, 16), capacity)
    own = pltpu.make_async_copy(xs.at[rows_of(me), :], xall.at[rows_of(me), :], local.at[3])
    own.start()
    for copy in loads:
        copy.start()
    pl.semaphore_wait(barrier, experts - 1)

    def partner(step):
        flip = lax.rem(chips - step, chips)
        high, low = place // 2, lax.rem(place, 2)
        fhigh, flow = flip // 2, lax.rem(flip, 2)
        return 2 * (high + fhigh - 2 * high * fhigh) + low + flow - 2 * low * flow

    def send_rows(peer):
        return pltpu.make_async_remote_copy(
            src_ref=xs.at[rows_of(peer), :], dst_ref=xall.at[rows_of(me), :],
            send_sem=send_x.at[peer], recv_sem=recv_x.at[me], device_id={"expert": peer},
        )

    def got_rows(peer):
        return pltpu.make_async_remote_copy(
            src_ref=xs.at[rows_of(peer), :], dst_ref=xall.at[rows_of(peer), :],
            send_sem=send_x.at[peer], recv_sem=recv_x.at[peer], device_id={"expert": peer},
        )

    def send_back(peer):
        return pltpu.make_async_remote_copy(
            src_ref=gsend.at[rows_of(peer), :], dst_ref=gback.at[rows_of(me), :],
            send_sem=send_g.at[peer], recv_sem=recv_g.at[me], device_id={"expert": peer},
        )

    def got_back(peer):
        return pltpu.make_async_remote_copy(
            src_ref=gsend.at[rows_of(peer), :], dst_ref=gback.at[rows_of(peer), :],
            send_sem=send_g.at[peer], recv_sem=recv_g.at[peer], device_id={"expert": peer},
        )

    sibling = me + 1 - 2 * lax.rem(me, 2)
    send_rows(sibling).start()
    for step in range(1, chips):
        for core in range(2):
            send_rows(2 * partner(step) + lax.rem(me + core, 2)).start()
    for copy in loads:
        copy.wait()

    lanes = lax.broadcasted_iota(jnp.int32, (span, rw.shape[1]), 1)
    mine = jnp.where(lanes == me, 1.0, 0.0)

    def work(step, carry):
        where = partner(step)
        base = pl.multiple_of(where * span, 32)

        @pl.when(step == 0)
        def _():
            own.wait()
            got_rows(sibling).wait_recv()

        @pl.when(step > 0)
        def _():
            got_rows(2 * where).wait_recv()
            got_rows(2 * where + 1).wait_recv()

        rows = pl.ds(base, span)
        x = xall[rows, :]
        logits = jnp.where(lanes < experts, dot_f32(x, rw[...]), -1e30)
        weights = jnp.exp(logits - jnp.max(logits, axis=-1, keepdims=True))
        probs = weights / jnp.sum(weights, axis=-1, keepdims=True)
        gate = jnp.sum(probs * mine, axis=-1, keepdims=True)
        gp[rows, :] = (gr[rows, :].astype(f32) * gate).astype(bf16)
        acc_p[...] = jnp.zeros_like(acc_p)
        acc_g[...] = jnp.zeros_like(acc_g)

        def block(idx, carry):
            cols = pl.ds(pl.multiple_of(idx * tile, tile), tile)
            h = dot_f32(xall[rows, :], win[:, cols])
            grad = dot_nt(gp[rows, :], wout[cols, :])
            value, slope = gelu_both(h)
            value = value.astype(bf16)
            grad = (grad * slope).astype(bf16)
            act[rows, cols] = value
            gpre[rows, cols] = grad
            acc_p[...] += dot_f32(value, wout[cols, :])
            acc_g[...] += dot_nt(grad, win[:, cols])
            return carry

        lax.fori_loop(0, hidden // tile, block, 0)
        made = acc_p[...].astype(bf16)
        prod[rows, :] = made
        gate_grad = jnp.sum(gr[rows, :].astype(f32) * made.astype(f32), axis=-1, keepdims=True)
        low = (gate_grad * gate * (mine - probs)).astype(bf16)
        low = jnp.where(lanes < experts, low, jnp.zeros_like(low))
        logit[rows, :] = low
        gsend[rows, :] = (acc_g[...] + dot_nt(low, rw[...])).astype(bf16)

        @pl.when(step == 0)
        def _():
            send_back(sibling).start()

        @pl.when(step > 0)
        def _():
            send_back(2 * where).start()
            send_back(2 * where + 1).start()

        return carry

    lax.fori_loop(0, chips, work, 0)
    outs = [
        pltpu.make_async_copy(prod, prod_o, local.at[0]),
        pltpu.make_async_copy(gsend.at[rows_of(me), :], gback.at[rows_of(me), :], local.at[3]),
    ]
    for copy in outs:
        copy.start()
    xt[...] = xall[...].T
    gpt[...] = gp[...].T
    drw_o[...] = dot_f32(xt[...], logit[...])

    def weight_block(idx, carry):
        cols = pl.ds(pl.multiple_of(idx * tile, tile), tile)

        def put(slot, out):
            return pltpu.make_async_copy(stage.at[slot], out.at[:, cols], out_sem.at[slot])

        for slot, (left, right, out) in enumerate(((gpt, act, dwout_o), (xt, gpre, dwin_o))):
            @pl.when(idx > 0)
            def _():
                put(slot, out).wait()

            stage[slot] = dot_f32(left[...], right[:, cols]).astype(bf16)
            put(slot, out).start()
        return carry

    lax.fori_loop(0, hidden // tile, weight_block, 0)
    for slot, out in enumerate((dwout_o, dwin_o)):
        pltpu.make_async_copy(stage.at[slot], out.at[:, 0:tile], out_sem.at[slot]).wait()
    for copy in outs:
        copy.wait()
    for k in range(1, experts):
        peer = lax.rem(me + k, experts)
        got_rows(peer).wait_send()
        got_back(peer).wait_send()
        got_back(peer).wait_recv()
    back = pltpu.make_async_copy(gback, gback_o, local.at[1])
    back.start()
    back.wait()


def expert_pass(xs, gr, weight_in, weight_out, router_pad, experts, capacity):
    slots, width = xs.shape
    hidden = weight_in.shape[1]
    tile = 512
    span = 2 * capacity
    hbm = pl.BlockSpec(memory_space=pl.ANY)
    vmem = pl.BlockSpec(memory_space=pltpu.VMEM)
    return pl.pallas_call(
        functools.partial(expert_kernel, experts, capacity, tile),
        in_specs=[hbm, hbm, hbm, hbm, vmem],
        out_specs=[hbm, hbm, hbm, hbm, vmem],
        out_shape=[
            jax.ShapeDtypeStruct((slots, width), bf16),
            jax.ShapeDtypeStruct((slots, width), bf16),
            jax.ShapeDtypeStruct((width, hidden), bf16),
            jax.ShapeDtypeStruct((width, hidden), bf16),
            jax.ShapeDtypeStruct((width, router_pad.shape[1]), f32),
        ],
        scratch_shapes=[
            pltpu.VMEM((slots, width), bf16),
            pltpu.VMEM((slots, width), bf16),
            pltpu.VMEM((slots, width), bf16),
            pltpu.VMEM((width, hidden), bf16),
            pltpu.VMEM((hidden, width), bf16),
            pltpu.VMEM((slots, hidden), bf16),
            pltpu.VMEM((slots, hidden), bf16),
            pltpu.VMEM((slots, width), bf16),
            pltpu.VMEM((slots, width), bf16),
            pltpu.VMEM((slots, width), bf16),
            pltpu.VMEM((slots, router_pad.shape[1]), bf16),
            pltpu.VMEM((span, width), f32),
            pltpu.VMEM((span, width), f32),
            pltpu.VMEM((width, slots), bf16),
            pltpu.VMEM((width, slots), bf16),
            pltpu.VMEM((2, width, tile), bf16),
            pltpu.SemaphoreType.DMA((experts,)),
            pltpu.SemaphoreType.DMA((experts,)),
            pltpu.SemaphoreType.DMA((experts,)),
            pltpu.SemaphoreType.DMA((experts,)),
            pltpu.SemaphoreType.DMA((4,)),
            pltpu.SemaphoreType.DMA((2,)),
        ],
        compiler_params=pltpu.CompilerParams(
            vmem_limit_bytes=60 << 20, collective_id=1, has_side_effects=True
        ),
        cost_estimate=pl.CostEstimate(
            flops=12 * slots * width * hidden, bytes_accessed=8 * width * hidden, transcendentals=slots * hidden
        ),
        name="experts",
    )(xs, gr, weight_in, weight_out, router_pad)


def remote(src, dst, send_sem, recv_sem, axis, peer):
    return pltpu.make_async_remote_copy(
        src_ref=src, dst_ref=dst, send_sem=send_sem, recv_sem=recv_sem, device_id={axis: peer}
    )


def tail_kernel(
    groups, experts,
    tok, gain, nl, dq, dk, dv, wq, wk, wv, ghid, dwo, small,
    wout_o, ing_o, small_o,
    part, r1, s1, r2, r3, s3, g4, full, nt, sbuf, srecv, sone, stwo,
    send1, recv1, send2, recv2, send3, recv3, send4, recv4, send5, recv5, send6, recv6, send7, recv7,
):
    me = lax.axis_index("expert")
    my_dp = lax.axis_index("dp")
    core = lax.rem(me, 2)
    place = me // 2
    chips = experts // 2
    sibling = me + 1 - 2 * core
    width = part.shape[2]
    half = width // 2
    piece = half // groups
    barrier = pltpu.get_barrier_semaphore()
    for k in range(1, experts):
        pl.semaphore_signal(barrier, inc=1, device_id={"expert": lax.rem(me + k, experts)})
    for k in range(1, groups):
        pl.semaphore_signal(barrier, inc=1, device_id={"dp": lax.rem(my_dp + k, groups)})

    def half_rows(which):
        return pl.ds(pl.multiple_of(which * half, 16), half)

    def piece_rows(which):
        return pl.ds(pl.multiple_of(which * piece, 16), piece)

    def copy1(c):
        return remote(part.at[c, half_rows(1 - core), :], r1.at[c], send1.at[c], recv1.at[c], "expert", sibling)

    def copy2(c, peer, slot):
        return remote(s1.at[c, piece_rows(peer), :], r2.at[c, slot], send2.at[c, peer], recv2.at[c, slot], "dp", peer)

    def copy3(c, peer, slot):
        return remote(
            r3.at[c, place], r3.at[c, slot], send3.at[c, peer], recv3.at[c, slot], "expert", 2 * peer + core
        )

    def copy4(c, peer, slot):
        return remote(
            g4.at[c, piece_rows(my_dp), :], g4.at[c, piece_rows(slot), :],
            send4.at[c, peer], recv4.at[c, slot], "dp", peer,
        )

    def copy5(c):
        return remote(
            full.at[c, half_rows(core), :], full.at[c, half_rows(core), :], send5.at[c], recv5.at[c], "expert", sibling
        )

    def got5(c):
        return remote(
            full.at[c, half_rows(1 - core), :], full.at[c, half_rows(1 - core), :],
            send5.at[c], recv5.at[c], "expert", sibling,
        )

    def others(count, mine):
        return [lax.rem(mine + k, count) for k in range(1, count)]

    def stage1(c):
        copy1(c).start()

    def stage2(c):
        copy1(c).wait_recv()
        s1[c] = (part[c, half_rows(core), :].astype(f32) + r1[c].astype(f32)).astype(bf16)
        for peer in others(groups, my_dp):
            copy2(c, peer, my_dp).start()

    def stage3(c):
        total = s1[c, piece_rows(my_dp), :].astype(f32)
        for peer in others(groups, my_dp):
            copy2(c, peer, peer).wait_recv()
            total = total + r2[c, peer].astype(f32)
        r3[c, place] = total.astype(bf16)
        for peer in others(chips, place):
            copy3(c, peer, place).start()

    def stage4(c):
        for peer in others(chips, place):
            copy3(c, peer, peer).wait_recv()
        total = r3[c, 0].astype(f32)
        for slot in range(1, chips):
            total = total + r3[c, slot].astype(f32)
        g4[c, piece_rows(my_dp), :] = total.astype(bf16)
        for peer in others(groups, my_dp):
            copy4(c, peer, my_dp).start()

    def stage5(c):
        for peer in others(groups, my_dp):
            copy4(c, peer, peer).wait_recv()
        full[c, half_rows(core), :] = g4[c]
        copy5(c).start()

    def stage6(c):
        got5(c).wait_recv()
        wout_o[c] = full[c]

    def finish(c):
        copy1(c).wait_send()
        for peer in others(groups, my_dp):
            copy2(c, peer, my_dp).wait_send()
            copy4(c, peer, my_dp).wait_send()
        for peer in others(chips, place):
            copy3(c, peer, place).wait_send()
        copy5(c).wait_send()

    def weight_grad(c, grad):
        def block(idx, carry):
            rows = pl.ds(pl.multiple_of(idx * 256, 256), 256)
            part[c, rows, :] = dot_f32(nt[rows, :], grad[...]).astype(bf16)
            return carry

        lax.fori_loop(0, width // 256, block, 0)

    rows_total = tok.shape[0]
    part[0] = dwo[...]
    nt[...] = nl[...].T
    pl.semaphore_wait(barrier, experts + groups - 2)
    stage1(0)
    weight_grad(1, dq)
    stage1(1)
    stage2(0)
    weight_grad(2, dk)
    stage1(2)
    stage2(1)
    stage3(0)
    weight_grad(3, dv)
    stage1(3)
    stage2(2)
    stage3(1)
    stage4(0)

    def token_block(idx, carry):
        rows = pl.ds(pl.multiple_of(idx * 256, 256), 256)
        grad = dot_nt(dq[rows, :], wq[...]) + dot_nt(dk[rows, :], wk[...]) + dot_nt(dv[rows, :], wv[...])
        values = tok[rows, :].astype(f32)
        scale = lax.rsqrt(jnp.mean(values * values, axis=-1, keepdims=True) + epsilon)
        weighted = grad * gain[...]
        inner = jnp.mean(weighted * values, axis=-1, keepdims=True)
        ing_o[rows, :] = ghid[rows, :] + scale * weighted - values * (scale * scale * scale * inner)
        return carry + jnp.sum(grad * values * scale, axis=0, keepdims=True)

    gain_grad = jnp.zeros((1, width), f32)
    gain_grad = lax.fori_loop(0, rows_total // 512, token_block, gain_grad)
    stage2(3)
    stage3(2)
    stage4(1)
    stage5(0)
    gain_grad = lax.fori_loop(rows_total // 512, rows_total // 256, token_block, gain_grad)

    sbuf[...] = small[...]
    sbuf[0:1, :] = gain_grad
    srecv[me] = sbuf[...]

    def copy6(peer, slot):
        return remote(sbuf, srecv.at[slot], send6.at[peer], recv6.at[slot], "expert", peer)

    def copy7(peer, slot):
        return remote(sone, stwo.at[slot], send7.at[peer], recv7.at[slot], "dp", peer)

    for peer in others(experts, me):
        copy6(peer, me).start()
    stage3(3)
    stage4(2)
    stage5(1)
    stage6(0)
    for peer in others(experts, me):
        copy6(peer, peer).wait_recv()
    total = srecv[0]
    for slot in range(1, experts):
        total = total + srecv[slot]
    sone[...] = total
    stwo[my_dp] = total
    for peer in others(groups, my_dp):
        copy7(peer, my_dp).start()
    stage4(3)
    stage5(2)
    stage6(1)
    stage5(3)
    stage6(2)
    for peer in others(groups, my_dp):
        copy7(peer, peer).wait_recv()
    total = stwo[0]
    for slot in range(1, groups):
        total = total + stwo[slot]
    small_o[...] = total
    stage6(3)
    for c in range(4):
        finish(c)
    for peer in others(experts, me):
        copy6(peer, me).wait_send()
    for peer in others(groups, my_dp):
        copy7(peer, my_dp).wait_send()


def tail(tokens, gain, normed_low, dq, dk, dv, wq, wk, wv, grad_hidden, dwo, small, groups, experts):
    rows, width = tokens.shape
    half = width // 2
    piece = half // groups
    chips = experts // 2
    vmem = pl.BlockSpec(memory_space=pltpu.VMEM)
    dma = pltpu.SemaphoreType.DMA
    return pl.pallas_call(
        functools.partial(tail_kernel, groups, experts),
        in_specs=[vmem] * 12,
        out_specs=[vmem] * 3,
        out_shape=[
            jax.ShapeDtypeStruct((4, width, width), bf16),
            jax.ShapeDtypeStruct((rows, width), f32),
            jax.ShapeDtypeStruct(small.shape, f32),
        ],
        scratch_shapes=[
            pltpu.VMEM((4, width, width), bf16),
            pltpu.VMEM((4, half, width), bf16),
            pltpu.VMEM((4, half, width), bf16),
            pltpu.VMEM((4, groups, piece, width), bf16),
            pltpu.VMEM((4, chips, piece, width), bf16),
            pltpu.VMEM((4, piece, width), bf16),
            pltpu.VMEM((4, half, width), bf16),
            pltpu.VMEM((4, width, width), bf16),
            pltpu.VMEM((width, rows), bf16),
            pltpu.VMEM(small.shape, f32),
            pltpu.VMEM((experts,) + small.shape, f32),
            pltpu.VMEM(small.shape, f32),
            pltpu.VMEM((groups,) + small.shape, f32),
            dma((4,)), dma((4,)),
            dma((4, groups)), dma((4, groups)),
            dma((4, chips)), dma((4, chips)),
            dma((4, groups)), dma((4, groups)),
            dma((4,)), dma((4,)),
            dma((experts,)), dma((experts,)),
            dma((groups,)), dma((groups,)),
        ],
        compiler_params=pltpu.CompilerParams(
            vmem_limit_bytes=60 << 20, collective_id=2, has_side_effects=True
        ),
        cost_estimate=pl.CostEstimate(
            flops=12 * rows * width * width, bytes_accessed=20 * rows * width, transcendentals=rows
        ),
        name="tail",
    )(tokens, gain, normed_low, dq, dk, dv, wq, wk, wv, grad_hidden, dwo, small)


def rms_backward(grad_norm, values, row_scale, gain_vec):
    weighted = grad_norm * gain_vec
    gain_grad = jnp.sum(grad_norm * values * row_scale, axis=0)
    grad_in = row_scale * weighted - values * row_scale**3 * jnp.mean(
        weighted * values, axis=-1, keepdims=True
    )
    return grad_in, gain_grad


def rms_forward(values, gain_vec):
    row_scale = lax.rsqrt(jnp.mean(values * values, axis=-1, keepdims=True) + epsilon)
    return values * row_scale * gain_vec, row_scale


def gelu_tanh(values):
    return jax.nn.gelu(values, approximate=True)


def contract(left, right, dims):
    return lax.dot_general(left, right, (((dims[0],), (dims[1],)), ((), ())), preferred_element_type=f32)


def exchange(rows, experts):
    slots, width = rows.shape
    rows = rows.reshape(experts, slots // experts, width)
    return lax.all_to_all(rows, "expert", split_axis=0, concat_axis=0, tiled=True).reshape(slots, width)


def expert_native(send, grad_recv, weight_in, weight_out, router_w, experts):
    received = exchange(send, experts)
    own = lax.axis_index("expert")
    own_hot = (jnp.arange(experts, dtype=jnp.int32) == own).astype(f32)[None, :]
    probs = jax.nn.softmax(contract(received, router_w, (1, 0)), axis=-1)
    gate = jnp.sum(probs * own_hot, axis=-1, keepdims=True)
    grad_recv_f = grad_recv.astype(f32)
    grad_produced = (grad_recv_f * gate).astype(bf16)
    preact = contract(received, weight_in, (1, 0))
    gelu_values, gelu_pullback = jax.vjp(gelu_tanh, preact)
    active = gelu_values.astype(bf16)
    produced = contract(active, weight_out, (1, 0)).astype(bf16)
    gate_grad = jnp.sum(grad_recv_f * produced.astype(f32), axis=-1, keepdims=True)
    logit_low = (gate_grad * gate * (own_hot - probs)).astype(bf16)
    grad_active = contract(grad_produced, weight_out, (1, 1))
    grad_preact = gelu_pullback(grad_active)[0].astype(bf16)
    grad_received = contract(grad_preact, weight_in, (1, 1)) + contract(logit_low, router_w, (1, 1))
    grad_rows = exchange(grad_received.astype(bf16), experts)
    in_grad = contract(received, grad_preact, (0, 0)).astype(bf16)
    out_grad_t = contract(grad_produced, active, (0, 0)).astype(bf16)
    router_grad = contract(received, logit_low, (0, 0))
    return grad_rows, produced, in_grad, out_grad_t, router_grad


def tail_native(tokens, gain, normed_low, dq, dk, dv, wq, wk, wv, grad_hidden, dwo, small):
    tokens_f = tokens.astype(f32)
    grads = jnp.stack([dwo.astype(f32)] + [contract(normed_low, d, (0, 0)) for d in (dq, dk, dv)])
    grad_normed = contract(dq, wq, (1, 1)) + contract(dk, wk, (1, 1)) + contract(dv, wv, (1, 1))
    _, scale = rms_forward(tokens_f, gain)
    grad_tokens, gain_grad = rms_backward(grad_normed, tokens_f, scale, gain)
    small = jnp.concatenate([gain_grad[None], small[1:]])
    grads, small = lax.psum((grads, small), ("dp", "expert"))
    return grads, grad_hidden + grad_tokens, small


def on_device(
    tokens, gain_one, query_w, key_w, value_w, out_w, rel_table, gain_two, router_w,
    expert_in, expert_out, routes, buckets, cotangent,
):
    seq_len, width = tokens.shape
    heads = rel_table.shape[1]
    groups = lax.axis_size("dp")
    experts = lax.axis_size("expert")
    capacity = (5 * seq_len + 4 * experts - 1) // (4 * experts)
    slots = experts * capacity
    weight_in = expert_in[0]
    weight_out = expert_out[0]
    kernels = capacity % 16 == 0 and experts == 8 and groups == 4

    route_ids = routes[:, 0]
    route_hot = route_ids[:, None] == jnp.arange(experts, dtype=jnp.int32)[None, :]
    route_int = route_hot.astype(jnp.int32)
    route_float = route_hot.astype(f32)
    position = jnp.sum((jnp.cumsum(route_int, axis=0) - 1) * route_int, axis=1)
    slot_index = jnp.where(position < capacity, route_ids * capacity + position, slots)
    pick = (jnp.arange(slots, dtype=jnp.int32)[:, None] == slot_index[None, :]).astype(bf16)

    def scatter_rows(rows):
        return contract(pick, rows, (1, 0)).astype(bf16)

    def gather_rows(rows):
        return contract(pick, rows, (0, 0))

    grad_recv = exchange(scatter_rows(cotangent), experts)

    tokens_f = tokens.astype(f32)
    normed, scale_one = rms_forward(tokens_f, gain_one)
    normed_low = normed.astype(bf16)
    queries = contract(normed_low, query_w, (1, 0)).astype(bf16)
    key_rows = contract(normed_low, key_w, (1, 0)).astype(bf16)
    value_rows = contract(normed_low, value_w, (1, 0)).astype(bf16)
    reach = jnp.concatenate([buckets, jnp.full((1,), -1, jnp.int32)])[::-1]
    bucket_hot = (jnp.arange(rel_table.shape[0], dtype=jnp.int32)[:, None] == reach[None, :]).astype(f32)
    spread = jnp.einsum("bh,bx->hx", rel_table, bucket_hot, precision=highest)
    spread = spread.reshape(heads // 2, 2, 2 * seq_len)
    context, context_t, logsum = attend(queries, key_rows, value_rows, spread)
    context, grad_recv = lax.optimization_barrier((context, grad_recv))
    hidden = tokens_f + contract(context, out_w, (1, 0))
    normed_two, scale_two = rms_forward(hidden, gain_two)
    normed_two_low = normed_two.astype(bf16)

    send = scatter_rows(normed_two_low)
    if kernels:
        router_pad = jnp.pad(router_w, ((0, 0), (0, 128 - experts)))
        grad_rows, produced, in_grad, out_grad_t, router_grad = expert_pass(
            send, grad_recv, weight_in, weight_out, router_pad, experts, capacity
        )
        router_grad = router_grad[:, :experts]
    else:
        grad_rows, produced, in_grad, out_grad_t, router_grad = expert_native(
            send, grad_recv, weight_in, weight_out, router_w, experts
        )
    returned = exchange(produced, experts)
    in_share = lax.psum_scatter(in_grad, "dp", scatter_dimension=0, tiled=True).astype(f32)
    out_share = lax.psum_scatter(out_grad_t, "dp", scatter_dimension=0, tiled=True).astype(f32).T

    router_probs = jax.nn.softmax(contract(normed_two_low, router_w, (1, 0)), axis=-1)
    gate_value = jnp.sum(router_probs * route_float, axis=-1, keepdims=True)
    output = (hidden + gate_value * gather_rows(returned)).astype(bf16)

    grad_out = cotangent.astype(f32)
    grad_normed_two = gather_rows(grad_rows)
    grad_hidden_norm, gain_two_grad = rms_backward(grad_normed_two, hidden, scale_two, gain_two)
    grad_hidden = grad_out + grad_hidden_norm
    branch_low = grad_hidden.astype(bf16)
    out_w_grad = contract(context, branch_low, (0, 0)).astype(bf16)
    grad_context = contract(branch_low, out_w, (1, 1)).astype(bf16)
    query_grad, key_grad, value_grad, diagonals = attend_back(
        queries, key_rows, value_rows, grad_context, spread, context_t, logsum
    )
    diagonals = diagonals[:, :2].reshape(heads, 2 * seq_len)
    rel_grad = jnp.einsum("bx,hx->bh", bucket_hot, diagonals, precision=highest)
    rel_flat = rel_grad.reshape(1, -1)
    small = jnp.concatenate(
        [
            jnp.zeros((1, width), f32),
            gain_two_grad[None],
            jnp.pad(rel_flat, ((0, 5), (0, width - rel_flat.shape[1]))),
            router_grad.T,
        ]
    )
    run = functools.partial(tail, groups=groups, experts=experts) if kernels else tail_native
    grads, input_grad, small = run(
        tokens, gain_one[None], normed_low, query_grad, key_grad, value_grad,
        query_w, key_w, value_w, grad_hidden, out_w_grad, small,
    )
    grads = grads.astype(f32)
    rel_grad = small[2, : rel_flat.shape[1]].reshape(rel_grad.shape)
    router_grad = small[8:].T
    return (
        output, input_grad, grads[1], grads[2], grads[3], grads[0], rel_grad,
        small[0], small[1], router_grad, in_share[None], out_share[None],
    )


def solution(mesh):
    rows = P(("dp", "expert"), None)
    whole = P()
    split = P("expert", None, None)
    return jax.shard_map(
        on_device,
        mesh=mesh,
        in_specs=(
            rows, whole, whole, whole, whole, whole, whole, whole, whole, split, split, rows, whole, rows,
        ),
        out_specs=(
            rows, rows, whole, whole, whole, whole, whole, whole, whole, whole,
            P("expert", "dp", None), P("expert", None, "dp"),
        ),
        check_vma=False,
    )
```

```python
import functools

import jax
import jax.numpy as jnp
from jax import lax
from jax.experimental import pallas as pl
from jax.experimental.pallas import tpu as pltpu
from jax.sharding import PartitionSpec as P

bf16 = jnp.bfloat16
f32 = jnp.float32
epsilon = 1e-06
highest = lax.Precision.HIGHEST

def dot_f32(left, right):
    return lax.dot_general(left, right, (((1,), (0,)), ((), ())), preferred_element_type=f32)


def dot_nt(left, right):
    return lax.dot_general(left, right, (((1,), (1,)), ((), ())), preferred_element_type=f32)


def fill_toeplitz(base_ref, head, row):
    rows, width = base_ref.shape[1:]
    spread = jnp.broadcast_to(row, (8, width))
    eight = pltpu.roll(spread, 0, 1, stride=1, stride_axis=0)
    for group in range(rows // 8):
        base_ref[head, 8 * group : 8 * group + 8, :] = (
            eight if group == 0 else pltpu.roll(eight, 8 * group, 1)
        )


def attend_kernel(q_ref, k_ref, v_ref, u_ref, ctx_ref, ctxt_ref, lse_ref, base, qt, vt, s_scr, p_scr):
    seq = q_ref.shape[0]
    span = 256
    half = seq
    qt[...] = q_ref[...].T
    vt[...] = v_ref[...].T
    for head in range(2):
        fill_toeplitz(base, head, u_ref[0, head : head + 1, :])
    zeros = jnp.zeros((64, span), bf16)

    def step(idx, carry):
        cols = pl.ds(pl.multiple_of(idx * span, span), span)
        outs = []
        for head in range(2):
            part = qt[64 * head : 64 * head + 64, cols]
            rhs = jnp.concatenate([part, zeros] if head == 0 else [zeros, part], axis=0)
            peak = None
            for kb in range(seq // 128):
                rows = slice(128 * kb, 128 * kb + 128)
                offs = pl.multiple_of(half + span * idx - 128 * kb, 128)
                s = dot_f32(k_ref[rows, :], rhs) + base[head, :, pl.ds(offs, span)]
                s_scr[head, rows, :] = s
                now = jnp.max(s.reshape(16, 8, span), axis=0)
                peak = now if peak is None else jnp.maximum(peak, now)
            peak = jnp.max(peak, axis=0, keepdims=True)
            total = None
            for kb in range(seq // 128):
                rows = slice(128 * kb, 128 * kb + 128)
                e = jnp.exp(s_scr[head, rows, :] - peak)
                s_scr[head, rows, :] = e
                now = jnp.sum(e.reshape(16, 8, span), axis=0)
                total = now if total is None else total + now
            total = jnp.sum(total, axis=0, keepdims=True)
            inv = 1.0 / total
            for kb in range(seq // 128):
                rows = slice(128 * kb, 128 * kb + 128)
                p_scr[head, rows, :] = (s_scr[head, rows, :] * inv).astype(bf16)
            lse_ref[0, head : head + 1, cols] = peak + jnp.log(total)
            outs.append(dot_f32(vt[64 * head : 64 * head + 64, :], p_scr[head]))
        both = jnp.concatenate(outs, axis=0)
        ctxt_ref[:, cols] = both
        ctx_ref[cols, :] = both.T.astype(bf16)
        return carry

    lax.fori_loop(0, seq // span, step, 0)


def attend(q, k, v, u):
    seq, width = q.shape
    pairs = width // 128
    blk = pl.BlockSpec((seq, 128), lambda p: (0, p))
    return pl.pallas_call(
        attend_kernel,
        grid=(pairs,),
        in_specs=[blk, blk, blk, pl.BlockSpec((1, 2, 2 * seq), lambda p: (p, 0, 0))],
        out_specs=[
            blk,
            pl.BlockSpec((128, seq), lambda p: (p, 0)),
            pl.BlockSpec((1, 8, seq), lambda p: (p, 0, 0)),
        ],
        out_shape=[
            jax.ShapeDtypeStruct((seq, width), bf16),
            jax.ShapeDtypeStruct((width, seq), f32),
            jax.ShapeDtypeStruct((pairs, 8, seq), f32),
        ],
        scratch_shapes=[
            pltpu.VMEM((2, 128, 2 * seq), f32),
            pltpu.VMEM((128, seq), bf16),
            pltpu.VMEM((128, seq), bf16),
            pltpu.VMEM((2, seq, 256), f32),
            pltpu.VMEM((2, seq, 256), bf16),
        ],
        compiler_params=pltpu.CompilerParams(vmem_limit_bytes=48 << 20),
        cost_estimate=pl.CostEstimate(
            flops=16 * seq * seq * width, bytes_accessed=20 * seq * width, transcendentals=seq * seq * 12
        ),
        name="attend",
    )(q, k, v, u)


def split_rows(row):
    hi = row.astype(bf16).astype(f32)
    mid = (row - hi).astype(bf16).astype(f32)
    low = row - hi - mid
    idx = lax.broadcasted_iota(jnp.int32, (16, row.shape[1]), 0)
    return jnp.where(idx == 0, hi, jnp.where(idx == 1, mid, jnp.where(idx == 2, low, 0.0))).astype(bf16)


def attend_back_kernel(
    q_ref, k_ref, v_ref, g_ref, u_ref, ctxt_ref, lse_ref,
    dq_ref, dk_ref, dv_ref, diag_ref,
    base, acc, kaug, vaug, qaug, gaug, qz, gz, kt, dqt,
):
    seq = q_ref.shape[0]
    span = 256
    lane = lax.broadcasted_iota(jnp.int32, (seq, 128), 1)
    gt = g_ref[...].T
    qtv = q_ref[...].T
    kt[...] = k_ref[...].T
    gtf = gt.astype(f32)
    pad = jnp.zeros((48, seq), bf16)
    one = jnp.ones((seq, 128), bf16)
    nil = jnp.zeros((seq, 128), bf16)
    acc[...] = jnp.zeros_like(acc)
    for head in range(2):
        fill_toeplitz(base, head, u_ref[0, head : head + 1, :])
        own = (lane < 64) if head == 0 else (lane >= 64)
        origin = 64 if head == 0 else 0
        extra = jnp.where((lane >= origin) & (lane < origin + 3), one, nil)
        kaug[head] = jnp.where(own, k_ref[...], extra)
        vaug[head] = jnp.where(own, v_ref[...], extra)
        qz[head] = jnp.where(own, q_ref[...], nil)
        gz[head] = jnp.where(own, g_ref[...], nil)
        rows = slice(64 * head, 64 * head + 64)
        lse = split_rows(-lse_ref[0, head : head + 1, :])
        dsum = split_rows(-jnp.sum(gtf[rows] * ctxt_ref[rows, :], axis=0, keepdims=True))
        for dst, src, aug in ((qaug, qtv, lse), (gaug, gt, dsum)):
            dst[head, rows, :] = src[rows]
            dst[head, origin : origin + 16, :] = aug
            dst[head, origin + 16 : origin + 64, :] = pad

    dqt[...] = jnp.zeros_like(dqt)

    def step(idx, carry):
        rows = pl.ds(pl.multiple_of(idx * span, span), span)
        dv = None
        dk = None
        for head in range(2):
            s = dot_f32(kaug[head, rows, :], qaug[head])
            dp = dot_f32(vaug[head, rows, :], gaug[head])
            tops = []
            grads = []
            for part in range(2):
                offs = pl.ds(pl.multiple_of(seq - span * idx - 128 * part, 128), seq)
                p = jnp.exp(s[128 * part : 128 * part + 128] + base[head, :, offs])
                ds_ = p * dp[128 * part : 128 * part + 128]
                acc[head, :, offs] += ds_
                tops.append(p.astype(bf16))
                grads.append(ds_.astype(bf16))
            p = jnp.concatenate(tops, axis=0)
            ds_ = jnp.concatenate(grads, axis=0)
            now = dot_f32(p, gz[head])
            dv = now if dv is None else dv + now
            now = dot_f32(ds_, qz[head])
            dk = now if dk is None else dk + now
            dqt[64 * head : 64 * head + 64, :] += dot_f32(kt[64 * head : 64 * head + 64, rows], ds_)
        dv_ref[rows, :] = dv.astype(bf16)
        dk_ref[rows, :] = dk.astype(bf16)
        return carry

    lax.fori_loop(0, seq // span, step, 0)
    dq_ref[...] = dqt[...].T.astype(bf16)
    width = 2 * seq
    for head in range(2):
        total = acc[head, 0:8, :]
        for group in range(1, 16):
            total = total + pltpu.roll(acc[head, 8 * group : 8 * group + 8, :], width - 8 * group, 1)
        sub = lax.broadcasted_iota(jnp.int32, (8, width), 0)
        for bit in (1, 2, 4):
            total = jnp.where((sub & bit) != 0, pltpu.roll(total, width - bit, 1), total)
        diag_ref[0, head : head + 1, :] = jnp.sum(total, axis=0, keepdims=True)


def attend_back(q, k, v, g, u, ctxt, lse):
    seq, width = q.shape
    pairs = width // 128
    blk = pl.BlockSpec((seq, 128), lambda p: (0, p))
    return pl.pallas_call(
        attend_back_kernel,
        grid=(pairs,),
        in_specs=[
            blk, blk, blk, blk,
            pl.BlockSpec((1, 2, 2 * seq), lambda p: (p, 0, 0)),
            pl.BlockSpec((128, seq), lambda p: (p, 0)),
            pl.BlockSpec((1, 8, seq), lambda p: (p, 0, 0)),
        ],
        out_specs=[blk, blk, blk, pl.BlockSpec((1, 8, 2 * seq), lambda p: (p, 0, 0))],
        out_shape=[jax.ShapeDtypeStruct((seq, width), bf16)] * 3
        + [jax.ShapeDtypeStruct((pairs, 8, 2 * seq), f32)],
        scratch_shapes=[
            pltpu.VMEM((2, 128, 2 * seq), f32),
            pltpu.VMEM((2, 128, 2 * seq), f32),
            pltpu.VMEM((2, seq, 128), bf16),
            pltpu.VMEM((2, seq, 128), bf16),
            pltpu.VMEM((2, 128, seq), bf16),
            pltpu.VMEM((2, 128, seq), bf16),
            pltpu.VMEM((2, seq, 128), bf16),
            pltpu.VMEM((2, seq, 128), bf16),
            pltpu.VMEM((128, seq), bf16),
            pltpu.VMEM((128, seq), f32),
        ],
        compiler_params=pltpu.CompilerParams(vmem_limit_bytes=56 << 20),
        cost_estimate=pl.CostEstimate(
            flops=40 * seq * seq * width, bytes_accessed=20 * seq * width, transcendentals=seq * seq * 12
        ),
        name="attend_back",
    )(q, k, v, g, u, ctxt, lse)


def gelu_both(v):
    scale = 0.7978845608028654
    square = v * v
    t = jnp.tanh(scale * v * (1.0 + 0.044715 * square))
    half = 0.5 * (1.0 + t)
    slope = half + 0.5 * v * (1.0 - t * t) * (scale * (1.0 + 3 * 0.044715 * square))
    return v * half, slope


def expert_kernel(
    experts, capacity, tile,
    xs, gr_h, win_h, wout_h, rw,
    gback_o, prod_o, dwin_o, dwout_o, drw_o,
    xall, gr, gp, win, wout, act, gpre, gback, gsend, prod, logit, acc_p, acc_g, xt, gpt, stage,
    send_x, recv_x, send_g, recv_g, local, out_sem,
):
    me = lax.axis_index("expert")
    place = me // 2
    chips = experts // 2
    span = 2 * capacity
    width = xall.shape[1]
    hidden = win.shape[1]
    barrier = pltpu.get_barrier_semaphore()
    for k in range(1, experts):
        pl.semaphore_signal(barrier, inc=1, device_id={"expert": lax.rem(me + k, experts)})
    loads = [
        pltpu.make_async_copy(win_h, win, local.at[0]),
        pltpu.make_async_copy(wout_h, wout, local.at[1]),
        pltpu.make_async_copy(gr_h, gr, local.at[2]),
    ]
    rows_of = lambda who: pl.ds(pl.multiple_of(who * capacity, 16), capacity)
    own = pltpu.make_async_copy(xs.at[rows_of(me), :], xall.at[rows_of(me), :], local.at[3])
    own.start()
    for copy in loads:
        copy.start()
    pl.semaphore_wait(barrier, experts - 1)

    def partner(step):
        high, low = place // 2, lax.rem(place, 2)
        fhigh, flow = step // 2, lax.rem(step, 2)
        return 2 * (high + fhigh - 2 * high * fhigh) + low + flow - 2 * low * flow

    def send_rows(peer):
        return pltpu.make_async_remote_copy(
            src_ref=xs.at[rows_of(peer), :], dst_ref=xall.at[rows_of(me), :],
            send_sem=send_x.at[peer], recv_sem=recv_x.at[me], device_id={"expert": peer},
        )

    def got_rows(peer):
        return pltpu.make_async_remote_copy(
            src_ref=xs.at[rows_of(peer), :], dst_ref=xall.at[rows_of(peer), :],
            send_sem=send_x.at[peer], recv_sem=recv_x.at[peer], device_id={"expert": peer},
        )

    def send_back(peer):
        return pltpu.make_async_remote_copy(
            src_ref=gsend.at[rows_of(peer), :], dst_ref=gback.at[rows_of(me), :],
            send_sem=send_g.at[peer], recv_sem=recv_g.at[me], device_id={"expert": peer},
        )

    def got_back(peer):
        return pltpu.make_async_remote_copy(
            src_ref=gsend.at[rows_of(peer), :], dst_ref=gback.at[rows_of(peer), :],
            send_sem=send_g.at[peer], recv_sem=recv_g.at[peer], device_id={"expert": peer},
        )

    sibling = me + 1 - 2 * lax.rem(me, 2)
    send_rows(sibling).start()
    for step in range(1, chips):
        for core in range(2):
            send_rows(2 * partner(step) + lax.rem(me + core, 2)).start()
    for copy in loads:
        copy.wait()

    lanes = lax.broadcasted_iota(jnp.int32, (span, rw.shape[1]), 1)
    mine = jnp.where(lanes == me, 1.0, 0.0)

    def work(step, carry):
        where = partner(step)
        base = pl.multiple_of(where * span, 32)

        @pl.when(step == 0)
        def _():
            own.wait()
            got_rows(sibling).wait_recv()

        @pl.when(step > 0)
        def _():
            got_rows(2 * where).wait_recv()
            got_rows(2 * where + 1).wait_recv()

        rows = pl.ds(base, span)
        x = xall[rows, :]
        logits = jnp.where(lanes < experts, dot_f32(x, rw[...]), -1e30)
        weights = jnp.exp(logits - jnp.max(logits, axis=-1, keepdims=True))
        probs = weights / jnp.sum(weights, axis=-1, keepdims=True)
        gate = jnp.sum(probs * mine, axis=-1, keepdims=True)
        gp[rows, :] = (gr[rows, :].astype(f32) * gate).astype(bf16)
        acc_p[...] = jnp.zeros_like(acc_p)
        acc_g[...] = jnp.zeros_like(acc_g)

        def block(idx, carry):
            cols = pl.ds(pl.multiple_of(idx * tile, tile), tile)
            h = dot_f32(xall[rows, :], win[:, cols])
            grad = dot_nt(gp[rows, :], wout[cols, :])
            value, slope = gelu_both(h)
            value = value.astype(bf16)
            grad = (grad * slope).astype(bf16)
            act[rows, cols] = value
            gpre[rows, cols] = grad
            acc_p[...] += dot_f32(value, wout[cols, :])
            acc_g[...] += dot_nt(grad, win[:, cols])
            return carry

        lax.fori_loop(0, hidden // tile, block, 0)
        made = acc_p[...].astype(bf16)
        prod[rows, :] = made
        gate_grad = jnp.sum(gr[rows, :].astype(f32) * made.astype(f32), axis=-1, keepdims=True)
        low = (gate_grad * gate * (mine - probs)).astype(bf16)
        low = jnp.where(lanes < experts, low, jnp.zeros_like(low))
        logit[rows, :] = low
        gsend[rows, :] = (acc_g[...] + dot_nt(low, rw[...])).astype(bf16)

        @pl.when(step == 0)
        def _():
            send_back(sibling).start()

        @pl.when(step > 0)
        def _():
            send_back(2 * where).start()
            send_back(2 * where + 1).start()

        return carry

    lax.fori_loop(0, chips, work, 0)
    outs = [
        pltpu.make_async_copy(prod, prod_o, local.at[0]),
        pltpu.make_async_copy(gsend.at[rows_of(me), :], gback.at[rows_of(me), :], local.at[3]),
    ]
    for copy in outs:
        copy.start()
    xt[...] = xall[...].T
    gpt[...] = gp[...].T
    drw_o[...] = dot_f32(xt[...], logit[...])

    def weight_block(idx, carry):
        cols = pl.ds(pl.multiple_of(idx * tile, tile), tile)

        def put(slot, out):
            return pltpu.make_async_copy(stage.at[slot], out.at[:, cols], out_sem.at[slot])

        for slot, (left, right, out) in enumerate(((gpt, act, dwout_o), (xt, gpre, dwin_o))):
            @pl.when(idx > 0)
            def _():
                put(slot, out).wait()

            stage[slot] = dot_f32(left[...], right[:, cols]).astype(bf16)
            put(slot, out).start()
        return carry

    lax.fori_loop(0, hidden // tile, weight_block, 0)
    for slot, out in enumerate((dwout_o, dwin_o)):
        pltpu.make_async_copy(stage.at[slot], out.at[:, 0:tile], out_sem.at[slot]).wait()
    for copy in outs:
        copy.wait()
    for k in range(1, experts):
        peer = lax.rem(me + k, experts)
        got_rows(peer).wait_send()
        got_back(peer).wait_send()
        got_back(peer).wait_recv()
    back = pltpu.make_async_copy(gback, gback_o, local.at[1])
    back.start()
    back.wait()


def expert_pass(xs, gr, weight_in, weight_out, router_pad, experts, capacity):
    slots, width = xs.shape
    hidden = weight_in.shape[1]
    tile = 512
    span = 2 * capacity
    hbm = pl.BlockSpec(memory_space=pl.ANY)
    vmem = pl.BlockSpec(memory_space=pltpu.VMEM)
    return pl.pallas_call(
        functools.partial(expert_kernel, experts, capacity, tile),
        in_specs=[hbm, hbm, hbm, hbm, vmem],
        out_specs=[hbm, hbm, hbm, hbm, vmem],
        out_shape=[
            jax.ShapeDtypeStruct((slots, width), bf16),
            jax.ShapeDtypeStruct((slots, width), bf16),
            jax.ShapeDtypeStruct((width, hidden), bf16),
            jax.ShapeDtypeStruct((width, hidden), bf16),
            jax.ShapeDtypeStruct((width, router_pad.shape[1]), f32),
        ],
        scratch_shapes=[
            pltpu.VMEM((slots, width), bf16),
            pltpu.VMEM((slots, width), bf16),
            pltpu.VMEM((slots, width), bf16),
            pltpu.VMEM((width, hidden), bf16),
            pltpu.VMEM((hidden, width), bf16),
            pltpu.VMEM((slots, hidden), bf16),
            pltpu.VMEM((slots, hidden), bf16),
            pltpu.VMEM((slots, width), bf16),
            pltpu.VMEM((slots, width), bf16),
            pltpu.VMEM((slots, width), bf16),
            pltpu.VMEM((slots, router_pad.shape[1]), bf16),
            pltpu.VMEM((span, width), f32),
            pltpu.VMEM((span, width), f32),
            pltpu.VMEM((width, slots), bf16),
            pltpu.VMEM((width, slots), bf16),
            pltpu.VMEM((2, width, tile), bf16),
            pltpu.SemaphoreType.DMA((experts,)),
            pltpu.SemaphoreType.DMA((experts,)),
            pltpu.SemaphoreType.DMA((experts,)),
            pltpu.SemaphoreType.DMA((experts,)),
            pltpu.SemaphoreType.DMA((4,)),
            pltpu.SemaphoreType.DMA((2,)),
        ],
        compiler_params=pltpu.CompilerParams(
            vmem_limit_bytes=60 << 20, collective_id=1, has_side_effects=True
        ),
        cost_estimate=pl.CostEstimate(
            flops=12 * slots * width * hidden, bytes_accessed=8 * width * hidden, transcendentals=slots * hidden
        ),
        name="experts",
    )(xs, gr, weight_in, weight_out, router_pad)


def remote(src, dst, send_sem, recv_sem, axis, peer):
    return pltpu.make_async_remote_copy(
        src_ref=src, dst_ref=dst, send_sem=send_sem, recv_sem=recv_sem, device_id={axis: peer}
    )


def others(count, mine):
    return [lax.rem(mine + k, count) for k in range(1, count)]


LAGS = (1, 4, 9, 13, 15)


def back_kernel(
    groups, experts, pairs,
    q_ref, k_ref, v_ref, g_ref, u_ref, ctxt_ref, lse_ref, wq, wk, wv, hot, gain, nl_h, tok_h, ghid_h, dwo_h, small_h,
    wsum_o, ing_o, small_o,
    base, acc, kaug, vaug, qaug, gaug, qz, gz, kt, dqt, dall, nt, tok,
    part, r1, r2, r3, full, sbuf, srecv, sone, stwo,
    send1, recv1, send2, recv2, send3, recv3, send4, recv4, send5, recv5, send6, recv6, send7, recv7, local,
):
    seq = q_ref.shape[0]
    width = tok.shape[1]
    span = 256
    pair = pl.program_id(0)
    me = lax.axis_index("expert")
    my_dp = lax.axis_index("dp")
    core = lax.rem(me, 2)
    place = me // 2
    chips = experts // 2
    sibling = me + 1 - 2 * core
    half = width // 2
    piece = half // groups
    thick = part.shape[2]
    gain_rows = width // 128

    def half_rows(which):
        return pl.ds(pl.multiple_of(which * half, 16), half)

    def own_piece(which):
        return pl.ds(pl.multiple_of(core * half + which * piece, 16), piece)

    def copy1(c):
        return remote(part.at[c, half_rows(1 - core), :], r1.at[c], send1.at[c], recv1.at[c], "expert", sibling)

    def copy2(c, peer, slot):
        return remote(part.at[c, own_piece(peer), :], r2.at[c, slot], send2.at[c, peer], recv2.at[c, slot], "dp", peer)

    def copy3(c, peer, slot):
        return remote(
            r3.at[c, place], r3.at[c, slot], send3.at[c, peer], recv3.at[c, slot], "expert", 2 * peer + core
        )

    def copy4(c, peer, slot):
        return remote(
            full.at[c, own_piece(my_dp), :], full.at[c, own_piece(slot), :],
            send4.at[c, peer], recv4.at[c, slot], "dp", peer,
        )

    def copy5(c, which):
        return remote(
            full.at[c, half_rows(which), :], full.at[c, half_rows(which), :],
            send5.at[c], recv5.at[c], "expert", sibling,
        )

    def stage1(c):
        copy1(c).start()

    def stage2(c):
        copy1(c).wait_recv()
        part[c, half_rows(core), :] = (part[c, half_rows(core), :].astype(f32) + r1[c].astype(f32)).astype(bf16)
        for peer in others(groups, my_dp):
            copy2(c, peer, my_dp).start()

    def stage3(c):
        total = part[c, own_piece(my_dp), :].astype(f32)
        for peer in others(groups, my_dp):
            copy2(c, peer, peer).wait_recv()
            total = total + r2[c, peer].astype(f32)
        r3[c, place] = total.astype(bf16)
        for peer in others(chips, place):
            copy3(c, peer, place).start()

    def stage4(c):
        for peer in others(chips, place):
            copy3(c, peer, peer).wait_recv()
        total = r3[c, 0].astype(f32)
        for slot in range(1, chips):
            total = total + r3[c, slot].astype(f32)
        full[c, own_piece(my_dp), :] = total.astype(bf16)
        for peer in others(groups, my_dp):
            copy4(c, peer, my_dp).start()

    def stage5(c):
        for peer in others(groups, my_dp):
            copy4(c, peer, peer).wait_recv()
        copy5(c, core).start()

    def stage6(c):
        copy5(c, 1 - core).wait_recv()

    early = pl.ds(8 + hot.shape[0], sbuf.shape[0] - 8 - hot.shape[0])
    late = pl.ds(0, 8 + hot.shape[0])

    def copy6(part_idx, rows, peer, slot):
        return remote(
            sbuf.at[rows, :], srecv.at[slot, rows, :],
            send6.at[part_idx, peer], recv6.at[part_idx, slot], "expert", peer,
        )

    def copy7(part_idx, rows, peer, slot):
        return remote(
            sone.at[rows, :], stwo.at[slot, rows, :],
            send7.at[part_idx, peer], recv7.at[part_idx, slot], "dp", peer,
        )

    def small1(part_idx, rows):
        srecv[me, rows, :] = sbuf[rows, :]
        for peer in others(experts, me):
            copy6(part_idx, rows, peer, me).start()

    def small2(part_idx, rows):
        for peer in others(experts, me):
            copy6(part_idx, rows, peer, peer).wait_recv()
        total = srecv[0, rows, :]
        for slot in range(1, experts):
            total = total + srecv[slot, rows, :]
        sone[rows, :] = total
        stwo[my_dp, rows, :] = total
        for peer in others(groups, my_dp):
            copy7(part_idx, rows, peer, my_dp).start()

    def small3(part_idx, rows):
        for peer in others(groups, my_dp):
            copy7(part_idx, rows, peer, peer).wait_recv()
        total = stwo[0, rows, :]
        for slot in range(1, groups):
            total = total + stwo[slot, rows, :]
        small_o[rows, :] = total

    stages = (stage2, stage3, stage4, stage5, stage6)

    def advance(slot):
        for lag, stage in reversed(list(zip(LAGS, stages))):
            since = slot - lag

            @pl.when((since >= 0) & (since <= 4 * pairs) & ((lax.rem(since, 4) == 0) | (since == 2)))
            def _():
                stage(since // 4 + jnp.minimum(since, 1))

    loads = [
        pltpu.make_async_copy(nl_h, tok, local.at[0]),
        pltpu.make_async_copy(ghid_h, ing_o, local.at[2]),
        pltpu.make_async_copy(dwo_h.at[:, 0:thick], part.at[0], local.at[3]),
        pltpu.make_async_copy(dwo_h.at[:, thick : 2 * thick], part.at[1], local.at[4]),
        pltpu.make_async_copy(small_h, sbuf, local.at[5]),
    ]

    @pl.when(pair == 0)
    def _():
        barrier = pltpu.get_barrier_semaphore()
        for peer in others(experts, me):
            pl.semaphore_signal(barrier, inc=1, device_id={"expert": peer})
        for peer in others(groups, my_dp):
            pl.semaphore_signal(barrier, inc=1, device_id={"dp": peer})
        for copy in loads:
            copy.start()
        for copy in loads:
            copy.wait()
        nt[...] = tok[...].T
        pl.semaphore_wait(barrier, experts + groups - 2)
        stage1(0)
        stage1(1)
        small1(0, early)

    mine = pl.ds(pl.multiple_of(128 * pair, 128), 128)
    lane = lax.broadcasted_iota(jnp.int32, (seq, 128), 1)
    gt = g_ref[...].T
    qtv = q_ref[...].T
    kt[...] = k_ref[...].T
    gtf = gt.astype(f32)
    pad = jnp.zeros((48, seq), bf16)
    one = jnp.ones((seq, 128), bf16)
    nil = jnp.zeros((seq, 128), bf16)
    acc[...] = jnp.zeros_like(acc)
    for head in range(2):
        fill_toeplitz(base, head, u_ref[0, head : head + 1, :])
        own = (lane < 64) if head == 0 else (lane >= 64)
        origin = 64 if head == 0 else 0
        extra = jnp.where((lane >= origin) & (lane < origin + 3), one, nil)
        kaug[head] = jnp.where(own, k_ref[...], extra)
        vaug[head] = jnp.where(own, v_ref[...], extra)
        qz[head] = jnp.where(own, q_ref[...], nil)
        gz[head] = jnp.where(own, g_ref[...], nil)
        rows = slice(64 * head, 64 * head + 64)
        lse = split_rows(-lse_ref[0, head : head + 1, :])
        dsum = split_rows(-jnp.sum(gtf[rows] * ctxt_ref[rows, :], axis=0, keepdims=True))
        for dst, src, aug in ((qaug, qtv, lse), (gaug, gt, dsum)):
            dst[head, rows, :] = src[rows]
            dst[head, origin : origin + 16, :] = aug
            dst[head, origin + 16 : origin + 64, :] = pad

    dqt[...] = jnp.zeros_like(dqt)

    def step(idx, carry):
        rows = pl.ds(pl.multiple_of(idx * span, span), span)
        dv = None
        dk = None
        for head in range(2):
            s = dot_f32(kaug[head, rows, :], qaug[head])
            dp = dot_f32(vaug[head, rows, :], gaug[head])
            tops = []
            grads = []
            for piece_idx in range(2):
                offs = pl.ds(pl.multiple_of(seq - span * idx - 128 * piece_idx, 128), seq)
                p = jnp.exp(s[128 * piece_idx : 128 * piece_idx + 128] + base[head, :, offs])
                ds_ = p * dp[128 * piece_idx : 128 * piece_idx + 128]
                acc[head, :, offs] += ds_
                tops.append(p.astype(bf16))
                grads.append(ds_.astype(bf16))
            p = jnp.concatenate(tops, axis=0)
            ds_ = jnp.concatenate(grads, axis=0)
            now = dot_f32(p, gz[head])
            dv = now if dv is None else dv + now
            now = dot_f32(ds_, qz[head])
            dk = now if dk is None else dk + now
            dqt[64 * head : 64 * head + 64, :] += dot_f32(kt[64 * head : 64 * head + 64, rows], ds_)
        dall[1, rows, mine] = dk.astype(bf16)
        dall[2, rows, mine] = dv.astype(bf16)
        advance(4 * pair + idx)

        @pl.when(4 * pair + idx == 7)
        def _():
            small2(0, early)

        @pl.when(4 * pair + idx == 11)
        def _():
            small3(0, early)

        return carry

    lax.fori_loop(0, seq // span, step, 0)
    dall[0, :, mine] = dqt[...].T.astype(bf16)
    twice = 2 * seq
    sub = lax.broadcasted_iota(jnp.int32, (8, twice), 0)
    head_lane = lax.broadcasted_iota(jnp.int32, (hot.shape[0], 128), 1)
    rel_rows = slice(8, 8 + hot.shape[0])
    for head in range(2):
        total = acc[head, 0:8, :]
        for group in range(1, 16):
            total = total + pltpu.roll(acc[head, 8 * group : 8 * group + 8, :], twice - 8 * group, 1)
        for bit in (1, 2, 4):
            total = jnp.where((sub & bit) != 0, pltpu.roll(total, twice - bit, 1), total)
        diag = jnp.sum(total, axis=0, keepdims=True)
        sums = jnp.sum(hot[...] * diag, axis=1, keepdims=True)
        sbuf[rel_rows, :] = jnp.where(head_lane == 2 * pair + head, sums, sbuf[rel_rows, :])

    def weight_block(idx, carry):
        rows = pl.ds(pl.multiple_of(idx * 256, 256), 256)
        grads = jnp.concatenate([dall[which, :, mine] for which in range(3)], axis=1)
        part[pair + 2, rows, :] = dot_f32(nt[rows, :], grads).astype(bf16)
        return carry

    lax.fori_loop(0, width // 256, weight_block, 0)
    stage1(pair + 2)

    @pl.when(pair == pairs - 1)
    def _():
        def token_block(idx, carry):
            rows = pl.ds(pl.multiple_of(idx * 256, 256), 256)
            grad = (
                dot_nt(dall[0, rows, :], wq[...])
                + dot_nt(dall[1, rows, :], wk[...])
                + dot_nt(dall[2, rows, :], wv[...])
            )
            values = tok[rows, :].astype(f32)
            scale = lax.rsqrt(jnp.mean(values * values, axis=-1, keepdims=True) + epsilon)
            weighted = grad * gain[...]
            inner = jnp.mean(weighted * values, axis=-1, keepdims=True)
            ing_o[rows, :] += scale * weighted - values * (scale * scale * scale * inner)
            return carry + jnp.sum(grad * values * scale, axis=0, keepdims=True)

        reload = pltpu.make_async_copy(tok_h, tok, local.at[1])
        reload.start()
        last = pairs + 1
        first = 4 * pairs
        older = sorted(
            (4 * c - 4 + lag, c, stage)
            for c in range(2, last)
            for lag, stage in zip(LAGS, range(2, 7))
            if 4 * c - 4 + lag >= first
        )

        def drain(until):
            while older and older[0][0] < first + until:
                _, c, stage = older.pop(0)
                stages[stage - 2](c)

        def tokens_done(lower, upper, gain_grad):
            return lax.fori_loop(lower, upper, token_block, gain_grad)

        drain(1)
        reload.wait()
        gain_grad = tokens_done(0, 1, jnp.zeros((1, width), f32))
        stage2(last)
        drain(2)
        gain_grad = tokens_done(1, seq // 512, gain_grad)
        drain(4)
        gain_grad = tokens_done(seq // 512, seq // 256, gain_grad)
        stage3(last)
        for row in range(gain_rows):
            sbuf[row : row + 1, :] = gain_grad[:, 128 * row : 128 * row + 128]
        small1(1, late)
        drain(8)
        small2(1, late)
        stage4(last)
        drain(99)
        small3(1, late)
        stage5(last)
        stage6(last)
        for c in range(2):
            wsum_o[0, :, thick * c : thick * c + thick] = full[c]
        for c in range(pairs):
            for which in range(3):
                wsum_o[1 + which, :, 128 * c : 128 * c + 128] = full[c + 2, :, 128 * which : 128 * which + 128]

        def finish(c, carry):
            copy1(c).wait_send()
            for peer in others(groups, my_dp):
                copy2(c, peer, my_dp).wait_send()
                copy4(c, peer, my_dp).wait_send()
            for peer in others(chips, place):
                copy3(c, peer, place).wait_send()
            copy5(c, core).wait_send()
            return carry

        lax.fori_loop(0, pairs + 2, finish, 0)
        for part_idx, rows in ((0, early), (1, late)):
            for peer in others(experts, me):
                copy6(part_idx, rows, peer, me).wait_send()
            for peer in others(groups, my_dp):
                copy7(part_idx, rows, peer, my_dp).wait_send()


def back_pass(
    q, k, v, g, u, ctxt, lse, wq, wk, wv, hot, gain, normed_low, tokens, grad_hidden, dwo, small, groups, experts
):
    seq, width = q.shape
    pairs = width // 128
    chunks = pairs + 2
    thick = width // 2
    half = width // 2
    piece = half // groups
    chips = experts // 2
    blk = pl.BlockSpec((seq, 128), lambda p: (0, p))
    hbm = pl.BlockSpec(memory_space=pl.ANY)
    fixed = lambda shape: pl.BlockSpec(shape, lambda p: (0,) * len(shape), pipeline_mode=pl.Buffered(1))
    dma = pltpu.SemaphoreType.DMA
    return pl.pallas_call(
        functools.partial(back_kernel, groups, experts, pairs),
        grid=(pairs,),
        in_specs=[
            blk, blk, blk, blk,
            pl.BlockSpec((1, 2, 2 * seq), lambda p: (p, 0, 0)),
            pl.BlockSpec((128, seq), lambda p: (p, 0)),
            pl.BlockSpec((1, 8, seq), lambda p: (p, 0, 0)),
            fixed((width, width)), fixed((width, width)), fixed((width, width)),
            fixed(hot.shape), fixed(gain.shape),
            hbm, hbm, hbm, hbm, hbm,
        ],
        out_specs=[fixed((4, width, width)), fixed((seq, width)), fixed(small.shape)],
        out_shape=[
            jax.ShapeDtypeStruct((4, width, width), bf16),
            jax.ShapeDtypeStruct((seq, width), f32),
            jax.ShapeDtypeStruct(small.shape, f32),
        ],
        scratch_shapes=[
            pltpu.VMEM((2, 128, 2 * seq), f32),
            pltpu.VMEM((2, 128, 2 * seq), f32),
            pltpu.VMEM((2, seq, 128), bf16),
            pltpu.VMEM((2, seq, 128), bf16),
            pltpu.VMEM((2, 128, seq), bf16),
            pltpu.VMEM((2, 128, seq), bf16),
            pltpu.VMEM((2, seq, 128), bf16),
            pltpu.VMEM((2, seq, 128), bf16),
            pltpu.VMEM((128, seq), bf16),
            pltpu.VMEM((128, seq), f32),
            pltpu.VMEM((3, seq, width), bf16),
            pltpu.VMEM((width, seq), bf16),
            pltpu.VMEM((seq, width), bf16),
            pltpu.VMEM((chunks, width, thick), bf16),
            pltpu.VMEM((chunks, half, thick), bf16),
            pltpu.VMEM((chunks, groups, piece, thick), bf16),
            pltpu.VMEM((chunks, chips, piece, thick), bf16),
            pltpu.VMEM((chunks, width, thick), bf16),
            pltpu.VMEM(small.shape, f32),
            pltpu.VMEM((experts,) + small.shape, f32),
            pltpu.VMEM(small.shape, f32),
            pltpu.VMEM((groups,) + small.shape, f32),
            dma((chunks,)), dma((chunks,)),
            dma((chunks, groups)), dma((chunks, groups)),
            dma((chunks, chips)), dma((chunks, chips)),
            dma((chunks, groups)), dma((chunks, groups)),
            dma((chunks,)), dma((chunks,)),
            dma((2, experts)), dma((2, experts)),
            dma((2, groups)), dma((2, groups)),
            dma((6,)),
        ],
        compiler_params=pltpu.CompilerParams(
            vmem_limit_bytes=62 << 20, collective_id=2, has_side_effects=True
        ),
        cost_estimate=pl.CostEstimate(
            flops=40 * seq * seq * width + 12 * seq * width * width,
            bytes_accessed=40 * seq * width, transcendentals=seq * seq * 12,
        ),
        name="attend_back",
    )(q, k, v, g, u, ctxt, lse, wq, wk, wv, hot, gain, normed_low, tokens, grad_hidden, dwo, small)


def rms_backward(grad_norm, values, row_scale, gain_vec):
    weighted = grad_norm * gain_vec
    gain_grad = jnp.sum(grad_norm * values * row_scale, axis=0)
    grad_in = row_scale * weighted - values * row_scale**3 * jnp.mean(
        weighted * values, axis=-1, keepdims=True
    )
    return grad_in, gain_grad


def rms_forward(values, gain_vec):
    row_scale = lax.rsqrt(jnp.mean(values * values, axis=-1, keepdims=True) + epsilon)
    return values * row_scale * gain_vec, row_scale


def gelu_tanh(values):
    return jax.nn.gelu(values, approximate=True)


def contract(left, right, dims):
    return lax.dot_general(left, right, (((dims[0],), (dims[1],)), ((), ())), preferred_element_type=f32)


def exchange(rows, experts):
    slots, width = rows.shape
    rows = rows.reshape(experts, slots // experts, width)
    return lax.all_to_all(rows, "expert", split_axis=0, concat_axis=0, tiled=True).reshape(slots, width)


def expert_native(send, grad_recv, weight_in, weight_out, router_w, experts):
    received = exchange(send, experts)
    own = lax.axis_index("expert")
    own_hot = (jnp.arange(experts, dtype=jnp.int32) == own).astype(f32)[None, :]
    probs = jax.nn.softmax(contract(received, router_w, (1, 0)), axis=-1)
    gate = jnp.sum(probs * own_hot, axis=-1, keepdims=True)
    grad_recv_f = grad_recv.astype(f32)
    grad_produced = (grad_recv_f * gate).astype(bf16)
    preact = contract(received, weight_in, (1, 0))
    gelu_values, gelu_pullback = jax.vjp(gelu_tanh, preact)
    active = gelu_values.astype(bf16)
    produced = contract(active, weight_out, (1, 0)).astype(bf16)
    gate_grad = jnp.sum(grad_recv_f * produced.astype(f32), axis=-1, keepdims=True)
    logit_low = (gate_grad * gate * (own_hot - probs)).astype(bf16)
    grad_active = contract(grad_produced, weight_out, (1, 1))
    grad_preact = gelu_pullback(grad_active)[0].astype(bf16)
    grad_received = contract(grad_preact, weight_in, (1, 1)) + contract(logit_low, router_w, (1, 1))
    grad_rows = exchange(grad_received.astype(bf16), experts)
    in_grad = contract(received, grad_preact, (0, 0)).astype(bf16)
    out_grad_t = contract(grad_produced, active, (0, 0)).astype(bf16)
    router_grad = contract(received, logit_low, (0, 0))
    return grad_rows, produced, in_grad, out_grad_t, router_grad


def tail_native(tokens, gain, normed_low, dq, dk, dv, wq, wk, wv, grad_hidden, dwo, small):
    tokens_f = tokens.astype(f32)
    grads = jnp.stack([dwo.astype(f32)] + [contract(normed_low, d, (0, 0)) for d in (dq, dk, dv)])
    grad_normed = contract(dq, wq, (1, 1)) + contract(dk, wk, (1, 1)) + contract(dv, wv, (1, 1))
    _, scale = rms_forward(tokens_f, gain)
    grad_tokens, gain_grad = rms_backward(grad_normed, tokens_f, scale, gain)
    grads, gain_grad, small = lax.psum((grads, gain_grad, small), ("dp", "expert"))
    return grads, grad_hidden + grad_tokens, gain_grad, small


def on_device(
    tokens, gain_one, query_w, key_w, value_w, out_w, rel_table, gain_two, router_w,
    expert_in, expert_out, routes, buckets, cotangent,
):
    seq_len, width = tokens.shape
    heads = rel_table.shape[1]
    groups = lax.axis_size("dp")
    experts = lax.axis_size("expert")
    capacity = (5 * seq_len + 4 * experts - 1) // (4 * experts)
    slots = experts * capacity
    weight_in = expert_in[0]
    weight_out = expert_out[0]
    kernels = capacity % 16 == 0 and experts == 8 and groups == 4

    route_ids = routes[:, 0]
    route_hot = route_ids[:, None] == jnp.arange(experts, dtype=jnp.int32)[None, :]
    route_int = route_hot.astype(jnp.int32)
    route_float = route_hot.astype(f32)
    position = jnp.sum((jnp.cumsum(route_int, axis=0) - 1) * route_int, axis=1)
    slot_index = jnp.where(position < capacity, route_ids * capacity + position, slots)
    pick = (jnp.arange(slots, dtype=jnp.int32)[:, None] == slot_index[None, :]).astype(bf16)

    def scatter_rows(rows):
        return contract(pick, rows, (1, 0)).astype(bf16)

    def gather_rows(rows):
        return contract(pick, rows, (0, 0))

    grad_recv = exchange(scatter_rows(cotangent), experts)

    tokens_f = tokens.astype(f32)
    normed, scale_one = rms_forward(tokens_f, gain_one)
    normed_low = normed.astype(bf16)
    queries = contract(normed_low, query_w, (1, 0)).astype(bf16)
    key_rows = contract(normed_low, key_w, (1, 0)).astype(bf16)
    value_rows = contract(normed_low, value_w, (1, 0)).astype(bf16)
    reach = jnp.concatenate([buckets, jnp.full((1,), -1, jnp.int32)])[::-1]
    bucket_hot = (jnp.arange(rel_table.shape[0], dtype=jnp.int32)[:, None] == reach[None, :]).astype(f32)
    spread = jnp.einsum("bh,bx->hx", rel_table, bucket_hot, precision=highest)
    spread = spread.reshape(heads // 2, 2, 2 * seq_len)
    context, context_t, logsum = attend(queries, key_rows, value_rows, spread)
    context, grad_recv = lax.optimization_barrier((context, grad_recv))
    hidden = tokens_f + contract(context, out_w, (1, 0))
    normed_two, scale_two = rms_forward(hidden, gain_two)
    normed_two_low = normed_two.astype(bf16)

    send = scatter_rows(normed_two_low)
    if kernels:
        router_pad = jnp.pad(router_w, ((0, 0), (0, 128 - experts)))
        grad_rows, produced, in_grad, out_grad_t, router_grad = expert_pass(
            send, grad_recv, weight_in, weight_out, router_pad, experts, capacity
        )
        router_grad = router_grad[:, :experts]
    else:
        grad_rows, produced, in_grad, out_grad_t, router_grad = expert_native(
            send, grad_recv, weight_in, weight_out, router_w, experts
        )
    returned = exchange(produced, experts)
    in_share = lax.psum_scatter(in_grad, "dp", scatter_dimension=0, tiled=True).astype(f32)
    out_share = lax.psum_scatter(out_grad_t, "dp", scatter_dimension=0, tiled=True).astype(f32).T

    router_probs = jax.nn.softmax(contract(normed_two_low, router_w, (1, 0)), axis=-1)
    gate_value = jnp.sum(router_probs * route_float, axis=-1, keepdims=True)
    output = (hidden + gate_value * gather_rows(returned)).astype(bf16)

    grad_out = cotangent.astype(f32)
    grad_normed_two = gather_rows(grad_rows)
    grad_hidden_norm, gain_two_grad = rms_backward(grad_normed_two, hidden, scale_two, gain_two)
    grad_hidden = grad_out + grad_hidden_norm
    branch_low = grad_hidden.astype(bf16)
    out_w_grad = contract(context, branch_low, (0, 0)).astype(bf16)
    grad_context = contract(branch_low, out_w, (1, 1)).astype(bf16)
    if kernels:
        small = jnp.concatenate(
            [
                jnp.zeros((8 + rel_table.shape[0], 128), f32),
                jnp.pad(gain_two_grad.reshape(-1, 128), ((0, 2), (0, 0))),
                router_grad.T.reshape(-1, 128),
            ]
        )
        grads, input_grad, small = back_pass(
            queries, key_rows, value_rows, grad_context, spread, context_t, logsum, query_w, key_w, value_w,
            bucket_hot, gain_one[None], normed_low, tokens, grad_hidden, out_w_grad, small, groups, experts,
        )
        tiles = width // 128
        first = 8 + rel_table.shape[0]
        gain_one_grad = small[:tiles].reshape(-1)
        rel_grad = small[8:first, :heads]
        gain_two_grad = small[first : first + tiles].reshape(-1)
        router_grad = small[first + 8 :].reshape(experts, width).T
    else:
        query_grad, key_grad, value_grad, diagonals = attend_back(
            queries, key_rows, value_rows, grad_context, spread, context_t, logsum
        )
        diagonals = diagonals[:, :2].reshape(heads, 2 * seq_len)
        rel_grad = jnp.einsum("bx,hx->bh", bucket_hot, diagonals, precision=highest)
        grads, input_grad, gain_one_grad, small = tail_native(
            tokens, gain_one, normed_low, query_grad, key_grad, value_grad,
            query_w, key_w, value_w, grad_hidden, out_w_grad, (rel_grad, gain_two_grad, router_grad),
        )
        rel_grad, gain_two_grad, router_grad = small
    grads = grads.astype(f32)
    return (
        output, input_grad, grads[1], grads[2], grads[3], grads[0], rel_grad,
        gain_one_grad, gain_two_grad, router_grad, in_share[None], out_share[None],
    )


def solution(mesh):
    rows = P(("dp", "expert"), None)
    whole = P()
    split = P("expert", None, None)
    return jax.shard_map(
        on_device,
        mesh=mesh,
        in_specs=(
            rows, whole, whole, whole, whole, whole, whole, whole, whole, split, split, rows, whole, rows,
        ),
        out_specs=(
            rows, rows, whole, whole, whole, whole, whole, whole, whole, whole,
            P("expert", "dp", None), P("expert", None, "dp"),
        ),
        check_vma=False,
    )
```

```python
import functools

import jax
import jax.numpy as jnp
from jax import lax
from jax.experimental import pallas as pl
from jax.experimental.pallas import tpu as pltpu
from jax.sharding import PartitionSpec as P

bf16 = jnp.bfloat16
f32 = jnp.float32
epsilon = 1e-06
highest = lax.Precision.HIGHEST

def dot_f32(left, right):
    return lax.dot_general(left, right, (((1,), (0,)), ((), ())), preferred_element_type=f32)


def dot_nt(left, right):
    return lax.dot_general(left, right, (((1,), (1,)), ((), ())), preferred_element_type=f32)


def fill_toeplitz(base_ref, head, row):
    rows, width = base_ref.shape[1:]
    spread = jnp.broadcast_to(row, (8, width))
    eight = pltpu.roll(spread, 0, 1, stride=1, stride_axis=0)
    for group in range(rows // 8):
        base_ref[head, 8 * group : 8 * group + 8, :] = (
            eight if group == 0 else pltpu.roll(eight, 8 * group, 1)
        )


def attend_kernel(q_ref, k_ref, v_ref, u_ref, ctx_ref, ctxt_ref, lse_ref, base, qt, vt, s_scr, p_scr):
    seq = q_ref.shape[0]
    span = 256
    half = seq
    qt[...] = q_ref[...].T
    vt[...] = v_ref[...].T
    for head in range(2):
        fill_toeplitz(base, head, u_ref[0, head : head + 1, :])
    zeros = jnp.zeros((64, span), bf16)

    def step(idx, carry):
        cols = pl.ds(pl.multiple_of(idx * span, span), span)
        outs = []
        for head in range(2):
            part = qt[64 * head : 64 * head + 64, cols]
            rhs = jnp.concatenate([part, zeros] if head == 0 else [zeros, part], axis=0)
            peak = None
            for kb in range(seq // 128):
                rows = slice(128 * kb, 128 * kb + 128)
                offs = pl.multiple_of(half + span * idx - 128 * kb, 128)
                s = dot_f32(k_ref[rows, :], rhs) + base[head, :, pl.ds(offs, span)]
                s_scr[head, rows, :] = s
                now = jnp.max(s.reshape(16, 8, span), axis=0)
                peak = now if peak is None else jnp.maximum(peak, now)
            peak = jnp.max(peak, axis=0, keepdims=True)
            total = None
            for kb in range(seq // 128):
                rows = slice(128 * kb, 128 * kb + 128)
                e = jnp.exp(s_scr[head, rows, :] - peak)
                s_scr[head, rows, :] = e
                now = jnp.sum(e.reshape(16, 8, span), axis=0)
                total = now if total is None else total + now
            total = jnp.sum(total, axis=0, keepdims=True)
            inv = 1.0 / total
            for kb in range(seq // 128):
                rows = slice(128 * kb, 128 * kb + 128)
                p_scr[head, rows, :] = (s_scr[head, rows, :] * inv).astype(bf16)
            lse_ref[0, head : head + 1, cols] = peak + jnp.log(total)
            outs.append(dot_f32(vt[64 * head : 64 * head + 64, :], p_scr[head]))
        both = jnp.concatenate(outs, axis=0)
        ctxt_ref[:, cols] = both
        ctx_ref[cols, :] = both.T.astype(bf16)
        return carry

    lax.fori_loop(0, seq // span, step, 0)


def attend(q, k, v, u):
    seq, width = q.shape
    pairs = width // 128
    blk = pl.BlockSpec((seq, 128), lambda p: (0, p))
    return pl.pallas_call(
        attend_kernel,
        grid=(pairs,),
        in_specs=[blk, blk, blk, pl.BlockSpec((1, 2, 2 * seq), lambda p: (p, 0, 0))],
        out_specs=[
            blk,
            pl.BlockSpec((128, seq), lambda p: (p, 0)),
            pl.BlockSpec((1, 8, seq), lambda p: (p, 0, 0)),
        ],
        out_shape=[
            jax.ShapeDtypeStruct((seq, width), bf16),
            jax.ShapeDtypeStruct((width, seq), f32),
            jax.ShapeDtypeStruct((pairs, 8, seq), f32),
        ],
        scratch_shapes=[
            pltpu.VMEM((2, 128, 2 * seq), f32),
            pltpu.VMEM((128, seq), bf16),
            pltpu.VMEM((128, seq), bf16),
            pltpu.VMEM((2, seq, 256), f32),
            pltpu.VMEM((2, seq, 256), bf16),
        ],
        compiler_params=pltpu.CompilerParams(vmem_limit_bytes=48 << 20),
        cost_estimate=pl.CostEstimate(
            flops=16 * seq * seq * width, bytes_accessed=20 * seq * width, transcendentals=seq * seq * 12
        ),
        name="attend",
    )(q, k, v, u)


def split_rows(row):
    hi = row.astype(bf16).astype(f32)
    mid = (row - hi).astype(bf16).astype(f32)
    low = row - hi - mid
    idx = lax.broadcasted_iota(jnp.int32, (16, row.shape[1]), 0)
    return jnp.where(idx == 0, hi, jnp.where(idx == 1, mid, jnp.where(idx == 2, low, 0.0))).astype(bf16)


def attend_back_kernel(
    q_ref, k_ref, v_ref, g_ref, u_ref, ctxt_ref, lse_ref,
    dq_ref, dk_ref, dv_ref, diag_ref,
    base, acc, kaug, vaug, qaug, gaug, qz, gz, kt, dqt,
):
    seq = q_ref.shape[0]
    span = 256
    lane = lax.broadcasted_iota(jnp.int32, (seq, 128), 1)
    gt = g_ref[...].T
    qtv = q_ref[...].T
    kt[...] = k_ref[...].T
    gtf = gt.astype(f32)
    pad = jnp.zeros((48, seq), bf16)
    one = jnp.ones((seq, 128), bf16)
    nil = jnp.zeros((seq, 128), bf16)
    acc[...] = jnp.zeros_like(acc)
    for head in range(2):
        fill_toeplitz(base, head, u_ref[0, head : head + 1, :])
        own = (lane < 64) if head == 0 else (lane >= 64)
        origin = 64 if head == 0 else 0
        extra = jnp.where((lane >= origin) & (lane < origin + 3), one, nil)
        kaug[head] = jnp.where(own, k_ref[...], extra)
        vaug[head] = jnp.where(own, v_ref[...], extra)
        qz[head] = jnp.where(own, q_ref[...], nil)
        gz[head] = jnp.where(own, g_ref[...], nil)
        rows = slice(64 * head, 64 * head + 64)
        lse = split_rows(-lse_ref[0, head : head + 1, :])
        dsum = split_rows(-jnp.sum(gtf[rows] * ctxt_ref[rows, :], axis=0, keepdims=True))
        for dst, src, aug in ((qaug, qtv, lse), (gaug, gt, dsum)):
            dst[head, rows, :] = src[rows]
            dst[head, origin : origin + 16, :] = aug
            dst[head, origin + 16 : origin + 64, :] = pad

    dqt[...] = jnp.zeros_like(dqt)

    def step(idx, carry):
        rows = pl.ds(pl.multiple_of(idx * span, span), span)
        dv = None
        dk = None
        for head in range(2):
            s = dot_f32(kaug[head, rows, :], qaug[head])
            dp = dot_f32(vaug[head, rows, :], gaug[head])
            tops = []
            grads = []
            for part in range(2):
                offs = pl.ds(pl.multiple_of(seq - span * idx - 128 * part, 128), seq)
                p = jnp.exp(s[128 * part : 128 * part + 128] + base[head, :, offs])
                ds_ = p * dp[128 * part : 128 * part + 128]
                acc[head, :, offs] += ds_
                tops.append(p.astype(bf16))
                grads.append(ds_.astype(bf16))
            p = jnp.concatenate(tops, axis=0)
            ds_ = jnp.concatenate(grads, axis=0)
            now = dot_f32(p, gz[head])
            dv = now if dv is None else dv + now
            now = dot_f32(ds_, qz[head])
            dk = now if dk is None else dk + now
            dqt[64 * head : 64 * head + 64, :] += dot_f32(kt[64 * head : 64 * head + 64, rows], ds_)
        dv_ref[rows, :] = dv.astype(bf16)
        dk_ref[rows, :] = dk.astype(bf16)
        return carry

    lax.fori_loop(0, seq // span, step, 0)
    dq_ref[...] = dqt[...].T.astype(bf16)
    width = 2 * seq
    for head in range(2):
        total = acc[head, 0:8, :]
        for group in range(1, 16):
            total = total + pltpu.roll(acc[head, 8 * group : 8 * group + 8, :], width - 8 * group, 1)
        sub = lax.broadcasted_iota(jnp.int32, (8, width), 0)
        for bit in (1, 2, 4):
            total = jnp.where((sub & bit) != 0, pltpu.roll(total, width - bit, 1), total)
        diag_ref[0, head : head + 1, :] = jnp.sum(total, axis=0, keepdims=True)


def attend_back(q, k, v, g, u, ctxt, lse):
    seq, width = q.shape
    pairs = width // 128
    blk = pl.BlockSpec((seq, 128), lambda p: (0, p))
    return pl.pallas_call(
        attend_back_kernel,
        grid=(pairs,),
        in_specs=[
            blk, blk, blk, blk,
            pl.BlockSpec((1, 2, 2 * seq), lambda p: (p, 0, 0)),
            pl.BlockSpec((128, seq), lambda p: (p, 0)),
            pl.BlockSpec((1, 8, seq), lambda p: (p, 0, 0)),
        ],
        out_specs=[blk, blk, blk, pl.BlockSpec((1, 8, 2 * seq), lambda p: (p, 0, 0))],
        out_shape=[jax.ShapeDtypeStruct((seq, width), bf16)] * 3
        + [jax.ShapeDtypeStruct((pairs, 8, 2 * seq), f32)],
        scratch_shapes=[
            pltpu.VMEM((2, 128, 2 * seq), f32),
            pltpu.VMEM((2, 128, 2 * seq), f32),
            pltpu.VMEM((2, seq, 128), bf16),
            pltpu.VMEM((2, seq, 128), bf16),
            pltpu.VMEM((2, 128, seq), bf16),
            pltpu.VMEM((2, 128, seq), bf16),
            pltpu.VMEM((2, seq, 128), bf16),
            pltpu.VMEM((2, seq, 128), bf16),
            pltpu.VMEM((128, seq), bf16),
            pltpu.VMEM((128, seq), f32),
        ],
        compiler_params=pltpu.CompilerParams(vmem_limit_bytes=56 << 20),
        cost_estimate=pl.CostEstimate(
            flops=40 * seq * seq * width, bytes_accessed=20 * seq * width, transcendentals=seq * seq * 12
        ),
        name="attend_back",
    )(q, k, v, g, u, ctxt, lse)


def gelu_both(v):
    scale = 0.7978845608028654
    square = v * v
    t = jnp.tanh(scale * v * (1.0 + 0.044715 * square))
    half = 0.5 * (1.0 + t)
    slope = half + 0.5 * v * (1.0 - t * t) * (scale * (1.0 + 3 * 0.044715 * square))
    return v * half, slope


def expert_kernel(
    experts, capacity, tile,
    xs, gr_h, win_h, wout_h, rw,
    gback_o, prod_o, dwin_o, dwout_o, drw_o, shared_o,
    xall, gr, gp, win, wout, act, gpre, gback, gsend, prod, logit, acc_p, acc_g, xt, gpt, stage, dwt,
    send_x, recv_x, send_g, recv_g, local, out_sem, send_s, recv_s,
):
    me = lax.axis_index("expert")
    place = me // 2
    chips = experts // 2
    span = 2 * capacity
    width = xall.shape[1]
    hidden = win.shape[1]
    barrier = pltpu.get_barrier_semaphore()
    for k in range(1, experts):
        pl.semaphore_signal(barrier, inc=1, device_id={"expert": lax.rem(me + k, experts)})
    my_dp = lax.axis_index("dp")
    dp_x, dp_y = lax.rem(my_dp, 2), my_dp // 2
    peer_x, peer_y = my_dp + 1 - 2 * dp_x, my_dp + 2 - 4 * dp_y
    for peer in (peer_x, peer_y):
        pl.semaphore_signal(barrier, inc=1, device_id={"dp": peer})
    loads = [
        pltpu.make_async_copy(win_h, win, local.at[0]),
        pltpu.make_async_copy(wout_h, wout, local.at[1]),
        pltpu.make_async_copy(gr_h, gr, local.at[2]),
    ]
    rows_of = lambda who: pl.ds(pl.multiple_of(who * capacity, 16), capacity)
    own = pltpu.make_async_copy(xs.at[rows_of(me), :], xall.at[rows_of(me), :], local.at[3])
    own.start()
    for copy in loads:
        copy.start()
    pl.semaphore_wait(barrier, experts + 1)

    def partner(step):
        high, low = place // 2, lax.rem(place, 2)
        fhigh, flow = step // 2, lax.rem(step, 2)
        return 2 * (high + fhigh - 2 * high * fhigh) + low + flow - 2 * low * flow

    def send_rows(peer):
        return pltpu.make_async_remote_copy(
            src_ref=xs.at[rows_of(peer), :], dst_ref=xall.at[rows_of(me), :],
            send_sem=send_x.at[peer], recv_sem=recv_x.at[me], device_id={"expert": peer},
        )

    def got_rows(peer):
        return pltpu.make_async_remote_copy(
            src_ref=xs.at[rows_of(peer), :], dst_ref=xall.at[rows_of(peer), :],
            send_sem=send_x.at[peer], recv_sem=recv_x.at[peer], device_id={"expert": peer},
        )

    def send_back(peer):
        return pltpu.make_async_remote_copy(
            src_ref=gsend.at[rows_of(peer), :], dst_ref=gback.at[rows_of(me), :],
            send_sem=send_g.at[peer], recv_sem=recv_g.at[me], device_id={"expert": peer},
        )

    def got_back(peer):
        return pltpu.make_async_remote_copy(
            src_ref=gsend.at[rows_of(peer), :], dst_ref=gback.at[rows_of(peer), :],
            send_sem=send_g.at[peer], recv_sem=recv_g.at[peer], device_id={"expert": peer},
        )

    sibling = me + 1 - 2 * lax.rem(me, 2)
    send_rows(sibling).start()
    for step in range(1, chips):
        for core in range(2):
            send_rows(2 * partner(step) + lax.rem(me + core, 2)).start()
    for copy in loads:
        copy.wait()

    lanes = lax.broadcasted_iota(jnp.int32, (span, rw.shape[1]), 1)
    mine = jnp.where(lanes == me, 1.0, 0.0)

    def work(step, carry):
        where = partner(step)
        base = pl.multiple_of(where * span, 32)

        @pl.when(step == 0)
        def _():
            own.wait()
            got_rows(sibling).wait_recv()

        @pl.when(step > 0)
        def _():
            got_rows(2 * where).wait_recv()
            got_rows(2 * where + 1).wait_recv()

        rows = pl.ds(base, span)
        x = xall[rows, :]
        logits = jnp.where(lanes < experts, dot_f32(x, rw[...]), -1e30)
        weights = jnp.exp(logits - jnp.max(logits, axis=-1, keepdims=True))
        probs = weights / jnp.sum(weights, axis=-1, keepdims=True)
        gate = jnp.sum(probs * mine, axis=-1, keepdims=True)
        gp[rows, :] = (gr[rows, :].astype(f32) * gate).astype(bf16)
        acc_p[...] = jnp.zeros_like(acc_p)
        acc_g[...] = jnp.zeros_like(acc_g)

        def block(idx, carry):
            cols = pl.ds(pl.multiple_of(idx * tile, tile), tile)
            h = dot_f32(xall[rows, :], win[:, cols])
            grad = dot_nt(gp[rows, :], wout[cols, :])
            value, slope = gelu_both(h)
            value = value.astype(bf16)
            grad = (grad * slope).astype(bf16)
            act[rows, cols] = value
            gpre[rows, cols] = grad
            acc_p[...] += dot_f32(value, wout[cols, :])
            acc_g[...] += dot_nt(grad, win[:, cols])
            return carry

        lax.fori_loop(0, hidden // tile, block, 0)
        made = acc_p[...].astype(bf16)
        prod[rows, :] = made
        gate_grad = jnp.sum(gr[rows, :].astype(f32) * made.astype(f32), axis=-1, keepdims=True)
        low = (gate_grad * gate * (mine - probs)).astype(bf16)
        low = jnp.where(lanes < experts, low, jnp.zeros_like(low))
        logit[rows, :] = low
        gsend[rows, :] = (acc_g[...] + dot_nt(low, rw[...])).astype(bf16)

        @pl.when(step == 0)
        def _():
            send_back(sibling).start()

        @pl.when(step > 0)
        def _():
            send_back(2 * where).start()
            send_back(2 * where + 1).start()

        return carry

    lax.fori_loop(0, chips, work, 0)
    outs = [
        pltpu.make_async_copy(prod, prod_o, local.at[0]),
        pltpu.make_async_copy(gsend.at[rows_of(me), :], gback.at[rows_of(me), :], local.at[3]),
    ]
    for copy in outs:
        copy.start()
    xt[...] = xall[...].T
    gpt[...] = gp[...].T
    drw_o[...] = dot_f32(xt[...], logit[...])

    share = width // 4
    tiles = hidden // tile
    split = tiles // 2

    def left_copy(idx, block):
        cols = pl.ds(pl.multiple_of(idx * tile, tile), tile)
        rows = pl.ds(pl.multiple_of((1 - dp_x + 2 * block) * share, 16), share)
        return pltpu.make_async_remote_copy(
            src_ref=dwt.at[rows, cols], dst_ref=shared_o.at[pl.ds(block * share, share), cols],
            send_sem=send_s.at[block, idx], recv_sem=recv_s.at[block, idx], device_id={"dp": peer_x},
        )

    def right_copy(idx, block):
        cols = pl.ds(pl.multiple_of(idx * tile, tile), tile)
        rows = pl.ds(pl.multiple_of((2 - 2 * dp_y + block) * share, 16), share)
        dst_cols = pl.ds(pl.multiple_of((idx - split) * tile, tile), tile)
        return pltpu.make_async_remote_copy(
            src_ref=dwt.at[rows, cols], dst_ref=shared_o.at[pl.ds((2 + block) * share, share), dst_cols],
            send_sem=send_s.at[block, idx], recv_sem=recv_s.at[block, idx], device_id={"dp": peer_y},
        )

    def out_block(step, carry):
        idx = lax.rem(step, 2) * split + step // 2
        cols = pl.ds(pl.multiple_of(idx * tile, tile), tile)
        dwt[:, cols] = dot_f32(gpt[...], act[:, cols]).astype(bf16)

        @pl.when(idx < split)
        def _():
            for block in range(2):
                left_copy(idx, block).start()

        @pl.when(idx >= split)
        def _():
            for block in range(2):
                right_copy(idx, block).start()

        return carry

    lax.fori_loop(0, tiles, out_block, 0)
    whole = pltpu.make_async_copy(dwt, dwout_o, local.at[2])
    whole.start()

    def put(slot, cols):
        return pltpu.make_async_copy(stage.at[slot], dwin_o.at[:, cols], out_sem.at[slot])

    def in_block(idx, carry):
        cols = pl.ds(pl.multiple_of(idx * tile, tile), tile)
        slot = lax.rem(idx, 2)

        @pl.when(idx > 1)
        def _():
            put(slot, cols).wait()

        stage[slot] = dot_f32(xt[...], gpre[:, cols]).astype(bf16)
        put(slot, cols).start()
        return carry

    lax.fori_loop(0, tiles, in_block, 0)
    for slot in range(2):
        put(slot, pl.ds(0, tile)).wait()
    whole.wait()
    for copy in outs:
        copy.wait()
    for k in range(1, experts):
        peer = lax.rem(me + k, experts)
        got_rows(peer).wait_send()
        got_back(peer).wait_send()
        got_back(peer).wait_recv()
    back = pltpu.make_async_copy(gback, gback_o, local.at[1])
    back.start()
    for idx in range(tiles):
        for block in range(2):
            (left_copy if idx < split else right_copy)(idx, block).wait()
    back.wait()


def expert_pass(xs, gr, weight_in, weight_out, router_pad, experts, capacity):
    slots, width = xs.shape
    hidden = weight_in.shape[1]
    tile = 512
    span = 2 * capacity
    hbm = pl.BlockSpec(memory_space=pl.ANY)
    vmem = pl.BlockSpec(memory_space=pltpu.VMEM)
    return pl.pallas_call(
        functools.partial(expert_kernel, experts, capacity, tile),
        in_specs=[hbm, hbm, hbm, hbm, vmem],
        out_specs=[hbm, hbm, hbm, hbm, vmem, hbm],
        out_shape=[
            jax.ShapeDtypeStruct((slots, width), bf16),
            jax.ShapeDtypeStruct((slots, width), bf16),
            jax.ShapeDtypeStruct((width, hidden), bf16),
            jax.ShapeDtypeStruct((width, hidden), bf16),
            jax.ShapeDtypeStruct((width, router_pad.shape[1]), f32),
            jax.ShapeDtypeStruct((width, hidden // 2), bf16),
        ],
        scratch_shapes=[
            pltpu.VMEM((slots, width), bf16),
            pltpu.VMEM((slots, width), bf16),
            pltpu.VMEM((slots, width), bf16),
            pltpu.VMEM((width, hidden), bf16),
            pltpu.VMEM((hidden, width), bf16),
            pltpu.VMEM((slots, hidden), bf16),
            pltpu.VMEM((slots, hidden), bf16),
            pltpu.VMEM((slots, width), bf16),
            pltpu.VMEM((slots, width), bf16),
            pltpu.VMEM((slots, width), bf16),
            pltpu.VMEM((slots, router_pad.shape[1]), bf16),
            pltpu.VMEM((span, width), f32),
            pltpu.VMEM((span, width), f32),
            pltpu.VMEM((width, slots), bf16),
            pltpu.VMEM((width, slots), bf16),
            pltpu.VMEM((2, width, tile), bf16),
            pltpu.VMEM((width, hidden), bf16),
            pltpu.SemaphoreType.DMA((experts,)),
            pltpu.SemaphoreType.DMA((experts,)),
            pltpu.SemaphoreType.DMA((experts,)),
            pltpu.SemaphoreType.DMA((experts,)),
            pltpu.SemaphoreType.DMA((4,)),
            pltpu.SemaphoreType.DMA((2,)),
            pltpu.SemaphoreType.DMA((2, hidden // tile)),
            pltpu.SemaphoreType.DMA((2, hidden // tile)),
        ],
        compiler_params=pltpu.CompilerParams(
            vmem_limit_bytes=60 << 20, collective_id=1, has_side_effects=True
        ),
        cost_estimate=pl.CostEstimate(
            flops=12 * slots * width * hidden, bytes_accessed=8 * width * hidden, transcendentals=slots * hidden
        ),
        name="experts",
    )(xs, gr, weight_in, weight_out, router_pad)


def remote(src, dst, send_sem, recv_sem, axis, peer):
    return pltpu.make_async_remote_copy(
        src_ref=src, dst_ref=dst, send_sem=send_sem, recv_sem=recv_sem, device_id={axis: peer}
    )


def others(count, mine):
    return [lax.rem(mine + k, count) for k in range(1, count)]


PLAN = (
    (11, 16, 19, 22, 24),
    (12, 17, 20, 23, 25),
    (5, 13, 16, 19, 21),
    (9, 15, 18, 21, 23),
    (13, 18, 21, 24, 26),
    (17, 21, 24, 27, 29),
    (21, 24, 27, 29, 31),
)
EXPERT_SLOTS = ((6, 2, 0), (14, 3, 0), (15, 2, 1), (22, 3, 1))


def back_kernel(
    groups, experts, pairs,
    q_ref, k_ref, v_ref, g_ref, u_ref, ctxt_ref, lse_ref, wq, wk, wv, hot, gain, nl_h, tok_h, ghid_h, dwo_h, small_h,
    eout_h, shared_h, ein_h,
    wsum_o, ing_o, small_o, esum_o,
    base, acc, kaug, vaug, qaug, gaug, qz, gz, kt, dqt, dall, nt, tok,
    part, r1, r2, r3, full, sbuf, srecv, sone, stwo, keep, other, final,
    send1, recv1, send2, recv2, send3, recv3, send4, recv4, send5, recv5, send6, recv6, send7, recv7, local,
    send_a, recv_a, send_b, recv_b, out_sem, copy_sem,
):
    seq = q_ref.shape[0]
    width = tok.shape[1]
    span = 256
    pair = pl.program_id(0)
    me = lax.axis_index("expert")
    my_dp = lax.axis_index("dp")
    core = lax.rem(me, 2)
    place = me // 2
    chips = experts // 2
    sibling = me + 1 - 2 * core
    half = width // 2
    piece = half // groups
    thick = part.shape[2]
    gain_rows = width // 128

    def half_rows(which):
        return pl.ds(pl.multiple_of(which * half, 16), half)

    def own_piece(which):
        return pl.ds(pl.multiple_of(core * half + which * piece, 16), piece)

    def copy1(c):
        return remote(part.at[c, half_rows(1 - core), :], r1.at[c], send1.at[c], recv1.at[c], "expert", sibling)

    def copy2(c, peer, slot):
        return remote(part.at[c, own_piece(peer), :], r2.at[c, slot], send2.at[c, peer], recv2.at[c, slot], "dp", peer)

    def copy3(c, peer, slot):
        return remote(
            r3.at[c, place], r3.at[c, slot], send3.at[c, peer], recv3.at[c, slot], "expert", 2 * peer + core
        )

    def copy4(c, peer, slot):
        return remote(
            full.at[c, own_piece(my_dp), :], full.at[c, own_piece(slot), :],
            send4.at[c, peer], recv4.at[c, slot], "dp", peer,
        )

    def copy5(c, which):
        return remote(
            full.at[c, half_rows(which), :], full.at[c, half_rows(which), :],
            send5.at[c], recv5.at[c], "expert", sibling,
        )

    def stage1(c):
        copy1(c).start()

    def stage2(c):
        copy1(c).wait_recv()
        part[c, half_rows(core), :] = (part[c, half_rows(core), :].astype(f32) + r1[c].astype(f32)).astype(bf16)
        for peer in others(groups, my_dp):
            copy2(c, peer, my_dp).start()

    def stage3(c):
        total = part[c, own_piece(my_dp), :].astype(f32)
        for peer in others(groups, my_dp):
            copy2(c, peer, peer).wait_recv()
            total = total + r2[c, peer].astype(f32)
        r3[c, place] = total.astype(bf16)
        for peer in others(chips, place):
            copy3(c, peer, place).start()

    def stage4(c):
        for peer in others(chips, place):
            copy3(c, peer, peer).wait_recv()
        total = r3[c, 0].astype(f32)
        for slot in range(1, chips):
            total = total + r3[c, slot].astype(f32)
        full[c, own_piece(my_dp), :] = total.astype(bf16)
        for peer in others(groups, my_dp):
            copy4(c, peer, my_dp).start()

    def stage5(c):
        for peer in others(groups, my_dp):
            copy4(c, peer, peer).wait_recv()
        copy5(c, core).start()

    def put_first(c):
        return pltpu.make_async_copy(full.at[c], wsum_o.at[0, :, thick * c : thick * c + thick], out_sem.at[c, 0])

    def put_pair(c, which):
        cols = pl.ds(128 * (c - 2) if isinstance(c, int) else pl.multiple_of(128 * (c - 2), 128), 128)
        return pltpu.make_async_copy(
            full.at[c, :, 128 * which : 128 * which + 128], wsum_o.at[1 + which, :, cols], out_sem.at[c, which]
        )

    def stage6(c):
        copy5(c, 1 - core).wait_recv()

        if c < 2:
            put_first(c).start()
        else:
            for which in range(3):
                put_pair(c, which).start()

    share = width // 4
    dp_x, dp_y = lax.rem(my_dp, 2), my_dp // 2
    peer_x, peer_y = my_dp + 1 - 2 * dp_x, my_dp + 2 - 4 * dp_y
    middle = keep.shape[1]
    left, right = pl.ds(0, middle), pl.ds(middle, middle)

    def share_rows(which):
        return pl.ds(pl.multiple_of(which * share, 16), share)

    def first_left(block):
        return remote(
            ein_h.at[share_rows(1 - dp_x + 2 * block), left], other.at[1, share_rows(block), :],
            send_a.at[0, block], recv_a.at[0, block], "dp", peer_x,
        )

    def first_right(block):
        return remote(
            ein_h.at[share_rows(2 - 2 * dp_y + block), right], other.at[1, share_rows(2 + block), :],
            send_a.at[1, block], recv_a.at[1, block], "dp", peer_y,
        )

    def second_left(which):
        return remote(
            keep.at[share_rows(1 - dp_y), :], final.at[which, :, left],
            send_b.at[which, 0], recv_b.at[which, 0], "dp", peer_y,
        )

    def second_right(which):
        return remote(
            keep.at[share_rows(2 + 1 - dp_x), :], final.at[which, :, right],
            send_b.at[which, 1], recv_b.at[which, 1], "dp", peer_x,
        )

    def own_loads(src):
        loads = []
        for block in range(2):
            loads.append(
                pltpu.make_async_copy(
                    src.at[share_rows(dp_x + 2 * block), left], keep.at[share_rows(block), :], copy_sem.at[block]
                )
            )
            loads.append(
                pltpu.make_async_copy(
                    src.at[share_rows(2 * dp_y + block), right], keep.at[share_rows(2 + block), :], copy_sem.at[2 + block]
                )
            )
        return loads

    def shared_load():
        return pltpu.make_async_copy(shared_h, other.at[0], copy_sem.at[4])

    def save(which):
        return pltpu.make_async_copy(final.at[which], esum_o.at[which], copy_sem.at[5])

    def experts_begin():
        for copy in own_loads(eout_h) + [shared_load()]:
            copy.start()
        for block in range(2):
            first_left(block).start()
            first_right(block).start()

    def experts_second(which):
        for copy in own_loads(eout_h if which == 0 else ein_h):
            copy.wait()
        if which == 0:
            shared_load().wait()
        else:
            for block in range(2):
                first_left(block).wait_recv()
                first_right(block).wait_recv()

        def block(idx, carry):
            rows = pl.ds(pl.multiple_of(idx * 64, 64), 64)
            keep[rows, :] = (keep[rows, :].astype(f32) + other[which, rows, :].astype(f32)).astype(bf16)
            return carry

        lax.fori_loop(0, width // 64, block, 0)
        second_left(which).start()
        second_right(which).start()

    def experts_last(which):
        second_left(which).wait()
        second_right(which).wait()

        def block(idx, carry):
            rows = pl.ds(pl.multiple_of(idx * 64, 64), 64)
            mine_left = pl.ds(pl.multiple_of(dp_y * share + idx * 64, 64), 64)
            mine_right = pl.ds(pl.multiple_of((2 + dp_x) * share + idx * 64, 64), 64)
            final[which, rows, left] = (final[which, rows, left].astype(f32) + keep[mine_left, :].astype(f32)).astype(bf16)
            final[which, rows, right] = (final[which, rows, right].astype(f32) + keep[mine_right, :].astype(f32)).astype(bf16)
            return carry

        lax.fori_loop(0, share // 64, block, 0)
        if which == 0:
            for copy in own_loads(ein_h):
                copy.start()
        else:
            save(0).wait()
        save(which).start()

    early = pl.ds(8 + hot.shape[0], sbuf.shape[0] - 8 - hot.shape[0])
    late = pl.ds(0, 8 + hot.shape[0])

    def copy6(part_idx, rows, peer, slot):
        return remote(
            sbuf.at[rows, :], srecv.at[slot, rows, :],
            send6.at[part_idx, peer], recv6.at[part_idx, slot], "expert", peer,
        )

    def copy7(part_idx, rows, peer, slot):
        return remote(
            sone.at[rows, :], stwo.at[slot, rows, :],
            send7.at[part_idx, peer], recv7.at[part_idx, slot], "dp", peer,
        )

    def small1(part_idx, rows):
        srecv[me, rows, :] = sbuf[rows, :]
        for peer in others(experts, me):
            copy6(part_idx, rows, peer, me).start()

    def small2(part_idx, rows):
        for peer in others(experts, me):
            copy6(part_idx, rows, peer, peer).wait_recv()
        total = srecv[0, rows, :]
        for slot in range(1, experts):
            total = total + srecv[slot, rows, :]
        sone[rows, :] = total
        stwo[my_dp, rows, :] = total
        for peer in others(groups, my_dp):
            copy7(part_idx, rows, peer, my_dp).start()

    def small3(part_idx, rows):
        for peer in others(groups, my_dp):
            copy7(part_idx, rows, peer, peer).wait_recv()
        total = stwo[0, rows, :]
        for slot in range(1, groups):
            total = total + stwo[slot, rows, :]
        small_o[rows, :] = total

    stages = (stage2, stage3, stage4, stage5, stage6)

    def advance(slot):
        for c, slots in enumerate(PLAN):
            for at, stage in reversed(list(zip(slots, stages))):
                if at < 4 * pairs:
                    pl.when(slot == at)(functools.partial(stage, c))

    loads = [
        pltpu.make_async_copy(nl_h, tok, local.at[0]),
        pltpu.make_async_copy(ghid_h, ing_o, local.at[2]),
        pltpu.make_async_copy(dwo_h.at[:, 0:thick], part.at[0], local.at[3]),
        pltpu.make_async_copy(dwo_h.at[:, thick : 2 * thick], part.at[1], local.at[4]),
        pltpu.make_async_copy(small_h, sbuf, local.at[5]),
    ]

    @pl.when(pair == 0)
    def _():
        barrier = pltpu.get_barrier_semaphore()
        for peer in others(experts, me):
            pl.semaphore_signal(barrier, inc=1, device_id={"expert": peer})
        for peer in others(groups, my_dp):
            pl.semaphore_signal(barrier, inc=1, device_id={"dp": peer})
        for copy in loads:
            copy.start()
        for copy in loads:
            copy.wait()
        nt[...] = tok[...].T
        pl.semaphore_wait(barrier, experts + groups - 2)
        stage1(0)
        stage1(1)
        small1(0, early)
        experts_begin()

    mine = pl.ds(pl.multiple_of(128 * pair, 128), 128)
    lane = lax.broadcasted_iota(jnp.int32, (seq, 128), 1)
    gt = g_ref[...].T
    qtv = q_ref[...].T
    kt[...] = k_ref[...].T
    gtf = gt.astype(f32)
    pad = jnp.zeros((48, seq), bf16)
    one = jnp.ones((seq, 128), bf16)
    nil = jnp.zeros((seq, 128), bf16)
    acc[...] = jnp.zeros_like(acc)
    for head in range(2):
        fill_toeplitz(base, head, u_ref[0, head : head + 1, :])
        own = (lane < 64) if head == 0 else (lane >= 64)
        origin = 64 if head == 0 else 0
        extra = jnp.where((lane >= origin) & (lane < origin + 3), one, nil)
        kaug[head] = jnp.where(own, k_ref[...], extra)
        vaug[head] = jnp.where(own, v_ref[...], extra)
        qz[head] = jnp.where(own, q_ref[...], nil)
        gz[head] = jnp.where(own, g_ref[...], nil)
        rows = slice(64 * head, 64 * head + 64)
        lse = split_rows(-lse_ref[0, head : head + 1, :])
        dsum = split_rows(-jnp.sum(gtf[rows] * ctxt_ref[rows, :], axis=0, keepdims=True))
        for dst, src, aug in ((qaug, qtv, lse), (gaug, gt, dsum)):
            dst[head, rows, :] = src[rows]
            dst[head, origin : origin + 16, :] = aug
            dst[head, origin + 16 : origin + 64, :] = pad

    dqt[...] = jnp.zeros_like(dqt)

    def step(idx, carry):
        rows = pl.ds(pl.multiple_of(idx * span, span), span)
        dv = None
        dk = None
        for head in range(2):
            s = dot_f32(kaug[head, rows, :], qaug[head])
            dp = dot_f32(vaug[head, rows, :], gaug[head])
            tops = []
            grads = []
            for piece_idx in range(2):
                offs = pl.ds(pl.multiple_of(seq - span * idx - 128 * piece_idx, 128), seq)
                p = jnp.exp(s[128 * piece_idx : 128 * piece_idx + 128] + base[head, :, offs])
                ds_ = p * dp[128 * piece_idx : 128 * piece_idx + 128]
                acc[head, :, offs] += ds_
                tops.append(p.astype(bf16))
                grads.append(ds_.astype(bf16))
            p = jnp.concatenate(tops, axis=0)
            ds_ = jnp.concatenate(grads, axis=0)
            now = dot_f32(p, gz[head])
            dv = now if dv is None else dv + now
            now = dot_f32(ds_, qz[head])
            dk = now if dk is None else dk + now
            dqt[64 * head : 64 * head + 64, :] += dot_f32(kt[64 * head : 64 * head + 64, rows], ds_)
        dall[1, rows, mine] = dk.astype(bf16)
        dall[2, rows, mine] = dv.astype(bf16)
        advance(4 * pair + idx)

        for at, task, which in EXPERT_SLOTS:
            @pl.when(4 * pair + idx == at)
            def _():
                (experts_second if task == 2 else experts_last)(which)

        @pl.when(4 * pair + idx == 7)
        def _():
            small2(0, early)

        @pl.when(4 * pair + idx == 11)
        def _():
            small3(0, early)

        return carry

    lax.fori_loop(0, seq // span, step, 0)
    dall[0, :, mine] = dqt[...].T.astype(bf16)
    twice = 2 * seq
    sub = lax.broadcasted_iota(jnp.int32, (8, twice), 0)
    head_lane = lax.broadcasted_iota(jnp.int32, (hot.shape[0], 128), 1)
    rel_rows = slice(8, 8 + hot.shape[0])
    for head in range(2):
        total = acc[head, 0:8, :]
        for group in range(1, 16):
            total = total + pltpu.roll(acc[head, 8 * group : 8 * group + 8, :], twice - 8 * group, 1)
        for bit in (1, 2, 4):
            total = jnp.where((sub & bit) != 0, pltpu.roll(total, twice - bit, 1), total)
        diag = jnp.sum(total, axis=0, keepdims=True)
        sums = jnp.sum(hot[...] * diag, axis=1, keepdims=True)
        sbuf[rel_rows, :] = jnp.where(head_lane == 2 * pair + head, sums, sbuf[rel_rows, :])

    def weight_block(idx, carry):
        rows = pl.ds(pl.multiple_of(idx * 256, 256), 256)
        grads = jnp.concatenate([dall[which, :, mine] for which in range(3)], axis=1)
        part[pair + 2, rows, :] = dot_f32(nt[rows, :], grads).astype(bf16)
        return carry

    lax.fori_loop(0, width // 256, weight_block, 0)
    stage1(pair + 2)

    @pl.when(pair == pairs - 1)
    def _():
        def token_block(idx, carry):
            rows = pl.ds(pl.multiple_of(idx * 256, 256), 256)
            grad = (
                dot_nt(dall[0, rows, :], wq[...])
                + dot_nt(dall[1, rows, :], wk[...])
                + dot_nt(dall[2, rows, :], wv[...])
            )
            values = tok[rows, :].astype(f32)
            scale = lax.rsqrt(jnp.mean(values * values, axis=-1, keepdims=True) + epsilon)
            weighted = grad * gain[...]
            inner = jnp.mean(weighted * values, axis=-1, keepdims=True)
            ing_o[rows, :] += scale * weighted - values * (scale * scale * scale * inner)
            return carry + jnp.sum(grad * values * scale, axis=0, keepdims=True)

        reload = pltpu.make_async_copy(tok_h, tok, local.at[1])
        reload.start()
        last = pairs + 1
        first = 4 * pairs
        older = sorted(
            (at, c, stage)
            for c, slots in enumerate(PLAN)
            for stage, at in enumerate(slots)
            if at >= first
        )

        def drain(until):
            while older and older[0][0] < first + until:
                _, c, stage = older.pop(0)
                stages[stage](c)

        def tokens_done(lower, upper, gain_grad):
            return lax.fori_loop(lower, upper, token_block, gain_grad)

        drain(1)
        reload.wait()
        gain_grad = tokens_done(0, 1, jnp.zeros((1, width), f32))
        stage2(last)
        drain(2)
        gain_grad = tokens_done(1, seq // 512, gain_grad)
        drain(4)
        gain_grad = tokens_done(seq // 512, seq // 256, gain_grad)
        stage3(last)
        for row in range(gain_rows):
            sbuf[row : row + 1, :] = gain_grad[:, 128 * row : 128 * row + 128]
        small1(1, late)
        drain(8)
        small2(1, late)
        stage4(last)
        drain(99)
        small3(1, late)
        stage5(last)
        stage6(last)
        for c in range(2):
            put_first(c).wait()
        save(1).wait()
        for block in range(2):
            first_left(block).wait_send()
            first_right(block).wait_send()

        def finish(c, carry):
            copy1(c).wait_send()
            for peer in others(groups, my_dp):
                copy2(c, peer, my_dp).wait_send()
                copy4(c, peer, my_dp).wait_send()
            for peer in others(chips, place):
                copy3(c, peer, place).wait_send()
            copy5(c, core).wait_send()

            @pl.when(c >= 2)
            def _():
                for which in range(3):
                    put_pair(c, which).wait()

            return carry

        lax.fori_loop(0, pairs + 2, finish, 0)
        for part_idx, rows in ((0, early), (1, late)):
            for peer in others(experts, me):
                copy6(part_idx, rows, peer, me).wait_send()
            for peer in others(groups, my_dp):
                copy7(part_idx, rows, peer, my_dp).wait_send()


def back_pass(
    q, k, v, g, u, ctxt, lse, wq, wk, wv, hot, gain, normed_low, tokens, grad_hidden, dwo, small,
    expert_out_grad, shared, expert_in_grad, groups, experts
):
    seq, width = q.shape
    pairs = width // 128
    chunks = pairs + 2
    hidden = expert_in_grad.shape[1]
    thick = width // 2
    half = width // 2
    piece = half // groups
    chips = experts // 2
    blk = pl.BlockSpec((seq, 128), lambda p: (0, p))
    hbm = pl.BlockSpec(memory_space=pl.ANY)
    fixed = lambda shape: pl.BlockSpec(shape, lambda p: (0,) * len(shape), pipeline_mode=pl.Buffered(1))
    dma = pltpu.SemaphoreType.DMA
    return pl.pallas_call(
        functools.partial(back_kernel, groups, experts, pairs),
        grid=(pairs,),
        in_specs=[
            blk, blk, blk, blk,
            pl.BlockSpec((1, 2, 2 * seq), lambda p: (p, 0, 0)),
            pl.BlockSpec((128, seq), lambda p: (p, 0)),
            pl.BlockSpec((1, 8, seq), lambda p: (p, 0, 0)),
            fixed((width, width)), fixed((width, width)), fixed((width, width)),
            fixed(hot.shape), fixed(gain.shape),
            hbm, hbm, hbm, hbm, hbm, hbm, hbm, hbm,
        ],
        out_specs=[hbm, fixed((seq, width)), fixed(small.shape), hbm],
        out_shape=[
            jax.ShapeDtypeStruct((4, width, width), bf16),
            jax.ShapeDtypeStruct((seq, width), f32),
            jax.ShapeDtypeStruct(small.shape, f32),
            jax.ShapeDtypeStruct((2, width // 4, hidden), bf16),
        ],
        scratch_shapes=[
            pltpu.VMEM((2, 128, 2 * seq), f32),
            pltpu.VMEM((2, 128, 2 * seq), f32),
            pltpu.VMEM((2, seq, 128), bf16),
            pltpu.VMEM((2, seq, 128), bf16),
            pltpu.VMEM((2, 128, seq), bf16),
            pltpu.VMEM((2, 128, seq), bf16),
            pltpu.VMEM((2, seq, 128), bf16),
            pltpu.VMEM((2, seq, 128), bf16),
            pltpu.VMEM((128, seq), bf16),
            pltpu.VMEM((128, seq), f32),
            pltpu.VMEM((3, seq, width), bf16),
            pltpu.VMEM((width, seq), bf16),
            pltpu.VMEM((seq, width), bf16),
            pltpu.VMEM((chunks, width, thick), bf16),
            pltpu.VMEM((chunks, half, thick), bf16),
            pltpu.VMEM((chunks, groups, piece, thick), bf16),
            pltpu.VMEM((chunks, chips, piece, thick), bf16),
            pltpu.VMEM((chunks, width, thick), bf16),
            pltpu.VMEM(small.shape, f32),
            pltpu.VMEM((experts,) + small.shape, f32),
            pltpu.VMEM(small.shape, f32),
            pltpu.VMEM((groups,) + small.shape, f32),
            pltpu.VMEM((width, hidden // 2), bf16),
            pltpu.VMEM((2, width, hidden // 2), bf16),
            pltpu.VMEM((2, width // 4, hidden), bf16),
            dma((chunks,)), dma((chunks,)),
            dma((chunks, groups)), dma((chunks, groups)),
            dma((chunks, chips)), dma((chunks, chips)),
            dma((chunks, groups)), dma((chunks, groups)),
            dma((chunks,)), dma((chunks,)),
            dma((2, experts)), dma((2, experts)),
            dma((2, groups)), dma((2, groups)),
            dma((6,)),
            dma((2, 2)), dma((2, 2)),
            dma((2, 2)), dma((2, 2)),
            dma((chunks, 3)), dma((6,)),
        ],
        compiler_params=pltpu.CompilerParams(
            vmem_limit_bytes=62 << 20, collective_id=2, has_side_effects=True
        ),
        cost_estimate=pl.CostEstimate(
            flops=40 * seq * seq * width + 12 * seq * width * width,
            bytes_accessed=40 * seq * width, transcendentals=seq * seq * 12,
        ),
        name="attend_back",
    )(q, k, v, g, u, ctxt, lse, wq, wk, wv, hot, gain, normed_low, tokens, grad_hidden, dwo, small, expert_out_grad, shared, expert_in_grad)


def rms_backward(grad_norm, values, row_scale, gain_vec):
    weighted = grad_norm * gain_vec
    gain_grad = jnp.sum(grad_norm * values * row_scale, axis=0)
    grad_in = row_scale * weighted - values * row_scale**3 * jnp.mean(
        weighted * values, axis=-1, keepdims=True
    )
    return grad_in, gain_grad


def rms_forward(values, gain_vec):
    row_scale = lax.rsqrt(jnp.mean(values * values, axis=-1, keepdims=True) + epsilon)
    return values * row_scale * gain_vec, row_scale


def gelu_tanh(values):
    return jax.nn.gelu(values, approximate=True)


def contract(left, right, dims):
    return lax.dot_general(left, right, (((dims[0],), (dims[1],)), ((), ())), preferred_element_type=f32)


def exchange(rows, experts):
    slots, width = rows.shape
    rows = rows.reshape(experts, slots // experts, width)
    return lax.all_to_all(rows, "expert", split_axis=0, concat_axis=0, tiled=True).reshape(slots, width)


def expert_native(send, grad_recv, weight_in, weight_out, router_w, experts):
    received = exchange(send, experts)
    own = lax.axis_index("expert")
    own_hot = (jnp.arange(experts, dtype=jnp.int32) == own).astype(f32)[None, :]
    probs = jax.nn.softmax(contract(received, router_w, (1, 0)), axis=-1)
    gate = jnp.sum(probs * own_hot, axis=-1, keepdims=True)
    grad_recv_f = grad_recv.astype(f32)
    grad_produced = (grad_recv_f * gate).astype(bf16)
    preact = contract(received, weight_in, (1, 0))
    gelu_values, gelu_pullback = jax.vjp(gelu_tanh, preact)
    active = gelu_values.astype(bf16)
    produced = contract(active, weight_out, (1, 0)).astype(bf16)
    gate_grad = jnp.sum(grad_recv_f * produced.astype(f32), axis=-1, keepdims=True)
    logit_low = (gate_grad * gate * (own_hot - probs)).astype(bf16)
    grad_active = contract(grad_produced, weight_out, (1, 1))
    grad_preact = gelu_pullback(grad_active)[0].astype(bf16)
    grad_received = contract(grad_preact, weight_in, (1, 1)) + contract(logit_low, router_w, (1, 1))
    grad_rows = exchange(grad_received.astype(bf16), experts)
    in_grad = contract(received, grad_preact, (0, 0)).astype(bf16)
    out_grad_t = contract(grad_produced, active, (0, 0)).astype(bf16)
    router_grad = contract(received, logit_low, (0, 0))
    return grad_rows, produced, in_grad, out_grad_t, router_grad


def tail_native(tokens, gain, normed_low, dq, dk, dv, wq, wk, wv, grad_hidden, dwo, small):
    tokens_f = tokens.astype(f32)
    grads = jnp.stack([dwo.astype(f32)] + [contract(normed_low, d, (0, 0)) for d in (dq, dk, dv)])
    grad_normed = contract(dq, wq, (1, 1)) + contract(dk, wk, (1, 1)) + contract(dv, wv, (1, 1))
    _, scale = rms_forward(tokens_f, gain)
    grad_tokens, gain_grad = rms_backward(grad_normed, tokens_f, scale, gain)
    grads, gain_grad, small = lax.psum((grads, gain_grad, small), ("dp", "expert"))
    return grads, grad_hidden + grad_tokens, gain_grad, small


def on_device(
    tokens, gain_one, query_w, key_w, value_w, out_w, rel_table, gain_two, router_w,
    expert_in, expert_out, routes, buckets, cotangent,
):
    seq_len, width = tokens.shape
    heads = rel_table.shape[1]
    groups = lax.axis_size("dp")
    experts = lax.axis_size("expert")
    capacity = (5 * seq_len + 4 * experts - 1) // (4 * experts)
    slots = experts * capacity
    weight_in = expert_in[0]
    weight_out = expert_out[0]
    kernels = capacity % 16 == 0 and experts == 8 and groups == 4

    route_ids = routes[:, 0]
    route_hot = route_ids[:, None] == jnp.arange(experts, dtype=jnp.int32)[None, :]
    route_int = route_hot.astype(jnp.int32)
    route_float = route_hot.astype(f32)
    position = jnp.sum((jnp.cumsum(route_int, axis=0) - 1) * route_int, axis=1)
    slot_index = jnp.where(position < capacity, route_ids * capacity + position, slots)
    pick = (jnp.arange(slots, dtype=jnp.int32)[:, None] == slot_index[None, :]).astype(bf16)

    def scatter_rows(rows):
        return contract(pick, rows, (1, 0)).astype(bf16)

    def gather_rows(rows):
        return contract(pick, rows, (0, 0))

    grad_recv = exchange(scatter_rows(cotangent), experts)

    tokens_f = tokens.astype(f32)
    normed, scale_one = rms_forward(tokens_f, gain_one)
    normed_low = normed.astype(bf16)
    queries = contract(normed_low, query_w, (1, 0)).astype(bf16)
    key_rows = contract(normed_low, key_w, (1, 0)).astype(bf16)
    value_rows = contract(normed_low, value_w, (1, 0)).astype(bf16)
    reach = jnp.concatenate([buckets, jnp.full((1,), -1, jnp.int32)])[::-1]
    bucket_hot = (jnp.arange(rel_table.shape[0], dtype=jnp.int32)[:, None] == reach[None, :]).astype(f32)
    spread = jnp.einsum("bh,bx->hx", rel_table, bucket_hot, precision=highest)
    spread = spread.reshape(heads // 2, 2, 2 * seq_len)
    context, context_t, logsum = attend(queries, key_rows, value_rows, spread)
    context, grad_recv = lax.optimization_barrier((context, grad_recv))
    hidden = tokens_f + contract(context, out_w, (1, 0))
    normed_two, scale_two = rms_forward(hidden, gain_two)
    normed_two_low = normed_two.astype(bf16)

    send = scatter_rows(normed_two_low)
    if kernels:
        router_pad = jnp.pad(router_w, ((0, 0), (0, 128 - experts)))
        grad_rows, produced, in_grad, out_grad_t, router_grad, shared = expert_pass(
            send, grad_recv, weight_in, weight_out, router_pad, experts, capacity
        )
        router_grad = router_grad[:, :experts]
    else:
        grad_rows, produced, in_grad, out_grad_t, router_grad = expert_native(
            send, grad_recv, weight_in, weight_out, router_w, experts
        )
    returned = exchange(produced, experts)

    router_probs = jax.nn.softmax(contract(normed_two_low, router_w, (1, 0)), axis=-1)
    gate_value = jnp.sum(router_probs * route_float, axis=-1, keepdims=True)
    output = (hidden + gate_value * gather_rows(returned)).astype(bf16)

    grad_out = cotangent.astype(f32)
    grad_normed_two = gather_rows(grad_rows)
    grad_hidden_norm, gain_two_grad = rms_backward(grad_normed_two, hidden, scale_two, gain_two)
    grad_hidden = grad_out + grad_hidden_norm
    branch_low = grad_hidden.astype(bf16)
    out_w_grad = contract(context, branch_low, (0, 0)).astype(bf16)
    grad_context = contract(branch_low, out_w, (1, 1)).astype(bf16)
    if kernels:
        small = jnp.concatenate(
            [
                jnp.zeros((8 + rel_table.shape[0], 128), f32),
                jnp.pad(gain_two_grad.reshape(-1, 128), ((0, 2), (0, 0))),
                router_grad.T.reshape(-1, 128),
            ]
        )
        grads, input_grad, small, shares = back_pass(
            queries, key_rows, value_rows, grad_context, spread, context_t, logsum, query_w, key_w, value_w,
            bucket_hot, gain_one[None], normed_low, tokens, grad_hidden, out_w_grad, small,
            out_grad_t, shared, in_grad, groups, experts,
        )
        tiles = width // 128
        first = 8 + rel_table.shape[0]
        gain_one_grad = small[:tiles].reshape(-1)
        rel_grad = small[8:first, :heads]
        gain_two_grad = small[first : first + tiles].reshape(-1)
        router_grad = small[first + 8 :].reshape(experts, width).T
        out_share, in_share = shares[0], shares[1]
    else:
        in_share = lax.psum_scatter(in_grad, "dp", scatter_dimension=0, tiled=True)
        out_share = lax.psum_scatter(out_grad_t, "dp", scatter_dimension=0, tiled=True)
        query_grad, key_grad, value_grad, diagonals = attend_back(
            queries, key_rows, value_rows, grad_context, spread, context_t, logsum
        )
        diagonals = diagonals[:, :2].reshape(heads, 2 * seq_len)
        rel_grad = jnp.einsum("bx,hx->bh", bucket_hot, diagonals, precision=highest)
        grads, input_grad, gain_one_grad, small = tail_native(
            tokens, gain_one, normed_low, query_grad, key_grad, value_grad,
            query_w, key_w, value_w, grad_hidden, out_w_grad, (rel_grad, gain_two_grad, router_grad),
        )
        rel_grad, gain_two_grad, router_grad = small
    grads = grads.astype(f32)
    return (
        output, input_grad, grads[1], grads[2], grads[3], grads[0], rel_grad,
        gain_one_grad, gain_two_grad, router_grad, in_share.astype(f32)[None], out_share.astype(f32).T[None],
    )


def solution(mesh):
    rows = P(("dp", "expert"), None)
    whole = P()
    split = P("expert", None, None)
    return jax.shard_map(
        on_device,
        mesh=mesh,
        in_specs=(
            rows, whole, whole, whole, whole, whole, whole, whole, whole, split, split, rows, whole, rows,
        ),
        out_specs=(
            rows, rows, whole, whole, whole, whole, whole, whole, whole, whole,
            P("expert", "dp", None), P("expert", None, "dp"),
        ),
        check_vma=False,
    )
```

```python
import functools

import jax
import jax.numpy as jnp
from jax import lax
from jax.experimental import pallas as pl
from jax.experimental.pallas import tpu as pltpu
from jax.sharding import PartitionSpec as P

bf16 = jnp.bfloat16
f32 = jnp.float32
epsilon = 1e-06
highest = lax.Precision.HIGHEST

def dot_f32(left, right):
    return lax.dot_general(left, right, (((1,), (0,)), ((), ())), preferred_element_type=f32)


def dot_nt(left, right):
    return lax.dot_general(left, right, (((1,), (1,)), ((), ())), preferred_element_type=f32)


def fill_toeplitz(base_ref, head, row):
    rows, width = base_ref.shape[1:]
    spread = jnp.broadcast_to(row, (8, width))
    eight = pltpu.roll(spread, 0, 1, stride=1, stride_axis=0)
    for group in range(rows // 8):
        base_ref[head, 8 * group : 8 * group + 8, :] = (
            eight if group == 0 else pltpu.roll(eight, 8 * group, 1)
        )


def attend_kernel(
    q_ref, k_ref, v_ref, u_ref, ctx_ref, ctxt_ref, lse_ref, p_h, base, qt, vt, s_scr, p_scr, p_sem
):
    seq = q_ref.shape[0]
    span = 256
    half = seq
    qt[...] = q_ref[...].T
    vt[...] = v_ref[...].T
    for head in range(2):
        fill_toeplitz(base, head, u_ref[0, head : head + 1, :])
    zeros = jnp.zeros((64, span), bf16)
    pair = pl.program_id(0)

    def save(idx, slot):
        cols = pl.ds(pl.multiple_of(idx * span, span), span)
        return pltpu.make_async_copy(p_scr.at[slot], p_h.at[pl.ds(2 * pair, 2), :, cols], p_sem.at[slot])

    def step(idx, carry):
        slot = lax.rem(idx, 2)

        @pl.when((pair > 0) | (idx > 1))
        def _():
            save(idx, slot).wait()

        cols = pl.ds(pl.multiple_of(idx * span, span), span)
        outs = []
        for head in range(2):
            part = qt[64 * head : 64 * head + 64, cols]
            rhs = jnp.concatenate([part, zeros] if head == 0 else [zeros, part], axis=0)
            peak = None
            for kb in range(seq // 128):
                rows = slice(128 * kb, 128 * kb + 128)
                offs = pl.multiple_of(half + span * idx - 128 * kb, 128)
                s = dot_f32(k_ref[rows, :], rhs) + base[head, :, pl.ds(offs, span)]
                s_scr[head, rows, :] = s
                now = jnp.max(s.reshape(16, 8, span), axis=0)
                peak = now if peak is None else jnp.maximum(peak, now)
            peak = jnp.max(peak, axis=0, keepdims=True)
            total = None
            for kb in range(seq // 128):
                rows = slice(128 * kb, 128 * kb + 128)
                e = jnp.exp(s_scr[head, rows, :] - peak)
                s_scr[head, rows, :] = e
                now = jnp.sum(e.reshape(16, 8, span), axis=0)
                total = now if total is None else total + now
            total = jnp.sum(total, axis=0, keepdims=True)
            inv = 1.0 / total
            for kb in range(seq // 128):
                rows = slice(128 * kb, 128 * kb + 128)
                p_scr[slot, head, rows, :] = (s_scr[head, rows, :] * inv).astype(bf16)
            lse_ref[0, head : head + 1, cols] = peak + jnp.log(total)
            outs.append(dot_f32(vt[64 * head : 64 * head + 64, :], p_scr[slot, head]))
        save(idx, slot).start()
        both = jnp.concatenate(outs, axis=0)
        ctxt_ref[:, cols] = both
        ctx_ref[cols, :] = both.T.astype(bf16)
        return carry

    lax.fori_loop(0, seq // span, step, 0)

    @pl.when(pair == pl.num_programs(0) - 1)
    def _():
        for slot in range(2):
            save(slot, slot).wait()


def attend(q, k, v, u):
    seq, width = q.shape
    pairs = width // 128
    blk = pl.BlockSpec((seq, 128), lambda p: (0, p))
    return pl.pallas_call(
        attend_kernel,
        grid=(pairs,),
        in_specs=[blk, blk, blk, pl.BlockSpec((1, 2, 2 * seq), lambda p: (p, 0, 0))],
        out_specs=[
            blk,
            pl.BlockSpec((128, seq), lambda p: (p, 0)),
            pl.BlockSpec((1, 8, seq), lambda p: (p, 0, 0)),
            pl.BlockSpec(memory_space=pl.ANY),
        ],
        out_shape=[
            jax.ShapeDtypeStruct((seq, width), bf16),
            jax.ShapeDtypeStruct((width, seq), f32),
            jax.ShapeDtypeStruct((pairs, 8, seq), f32),
            jax.ShapeDtypeStruct((2 * pairs, seq, seq), bf16),
        ],
        scratch_shapes=[
            pltpu.VMEM((2, 128, 2 * seq), f32),
            pltpu.VMEM((128, seq), bf16),
            pltpu.VMEM((128, seq), bf16),
            pltpu.VMEM((2, seq, 256), f32),
            pltpu.VMEM((2, 2, seq, 256), bf16),
            pltpu.SemaphoreType.DMA((2,)),
        ],
        compiler_params=pltpu.CompilerParams(vmem_limit_bytes=48 << 20),
        cost_estimate=pl.CostEstimate(
            flops=16 * seq * seq * width, bytes_accessed=20 * seq * width, transcendentals=seq * seq * 12
        ),
        name="attend",
    )(q, k, v, u)


def split_rows(row):
    hi = row.astype(bf16).astype(f32)
    mid = (row - hi).astype(bf16).astype(f32)
    low = row - hi - mid
    idx = lax.broadcasted_iota(jnp.int32, (16, row.shape[1]), 0)
    return jnp.where(idx == 0, hi, jnp.where(idx == 1, mid, jnp.where(idx == 2, low, 0.0))).astype(bf16)


def attend_back_kernel(
    q_ref, k_ref, v_ref, g_ref, u_ref, ctxt_ref, lse_ref,
    dq_ref, dk_ref, dv_ref, diag_ref,
    base, acc, kaug, vaug, qaug, gaug, qz, gz, kt, dqt,
):
    seq = q_ref.shape[0]
    span = 256
    lane = lax.broadcasted_iota(jnp.int32, (seq, 128), 1)
    gt = g_ref[...].T
    qtv = q_ref[...].T
    kt[...] = k_ref[...].T
    gtf = gt.astype(f32)
    pad = jnp.zeros((48, seq), bf16)
    one = jnp.ones((seq, 128), bf16)
    nil = jnp.zeros((seq, 128), bf16)
    acc[...] = jnp.zeros_like(acc)
    for head in range(2):
        fill_toeplitz(base, head, u_ref[0, head : head + 1, :])
        own = (lane < 64) if head == 0 else (lane >= 64)
        origin = 64 if head == 0 else 0
        extra = jnp.where((lane >= origin) & (lane < origin + 3), one, nil)
        kaug[head] = jnp.where(own, k_ref[...], extra)
        vaug[head] = jnp.where(own, v_ref[...], extra)
        qz[head] = jnp.where(own, q_ref[...], nil)
        gz[head] = jnp.where(own, g_ref[...], nil)
        rows = slice(64 * head, 64 * head + 64)
        lse = split_rows(-lse_ref[0, head : head + 1, :])
        dsum = split_rows(-jnp.sum(gtf[rows] * ctxt_ref[rows, :], axis=0, keepdims=True))
        for dst, src, aug in ((qaug, qtv, lse), (gaug, gt, dsum)):
            dst[head, rows, :] = src[rows]
            dst[head, origin : origin + 16, :] = aug
            dst[head, origin + 16 : origin + 64, :] = pad

    dqt[...] = jnp.zeros_like(dqt)

    def step(idx, carry):
        rows = pl.ds(pl.multiple_of(idx * span, span), span)
        dv = None
        dk = None
        for head in range(2):
            s = dot_f32(kaug[head, rows, :], qaug[head])
            dp = dot_f32(vaug[head, rows, :], gaug[head])
            tops = []
            grads = []
            for part in range(2):
                offs = pl.ds(pl.multiple_of(seq - span * idx - 128 * part, 128), seq)
                p = jnp.exp(s[128 * part : 128 * part + 128] + base[head, :, offs])
                ds_ = p * dp[128 * part : 128 * part + 128]
                acc[head, :, offs] += ds_
                tops.append(p.astype(bf16))
                grads.append(ds_.astype(bf16))
            p = jnp.concatenate(tops, axis=0)
            ds_ = jnp.concatenate(grads, axis=0)
            now = dot_f32(p, gz[head])
            dv = now if dv is None else dv + now
            now = dot_f32(ds_, qz[head])
            dk = now if dk is None else dk + now
            dqt[64 * head : 64 * head + 64, :] += dot_f32(kt[64 * head : 64 * head + 64, rows], ds_)
        dv_ref[rows, :] = dv.astype(bf16)
        dk_ref[rows, :] = dk.astype(bf16)
        return carry

    lax.fori_loop(0, seq // span, step, 0)
    dq_ref[...] = dqt[...].T.astype(bf16)
    width = 2 * seq
    for head in range(2):
        total = acc[head, 0:8, :]
        for group in range(1, 16):
            total = total + pltpu.roll(acc[head, 8 * group : 8 * group + 8, :], width - 8 * group, 1)
        sub = lax.broadcasted_iota(jnp.int32, (8, width), 0)
        for bit in (1, 2, 4):
            total = jnp.where((sub & bit) != 0, pltpu.roll(total, width - bit, 1), total)
        diag_ref[0, head : head + 1, :] = jnp.sum(total, axis=0, keepdims=True)


def attend_back(q, k, v, g, u, ctxt, lse):
    seq, width = q.shape
    pairs = width // 128
    blk = pl.BlockSpec((seq, 128), lambda p: (0, p))
    return pl.pallas_call(
        attend_back_kernel,
        grid=(pairs,),
        in_specs=[
            blk, blk, blk, blk,
            pl.BlockSpec((1, 2, 2 * seq), lambda p: (p, 0, 0)),
            pl.BlockSpec((128, seq), lambda p: (p, 0)),
            pl.BlockSpec((1, 8, seq), lambda p: (p, 0, 0)),
        ],
        out_specs=[blk, blk, blk, pl.BlockSpec((1, 8, 2 * seq), lambda p: (p, 0, 0))],
        out_shape=[jax.ShapeDtypeStruct((seq, width), bf16)] * 3
        + [jax.ShapeDtypeStruct((pairs, 8, 2 * seq), f32)],
        scratch_shapes=[
            pltpu.VMEM((2, 128, 2 * seq), f32),
            pltpu.VMEM((2, 128, 2 * seq), f32),
            pltpu.VMEM((2, seq, 128), bf16),
            pltpu.VMEM((2, seq, 128), bf16),
            pltpu.VMEM((2, 128, seq), bf16),
            pltpu.VMEM((2, 128, seq), bf16),
            pltpu.VMEM((2, seq, 128), bf16),
            pltpu.VMEM((2, seq, 128), bf16),
            pltpu.VMEM((128, seq), bf16),
            pltpu.VMEM((128, seq), f32),
        ],
        compiler_params=pltpu.CompilerParams(vmem_limit_bytes=56 << 20),
        cost_estimate=pl.CostEstimate(
            flops=40 * seq * seq * width, bytes_accessed=20 * seq * width, transcendentals=seq * seq * 12
        ),
        name="attend_back",
    )(q, k, v, g, u, ctxt, lse)


def gelu_both(v):
    scale = 0.7978845608028654
    square = v * v
    t = jnp.tanh(scale * v * (1.0 + 0.044715 * square))
    half = 0.5 * (1.0 + t)
    slope = half + 0.5 * v * (1.0 - t * t) * (scale * (1.0 + 3 * 0.044715 * square))
    return v * half, slope


def expert_kernel(
    experts, capacity, tile,
    xs, gr_h, win_h, wout_h, rw,
    gback_o, prod_o, dwin_o, dwout_o, drw_o, shared_o,
    xall, gr, gp, win, wout, act, gpre, gback, gsend, prod, logit, acc_p, acc_g, xt, gpt, stage, dwt,
    send_x, recv_x, send_g, recv_g, local, out_sem, send_s, recv_s,
):
    me = lax.axis_index("expert")
    place = me // 2
    chips = experts // 2
    span = 2 * capacity
    width = xall.shape[1]
    hidden = win.shape[1]
    barrier = pltpu.get_barrier_semaphore()
    for k in range(1, experts):
        pl.semaphore_signal(barrier, inc=1, device_id={"expert": lax.rem(me + k, experts)})
    my_dp = lax.axis_index("dp")
    dp_x, dp_y = lax.rem(my_dp, 2), my_dp // 2
    peer_x, peer_y = my_dp + 1 - 2 * dp_x, my_dp + 2 - 4 * dp_y
    for peer in (peer_x, peer_y):
        pl.semaphore_signal(barrier, inc=1, device_id={"dp": peer})
    loads = [
        pltpu.make_async_copy(win_h, win, local.at[0]),
        pltpu.make_async_copy(wout_h, wout, local.at[1]),
        pltpu.make_async_copy(gr_h, gr, local.at[2]),
    ]
    rows_of = lambda who: pl.ds(pl.multiple_of(who * capacity, 16), capacity)
    own = pltpu.make_async_copy(xs.at[rows_of(me), :], xall.at[rows_of(me), :], local.at[3])
    own.start()
    for copy in loads:
        copy.start()
    pl.semaphore_wait(barrier, experts + 1)

    def partner(step):
        high, low = place // 2, lax.rem(place, 2)
        fhigh, flow = step // 2, lax.rem(step, 2)
        return 2 * (high + fhigh - 2 * high * fhigh) + low + flow - 2 * low * flow

    def send_rows(peer):
        return pltpu.make_async_remote_copy(
            src_ref=xs.at[rows_of(peer), :], dst_ref=xall.at[rows_of(me), :],
            send_sem=send_x.at[peer], recv_sem=recv_x.at[me], device_id={"expert": peer},
        )

    def got_rows(peer):
        return pltpu.make_async_remote_copy(
            src_ref=xs.at[rows_of(peer), :], dst_ref=xall.at[rows_of(peer), :],
            send_sem=send_x.at[peer], recv_sem=recv_x.at[peer], device_id={"expert": peer},
        )

    def send_back(peer):
        return pltpu.make_async_remote_copy(
            src_ref=gsend.at[rows_of(peer), :], dst_ref=gback.at[rows_of(me), :],
            send_sem=send_g.at[peer], recv_sem=recv_g.at[me], device_id={"expert": peer},
        )

    def got_back(peer):
        return pltpu.make_async_remote_copy(
            src_ref=gsend.at[rows_of(peer), :], dst_ref=gback.at[rows_of(peer), :],
            send_sem=send_g.at[peer], recv_sem=recv_g.at[peer], device_id={"expert": peer},
        )

    sibling = me + 1 - 2 * lax.rem(me, 2)
    send_rows(sibling).start()
    for step in range(1, chips):
        for core in range(2):
            send_rows(2 * partner(step) + lax.rem(me + core, 2)).start()
    for copy in loads:
        copy.wait()

    lanes = lax.broadcasted_iota(jnp.int32, (span, rw.shape[1]), 1)
    mine = jnp.where(lanes == me, 1.0, 0.0)

    def work(step, carry):
        where = partner(step)
        base = pl.multiple_of(where * span, 32)

        @pl.when(step == 0)
        def _():
            own.wait()
            got_rows(sibling).wait_recv()

        @pl.when(step > 0)
        def _():
            got_rows(2 * where).wait_recv()
            got_rows(2 * where + 1).wait_recv()

        rows = pl.ds(base, span)
        x = xall[rows, :]
        logits = jnp.where(lanes < experts, dot_f32(x, rw[...]), -1e30)
        weights = jnp.exp(logits - jnp.max(logits, axis=-1, keepdims=True))
        probs = weights / jnp.sum(weights, axis=-1, keepdims=True)
        gate = jnp.sum(probs * mine, axis=-1, keepdims=True)
        gp[rows, :] = (gr[rows, :].astype(f32) * gate).astype(bf16)
        acc_p[...] = jnp.zeros_like(acc_p)
        acc_g[...] = jnp.zeros_like(acc_g)

        def block(idx, carry):
            cols = pl.ds(pl.multiple_of(idx * tile, tile), tile)
            h = dot_f32(xall[rows, :], win[:, cols])
            grad = dot_nt(gp[rows, :], wout[cols, :])
            value, slope = gelu_both(h)
            value = value.astype(bf16)
            grad = (grad * slope).astype(bf16)
            act[rows, cols] = value
            gpre[rows, cols] = grad
            acc_p[...] += dot_f32(value, wout[cols, :])
            acc_g[...] += dot_nt(grad, win[:, cols])
            return carry

        lax.fori_loop(0, hidden // tile, block, 0)
        made = acc_p[...].astype(bf16)
        prod[rows, :] = made
        gate_grad = jnp.sum(gr[rows, :].astype(f32) * made.astype(f32), axis=-1, keepdims=True)
        low = (gate_grad * gate * (mine - probs)).astype(bf16)
        low = jnp.where(lanes < experts, low, jnp.zeros_like(low))
        logit[rows, :] = low
        gsend[rows, :] = (acc_g[...] + dot_nt(low, rw[...])).astype(bf16)

        @pl.when(step == 0)
        def _():
            send_back(sibling).start()

        @pl.when(step > 0)
        def _():
            send_back(2 * where).start()
            send_back(2 * where + 1).start()

        return carry

    lax.fori_loop(0, chips, work, 0)
    outs = [
        pltpu.make_async_copy(prod, prod_o, local.at[0]),
        pltpu.make_async_copy(gsend.at[rows_of(me), :], gback.at[rows_of(me), :], local.at[3]),
    ]
    for copy in outs:
        copy.start()
    xt[...] = xall[...].T
    gpt[...] = gp[...].T
    drw_o[...] = dot_f32(xt[...], logit[...])

    share = width // 4
    tiles = hidden // tile
    split = tiles // 2

    def left_copy(idx, block):
        cols = pl.ds(pl.multiple_of(idx * tile, tile), tile)
        rows = pl.ds(pl.multiple_of((1 - dp_x + 2 * block) * share, 16), share)
        return pltpu.make_async_remote_copy(
            src_ref=dwt.at[rows, cols], dst_ref=shared_o.at[pl.ds(block * share, share), cols],
            send_sem=send_s.at[block, idx], recv_sem=recv_s.at[block, idx], device_id={"dp": peer_x},
        )

    def right_copy(idx, block):
        cols = pl.ds(pl.multiple_of(idx * tile, tile), tile)
        rows = pl.ds(pl.multiple_of((2 - 2 * dp_y + block) * share, 16), share)
        dst_cols = pl.ds(pl.multiple_of((idx - split) * tile, tile), tile)
        return pltpu.make_async_remote_copy(
            src_ref=dwt.at[rows, cols], dst_ref=shared_o.at[pl.ds((2 + block) * share, share), dst_cols],
            send_sem=send_s.at[block, idx], recv_sem=recv_s.at[block, idx], device_id={"dp": peer_y},
        )

    def out_block(step, carry):
        idx = lax.rem(step, 2) * split + step // 2
        cols = pl.ds(pl.multiple_of(idx * tile, tile), tile)
        dwt[:, cols] = dot_f32(gpt[...], act[:, cols]).astype(bf16)

        @pl.when(idx < split)
        def _():
            for block in range(2):
                left_copy(idx, block).start()

        @pl.when(idx >= split)
        def _():
            for block in range(2):
                right_copy(idx, block).start()

        return carry

    lax.fori_loop(0, tiles, out_block, 0)
    whole = pltpu.make_async_copy(dwt, dwout_o, local.at[2])
    whole.start()

    def put(slot, cols):
        return pltpu.make_async_copy(stage.at[slot], dwin_o.at[:, cols], out_sem.at[slot])

    def in_block(idx, carry):
        cols = pl.ds(pl.multiple_of(idx * tile, tile), tile)
        slot = lax.rem(idx, 2)

        @pl.when(idx > 1)
        def _():
            put(slot, cols).wait()

        stage[slot] = dot_f32(xt[...], gpre[:, cols]).astype(bf16)
        put(slot, cols).start()
        return carry

    lax.fori_loop(0, tiles, in_block, 0)
    for slot in range(2):
        put(slot, pl.ds(0, tile)).wait()
    whole.wait()
    for copy in outs:
        copy.wait()
    for k in range(1, experts):
        peer = lax.rem(me + k, experts)
        got_rows(peer).wait_send()
        got_back(peer).wait_send()
        got_back(peer).wait_recv()
    back = pltpu.make_async_copy(gback, gback_o, local.at[1])
    back.start()
    for idx in range(tiles):
        for block in range(2):
            (left_copy if idx < split else right_copy)(idx, block).wait()
    back.wait()


def expert_pass(xs, gr, weight_in, weight_out, router_pad, experts, capacity):
    slots, width = xs.shape
    hidden = weight_in.shape[1]
    tile = 512
    span = 2 * capacity
    hbm = pl.BlockSpec(memory_space=pl.ANY)
    vmem = pl.BlockSpec(memory_space=pltpu.VMEM)
    return pl.pallas_call(
        functools.partial(expert_kernel, experts, capacity, tile),
        in_specs=[hbm, hbm, hbm, hbm, vmem],
        out_specs=[hbm, hbm, hbm, hbm, vmem, hbm],
        out_shape=[
            jax.ShapeDtypeStruct((slots, width), bf16),
            jax.ShapeDtypeStruct((slots, width), bf16),
            jax.ShapeDtypeStruct((width, hidden), bf16),
            jax.ShapeDtypeStruct((width, hidden), bf16),
            jax.ShapeDtypeStruct((width, router_pad.shape[1]), f32),
            jax.ShapeDtypeStruct((width, hidden // 2), bf16),
        ],
        scratch_shapes=[
            pltpu.VMEM((slots, width), bf16),
            pltpu.VMEM((slots, width), bf16),
            pltpu.VMEM((slots, width), bf16),
            pltpu.VMEM((width, hidden), bf16),
            pltpu.VMEM((hidden, width), bf16),
            pltpu.VMEM((slots, hidden), bf16),
            pltpu.VMEM((slots, hidden), bf16),
            pltpu.VMEM((slots, width), bf16),
            pltpu.VMEM((slots, width), bf16),
            pltpu.VMEM((slots, width), bf16),
            pltpu.VMEM((slots, router_pad.shape[1]), bf16),
            pltpu.VMEM((span, width), f32),
            pltpu.VMEM((span, width), f32),
            pltpu.VMEM((width, slots), bf16),
            pltpu.VMEM((width, slots), bf16),
            pltpu.VMEM((2, width, tile), bf16),
            pltpu.VMEM((width, hidden), bf16),
            pltpu.SemaphoreType.DMA((experts,)),
            pltpu.SemaphoreType.DMA((experts,)),
            pltpu.SemaphoreType.DMA((experts,)),
            pltpu.SemaphoreType.DMA((experts,)),
            pltpu.SemaphoreType.DMA((4,)),
            pltpu.SemaphoreType.DMA((2,)),
            pltpu.SemaphoreType.DMA((2, hidden // tile)),
            pltpu.SemaphoreType.DMA((2, hidden // tile)),
        ],
        compiler_params=pltpu.CompilerParams(
            vmem_limit_bytes=60 << 20, collective_id=1, has_side_effects=True
        ),
        cost_estimate=pl.CostEstimate(
            flops=12 * slots * width * hidden, bytes_accessed=8 * width * hidden, transcendentals=slots * hidden
        ),
        name="experts",
    )(xs, gr, weight_in, weight_out, router_pad)


def remote(src, dst, send_sem, recv_sem, axis, peer):
    return pltpu.make_async_remote_copy(
        src_ref=src, dst_ref=dst, send_sem=send_sem, recv_sem=recv_sem, device_id={axis: peer}
    )


def others(count, mine):
    return [lax.rem(mine + k, count) for k in range(1, count)]


PLAN = (
    (11, 16, 19, 22, 24),
    (12, 17, 20, 23, 25),
    (5, 13, 16, 19, 21),
    (9, 15, 18, 21, 23),
    (13, 18, 21, 24, 26),
    (17, 21, 24, 27, 29),
    (21, 24, 27, 29, 31),
)
OUTPUT_SLOT = 17
EXPERT_SLOTS = ((6, 2, 0), (14, 3, 0), (15, 2, 1), (22, 3, 1))


def back_kernel(
    groups, experts, pairs,
    q_ref, k_ref, v_ref, g_ref, ctxt_ref, wq, wk, wv, hot, gain, nl_h, tok_h, ghid_h, dwo_h, small_h,
    eout_h, shared_h, ein_h, p_h, prod_h, hid_h, meta,
    wsum_o, ing_o, small_o, esum_o, out_o,
    acc, vaug, gaug, qz, gz, kt, dqt, pbuf, pret, hbuf, obuf, dall, nt, tok,
    part, r1, r2, r3, full, sbuf, srecv, sone, stwo, keep, other, final,
    send1, recv1, send2, recv2, send3, recv3, send4, recv4, send5, recv5, send6, recv6, send7, recv7, local,
    send_a, recv_a, send_b, recv_b, out_sem, copy_sem, p_sem, send_p, recv_p, o_sem,
):
    seq = q_ref.shape[0]
    width = tok.shape[1]
    span = 256
    pair = pl.program_id(0)
    me = lax.axis_index("expert")
    my_dp = lax.axis_index("dp")
    core = lax.rem(me, 2)
    place = me // 2
    chips = experts // 2
    sibling = me + 1 - 2 * core
    half = width // 2
    piece = half // groups
    thick = part.shape[2]
    gain_rows = width // 128

    def half_rows(which):
        return pl.ds(pl.multiple_of(which * half, 16), half)

    def own_piece(which):
        return pl.ds(pl.multiple_of(core * half + which * piece, 16), piece)

    def copy1(c):
        return remote(part.at[c, half_rows(1 - core), :], r1.at[c], send1.at[c], recv1.at[c], "expert", sibling)

    def copy2(c, peer, slot):
        return remote(part.at[c, own_piece(peer), :], r2.at[c, slot], send2.at[c, peer], recv2.at[c, slot], "dp", peer)

    def copy3(c, peer, slot):
        return remote(
            r3.at[c, place], r3.at[c, slot], send3.at[c, peer], recv3.at[c, slot], "expert", 2 * peer + core
        )

    def copy4(c, peer, slot):
        return remote(
            full.at[c, own_piece(my_dp), :], full.at[c, own_piece(slot), :],
            send4.at[c, peer], recv4.at[c, slot], "dp", peer,
        )

    def copy5(c, which):
        return remote(
            full.at[c, half_rows(which), :], full.at[c, half_rows(which), :],
            send5.at[c], recv5.at[c], "expert", sibling,
        )

    def stage1(c):
        copy1(c).start()

    def stage2(c):
        copy1(c).wait_recv()
        part[c, half_rows(core), :] = (part[c, half_rows(core), :].astype(f32) + r1[c].astype(f32)).astype(bf16)
        for peer in others(groups, my_dp):
            copy2(c, peer, my_dp).start()

    def stage3(c):
        total = part[c, own_piece(my_dp), :].astype(f32)
        for peer in others(groups, my_dp):
            copy2(c, peer, peer).wait_recv()
            total = total + r2[c, peer].astype(f32)
        r3[c, place] = total.astype(bf16)
        for peer in others(chips, place):
            copy3(c, peer, place).start()

    def stage4(c):
        for peer in others(chips, place):
            copy3(c, peer, peer).wait_recv()
        total = r3[c, 0].astype(f32)
        for slot in range(1, chips):
            total = total + r3[c, slot].astype(f32)
        full[c, own_piece(my_dp), :] = total.astype(bf16)
        for peer in others(groups, my_dp):
            copy4(c, peer, my_dp).start()

    def stage5(c):
        for peer in others(groups, my_dp):
            copy4(c, peer, peer).wait_recv()
        copy5(c, core).start()

    def put_first(c):
        return pltpu.make_async_copy(full.at[c], wsum_o.at[0, :, thick * c : thick * c + thick], out_sem.at[c, 0])

    def put_pair(c, which):
        cols = pl.ds(128 * (c - 2) if isinstance(c, int) else pl.multiple_of(128 * (c - 2), 128), 128)
        return pltpu.make_async_copy(
            full.at[c, :, 128 * which : 128 * which + 128], wsum_o.at[1 + which, :, cols], out_sem.at[c, which]
        )

    def stage6(c):
        copy5(c, 1 - core).wait_recv()

        if c < 2:
            put_first(c).start()
        else:
            for which in range(3):
                put_pair(c, which).start()

    share = width // 4
    dp_x, dp_y = lax.rem(my_dp, 2), my_dp // 2
    peer_x, peer_y = my_dp + 1 - 2 * dp_x, my_dp + 2 - 4 * dp_y
    middle = keep.shape[1]
    left, right = pl.ds(0, middle), pl.ds(middle, middle)

    def share_rows(which):
        return pl.ds(pl.multiple_of(which * share, 16), share)

    def first_left(block):
        return remote(
            ein_h.at[share_rows(1 - dp_x + 2 * block), left], other.at[1, share_rows(block), :],
            send_a.at[0, block], recv_a.at[0, block], "dp", peer_x,
        )

    def first_right(block):
        return remote(
            ein_h.at[share_rows(2 - 2 * dp_y + block), right], other.at[1, share_rows(2 + block), :],
            send_a.at[1, block], recv_a.at[1, block], "dp", peer_y,
        )

    def second_left(which):
        return remote(
            keep.at[share_rows(1 - dp_y), :], final.at[which, :, left],
            send_b.at[which, 0], recv_b.at[which, 0], "dp", peer_y,
        )

    def second_right(which):
        return remote(
            keep.at[share_rows(2 + 1 - dp_x), :], final.at[which, :, right],
            send_b.at[which, 1], recv_b.at[which, 1], "dp", peer_x,
        )

    def own_loads(src):
        loads = []
        for block in range(2):
            loads.append(
                pltpu.make_async_copy(
                    src.at[share_rows(dp_x + 2 * block), left], keep.at[share_rows(block), :], copy_sem.at[block]
                )
            )
            loads.append(
                pltpu.make_async_copy(
                    src.at[share_rows(2 * dp_y + block), right], keep.at[share_rows(2 + block), :], copy_sem.at[2 + block]
                )
            )
        return loads

    def shared_load():
        return pltpu.make_async_copy(shared_h, other.at[0], copy_sem.at[4])

    def save(which):
        return pltpu.make_async_copy(final.at[which], esum_o.at[which], copy_sem.at[5])

    def experts_begin():
        for copy in own_loads(eout_h) + [shared_load()]:
            copy.start()
        for block in range(2):
            first_left(block).start()
            first_right(block).start()

    def experts_second(which):
        for copy in own_loads(eout_h if which == 0 else ein_h):
            copy.wait()
        if which == 0:
            shared_load().wait()
        else:
            for block in range(2):
                first_left(block).wait_recv()
                first_right(block).wait_recv()

        def block(idx, carry):
            rows = pl.ds(pl.multiple_of(idx * 64, 64), 64)
            keep[rows, :] = (keep[rows, :].astype(f32) + other[which, rows, :].astype(f32)).astype(bf16)
            return carry

        lax.fori_loop(0, width // 64, block, 0)
        second_left(which).start()
        second_right(which).start()

    def experts_last(which):
        second_left(which).wait()
        second_right(which).wait()

        def block(idx, carry):
            rows = pl.ds(pl.multiple_of(idx * 64, 64), 64)
            mine_left = pl.ds(pl.multiple_of(dp_y * share + idx * 64, 64), 64)
            mine_right = pl.ds(pl.multiple_of((2 + dp_x) * share + idx * 64, 64), 64)
            final[which, rows, left] = (final[which, rows, left].astype(f32) + keep[mine_left, :].astype(f32)).astype(bf16)
            final[which, rows, right] = (final[which, rows, right].astype(f32) + keep[mine_right, :].astype(f32)).astype(bf16)
            return carry

        lax.fori_loop(0, share // 64, block, 0)
        if which == 0:
            for copy in own_loads(ein_h):
                copy.start()
        else:
            save(0).wait()
        save(which).start()

    early = pl.ds(8 + hot.shape[0], sbuf.shape[0] - 8 - hot.shape[0])
    late = pl.ds(0, 8 + hot.shape[0])

    def copy6(part_idx, rows, peer, slot):
        return remote(
            sbuf.at[rows, :], srecv.at[slot, rows, :],
            send6.at[part_idx, peer], recv6.at[part_idx, slot], "expert", peer,
        )

    def copy7(part_idx, rows, peer, slot):
        return remote(
            sone.at[rows, :], stwo.at[slot, rows, :],
            send7.at[part_idx, peer], recv7.at[part_idx, slot], "dp", peer,
        )

    def small1(part_idx, rows):
        srecv[me, rows, :] = sbuf[rows, :]
        for peer in others(experts, me):
            copy6(part_idx, rows, peer, me).start()

    def small2(part_idx, rows):
        for peer in others(experts, me):
            copy6(part_idx, rows, peer, peer).wait_recv()
        total = srecv[0, rows, :]
        for slot in range(1, experts):
            total = total + srecv[slot, rows, :]
        sone[rows, :] = total
        stwo[my_dp, rows, :] = total
        for peer in others(groups, my_dp):
            copy7(part_idx, rows, peer, my_dp).start()

    def small3(part_idx, rows):
        for peer in others(groups, my_dp):
            copy7(part_idx, rows, peer, peer).wait_recv()
        total = stwo[0, rows, :]
        for slot in range(1, groups):
            total = total + stwo[slot, rows, :]
        small_o[rows, :] = total

    stages = (stage2, stage3, stage4, stage5, stage6)

    def advance(slot):
        for c, slots in enumerate(PLAN):
            for at, stage in reversed(list(zip(slots, stages))):
                if at < 4 * pairs:
                    pl.when(slot == at)(functools.partial(stage, c))

    def load_p(slot_idx, slot):
        rows = pl.ds(pl.multiple_of(lax.rem(slot_idx, 4) * span, span), span)
        return pltpu.make_async_copy(p_h.at[pl.ds(2 * (slot_idx // 4), 2), rows, :], pbuf.at[slot], p_sem.at[slot])

    slots_each = pret.shape[0] // experts

    def slot_rows(which):
        return pl.ds(pl.multiple_of(which * slots_each, 16), slots_each)

    def give_back(peer):
        return remote(
            prod_h.at[slot_rows(peer), :], pret.at[slot_rows(me), :], send_p.at[peer], recv_p.at[me], "expert", peer
        )

    def got_back(peer):
        return remote(
            prod_h.at[slot_rows(peer), :], pret.at[slot_rows(peer), :], send_p.at[peer], recv_p.at[peer], "expert", peer
        )

    def own_back():
        return pltpu.make_async_copy(prod_h.at[slot_rows(me), :], pret.at[slot_rows(me), :], o_sem.at[0])

    def out_rows(block):
        return pl.ds(block * span, span)

    def load_hidden(block):
        return pltpu.make_async_copy(hid_h.at[out_rows(block), :], hbuf, o_sem.at[1])

    def save_out(block):
        return pltpu.make_async_copy(obuf, out_o.at[out_rows(block), :], o_sem.at[2])

    def output_block(block):
        if block == 0:
            own_back().wait()
            for peer in others(experts, me):
                got_back(peer).wait_recv()
        load_hidden(block).wait()
        where = lax.broadcasted_iota(jnp.int32, (span, pret.shape[0]), 1).astype(f32)
        pick = jnp.where(meta[out_rows(block), 1:2] == where, 1.0, 0.0).astype(bf16)
        gathered = dot_f32(pick, pret[...])
        if block > 0:
            save_out(block - 1).wait()
        obuf[...] = (hbuf[...] + meta[out_rows(block), 0:1] * gathered).astype(bf16)
        save_out(block).start()
        if (block + 1) * span < seq:
            load_hidden(block + 1).start()

    loads = [
        pltpu.make_async_copy(nl_h, tok, local.at[0]),
        pltpu.make_async_copy(ghid_h, ing_o, local.at[2]),
        pltpu.make_async_copy(dwo_h.at[:, 0:thick], part.at[0], local.at[3]),
        pltpu.make_async_copy(dwo_h.at[:, thick : 2 * thick], part.at[1], local.at[4]),
        pltpu.make_async_copy(small_h, sbuf, local.at[5]),
    ]

    @pl.when(pair == 0)
    def _():
        barrier = pltpu.get_barrier_semaphore()
        for peer in others(experts, me):
            pl.semaphore_signal(barrier, inc=1, device_id={"expert": peer})
        for peer in others(groups, my_dp):
            pl.semaphore_signal(barrier, inc=1, device_id={"dp": peer})
        for copy in loads:
            copy.start()
        load_p(0, 0).start()
        own_back().start()
        load_hidden(0).start()
        for copy in loads:
            copy.wait()
        nt[...] = tok[...].T
        pl.semaphore_wait(barrier, experts + groups - 2)
        stage1(0)
        stage1(1)
        small1(0, early)
        experts_begin()
        for peer in others(experts, me):
            give_back(peer).start()

    mine = pl.ds(pl.multiple_of(128 * pair, 128), 128)
    lane = lax.broadcasted_iota(jnp.int32, (seq, 128), 1)
    gt = g_ref[...].T
    kt[...] = k_ref[...].T
    gtf = gt.astype(f32)
    pad = jnp.zeros((48, seq), bf16)
    one = jnp.ones((seq, 128), bf16)
    nil = jnp.zeros((seq, 128), bf16)
    acc[...] = jnp.zeros_like(acc)
    for head in range(2):
        own = (lane < 64) if head == 0 else (lane >= 64)
        origin = 64 if head == 0 else 0
        extra = jnp.where((lane >= origin) & (lane < origin + 3), one, nil)
        vaug[head] = jnp.where(own, v_ref[...], extra)
        qz[head] = jnp.where(own, q_ref[...], nil)
        gz[head] = jnp.where(own, g_ref[...], nil)
        rows = slice(64 * head, 64 * head + 64)
        gaug[head, rows, :] = gt[rows]
        gaug[head, origin : origin + 16, :] = split_rows(
            -jnp.sum(gtf[rows] * ctxt_ref[rows, :], axis=0, keepdims=True)
        )
        gaug[head, origin + 16 : origin + 64, :] = pad

    dqt[...] = jnp.zeros_like(dqt)

    def step(idx, carry):
        rows = pl.ds(pl.multiple_of(idx * span, span), span)
        dv = None
        dk = None
        slot = lax.rem(idx, 2)
        load_p(4 * pair + idx, slot).wait()

        @pl.when(4 * pair + idx + 1 < 4 * pairs)
        def _():
            load_p(4 * pair + idx + 1, 1 - slot).start()

        for head in range(2):
            dp = dot_f32(vaug[head, rows, :], gaug[head])
            grads = []
            for part_idx in range(2):
                offs = pl.ds(pl.multiple_of(seq - span * idx - 128 * part_idx, 128), seq)
                band = slice(128 * part_idx, 128 * part_idx + 128)
                ds_ = pbuf[slot, head, band, :].astype(f32) * dp[band]
                acc[head, :, offs] += ds_
                grads.append(ds_.astype(bf16))
            ds_ = jnp.concatenate(grads, axis=0)
            now = dot_f32(pbuf[slot, head], gz[head])
            dv = now if dv is None else dv + now
            now = dot_f32(ds_, qz[head])
            dk = now if dk is None else dk + now
            dqt[64 * head : 64 * head + 64, :] += dot_f32(kt[64 * head : 64 * head + 64, rows], ds_)
        dall[1, rows, mine] = dk.astype(bf16)
        dall[2, rows, mine] = dv.astype(bf16)
        advance(4 * pair + idx)

        for block in range(seq // span):
            @pl.when(4 * pair + idx == OUTPUT_SLOT + block)
            def _():
                output_block(block)

        for at, task, which in EXPERT_SLOTS:
            @pl.when(4 * pair + idx == at)
            def _():
                (experts_second if task == 2 else experts_last)(which)

        @pl.when(4 * pair + idx == 7)
        def _():
            small2(0, early)

        @pl.when(4 * pair + idx == 11)
        def _():
            small3(0, early)

        return carry

    lax.fori_loop(0, seq // span, step, 0)
    dall[0, :, mine] = dqt[...].T.astype(bf16)
    twice = 2 * seq
    sub = lax.broadcasted_iota(jnp.int32, (8, twice), 0)
    head_lane = lax.broadcasted_iota(jnp.int32, (hot.shape[0], 128), 1)
    rel_rows = slice(8, 8 + hot.shape[0])
    for head in range(2):
        total = acc[head, 0:8, :]
        for group in range(1, 16):
            total = total + pltpu.roll(acc[head, 8 * group : 8 * group + 8, :], twice - 8 * group, 1)
        for bit in (1, 2, 4):
            total = jnp.where((sub & bit) != 0, pltpu.roll(total, twice - bit, 1), total)
        diag = jnp.sum(total, axis=0, keepdims=True)
        sums = jnp.sum(hot[...] * diag, axis=1, keepdims=True)
        sbuf[rel_rows, :] = jnp.where(head_lane == 2 * pair + head, sums, sbuf[rel_rows, :])

    def weight_block(idx, carry):
        rows = pl.ds(pl.multiple_of(idx * 256, 256), 256)
        grads = jnp.concatenate([dall[which, :, mine] for which in range(3)], axis=1)
        part[pair + 2, rows, :] = dot_f32(nt[rows, :], grads).astype(bf16)
        return carry

    lax.fori_loop(0, width // 256, weight_block, 0)
    stage1(pair + 2)

    @pl.when(pair == pairs - 1)
    def _():
        def token_block(idx, carry):
            rows = pl.ds(pl.multiple_of(idx * 256, 256), 256)
            grad = (
                dot_nt(dall[0, rows, :], wq[...])
                + dot_nt(dall[1, rows, :], wk[...])
                + dot_nt(dall[2, rows, :], wv[...])
            )
            values = tok[rows, :].astype(f32)
            scale = lax.rsqrt(jnp.mean(values * values, axis=-1, keepdims=True) + epsilon)
            weighted = grad * gain[...]
            inner = jnp.mean(weighted * values, axis=-1, keepdims=True)
            ing_o[rows, :] += scale * weighted - values * (scale * scale * scale * inner)
            return carry + jnp.sum(grad * values * scale, axis=0, keepdims=True)

        reload = pltpu.make_async_copy(tok_h, tok, local.at[1])
        reload.start()
        last = pairs + 1
        first = 4 * pairs
        older = sorted(
            (at, c, stage)
            for c, slots in enumerate(PLAN)
            for stage, at in enumerate(slots)
            if at >= first
        )

        def drain(until):
            while older and older[0][0] < first + until:
                _, c, stage = older.pop(0)
                stages[stage](c)

        def tokens_done(lower, upper, gain_grad):
            return lax.fori_loop(lower, upper, token_block, gain_grad)

        drain(1)
        reload.wait()
        gain_grad = tokens_done(0, 1, jnp.zeros((1, width), f32))
        stage2(last)
        drain(2)
        gain_grad = tokens_done(1, seq // 512, gain_grad)
        drain(4)
        gain_grad = tokens_done(seq // 512, seq // 256, gain_grad)
        stage3(last)
        for row in range(gain_rows):
            sbuf[row : row + 1, :] = gain_grad[:, 128 * row : 128 * row + 128]
        small1(1, late)
        drain(8)
        small2(1, late)
        stage4(last)
        drain(99)
        small3(1, late)
        stage5(last)
        stage6(last)
        for c in range(2):
            put_first(c).wait()
        save(1).wait()
        save_out(seq // span - 1).wait()
        for peer in others(experts, me):
            give_back(peer).wait_send()
        for block in range(2):
            first_left(block).wait_send()
            first_right(block).wait_send()

        def finish(c, carry):
            copy1(c).wait_send()
            for peer in others(groups, my_dp):
                copy2(c, peer, my_dp).wait_send()
                copy4(c, peer, my_dp).wait_send()
            for peer in others(chips, place):
                copy3(c, peer, place).wait_send()
            copy5(c, core).wait_send()

            @pl.when(c >= 2)
            def _():
                for which in range(3):
                    put_pair(c, which).wait()

            return carry

        lax.fori_loop(0, pairs + 2, finish, 0)
        for part_idx, rows in ((0, early), (1, late)):
            for peer in others(experts, me):
                copy6(part_idx, rows, peer, me).wait_send()
            for peer in others(groups, my_dp):
                copy7(part_idx, rows, peer, my_dp).wait_send()


def back_pass(
    q, k, v, g, ctxt, wq, wk, wv, hot, gain, normed_low, tokens, grad_hidden, dwo, small,
    expert_out_grad, shared, expert_in_grad, weights, produced, hidden_rows, meta, groups, experts
):
    seq, width = q.shape
    pairs = width // 128
    chunks = pairs + 2
    hidden = expert_in_grad.shape[1]
    thick = width // 2
    half = width // 2
    piece = half // groups
    chips = experts // 2
    blk = pl.BlockSpec((seq, 128), lambda p: (0, p))
    hbm = pl.BlockSpec(memory_space=pl.ANY)
    fixed = lambda shape: pl.BlockSpec(shape, lambda p: (0,) * len(shape), pipeline_mode=pl.Buffered(1))
    dma = pltpu.SemaphoreType.DMA
    return pl.pallas_call(
        functools.partial(back_kernel, groups, experts, pairs),
        grid=(pairs,),
        in_specs=[
            blk, blk, blk, blk,
            pl.BlockSpec((128, seq), lambda p: (p, 0)),
            fixed((width, width)), fixed((width, width)), fixed((width, width)),
            fixed(hot.shape), fixed(gain.shape),
            hbm, hbm, hbm, hbm, hbm, hbm, hbm, hbm,
            hbm, hbm, hbm, fixed(meta.shape),
        ],
        out_specs=[hbm, fixed((seq, width)), fixed(small.shape), hbm, hbm],
        out_shape=[
            jax.ShapeDtypeStruct((4, width, width), bf16),
            jax.ShapeDtypeStruct((seq, width), f32),
            jax.ShapeDtypeStruct(small.shape, f32),
            jax.ShapeDtypeStruct((2, width // 4, hidden), bf16),
            jax.ShapeDtypeStruct((seq, width), bf16),
        ],
        scratch_shapes=[
            pltpu.VMEM((2, 128, 2 * seq), f32),
            pltpu.VMEM((2, seq, 128), bf16),
            pltpu.VMEM((2, 128, seq), bf16),
            pltpu.VMEM((2, seq, 128), bf16),
            pltpu.VMEM((2, seq, 128), bf16),
            pltpu.VMEM((128, seq), bf16),
            pltpu.VMEM((128, seq), f32),
            pltpu.VMEM((2, 2, 256, seq), bf16),
            pltpu.VMEM(produced.shape, bf16),
            pltpu.VMEM((256, width), f32),
            pltpu.VMEM((256, width), bf16),
            pltpu.VMEM((3, seq, width), bf16),
            pltpu.VMEM((width, seq), bf16),
            pltpu.VMEM((seq, width), bf16),
            pltpu.VMEM((chunks, width, thick), bf16),
            pltpu.VMEM((chunks, half, thick), bf16),
            pltpu.VMEM((chunks, groups, piece, thick), bf16),
            pltpu.VMEM((chunks, chips, piece, thick), bf16),
            pltpu.VMEM((chunks, width, thick), bf16),
            pltpu.VMEM(small.shape, f32),
            pltpu.VMEM((experts,) + small.shape, f32),
            pltpu.VMEM(small.shape, f32),
            pltpu.VMEM((groups,) + small.shape, f32),
            pltpu.VMEM((width, hidden // 2), bf16),
            pltpu.VMEM((2, width, hidden // 2), bf16),
            pltpu.VMEM((2, width // 4, hidden), bf16),
            dma((chunks,)), dma((chunks,)),
            dma((chunks, groups)), dma((chunks, groups)),
            dma((chunks, chips)), dma((chunks, chips)),
            dma((chunks, groups)), dma((chunks, groups)),
            dma((chunks,)), dma((chunks,)),
            dma((2, experts)), dma((2, experts)),
            dma((2, groups)), dma((2, groups)),
            dma((6,)),
            dma((2, 2)), dma((2, 2)),
            dma((2, 2)), dma((2, 2)),
            dma((chunks, 3)), dma((6,)),
            dma((2,)), dma((experts,)), dma((experts,)), dma((3,)),
        ],
        compiler_params=pltpu.CompilerParams(
            vmem_limit_bytes=62 << 20, collective_id=2, has_side_effects=True
        ),
        cost_estimate=pl.CostEstimate(
            flops=40 * seq * seq * width + 12 * seq * width * width,
            bytes_accessed=40 * seq * width, transcendentals=seq * seq * 12,
        ),
        name="attend_back",
    )(
        q, k, v, g, ctxt, wq, wk, wv, hot, gain, normed_low, tokens, grad_hidden, dwo, small,
        expert_out_grad, shared, expert_in_grad, weights, produced, hidden_rows, meta,
    )


def rms_backward(grad_norm, values, row_scale, gain_vec):
    weighted = grad_norm * gain_vec
    gain_grad = jnp.sum(grad_norm * values * row_scale, axis=0)
    grad_in = row_scale * weighted - values * row_scale**3 * jnp.mean(
        weighted * values, axis=-1, keepdims=True
    )
    return grad_in, gain_grad


def rms_forward(values, gain_vec):
    row_scale = lax.rsqrt(jnp.mean(values * values, axis=-1, keepdims=True) + epsilon)
    return values * row_scale * gain_vec, row_scale


def gelu_tanh(values):
    return jax.nn.gelu(values, approximate=True)


def contract(left, right, dims):
    return lax.dot_general(left, right, (((dims[0],), (dims[1],)), ((), ())), preferred_element_type=f32)


def exchange(rows, experts):
    slots, width = rows.shape
    rows = rows.reshape(experts, slots // experts, width)
    return lax.all_to_all(rows, "expert", split_axis=0, concat_axis=0, tiled=True).reshape(slots, width)


def expert_native(send, grad_recv, weight_in, weight_out, router_w, experts):
    received = exchange(send, experts)
    own = lax.axis_index("expert")
    own_hot = (jnp.arange(experts, dtype=jnp.int32) == own).astype(f32)[None, :]
    probs = jax.nn.softmax(contract(received, router_w, (1, 0)), axis=-1)
    gate = jnp.sum(probs * own_hot, axis=-1, keepdims=True)
    grad_recv_f = grad_recv.astype(f32)
    grad_produced = (grad_recv_f * gate).astype(bf16)
    preact = contract(received, weight_in, (1, 0))
    gelu_values, gelu_pullback = jax.vjp(gelu_tanh, preact)
    active = gelu_values.astype(bf16)
    produced = contract(active, weight_out, (1, 0)).astype(bf16)
    gate_grad = jnp.sum(grad_recv_f * produced.astype(f32), axis=-1, keepdims=True)
    logit_low = (gate_grad * gate * (own_hot - probs)).astype(bf16)
    grad_active = contract(grad_produced, weight_out, (1, 1))
    grad_preact = gelu_pullback(grad_active)[0].astype(bf16)
    grad_received = contract(grad_preact, weight_in, (1, 1)) + contract(logit_low, router_w, (1, 1))
    grad_rows = exchange(grad_received.astype(bf16), experts)
    in_grad = contract(received, grad_preact, (0, 0)).astype(bf16)
    out_grad_t = contract(grad_produced, active, (0, 0)).astype(bf16)
    router_grad = contract(received, logit_low, (0, 0))
    return grad_rows, produced, in_grad, out_grad_t, router_grad


def tail_native(tokens, gain, normed_low, dq, dk, dv, wq, wk, wv, grad_hidden, dwo, small):
    tokens_f = tokens.astype(f32)
    grads = jnp.stack([dwo.astype(f32)] + [contract(normed_low, d, (0, 0)) for d in (dq, dk, dv)])
    grad_normed = contract(dq, wq, (1, 1)) + contract(dk, wk, (1, 1)) + contract(dv, wv, (1, 1))
    _, scale = rms_forward(tokens_f, gain)
    grad_tokens, gain_grad = rms_backward(grad_normed, tokens_f, scale, gain)
    grads, gain_grad, small = lax.psum((grads, gain_grad, small), ("dp", "expert"))
    return grads, grad_hidden + grad_tokens, gain_grad, small


def on_device(
    tokens, gain_one, query_w, key_w, value_w, out_w, rel_table, gain_two, router_w,
    expert_in, expert_out, routes, buckets, cotangent,
):
    seq_len, width = tokens.shape
    heads = rel_table.shape[1]
    groups = lax.axis_size("dp")
    experts = lax.axis_size("expert")
    capacity = (5 * seq_len + 4 * experts - 1) // (4 * experts)
    slots = experts * capacity
    weight_in = expert_in[0]
    weight_out = expert_out[0]
    kernels = capacity % 16 == 0 and experts == 8 and groups == 4

    route_ids = routes[:, 0]
    route_hot = route_ids[:, None] == jnp.arange(experts, dtype=jnp.int32)[None, :]
    route_int = route_hot.astype(jnp.int32)
    route_float = route_hot.astype(f32)
    position = jnp.sum((jnp.cumsum(route_int, axis=0) - 1) * route_int, axis=1)
    slot_index = jnp.where(position < capacity, route_ids * capacity + position, slots)
    pick = (jnp.arange(slots, dtype=jnp.int32)[:, None] == slot_index[None, :]).astype(bf16)

    def scatter_rows(rows):
        return contract(pick, rows, (1, 0)).astype(bf16)

    def gather_rows(rows):
        return contract(pick, rows, (0, 0))

    grad_recv = exchange(scatter_rows(cotangent), experts)

    tokens_f = tokens.astype(f32)
    normed, scale_one = rms_forward(tokens_f, gain_one)
    normed_low = normed.astype(bf16)
    queries = contract(normed_low, query_w, (1, 0)).astype(bf16)
    key_rows = contract(normed_low, key_w, (1, 0)).astype(bf16)
    value_rows = contract(normed_low, value_w, (1, 0)).astype(bf16)
    reach = jnp.concatenate([buckets, jnp.full((1,), -1, jnp.int32)])[::-1]
    bucket_hot = (jnp.arange(rel_table.shape[0], dtype=jnp.int32)[:, None] == reach[None, :]).astype(f32)
    spread = jnp.einsum("bh,bx->hx", rel_table, bucket_hot, precision=highest)
    spread = spread.reshape(heads // 2, 2, 2 * seq_len)
    context, context_t, logsum, weights = attend(queries, key_rows, value_rows, spread)
    context, grad_recv = lax.optimization_barrier((context, grad_recv))
    hidden = tokens_f + contract(context, out_w, (1, 0))
    normed_two, scale_two = rms_forward(hidden, gain_two)
    normed_two_low = normed_two.astype(bf16)

    send = scatter_rows(normed_two_low)
    if kernels:
        router_pad = jnp.pad(router_w, ((0, 0), (0, 128 - experts)))
        grad_rows, produced, in_grad, out_grad_t, router_grad, shared = expert_pass(
            send, grad_recv, weight_in, weight_out, router_pad, experts, capacity
        )
        router_grad = router_grad[:, :experts]
    else:
        grad_rows, produced, in_grad, out_grad_t, router_grad = expert_native(
            send, grad_recv, weight_in, weight_out, router_w, experts
        )

    router_probs = jax.nn.softmax(contract(normed_two_low, router_w, (1, 0)), axis=-1)
    gate_value = jnp.sum(router_probs * route_float, axis=-1, keepdims=True)

    grad_out = cotangent.astype(f32)
    grad_normed_two = gather_rows(grad_rows)
    grad_hidden_norm, gain_two_grad = rms_backward(grad_normed_two, hidden, scale_two, gain_two)
    grad_hidden = grad_out + grad_hidden_norm
    branch_low = grad_hidden.astype(bf16)
    out_w_grad = contract(context, branch_low, (0, 0)).astype(bf16)
    grad_context = contract(branch_low, out_w, (1, 1)).astype(bf16)
    if kernels:
        small = jnp.concatenate(
            [
                jnp.zeros((8 + rel_table.shape[0], 128), f32),
                jnp.pad(gain_two_grad.reshape(-1, 128), ((0, 2), (0, 0))),
                router_grad.T.reshape(-1, 128),
            ]
        )
        grads, input_grad, small, shares, output = back_pass(
            queries, key_rows, value_rows, grad_context, context_t, query_w, key_w, value_w,
            bucket_hot, gain_one[None], normed_low, tokens, grad_hidden, out_w_grad, small,
            out_grad_t, shared, in_grad, weights, produced, hidden,
            jnp.concatenate([gate_value, slot_index[:, None].astype(f32)], axis=1), groups, experts,
        )
        tiles = width // 128
        first = 8 + rel_table.shape[0]
        gain_one_grad = small[:tiles].reshape(-1)
        rel_grad = small[8:first, :heads]
        gain_two_grad = small[first : first + tiles].reshape(-1)
        router_grad = small[first + 8 :].reshape(experts, width).T
        out_share, in_share = shares[0], shares[1]
    else:
        output = (hidden + gate_value * gather_rows(exchange(produced, experts))).astype(bf16)
        in_share = lax.psum_scatter(in_grad, "dp", scatter_dimension=0, tiled=True)
        out_share = lax.psum_scatter(out_grad_t, "dp", scatter_dimension=0, tiled=True)
        query_grad, key_grad, value_grad, diagonals = attend_back(
            queries, key_rows, value_rows, grad_context, spread, context_t, logsum
        )
        diagonals = diagonals[:, :2].reshape(heads, 2 * seq_len)
        rel_grad = jnp.einsum("bx,hx->bh", bucket_hot, diagonals, precision=highest)
        grads, input_grad, gain_one_grad, small = tail_native(
            tokens, gain_one, normed_low, query_grad, key_grad, value_grad,
            query_w, key_w, value_w, grad_hidden, out_w_grad, (rel_grad, gain_two_grad, router_grad),
        )
        rel_grad, gain_two_grad, router_grad = small
    grads = grads.astype(f32)
    return (
        output, input_grad, grads[1], grads[2], grads[3], grads[0], rel_grad,
        gain_one_grad, gain_two_grad, router_grad, in_share.astype(f32)[None], out_share.astype(f32).T[None],
    )


def solution(mesh):
    rows = P(("dp", "expert"), None)
    whole = P()
    split = P("expert", None, None)
    return jax.shard_map(
        on_device,
        mesh=mesh,
        in_specs=(
            rows, whole, whole, whole, whole, whole, whole, whole, whole, split, split, rows, whole, rows,
        ),
        out_specs=(
            rows, rows, whole, whole, whole, whole, whole, whole, whole, whole,
            P("expert", "dp", None), P("expert", None, "dp"),
        ),
        check_vma=False,
    )
```

```python
import functools

import jax
import jax.numpy as jnp
from jax import lax
from jax.experimental import pallas as pl
from jax.experimental.pallas import tpu as pltpu
from jax.sharding import PartitionSpec as P

bf16 = jnp.bfloat16
f32 = jnp.float32
epsilon = 1e-06
highest = lax.Precision.HIGHEST

def dot_f32(left, right):
    return lax.dot_general(left, right, (((1,), (0,)), ((), ())), preferred_element_type=f32)


def dot_nt(left, right):
    return lax.dot_general(left, right, (((1,), (1,)), ((), ())), preferred_element_type=f32)


def fill_toeplitz(base_ref, head, row):
    rows, width = base_ref.shape[1:]
    spread = jnp.broadcast_to(row, (8, width))
    eight = pltpu.roll(spread, 0, 1, stride=1, stride_axis=0)
    for group in range(rows // 8):
        base_ref[head, 8 * group : 8 * group + 8, :] = (
            eight if group == 0 else pltpu.roll(eight, 8 * group, 1)
        )


def attend_kernel(
    experts, q_ref, k_ref, v_ref, u_ref, gsend_h, ctx_ref, ctxt_ref, lse_ref, p_h, grecv_h,
    base, qt, vt, s_scr, p_scr, p_sem, send_g, recv_g, own_sem,
):
    seq = q_ref.shape[0]
    span = 256
    half = seq
    qt[...] = q_ref[...].T
    vt[...] = v_ref[...].T
    for head in range(2):
        fill_toeplitz(base, head, u_ref[0, head : head + 1, :])
    zeros = jnp.zeros((64, span), bf16)
    pair = pl.program_id(0)

    if experts:
        me = lax.axis_index("expert")
        count = grecv_h.shape[0] // experts
        rows_of = lambda who: pl.ds(pl.multiple_of(who * count, 16), count)
        peers = [lax.rem(me + k, experts) for k in range(1, experts)]
        barrier = pltpu.get_barrier_semaphore()
        own = pltpu.make_async_copy(gsend_h.at[rows_of(me), :], grecv_h.at[rows_of(me), :], own_sem)

        def give(peer, slot):
            return pltpu.make_async_remote_copy(
                src_ref=gsend_h.at[rows_of(peer), :], dst_ref=grecv_h.at[rows_of(slot), :],
                send_sem=send_g.at[peer], recv_sem=recv_g.at[slot], device_id={"expert": peer},
            )

        @pl.when(pair == 0)
        def _():
            for peer in peers:
                pl.semaphore_signal(barrier, inc=1, device_id={"expert": peer})
            own.start()

    def save(idx, slot):
        cols = pl.ds(pl.multiple_of(idx * span, span), span)
        return pltpu.make_async_copy(p_scr.at[slot], p_h.at[pl.ds(2 * pair, 2), :, cols], p_sem.at[slot])

    def step(idx, carry):
        slot = lax.rem(idx, 2)

        @pl.when((pair > 0) | (idx > 1))
        def _():
            save(idx, slot).wait()

        cols = pl.ds(pl.multiple_of(idx * span, span), span)
        outs = []
        for head in range(2):
            part = qt[64 * head : 64 * head + 64, cols]
            rhs = jnp.concatenate([part, zeros] if head == 0 else [zeros, part], axis=0)
            peak = None
            for kb in range(seq // 128):
                rows = slice(128 * kb, 128 * kb + 128)
                offs = pl.multiple_of(half + span * idx - 128 * kb, 128)
                s = dot_f32(k_ref[rows, :], rhs) + base[head, :, pl.ds(offs, span)]
                s_scr[head, rows, :] = s
                now = jnp.max(s.reshape(16, 8, span), axis=0)
                peak = now if peak is None else jnp.maximum(peak, now)
            peak = jnp.max(peak, axis=0, keepdims=True)
            total = None
            for kb in range(seq // 128):
                rows = slice(128 * kb, 128 * kb + 128)
                e = jnp.exp(s_scr[head, rows, :] - peak)
                s_scr[head, rows, :] = e
                now = jnp.sum(e.reshape(16, 8, span), axis=0)
                total = now if total is None else total + now
            total = jnp.sum(total, axis=0, keepdims=True)
            inv = 1.0 / total
            for kb in range(seq // 128):
                rows = slice(128 * kb, 128 * kb + 128)
                p_scr[slot, head, rows, :] = (s_scr[head, rows, :] * inv).astype(bf16)
            lse_ref[0, head : head + 1, cols] = peak + jnp.log(total)
            outs.append(dot_f32(vt[64 * head : 64 * head + 64, :], p_scr[slot, head]))
        save(idx, slot).start()
        both = jnp.concatenate(outs, axis=0)
        ctxt_ref[:, cols] = both
        ctx_ref[cols, :] = both.T.astype(bf16)
        if experts:
            @pl.when((pair == 0) & (idx == 0))
            def _():
                pl.semaphore_wait(barrier, experts - 1)
                for peer in peers:
                    give(peer, me).start()

        return carry

    lax.fori_loop(0, seq // span, step, 0)

    @pl.when(pair == pl.num_programs(0) - 1)
    def _():
        for slot in range(2):
            save(slot, slot).wait()
        if experts:
            own.wait()
            for peer in peers:
                give(peer, me).wait_send()
                give(peer, peer).wait_recv()


def attend(q, k, v, u, gsend, experts=0):
    seq, width = q.shape
    pairs = width // 128
    blk = pl.BlockSpec((seq, 128), lambda p: (0, p))
    dma = pltpu.SemaphoreType.DMA
    return pl.pallas_call(
        functools.partial(attend_kernel, experts),
        grid=(pairs,),
        in_specs=[
            blk, blk, blk, pl.BlockSpec((1, 2, 2 * seq), lambda p: (p, 0, 0)), pl.BlockSpec(memory_space=pl.ANY),
        ],
        out_specs=[
            blk,
            pl.BlockSpec((128, seq), lambda p: (p, 0)),
            pl.BlockSpec((1, 8, seq), lambda p: (p, 0, 0)),
            pl.BlockSpec(memory_space=pl.ANY),
            pl.BlockSpec(memory_space=pl.ANY),
        ],
        out_shape=[
            jax.ShapeDtypeStruct((seq, width), bf16),
            jax.ShapeDtypeStruct((width, seq), f32),
            jax.ShapeDtypeStruct((pairs, 8, seq), f32),
            jax.ShapeDtypeStruct((2 * pairs, seq, seq), bf16),
            jax.ShapeDtypeStruct(gsend.shape, bf16),
        ],
        scratch_shapes=[
            pltpu.VMEM((2, 128, 2 * seq), f32),
            pltpu.VMEM((128, seq), bf16),
            pltpu.VMEM((128, seq), bf16),
            pltpu.VMEM((2, seq, 256), f32),
            pltpu.VMEM((2, 2, seq, 256), bf16),
            dma((2,)),
            dma((max(experts, 1),)), dma((max(experts, 1),)), dma(()),
        ],
        compiler_params=pltpu.CompilerParams(
            vmem_limit_bytes=48 << 20, has_side_effects=experts > 0, collective_id=3 if experts else None
        ),
        name="attend",
    )(q, k, v, u, gsend)


def first_kernel(
    capacity, experts, tok, gain, wq, wk, wv, route, cot, q_o, k_o, v_o, nl_o, gsend_o, slot_o, slot
):
    step = pl.program_id(0)
    slots = experts * capacity
    seq = route.shape[1]

    @pl.when(step == 0)
    def _():
        lane = lax.broadcasted_iota(jnp.int32, (8, seq), 1)
        hot = jnp.where(lax.broadcasted_iota(jnp.int32, (8, seq), 0) == route[...], 1.0, 0.0)
        count = hot
        shift = 1
        while shift < seq:
            count = count + jnp.where(lane >= shift, pltpu.roll(count, shift, 1), 0.0)
            shift *= 2
        position = jnp.sum(hot * (count - 1.0), axis=0, keepdims=True)
        place = route[...].astype(f32) * capacity + position
        slot[...] = jnp.where(position < capacity, place, float(slots))
        slot_o[...] = slot[...]

    values = tok[...].astype(f32)
    scale = lax.rsqrt(jnp.mean(values * values, axis=-1, keepdims=True) + epsilon)
    normed = (values * scale * gain[...]).astype(bf16)
    nl_o[...] = normed
    for weight, out in ((wq, q_o), (wk, k_o), (wv, v_o)):
        out[...] = dot_f32(normed, weight[...]).astype(bf16)
    rows = gsend_o.shape[0]
    number = lax.broadcasted_iota(jnp.int32, (rows, seq), 0) + step * rows
    pick = jnp.where(number.astype(f32) == slot[...], 1.0, 0.0).astype(bf16)
    gsend_o[...] = dot_f32(pick, cot[...]).astype(bf16)


def first_pass(tokens, gain, wq, wk, wv, route, cotangent, capacity, experts):
    seq, width = tokens.shape
    slots = experts * capacity
    steps = 4
    rows = pl.BlockSpec((seq // steps, width), lambda i: (i, 0))
    fixed = lambda shape: pl.BlockSpec(shape, lambda i: (0, 0))
    return pl.pallas_call(
        functools.partial(first_kernel, capacity, experts),
        grid=(steps,),
        in_specs=[rows, fixed(gain.shape)] + [fixed(wq.shape)] * 3 + [fixed(route.shape), fixed(cotangent.shape)],
        out_specs=[rows] * 4 + [pl.BlockSpec((slots // steps, width), lambda i: (i, 0)), fixed(route.shape)],
        out_shape=[jax.ShapeDtypeStruct((seq, width), bf16)] * 4
        + [jax.ShapeDtypeStruct((slots, width), bf16), jax.ShapeDtypeStruct(route.shape, f32)],
        scratch_shapes=[pltpu.VMEM(route.shape, f32)],
        compiler_params=pltpu.CompilerParams(vmem_limit_bytes=40 << 20),
        cost_estimate=pl.CostEstimate(
            flops=6 * seq * width * width + 2 * slots * seq * width, bytes_accessed=20 * seq * width, transcendentals=seq
        ),
        name="first",
    )(tokens, gain, wq, wk, wv, route, cotangent)


def split_rows(row):
    hi = row.astype(bf16).astype(f32)
    mid = (row - hi).astype(bf16).astype(f32)
    low = row - hi - mid
    idx = lax.broadcasted_iota(jnp.int32, (16, row.shape[1]), 0)
    return jnp.where(idx == 0, hi, jnp.where(idx == 1, mid, jnp.where(idx == 2, low, 0.0))).astype(bf16)


def attend_back_kernel(
    q_ref, k_ref, v_ref, g_ref, u_ref, ctxt_ref, lse_ref,
    dq_ref, dk_ref, dv_ref, diag_ref,
    base, acc, kaug, vaug, qaug, gaug, qz, gz, kt, dqt,
):
    seq = q_ref.shape[0]
    span = 256
    lane = lax.broadcasted_iota(jnp.int32, (seq, 128), 1)
    gt = g_ref[...].T
    qtv = q_ref[...].T
    kt[...] = k_ref[...].T
    gtf = gt.astype(f32)
    pad = jnp.zeros((48, seq), bf16)
    one = jnp.ones((seq, 128), bf16)
    nil = jnp.zeros((seq, 128), bf16)
    acc[...] = jnp.zeros_like(acc)
    for head in range(2):
        fill_toeplitz(base, head, u_ref[0, head : head + 1, :])
        own = (lane < 64) if head == 0 else (lane >= 64)
        origin = 64 if head == 0 else 0
        extra = jnp.where((lane >= origin) & (lane < origin + 3), one, nil)
        kaug[head] = jnp.where(own, k_ref[...], extra)
        vaug[head] = jnp.where(own, v_ref[...], extra)
        qz[head] = jnp.where(own, q_ref[...], nil)
        gz[head] = jnp.where(own, g_ref[...], nil)
        rows = slice(64 * head, 64 * head + 64)
        lse = split_rows(-lse_ref[0, head : head + 1, :])
        dsum = split_rows(-jnp.sum(gtf[rows] * ctxt_ref[rows, :], axis=0, keepdims=True))
        for dst, src, aug in ((qaug, qtv, lse), (gaug, gt, dsum)):
            dst[head, rows, :] = src[rows]
            dst[head, origin : origin + 16, :] = aug
            dst[head, origin + 16 : origin + 64, :] = pad

    dqt[...] = jnp.zeros_like(dqt)

    def step(idx, carry):
        rows = pl.ds(pl.multiple_of(idx * span, span), span)
        dv = None
        dk = None
        for head in range(2):
            s = dot_f32(kaug[head, rows, :], qaug[head])
            dp = dot_f32(vaug[head, rows, :], gaug[head])
            tops = []
            grads = []
            for part in range(2):
                offs = pl.ds(pl.multiple_of(seq - span * idx - 128 * part, 128), seq)
                p = jnp.exp(s[128 * part : 128 * part + 128] + base[head, :, offs])
                ds_ = p * dp[128 * part : 128 * part + 128]
                acc[head, :, offs] += ds_
                tops.append(p.astype(bf16))
                grads.append(ds_.astype(bf16))
            p = jnp.concatenate(tops, axis=0)
            ds_ = jnp.concatenate(grads, axis=0)
            now = dot_f32(p, gz[head])
            dv = now if dv is None else dv + now
            now = dot_f32(ds_, qz[head])
            dk = now if dk is None else dk + now
            dqt[64 * head : 64 * head + 64, :] += dot_f32(kt[64 * head : 64 * head + 64, rows], ds_)
        dv_ref[rows, :] = dv.astype(bf16)
        dk_ref[rows, :] = dk.astype(bf16)
        return carry

    lax.fori_loop(0, seq // span, step, 0)
    dq_ref[...] = dqt[...].T.astype(bf16)
    width = 2 * seq
    for head in range(2):
        total = acc[head, 0:8, :]
        for group in range(1, 16):
            total = total + pltpu.roll(acc[head, 8 * group : 8 * group + 8, :], width - 8 * group, 1)
        sub = lax.broadcasted_iota(jnp.int32, (8, width), 0)
        for bit in (1, 2, 4):
            total = jnp.where((sub & bit) != 0, pltpu.roll(total, width - bit, 1), total)
        diag_ref[0, head : head + 1, :] = jnp.sum(total, axis=0, keepdims=True)


def attend_back(q, k, v, g, u, ctxt, lse):
    seq, width = q.shape
    pairs = width // 128
    blk = pl.BlockSpec((seq, 128), lambda p: (0, p))
    return pl.pallas_call(
        attend_back_kernel,
        grid=(pairs,),
        in_specs=[
            blk, blk, blk, blk,
            pl.BlockSpec((1, 2, 2 * seq), lambda p: (p, 0, 0)),
            pl.BlockSpec((128, seq), lambda p: (p, 0)),
            pl.BlockSpec((1, 8, seq), lambda p: (p, 0, 0)),
        ],
        out_specs=[blk, blk, blk, pl.BlockSpec((1, 8, 2 * seq), lambda p: (p, 0, 0))],
        out_shape=[jax.ShapeDtypeStruct((seq, width), bf16)] * 3
        + [jax.ShapeDtypeStruct((pairs, 8, 2 * seq), f32)],
        scratch_shapes=[
            pltpu.VMEM((2, 128, 2 * seq), f32),
            pltpu.VMEM((2, 128, 2 * seq), f32),
            pltpu.VMEM((2, seq, 128), bf16),
            pltpu.VMEM((2, seq, 128), bf16),
            pltpu.VMEM((2, 128, seq), bf16),
            pltpu.VMEM((2, 128, seq), bf16),
            pltpu.VMEM((2, seq, 128), bf16),
            pltpu.VMEM((2, seq, 128), bf16),
            pltpu.VMEM((128, seq), bf16),
            pltpu.VMEM((128, seq), f32),
        ],
        compiler_params=pltpu.CompilerParams(vmem_limit_bytes=56 << 20),
        cost_estimate=pl.CostEstimate(
            flops=40 * seq * seq * width, bytes_accessed=20 * seq * width, transcendentals=seq * seq * 12
        ),
        name="attend_back",
    )(q, k, v, g, u, ctxt, lse)


def gelu_both(v):
    scale = 0.7978845608028654
    square = v * v
    t = jnp.tanh(scale * v * (1.0 + 0.044715 * square))
    half = 0.5 * (1.0 + t)
    slope = half + 0.5 * v * (1.0 - t * t) * (scale * (1.0 + 3 * 0.044715 * square))
    return v * half, slope


def expert_kernel(
    experts, capacity, tile,
    xs, gr_h, win_h, wout_h, rw,
    gback_o, prod_o, dwin_o, dwout_o, drw_o, shared_o,
    xall, gr, gp, win, wout, act, gpre, gback, gsend, prod, logit, acc_p, acc_g, xt, gpt, stage, dwt,
    send_x, recv_x, send_g, recv_g, local, out_sem, send_s, recv_s,
):
    me = lax.axis_index("expert")
    place = me // 2
    chips = experts // 2
    span = 2 * capacity
    width = xall.shape[1]
    hidden = win.shape[1]
    barrier = pltpu.get_barrier_semaphore()
    for k in range(1, experts):
        pl.semaphore_signal(barrier, inc=1, device_id={"expert": lax.rem(me + k, experts)})
    my_dp = lax.axis_index("dp")
    dp_x, dp_y = lax.rem(my_dp, 2), my_dp // 2
    peer_x, peer_y = my_dp + 1 - 2 * dp_x, my_dp + 2 - 4 * dp_y
    for peer in (peer_x, peer_y):
        pl.semaphore_signal(barrier, inc=1, device_id={"dp": peer})
    loads = [
        pltpu.make_async_copy(win_h, win, local.at[0]),
        pltpu.make_async_copy(wout_h, wout, local.at[1]),
        pltpu.make_async_copy(gr_h, gr, local.at[2]),
    ]
    rows_of = lambda who: pl.ds(pl.multiple_of(who * capacity, 16), capacity)
    own = pltpu.make_async_copy(xs.at[rows_of(me), :], xall.at[rows_of(me), :], local.at[3])
    own.start()
    for copy in loads:
        copy.start()
    pl.semaphore_wait(barrier, experts + 1)

    def partner(step):
        high, low = place // 2, lax.rem(place, 2)
        fhigh, flow = step // 2, lax.rem(step, 2)
        return 2 * (high + fhigh - 2 * high * fhigh) + low + flow - 2 * low * flow

    def send_rows(peer):
        return pltpu.make_async_remote_copy(
            src_ref=xs.at[rows_of(peer), :], dst_ref=xall.at[rows_of(me), :],
            send_sem=send_x.at[peer], recv_sem=recv_x.at[me], device_id={"expert": peer},
        )

    def got_rows(peer):
        return pltpu.make_async_remote_copy(
            src_ref=xs.at[rows_of(peer), :], dst_ref=xall.at[rows_of(peer), :],
            send_sem=send_x.at[peer], recv_sem=recv_x.at[peer], device_id={"expert": peer},
        )

    def send_back(peer):
        return pltpu.make_async_remote_copy(
            src_ref=gsend.at[rows_of(peer), :], dst_ref=gback.at[rows_of(me), :],
            send_sem=send_g.at[peer], recv_sem=recv_g.at[me], device_id={"expert": peer},
        )

    def got_back(peer):
        return pltpu.make_async_remote_copy(
            src_ref=gsend.at[rows_of(peer), :], dst_ref=gback.at[rows_of(peer), :],
            send_sem=send_g.at[peer], recv_sem=recv_g.at[peer], device_id={"expert": peer},
        )

    sibling = me + 1 - 2 * lax.rem(me, 2)
    send_rows(sibling).start()
    for step in range(1, chips):
        for core in range(2):
            send_rows(2 * partner(step) + lax.rem(me + core, 2)).start()
    for copy in loads:
        copy.wait()

    lanes = lax.broadcasted_iota(jnp.int32, (span, rw.shape[1]), 1)
    mine = jnp.where(lanes == me, 1.0, 0.0)

    def work(step, carry):
        where = partner(step)
        base = pl.multiple_of(where * span, 32)

        @pl.when(step == 0)
        def _():
            own.wait()
            got_rows(sibling).wait_recv()

        @pl.when(step > 0)
        def _():
            got_rows(2 * where).wait_recv()
            got_rows(2 * where + 1).wait_recv()

        rows = pl.ds(base, span)
        x = xall[rows, :]
        logits = jnp.where(lanes < experts, dot_f32(x, rw[...]), -1e30)
        weights = jnp.exp(logits - jnp.max(logits, axis=-1, keepdims=True))
        probs = weights / jnp.sum(weights, axis=-1, keepdims=True)
        gate = jnp.sum(probs * mine, axis=-1, keepdims=True)
        gp[rows, :] = (gr[rows, :].astype(f32) * gate).astype(bf16)
        acc_p[...] = jnp.zeros_like(acc_p)
        acc_g[...] = jnp.zeros_like(acc_g)

        def block(idx, carry):
            cols = pl.ds(pl.multiple_of(idx * tile, tile), tile)
            h = dot_f32(xall[rows, :], win[:, cols])
            grad = dot_nt(gp[rows, :], wout[cols, :])
            value, slope = gelu_both(h)
            value = value.astype(bf16)
            grad = (grad * slope).astype(bf16)
            act[rows, cols] = value
            gpre[rows, cols] = grad
            acc_p[...] += dot_f32(value, wout[cols, :])
            acc_g[...] += dot_nt(grad, win[:, cols])
            return carry

        lax.fori_loop(0, hidden // tile, block, 0)
        made = acc_p[...].astype(bf16)
        prod[rows, :] = made
        gate_grad = jnp.sum(gr[rows, :].astype(f32) * made.astype(f32), axis=-1, keepdims=True)
        low = (gate_grad * gate * (mine - probs)).astype(bf16)
        low = jnp.where(lanes < experts, low, jnp.zeros_like(low))
        logit[rows, :] = low
        gsend[rows, :] = (acc_g[...] + dot_nt(low, rw[...])).astype(bf16)

        @pl.when(step == 0)
        def _():
            send_back(sibling).start()

        @pl.when(step > 0)
        def _():
            send_back(2 * where).start()
            send_back(2 * where + 1).start()

        return carry

    lax.fori_loop(0, chips, work, 0)
    outs = [
        pltpu.make_async_copy(prod, prod_o, local.at[0]),
        pltpu.make_async_copy(gsend.at[rows_of(me), :], gback.at[rows_of(me), :], local.at[3]),
    ]
    for copy in outs:
        copy.start()
    xt[...] = xall[...].T
    gpt[...] = gp[...].T
    drw_o[...] = dot_f32(xt[...], logit[...])

    share = width // 4
    tiles = hidden // tile
    split = tiles // 2

    def left_copy(idx, block):
        cols = pl.ds(pl.multiple_of(idx * tile, tile), tile)
        rows = pl.ds(pl.multiple_of((1 - dp_x + 2 * block) * share, 16), share)
        return pltpu.make_async_remote_copy(
            src_ref=dwt.at[rows, cols], dst_ref=shared_o.at[pl.ds(block * share, share), cols],
            send_sem=send_s.at[block, idx], recv_sem=recv_s.at[block, idx], device_id={"dp": peer_x},
        )

    def right_copy(idx, block):
        cols = pl.ds(pl.multiple_of(idx * tile, tile), tile)
        rows = pl.ds(pl.multiple_of((2 - 2 * dp_y + block) * share, 16), share)
        dst_cols = pl.ds(pl.multiple_of((idx - split) * tile, tile), tile)
        return pltpu.make_async_remote_copy(
            src_ref=dwt.at[rows, cols], dst_ref=shared_o.at[pl.ds((2 + block) * share, share), dst_cols],
            send_sem=send_s.at[block, idx], recv_sem=recv_s.at[block, idx], device_id={"dp": peer_y},
        )

    def out_block(step, carry):
        idx = lax.rem(step, 2) * split + step // 2
        cols = pl.ds(pl.multiple_of(idx * tile, tile), tile)
        dwt[:, cols] = dot_f32(gpt[...], act[:, cols]).astype(bf16)

        @pl.when(idx < split)
        def _():
            for block in range(2):
                left_copy(idx, block).start()

        @pl.when(idx >= split)
        def _():
            for block in range(2):
                right_copy(idx, block).start()

        return carry

    lax.fori_loop(0, tiles, out_block, 0)
    whole = pltpu.make_async_copy(dwt, dwout_o, local.at[2])
    whole.start()

    def put(slot, cols):
        return pltpu.make_async_copy(stage.at[slot], dwin_o.at[:, cols], out_sem.at[slot])

    def in_block(idx, carry):
        cols = pl.ds(pl.multiple_of(idx * tile, tile), tile)
        slot = lax.rem(idx, 2)

        @pl.when(idx > 1)
        def _():
            put(slot, cols).wait()

        stage[slot] = dot_f32(xt[...], gpre[:, cols]).astype(bf16)
        put(slot, cols).start()
        return carry

    lax.fori_loop(0, tiles, in_block, 0)
    for slot in range(2):
        put(slot, pl.ds(0, tile)).wait()
    whole.wait()
    for copy in outs:
        copy.wait()
    for k in range(1, experts):
        peer = lax.rem(me + k, experts)
        got_rows(peer).wait_send()
        got_back(peer).wait_send()
        got_back(peer).wait_recv()
    back = pltpu.make_async_copy(gback, gback_o, local.at[1])
    back.start()
    for idx in range(tiles):
        for block in range(2):
            (left_copy if idx < split else right_copy)(idx, block).wait()
    back.wait()


def expert_pass(xs, gr, weight_in, weight_out, router_pad, experts, capacity):
    slots, width = xs.shape
    hidden = weight_in.shape[1]
    tile = 512
    span = 2 * capacity
    hbm = pl.BlockSpec(memory_space=pl.ANY)
    vmem = pl.BlockSpec(memory_space=pltpu.VMEM)
    return pl.pallas_call(
        functools.partial(expert_kernel, experts, capacity, tile),
        in_specs=[hbm, hbm, hbm, hbm, vmem],
        out_specs=[hbm, hbm, hbm, hbm, vmem, hbm],
        out_shape=[
            jax.ShapeDtypeStruct((slots, width), bf16),
            jax.ShapeDtypeStruct((slots, width), bf16),
            jax.ShapeDtypeStruct((width, hidden), bf16),
            jax.ShapeDtypeStruct((width, hidden), bf16),
            jax.ShapeDtypeStruct((width, router_pad.shape[1]), f32),
            jax.ShapeDtypeStruct((width, hidden // 2), bf16),
        ],
        scratch_shapes=[
            pltpu.VMEM((slots, width), bf16),
            pltpu.VMEM((slots, width), bf16),
            pltpu.VMEM((slots, width), bf16),
            pltpu.VMEM((width, hidden), bf16),
            pltpu.VMEM((hidden, width), bf16),
            pltpu.VMEM((slots, hidden), bf16),
            pltpu.VMEM((slots, hidden), bf16),
            pltpu.VMEM((slots, width), bf16),
            pltpu.VMEM((slots, width), bf16),
            pltpu.VMEM((slots, width), bf16),
            pltpu.VMEM((slots, router_pad.shape[1]), bf16),
            pltpu.VMEM((span, width), f32),
            pltpu.VMEM((span, width), f32),
            pltpu.VMEM((width, slots), bf16),
            pltpu.VMEM((width, slots), bf16),
            pltpu.VMEM((2, width, tile), bf16),
            pltpu.VMEM((width, hidden), bf16),
            pltpu.SemaphoreType.DMA((experts,)),
            pltpu.SemaphoreType.DMA((experts,)),
            pltpu.SemaphoreType.DMA((experts,)),
            pltpu.SemaphoreType.DMA((experts,)),
            pltpu.SemaphoreType.DMA((4,)),
            pltpu.SemaphoreType.DMA((2,)),
            pltpu.SemaphoreType.DMA((2, hidden // tile)),
            pltpu.SemaphoreType.DMA((2, hidden // tile)),
        ],
        compiler_params=pltpu.CompilerParams(
            vmem_limit_bytes=60 << 20, collective_id=1, has_side_effects=True
        ),
        cost_estimate=pl.CostEstimate(
            flops=12 * slots * width * hidden, bytes_accessed=8 * width * hidden, transcendentals=slots * hidden
        ),
        name="experts",
    )(xs, gr, weight_in, weight_out, router_pad)


def remote(src, dst, send_sem, recv_sem, axis, peer):
    return pltpu.make_async_remote_copy(
        src_ref=src, dst_ref=dst, send_sem=send_sem, recv_sem=recv_sem, device_id={axis: peer}
    )


def others(count, mine):
    return [lax.rem(mine + k, count) for k in range(1, count)]


PLAN = (
    (11, 16, 19, 22, 24),
    (12, 17, 20, 23, 25),
    (5, 13, 16, 19, 21),
    (9, 15, 18, 21, 23),
    (13, 18, 21, 24, 26),
    (17, 21, 24, 27, 29),
    (21, 24, 27, 29, 31),
)
OUTPUT_SLOT = 17
EXPERT_SLOTS = ((6, 2, 0), (14, 3, 0), (15, 2, 1), (22, 3, 1))


def back_kernel(
    groups, experts, pairs,
    q_ref, k_ref, v_ref, g_ref, ctxt_ref, wq, wk, wv, hot, gain, nl_h, tok_h, ghid_h, dwo_h, small_h,
    eout_h, shared_h, ein_h, p_h, prod_h, hid_h, meta,
    wsum_o, ing_o, small_o, esum_o, out_o,
    acc, vaug, gaug, qz, gz, kt, dqt, pbuf, pret, hbuf, obuf, dall, nt, tok,
    part, r1, r2, r3, full, sbuf, srecv, sone, stwo, keep, other, final,
    send1, recv1, send2, recv2, send3, recv3, send4, recv4, send5, recv5, send6, recv6, send7, recv7, local,
    send_a, recv_a, send_b, recv_b, out_sem, copy_sem, p_sem, send_p, recv_p, o_sem,
):
    seq = q_ref.shape[0]
    width = tok.shape[1]
    span = 256
    pair = pl.program_id(0)
    me = lax.axis_index("expert")
    my_dp = lax.axis_index("dp")
    core = lax.rem(me, 2)
    place = me // 2
    chips = experts // 2
    sibling = me + 1 - 2 * core
    half = width // 2
    piece = half // groups
    thick = part.shape[2]
    gain_rows = width // 128

    def half_rows(which):
        return pl.ds(pl.multiple_of(which * half, 16), half)

    def own_piece(which):
        return pl.ds(pl.multiple_of(core * half + which * piece, 16), piece)

    def copy1(c):
        return remote(part.at[c, half_rows(1 - core), :], r1.at[c], send1.at[c], recv1.at[c], "expert", sibling)

    def copy2(c, peer, slot):
        return remote(part.at[c, own_piece(peer), :], r2.at[c, slot], send2.at[c, peer], recv2.at[c, slot], "dp", peer)

    def copy3(c, peer, slot):
        return remote(
            r3.at[c, place], r3.at[c, slot], send3.at[c, peer], recv3.at[c, slot], "expert", 2 * peer + core
        )

    def copy4(c, peer, slot):
        return remote(
            full.at[c, own_piece(my_dp), :], full.at[c, own_piece(slot), :],
            send4.at[c, peer], recv4.at[c, slot], "dp", peer,
        )

    def copy5(c, which):
        return remote(
            full.at[c, half_rows(which), :], full.at[c, half_rows(which), :],
            send5.at[c], recv5.at[c], "expert", sibling,
        )

    def stage1(c):
        copy1(c).start()

    def stage2(c):
        copy1(c).wait_recv()
        part[c, half_rows(core), :] = (part[c, half_rows(core), :].astype(f32) + r1[c].astype(f32)).astype(bf16)
        for peer in others(groups, my_dp):
            copy2(c, peer, my_dp).start()

    def stage3(c):
        total = part[c, own_piece(my_dp), :].astype(f32)
        for peer in others(groups, my_dp):
            copy2(c, peer, peer).wait_recv()
            total = total + r2[c, peer].astype(f32)
        r3[c, place] = total.astype(bf16)
        for peer in others(chips, place):
            copy3(c, peer, place).start()

    def stage4(c):
        for peer in others(chips, place):
            copy3(c, peer, peer).wait_recv()
        total = r3[c, 0].astype(f32)
        for slot in range(1, chips):
            total = total + r3[c, slot].astype(f32)
        full[c, own_piece(my_dp), :] = total.astype(bf16)
        for peer in others(groups, my_dp):
            copy4(c, peer, my_dp).start()

    def stage5(c):
        for peer in others(groups, my_dp):
            copy4(c, peer, peer).wait_recv()
        copy5(c, core).start()

    def put_first(c):
        return pltpu.make_async_copy(full.at[c], wsum_o.at[0, :, thick * c : thick * c + thick], out_sem.at[c, 0])

    def put_pair(c, which):
        cols = pl.ds(128 * (c - 2) if isinstance(c, int) else pl.multiple_of(128 * (c - 2), 128), 128)
        return pltpu.make_async_copy(
            full.at[c, :, 128 * which : 128 * which + 128], wsum_o.at[1 + which, :, cols], out_sem.at[c, which]
        )

    def stage6(c):
        copy5(c, 1 - core).wait_recv()

        if c < 2:
            put_first(c).start()
        else:
            for which in range(3):
                put_pair(c, which).start()

    share = width // 4
    dp_x, dp_y = lax.rem(my_dp, 2), my_dp // 2
    peer_x, peer_y = my_dp + 1 - 2 * dp_x, my_dp + 2 - 4 * dp_y
    middle = keep.shape[1]
    left, right = pl.ds(0, middle), pl.ds(middle, middle)

    def share_rows(which):
        return pl.ds(pl.multiple_of(which * share, 16), share)

    def first_left(block):
        return remote(
            ein_h.at[share_rows(1 - dp_x + 2 * block), left], other.at[1, share_rows(block), :],
            send_a.at[0, block], recv_a.at[0, block], "dp", peer_x,
        )

    def first_right(block):
        return remote(
            ein_h.at[share_rows(2 - 2 * dp_y + block), right], other.at[1, share_rows(2 + block), :],
            send_a.at[1, block], recv_a.at[1, block], "dp", peer_y,
        )

    def second_left(which):
        return remote(
            keep.at[share_rows(1 - dp_y), :], final.at[which, :, left],
            send_b.at[which, 0], recv_b.at[which, 0], "dp", peer_y,
        )

    def second_right(which):
        return remote(
            keep.at[share_rows(2 + 1 - dp_x), :], final.at[which, :, right],
            send_b.at[which, 1], recv_b.at[which, 1], "dp", peer_x,
        )

    def own_loads(src):
        loads = []
        for block in range(2):
            loads.append(
                pltpu.make_async_copy(
                    src.at[share_rows(dp_x + 2 * block), left], keep.at[share_rows(block), :], copy_sem.at[block]
                )
            )
            loads.append(
                pltpu.make_async_copy(
                    src.at[share_rows(2 * dp_y + block), right], keep.at[share_rows(2 + block), :], copy_sem.at[2 + block]
                )
            )
        return loads

    def shared_load():
        return pltpu.make_async_copy(shared_h, other.at[0], copy_sem.at[4])

    def save(which):
        return pltpu.make_async_copy(final.at[which], esum_o.at[which], copy_sem.at[5])

    def experts_begin():
        for copy in own_loads(eout_h) + [shared_load()]:
            copy.start()
        for block in range(2):
            first_left(block).start()
            first_right(block).start()

    def experts_second(which):
        for copy in own_loads(eout_h if which == 0 else ein_h):
            copy.wait()
        if which == 0:
            shared_load().wait()
        else:
            for block in range(2):
                first_left(block).wait_recv()
                first_right(block).wait_recv()

        def block(idx, carry):
            rows = pl.ds(pl.multiple_of(idx * 64, 64), 64)
            keep[rows, :] = (keep[rows, :].astype(f32) + other[which, rows, :].astype(f32)).astype(bf16)
            return carry

        lax.fori_loop(0, width // 64, block, 0)
        second_left(which).start()
        second_right(which).start()

    def experts_last(which):
        second_left(which).wait()
        second_right(which).wait()

        def block(idx, carry):
            rows = pl.ds(pl.multiple_of(idx * 64, 64), 64)
            mine_left = pl.ds(pl.multiple_of(dp_y * share + idx * 64, 64), 64)
            mine_right = pl.ds(pl.multiple_of((2 + dp_x) * share + idx * 64, 64), 64)
            final[which, rows, left] = (final[which, rows, left].astype(f32) + keep[mine_left, :].astype(f32)).astype(bf16)
            final[which, rows, right] = (final[which, rows, right].astype(f32) + keep[mine_right, :].astype(f32)).astype(bf16)
            return carry

        lax.fori_loop(0, share // 64, block, 0)
        if which == 0:
            for copy in own_loads(ein_h):
                copy.start()
        else:
            save(0).wait()
        save(which).start()

    early = pl.ds(8 + hot.shape[0], sbuf.shape[0] - 8 - hot.shape[0])
    late = pl.ds(0, 8 + hot.shape[0])

    def copy6(part_idx, rows, peer, slot):
        return remote(
            sbuf.at[rows, :], srecv.at[slot, rows, :],
            send6.at[part_idx, peer], recv6.at[part_idx, slot], "expert", peer,
        )

    def copy7(part_idx, rows, peer, slot):
        return remote(
            sone.at[rows, :], stwo.at[slot, rows, :],
            send7.at[part_idx, peer], recv7.at[part_idx, slot], "dp", peer,
        )

    def small1(part_idx, rows):
        srecv[me, rows, :] = sbuf[rows, :]
        for peer in others(experts, me):
            copy6(part_idx, rows, peer, me).start()

    def small2(part_idx, rows):
        for peer in others(experts, me):
            copy6(part_idx, rows, peer, peer).wait_recv()
        total = srecv[0, rows, :]
        for slot in range(1, experts):
            total = total + srecv[slot, rows, :]
        sone[rows, :] = total
        stwo[my_dp, rows, :] = total
        for peer in others(groups, my_dp):
            copy7(part_idx, rows, peer, my_dp).start()

    def small3(part_idx, rows):
        for peer in others(groups, my_dp):
            copy7(part_idx, rows, peer, peer).wait_recv()
        total = stwo[0, rows, :]
        for slot in range(1, groups):
            total = total + stwo[slot, rows, :]
        small_o[rows, :] = total

    stages = (stage2, stage3, stage4, stage5, stage6)

    def advance(slot):
        for c, slots in enumerate(PLAN):
            for at, stage in reversed(list(zip(slots, stages))):
                if at < 4 * pairs:
                    pl.when(slot == at)(functools.partial(stage, c))

    def load_p(slot_idx, slot):
        rows = pl.ds(pl.multiple_of(lax.rem(slot_idx, 4) * span, span), span)
        return pltpu.make_async_copy(p_h.at[pl.ds(2 * (slot_idx // 4), 2), rows, :], pbuf.at[slot], p_sem.at[slot])

    slots_each = pret.shape[0] // experts

    def slot_rows(which):
        return pl.ds(pl.multiple_of(which * slots_each, 16), slots_each)

    def give_back(peer):
        return remote(
            prod_h.at[slot_rows(peer), :], pret.at[slot_rows(me), :], send_p.at[peer], recv_p.at[me], "expert", peer
        )

    def got_back(peer):
        return remote(
            prod_h.at[slot_rows(peer), :], pret.at[slot_rows(peer), :], send_p.at[peer], recv_p.at[peer], "expert", peer
        )

    def own_back():
        return pltpu.make_async_copy(prod_h.at[slot_rows(me), :], pret.at[slot_rows(me), :], o_sem.at[0])

    def out_rows(block):
        return pl.ds(block * span, span)

    def load_hidden(block):
        return pltpu.make_async_copy(hid_h.at[out_rows(block), :], hbuf, o_sem.at[1])

    def save_out(block):
        return pltpu.make_async_copy(obuf, out_o.at[out_rows(block), :], o_sem.at[2])

    def output_block(block):
        if block == 0:
            own_back().wait()
            for peer in others(experts, me):
                got_back(peer).wait_recv()
        load_hidden(block).wait()
        where = lax.broadcasted_iota(jnp.int32, (span, pret.shape[0]), 1).astype(f32)
        pick = jnp.where(meta[out_rows(block), 1:2] == where, 1.0, 0.0).astype(bf16)
        gathered = dot_f32(pick, pret[...])
        if block > 0:
            save_out(block - 1).wait()
        obuf[...] = (hbuf[...] + meta[out_rows(block), 0:1] * gathered).astype(bf16)
        save_out(block).start()
        if (block + 1) * span < seq:
            load_hidden(block + 1).start()

    loads = [
        pltpu.make_async_copy(nl_h, tok, local.at[0]),
        pltpu.make_async_copy(ghid_h, ing_o, local.at[2]),
        pltpu.make_async_copy(dwo_h.at[:, 0:thick], part.at[0], local.at[3]),
        pltpu.make_async_copy(dwo_h.at[:, thick : 2 * thick], part.at[1], local.at[4]),
        pltpu.make_async_copy(small_h, sbuf, local.at[5]),
    ]

    @pl.when(pair == 0)
    def _():
        barrier = pltpu.get_barrier_semaphore()
        for peer in others(experts, me):
            pl.semaphore_signal(barrier, inc=1, device_id={"expert": peer})
        for peer in others(groups, my_dp):
            pl.semaphore_signal(barrier, inc=1, device_id={"dp": peer})
        for copy in loads:
            copy.start()
        load_p(0, 0).start()
        own_back().start()
        load_hidden(0).start()
        for copy in loads:
            copy.wait()
        nt[...] = tok[...].T
        pl.semaphore_wait(barrier, experts + groups - 2)
        stage1(0)
        stage1(1)
        small1(0, early)
        experts_begin()
        for peer in others(experts, me):
            give_back(peer).start()

    mine = pl.ds(pl.multiple_of(128 * pair, 128), 128)
    lane = lax.broadcasted_iota(jnp.int32, (seq, 128), 1)
    gt = g_ref[...].T
    kt[...] = k_ref[...].T
    gtf = gt.astype(f32)
    pad = jnp.zeros((48, seq), bf16)
    one = jnp.ones((seq, 128), bf16)
    nil = jnp.zeros((seq, 128), bf16)
    acc[...] = jnp.zeros_like(acc)
    for head in range(2):
        own = (lane < 64) if head == 0 else (lane >= 64)
        origin = 64 if head == 0 else 0
        extra = jnp.where((lane >= origin) & (lane < origin + 3), one, nil)
        vaug[head] = jnp.where(own, v_ref[...], extra)
        qz[head] = jnp.where(own, q_ref[...], nil)
        gz[head] = jnp.where(own, g_ref[...], nil)
        rows = slice(64 * head, 64 * head + 64)
        gaug[head, rows, :] = gt[rows]
        gaug[head, origin : origin + 16, :] = split_rows(
            -jnp.sum(gtf[rows] * ctxt_ref[rows, :], axis=0, keepdims=True)
        )
        gaug[head, origin + 16 : origin + 64, :] = pad

    dqt[...] = jnp.zeros_like(dqt)

    def step(idx, carry):
        rows = pl.ds(pl.multiple_of(idx * span, span), span)
        dv = None
        dk = None
        slot = lax.rem(idx, 2)
        load_p(4 * pair + idx, slot).wait()

        @pl.when(4 * pair + idx + 1 < 4 * pairs)
        def _():
            load_p(4 * pair + idx + 1, 1 - slot).start()

        for head in range(2):
            dp = dot_f32(vaug[head, rows, :], gaug[head])
            grads = []
            for part_idx in range(2):
                offs = pl.ds(pl.multiple_of(seq - span * idx - 128 * part_idx, 128), seq)
                band = slice(128 * part_idx, 128 * part_idx + 128)
                ds_ = pbuf[slot, head, band, :].astype(f32) * dp[band]
                acc[head, :, offs] += ds_
                grads.append(ds_.astype(bf16))
            ds_ = jnp.concatenate(grads, axis=0)
            now = dot_f32(pbuf[slot, head], gz[head])
            dv = now if dv is None else dv + now
            now = dot_f32(ds_, qz[head])
            dk = now if dk is None else dk + now
            dqt[64 * head : 64 * head + 64, :] += dot_f32(kt[64 * head : 64 * head + 64, rows], ds_)
        dall[1, rows, mine] = dk.astype(bf16)
        dall[2, rows, mine] = dv.astype(bf16)
        advance(4 * pair + idx)

        for block in range(seq // span):
            @pl.when(4 * pair + idx == OUTPUT_SLOT + block)
            def _():
                output_block(block)

        for at, task, which in EXPERT_SLOTS:
            @pl.when(4 * pair + idx == at)
            def _():
                (experts_second if task == 2 else experts_last)(which)

        @pl.when(4 * pair + idx == 7)
        def _():
            small2(0, early)

        @pl.when(4 * pair + idx == 11)
        def _():
            small3(0, early)

        return carry

    lax.fori_loop(0, seq // span, step, 0)
    dall[0, :, mine] = dqt[...].T.astype(bf16)
    twice = 2 * seq
    sub = lax.broadcasted_iota(jnp.int32, (8, twice), 0)
    head_lane = lax.broadcasted_iota(jnp.int32, (hot.shape[0], 128), 1)
    rel_rows = slice(8, 8 + hot.shape[0])
    for head in range(2):
        total = acc[head, 0:8, :]
        for group in range(1, 16):
            total = total + pltpu.roll(acc[head, 8 * group : 8 * group + 8, :], twice - 8 * group, 1)
        for bit in (1, 2, 4):
            total = jnp.where((sub & bit) != 0, pltpu.roll(total, twice - bit, 1), total)
        diag = jnp.sum(total, axis=0, keepdims=True)
        sums = jnp.sum(hot[...] * diag, axis=1, keepdims=True)
        sbuf[rel_rows, :] = jnp.where(head_lane == 2 * pair + head, sums, sbuf[rel_rows, :])

    def weight_block(idx, carry):
        rows = pl.ds(pl.multiple_of(idx * 256, 256), 256)
        grads = jnp.concatenate([dall[which, :, mine] for which in range(3)], axis=1)
        part[pair + 2, rows, :] = dot_f32(nt[rows, :], grads).astype(bf16)
        return carry

    lax.fori_loop(0, width // 256, weight_block, 0)
    stage1(pair + 2)

    @pl.when(pair == pairs - 1)
    def _():
        def token_block(idx, carry):
            rows = pl.ds(pl.multiple_of(idx * 256, 256), 256)
            grad = (
                dot_nt(dall[0, rows, :], wq[...])
                + dot_nt(dall[1, rows, :], wk[...])
                + dot_nt(dall[2, rows, :], wv[...])
            )
            values = tok[rows, :].astype(f32)
            scale = lax.rsqrt(jnp.mean(values * values, axis=-1, keepdims=True) + epsilon)
            weighted = grad * gain[...]
            inner = jnp.mean(weighted * values, axis=-1, keepdims=True)
            ing_o[rows, :] += scale * weighted - values * (scale * scale * scale * inner)
            return carry + jnp.sum(grad * values * scale, axis=0, keepdims=True)

        reload = pltpu.make_async_copy(tok_h, tok, local.at[1])
        reload.start()
        last = pairs + 1
        first = 4 * pairs
        older = sorted(
            (at, c, stage)
            for c, slots in enumerate(PLAN)
            for stage, at in enumerate(slots)
            if at >= first
        )

        def drain(until):
            while older and older[0][0] < first + until:
                _, c, stage = older.pop(0)
                stages[stage](c)

        def tokens_done(lower, upper, gain_grad):
            return lax.fori_loop(lower, upper, token_block, gain_grad)

        drain(1)
        reload.wait()
        gain_grad = tokens_done(0, 1, jnp.zeros((1, width), f32))
        stage2(last)
        drain(2)
        gain_grad = tokens_done(1, seq // 512, gain_grad)
        drain(4)
        gain_grad = tokens_done(seq // 512, seq // 256, gain_grad)
        stage3(last)
        for row in range(gain_rows):
            sbuf[row : row + 1, :] = gain_grad[:, 128 * row : 128 * row + 128]
        small1(1, late)
        drain(8)
        small2(1, late)
        stage4(last)
        drain(99)
        small3(1, late)
        stage5(last)
        stage6(last)
        for c in range(2):
            put_first(c).wait()
        save(1).wait()
        save_out(seq // span - 1).wait()
        for peer in others(experts, me):
            give_back(peer).wait_send()
        for block in range(2):
            first_left(block).wait_send()
            first_right(block).wait_send()

        def finish(c, carry):
            copy1(c).wait_send()
            for peer in others(groups, my_dp):
                copy2(c, peer, my_dp).wait_send()
                copy4(c, peer, my_dp).wait_send()
            for peer in others(chips, place):
                copy3(c, peer, place).wait_send()
            copy5(c, core).wait_send()

            @pl.when(c >= 2)
            def _():
                for which in range(3):
                    put_pair(c, which).wait()

            return carry

        lax.fori_loop(0, pairs + 2, finish, 0)
        for part_idx, rows in ((0, early), (1, late)):
            for peer in others(experts, me):
                copy6(part_idx, rows, peer, me).wait_send()
            for peer in others(groups, my_dp):
                copy7(part_idx, rows, peer, my_dp).wait_send()


def back_pass(
    q, k, v, g, ctxt, wq, wk, wv, hot, gain, normed_low, tokens, grad_hidden, dwo, small,
    expert_out_grad, shared, expert_in_grad, weights, produced, hidden_rows, meta, groups, experts
):
    seq, width = q.shape
    pairs = width // 128
    chunks = pairs + 2
    hidden = expert_in_grad.shape[1]
    thick = width // 2
    half = width // 2
    piece = half // groups
    chips = experts // 2
    blk = pl.BlockSpec((seq, 128), lambda p: (0, p))
    hbm = pl.BlockSpec(memory_space=pl.ANY)
    fixed = lambda shape: pl.BlockSpec(shape, lambda p: (0,) * len(shape), pipeline_mode=pl.Buffered(1))
    dma = pltpu.SemaphoreType.DMA
    return pl.pallas_call(
        functools.partial(back_kernel, groups, experts, pairs),
        grid=(pairs,),
        in_specs=[
            blk, blk, blk, blk,
            pl.BlockSpec((128, seq), lambda p: (p, 0)),
            fixed((width, width)), fixed((width, width)), fixed((width, width)),
            fixed(hot.shape), fixed(gain.shape),
            hbm, hbm, hbm, hbm, hbm, hbm, hbm, hbm,
            hbm, hbm, hbm, fixed(meta.shape),
        ],
        out_specs=[hbm, fixed((seq, width)), fixed(small.shape), hbm, hbm],
        out_shape=[
            jax.ShapeDtypeStruct((4, width, width), bf16),
            jax.ShapeDtypeStruct((seq, width), f32),
            jax.ShapeDtypeStruct(small.shape, f32),
            jax.ShapeDtypeStruct((2, width // 4, hidden), bf16),
            jax.ShapeDtypeStruct((seq, width), bf16),
        ],
        scratch_shapes=[
            pltpu.VMEM((2, 128, 2 * seq), f32),
            pltpu.VMEM((2, seq, 128), bf16),
            pltpu.VMEM((2, 128, seq), bf16),
            pltpu.VMEM((2, seq, 128), bf16),
            pltpu.VMEM((2, seq, 128), bf16),
            pltpu.VMEM((128, seq), bf16),
            pltpu.VMEM((128, seq), f32),
            pltpu.VMEM((2, 2, 256, seq), bf16),
            pltpu.VMEM(produced.shape, bf16),
            pltpu.VMEM((256, width), f32),
            pltpu.VMEM((256, width), bf16),
            pltpu.VMEM((3, seq, width), bf16),
            pltpu.VMEM((width, seq), bf16),
            pltpu.VMEM((seq, width), bf16),
            pltpu.VMEM((chunks, width, thick), bf16),
            pltpu.VMEM((chunks, half, thick), bf16),
            pltpu.VMEM((chunks, groups, piece, thick), bf16),
            pltpu.VMEM((chunks, chips, piece, thick), bf16),
            pltpu.VMEM((chunks, width, thick), bf16),
            pltpu.VMEM(small.shape, f32),
            pltpu.VMEM((experts,) + small.shape, f32),
            pltpu.VMEM(small.shape, f32),
            pltpu.VMEM((groups,) + small.shape, f32),
            pltpu.VMEM((width, hidden // 2), bf16),
            pltpu.VMEM((2, width, hidden // 2), bf16),
            pltpu.VMEM((2, width // 4, hidden), bf16),
            dma((chunks,)), dma((chunks,)),
            dma((chunks, groups)), dma((chunks, groups)),
            dma((chunks, chips)), dma((chunks, chips)),
            dma((chunks, groups)), dma((chunks, groups)),
            dma((chunks,)), dma((chunks,)),
            dma((2, experts)), dma((2, experts)),
            dma((2, groups)), dma((2, groups)),
            dma((6,)),
            dma((2, 2)), dma((2, 2)),
            dma((2, 2)), dma((2, 2)),
            dma((chunks, 3)), dma((6,)),
            dma((2,)), dma((experts,)), dma((experts,)), dma((3,)),
        ],
        compiler_params=pltpu.CompilerParams(
            vmem_limit_bytes=62 << 20, collective_id=2, has_side_effects=True
        ),
        cost_estimate=pl.CostEstimate(
            flops=40 * seq * seq * width + 12 * seq * width * width,
            bytes_accessed=40 * seq * width, transcendentals=seq * seq * 12,
        ),
        name="attend_back",
    )(
        q, k, v, g, ctxt, wq, wk, wv, hot, gain, normed_low, tokens, grad_hidden, dwo, small,
        expert_out_grad, shared, expert_in_grad, weights, produced, hidden_rows, meta,
    )


def rms_backward(grad_norm, values, row_scale, gain_vec):
    weighted = grad_norm * gain_vec
    gain_grad = jnp.sum(grad_norm * values * row_scale, axis=0)
    grad_in = row_scale * weighted - values * row_scale**3 * jnp.mean(
        weighted * values, axis=-1, keepdims=True
    )
    return grad_in, gain_grad


def rms_forward(values, gain_vec):
    row_scale = lax.rsqrt(jnp.mean(values * values, axis=-1, keepdims=True) + epsilon)
    return values * row_scale * gain_vec, row_scale


def gelu_tanh(values):
    return jax.nn.gelu(values, approximate=True)


def contract(left, right, dims):
    return lax.dot_general(left, right, (((dims[0],), (dims[1],)), ((), ())), preferred_element_type=f32)


def exchange(rows, experts):
    slots, width = rows.shape
    rows = rows.reshape(experts, slots // experts, width)
    return lax.all_to_all(rows, "expert", split_axis=0, concat_axis=0, tiled=True).reshape(slots, width)


def expert_native(send, grad_recv, weight_in, weight_out, router_w, experts):
    received = exchange(send, experts)
    own = lax.axis_index("expert")
    own_hot = (jnp.arange(experts, dtype=jnp.int32) == own).astype(f32)[None, :]
    probs = jax.nn.softmax(contract(received, router_w, (1, 0)), axis=-1)
    gate = jnp.sum(probs * own_hot, axis=-1, keepdims=True)
    grad_recv_f = grad_recv.astype(f32)
    grad_produced = (grad_recv_f * gate).astype(bf16)
    preact = contract(received, weight_in, (1, 0))
    gelu_values, gelu_pullback = jax.vjp(gelu_tanh, preact)
    active = gelu_values.astype(bf16)
    produced = contract(active, weight_out, (1, 0)).astype(bf16)
    gate_grad = jnp.sum(grad_recv_f * produced.astype(f32), axis=-1, keepdims=True)
    logit_low = (gate_grad * gate * (own_hot - probs)).astype(bf16)
    grad_active = contract(grad_produced, weight_out, (1, 1))
    grad_preact = gelu_pullback(grad_active)[0].astype(bf16)
    grad_received = contract(grad_preact, weight_in, (1, 1)) + contract(logit_low, router_w, (1, 1))
    grad_rows = exchange(grad_received.astype(bf16), experts)
    in_grad = contract(received, grad_preact, (0, 0)).astype(bf16)
    out_grad_t = contract(grad_produced, active, (0, 0)).astype(bf16)
    router_grad = contract(received, logit_low, (0, 0))
    return grad_rows, produced, in_grad, out_grad_t, router_grad


def tail_native(tokens, gain, normed_low, dq, dk, dv, wq, wk, wv, grad_hidden, dwo, small):
    tokens_f = tokens.astype(f32)
    grads = jnp.stack([dwo.astype(f32)] + [contract(normed_low, d, (0, 0)) for d in (dq, dk, dv)])
    grad_normed = contract(dq, wq, (1, 1)) + contract(dk, wk, (1, 1)) + contract(dv, wv, (1, 1))
    _, scale = rms_forward(tokens_f, gain)
    grad_tokens, gain_grad = rms_backward(grad_normed, tokens_f, scale, gain)
    grads, gain_grad, small = lax.psum((grads, gain_grad, small), ("dp", "expert"))
    return grads, grad_hidden + grad_tokens, gain_grad, small


def on_device(
    tokens, gain_one, query_w, key_w, value_w, out_w, rel_table, gain_two, router_w,
    expert_in, expert_out, routes, buckets, cotangent,
):
    seq_len, width = tokens.shape
    heads = rel_table.shape[1]
    groups = lax.axis_size("dp")
    experts = lax.axis_size("expert")
    capacity = (5 * seq_len + 4 * experts - 1) // (4 * experts)
    slots = experts * capacity
    weight_in = expert_in[0]
    weight_out = expert_out[0]
    kernels = capacity % 16 == 0 and experts == 8 and groups == 4

    route_ids = routes[:, 0]
    route_hot = route_ids[:, None] == jnp.arange(experts, dtype=jnp.int32)[None, :]
    route_int = route_hot.astype(jnp.int32)
    route_float = route_hot.astype(f32)
    position = jnp.sum((jnp.cumsum(route_int, axis=0) - 1) * route_int, axis=1)
    slot_index = jnp.where(position < capacity, route_ids * capacity + position, slots)
    pick = (jnp.arange(slots, dtype=jnp.int32)[:, None] == slot_index[None, :]).astype(bf16)

    def scatter_rows(rows):
        return contract(pick, rows, (1, 0)).astype(bf16)

    def gather_rows(rows):
        return contract(pick, rows, (0, 0))

    tokens_f = tokens.astype(f32)
    if kernels:
        queries, key_rows, value_rows, normed_low, grad_send, slot_row = first_pass(
            tokens, gain_one[None], query_w, key_w, value_w, routes.reshape(1, seq_len), cotangent, capacity, experts
        )
        slot_index = slot_row[0].astype(jnp.int32)
        pick = (jnp.arange(slots, dtype=jnp.int32)[:, None] == slot_index[None, :]).astype(bf16)
    else:
        grad_send = scatter_rows(cotangent)
        normed_low = rms_forward(tokens_f, gain_one)[0].astype(bf16)
        queries = contract(normed_low, query_w, (1, 0)).astype(bf16)
        key_rows = contract(normed_low, key_w, (1, 0)).astype(bf16)
        value_rows = contract(normed_low, value_w, (1, 0)).astype(bf16)
    reach = jnp.concatenate([buckets, jnp.full((1,), -1, jnp.int32)])[::-1]
    bucket_hot = (jnp.arange(rel_table.shape[0], dtype=jnp.int32)[:, None] == reach[None, :]).astype(f32)
    spread = jnp.einsum("bh,bx->hx", rel_table, bucket_hot, precision=highest)
    spread = spread.reshape(heads // 2, 2, 2 * seq_len)
    context, context_t, logsum, weights, grad_recv = attend(
        queries, key_rows, value_rows, spread, grad_send, experts if kernels else 0
    )
    if not kernels:
        grad_recv = exchange(grad_send, experts)
    hidden = tokens_f + contract(context, out_w, (1, 0))
    normed_two, scale_two = rms_forward(hidden, gain_two)
    normed_two_low = normed_two.astype(bf16)

    send = scatter_rows(normed_two_low)
    if kernels:
        router_pad = jnp.pad(router_w, ((0, 0), (0, 128 - experts)))
        grad_rows, produced, in_grad, out_grad_t, router_grad, shared = expert_pass(
            send, grad_recv, weight_in, weight_out, router_pad, experts, capacity
        )
        router_grad = router_grad[:, :experts]
    else:
        grad_rows, produced, in_grad, out_grad_t, router_grad = expert_native(
            send, grad_recv, weight_in, weight_out, router_w, experts
        )

    router_probs = jax.nn.softmax(contract(normed_two_low, router_w, (1, 0)), axis=-1)
    gate_value = jnp.sum(router_probs * route_float, axis=-1, keepdims=True)

    grad_out = cotangent.astype(f32)
    grad_normed_two = gather_rows(grad_rows)
    grad_hidden_norm, gain_two_grad = rms_backward(grad_normed_two, hidden, scale_two, gain_two)
    grad_hidden = grad_out + grad_hidden_norm
    branch_low = grad_hidden.astype(bf16)
    out_w_grad = contract(context, branch_low, (0, 0)).astype(bf16)
    grad_context = contract(branch_low, out_w, (1, 1)).astype(bf16)
    if kernels:
        small = jnp.concatenate(
            [
                jnp.zeros((8 + rel_table.shape[0], 128), f32),
                jnp.pad(gain_two_grad.reshape(-1, 128), ((0, 2), (0, 0))),
                router_grad.T.reshape(-1, 128),
            ]
        )
        grads, input_grad, small, shares, output = back_pass(
            queries, key_rows, value_rows, grad_context, context_t, query_w, key_w, value_w,
            bucket_hot, gain_one[None], normed_low, tokens, grad_hidden, out_w_grad, small,
            out_grad_t, shared, in_grad, weights, produced, hidden,
            jnp.concatenate([gate_value, slot_index[:, None].astype(f32)], axis=1), groups, experts,
        )
        tiles = width // 128
        first = 8 + rel_table.shape[0]
        gain_one_grad = small[:tiles].reshape(-1)
        rel_grad = small[8:first, :heads]
        gain_two_grad = small[first : first + tiles].reshape(-1)
        router_grad = small[first + 8 :].reshape(experts, width).T
        out_share, in_share = shares[0], shares[1]
    else:
        output = (hidden + gate_value * gather_rows(exchange(produced, experts))).astype(bf16)
        in_share = lax.psum_scatter(in_grad, "dp", scatter_dimension=0, tiled=True)
        out_share = lax.psum_scatter(out_grad_t, "dp", scatter_dimension=0, tiled=True)
        query_grad, key_grad, value_grad, diagonals = attend_back(
            queries, key_rows, value_rows, grad_context, spread, context_t, logsum
        )
        diagonals = diagonals[:, :2].reshape(heads, 2 * seq_len)
        rel_grad = jnp.einsum("bx,hx->bh", bucket_hot, diagonals, precision=highest)
        grads, input_grad, gain_one_grad, small = tail_native(
            tokens, gain_one, normed_low, query_grad, key_grad, value_grad,
            query_w, key_w, value_w, grad_hidden, out_w_grad, (rel_grad, gain_two_grad, router_grad),
        )
        rel_grad, gain_two_grad, router_grad = small
    grads = grads.astype(f32)
    return (
        output, input_grad, grads[1], grads[2], grads[3], grads[0], rel_grad,
        gain_one_grad, gain_two_grad, router_grad, in_share.astype(f32)[None], out_share.astype(f32).T[None],
    )


def solution(mesh):
    rows = P(("dp", "expert"), None)
    whole = P()
    split = P("expert", None, None)
    return jax.shard_map(
        on_device,
        mesh=mesh,
        in_specs=(
            rows, whole, whole, whole, whole, whole, whole, whole, whole, split, split, rows, whole, rows,
        ),
        out_specs=(
            rows, rows, whole, whole, whole, whole, whole, whole, whole, whole,
            P("expert", "dp", None), P("expert", None, "dp"),
        ),
        check_vma=False,
    )
```

```python
import functools

import jax
import jax.numpy as jnp
from jax import lax
from jax.experimental import pallas as pl
from jax.experimental.pallas import tpu as pltpu
from jax.sharding import PartitionSpec as P

bf16 = jnp.bfloat16
f32 = jnp.float32
epsilon = 1e-06
highest = lax.Precision.HIGHEST

def dot_f32(left, right):
    return lax.dot_general(left, right, (((1,), (0,)), ((), ())), preferred_element_type=f32)


def dot_nt(left, right):
    return lax.dot_general(left, right, (((1,), (1,)), ((), ())), preferred_element_type=f32)


def fill_toeplitz(base_ref, head, row):
    rows, width = base_ref.shape[1:]
    spread = jnp.broadcast_to(row, (8, width))
    eight = pltpu.roll(spread, 0, 1, stride=1, stride_axis=0)
    for group in range(rows // 8):
        base_ref[head, 8 * group : 8 * group + 8, :] = (
            eight if group == 0 else pltpu.roll(eight, 8 * group, 1)
        )


def attend_kernel(
    experts, q_ref, k_ref, v_ref, u_ref, gsend_h, ctx_ref, ctxt_ref, lse_ref, p_h, grecv_h,
    base, qt, vt, s_scr, p_scr, p_sem, send_g, recv_g, own_sem,
):
    seq = q_ref.shape[0]
    span = 256
    half = seq
    qt[...] = q_ref[...].T
    vt[...] = v_ref[...].T
    for head in range(2):
        fill_toeplitz(base, head, u_ref[0, head : head + 1, :])
    zeros = jnp.zeros((64, span), bf16)
    pair = pl.program_id(0)

    if experts:
        me = lax.axis_index("expert")
        count = grecv_h.shape[0] // experts
        rows_of = lambda who: pl.ds(pl.multiple_of(who * count, 16), count)
        peers = [lax.rem(me + k, experts) for k in range(1, experts)]
        barrier = pltpu.get_barrier_semaphore()
        own = pltpu.make_async_copy(gsend_h.at[rows_of(me), :], grecv_h.at[rows_of(me), :], own_sem)

        def give(peer, slot):
            return pltpu.make_async_remote_copy(
                src_ref=gsend_h.at[rows_of(peer), :], dst_ref=grecv_h.at[rows_of(slot), :],
                send_sem=send_g.at[peer], recv_sem=recv_g.at[slot], device_id={"expert": peer},
            )

        @pl.when(pair == 0)
        def _():
            for peer in peers:
                pl.semaphore_signal(barrier, inc=1, device_id={"expert": peer})
            own.start()

    def save(idx, slot):
        cols = pl.ds(pl.multiple_of(idx * span, span), span)
        return pltpu.make_async_copy(p_scr.at[slot], p_h.at[pl.ds(2 * pair, 2), :, cols], p_sem.at[slot])

    def step(idx, carry):
        slot = lax.rem(idx, 2)

        @pl.when((pair > 0) | (idx > 1))
        def _():
            save(idx, slot).wait()

        cols = pl.ds(pl.multiple_of(idx * span, span), span)
        outs = []
        for head in range(2):
            part = qt[64 * head : 64 * head + 64, cols]
            rhs = jnp.concatenate([part, zeros] if head == 0 else [zeros, part], axis=0)
            peak = None
            for kb in range(seq // 128):
                rows = slice(128 * kb, 128 * kb + 128)
                offs = pl.multiple_of(half + span * idx - 128 * kb, 128)
                s = dot_f32(k_ref[rows, :], rhs) + base[head, :, pl.ds(offs, span)]
                s_scr[head, rows, :] = s
                now = jnp.max(s.reshape(16, 8, span), axis=0)
                peak = now if peak is None else jnp.maximum(peak, now)
            peak = jnp.max(peak, axis=0, keepdims=True)
            total = None
            for kb in range(seq // 128):
                rows = slice(128 * kb, 128 * kb + 128)
                e = jnp.exp(s_scr[head, rows, :] - peak)
                s_scr[head, rows, :] = e
                now = jnp.sum(e.reshape(16, 8, span), axis=0)
                total = now if total is None else total + now
            total = jnp.sum(total, axis=0, keepdims=True)
            inv = 1.0 / total
            for kb in range(seq // 128):
                rows = slice(128 * kb, 128 * kb + 128)
                p_scr[slot, head, rows, :] = (s_scr[head, rows, :] * inv).astype(bf16)
            lse_ref[0, head : head + 1, cols] = peak + jnp.log(total)
            outs.append(dot_f32(vt[64 * head : 64 * head + 64, :], p_scr[slot, head]))
        save(idx, slot).start()
        both = jnp.concatenate(outs, axis=0)
        ctxt_ref[:, cols] = both
        ctx_ref[cols, :] = both.T.astype(bf16)
        if experts:
            @pl.when((pair == 0) & (idx == 0))
            def _():
                pl.semaphore_wait(barrier, experts - 1)
                for peer in peers:
                    give(peer, me).start()

        return carry

    lax.fori_loop(0, seq // span, step, 0)

    @pl.when(pair == pl.num_programs(0) - 1)
    def _():
        for slot in range(2):
            save(slot, slot).wait()
        if experts:
            own.wait()
            for peer in peers:
                give(peer, me).wait_send()
                give(peer, peer).wait_recv()


def attend(q, k, v, u, gsend, experts=0):
    seq, width = q.shape
    pairs = width // 128
    blk = pl.BlockSpec((seq, 128), lambda p: (0, p))
    dma = pltpu.SemaphoreType.DMA
    return pl.pallas_call(
        functools.partial(attend_kernel, experts),
        grid=(pairs,),
        in_specs=[
            blk, blk, blk, pl.BlockSpec((1, 2, 2 * seq), lambda p: (p, 0, 0)), pl.BlockSpec(memory_space=pl.ANY),
        ],
        out_specs=[
            blk,
            pl.BlockSpec((128, seq), lambda p: (p, 0)),
            pl.BlockSpec((1, 8, seq), lambda p: (p, 0, 0)),
            pl.BlockSpec(memory_space=pl.ANY),
            pl.BlockSpec(memory_space=pl.ANY),
        ],
        out_shape=[
            jax.ShapeDtypeStruct((seq, width), bf16),
            jax.ShapeDtypeStruct((width, seq), f32),
            jax.ShapeDtypeStruct((pairs, 8, seq), f32),
            jax.ShapeDtypeStruct((2 * pairs, seq, seq), bf16),
            jax.ShapeDtypeStruct(gsend.shape, bf16),
        ],
        scratch_shapes=[
            pltpu.VMEM((2, 128, 2 * seq), f32),
            pltpu.VMEM((128, seq), bf16),
            pltpu.VMEM((128, seq), bf16),
            pltpu.VMEM((2, seq, 256), f32),
            pltpu.VMEM((2, 2, seq, 256), bf16),
            dma((2,)),
            dma((max(experts, 1),)), dma((max(experts, 1),)), dma(()),
        ],
        compiler_params=pltpu.CompilerParams(
            vmem_limit_bytes=62 << 20, has_side_effects=experts > 0, collective_id=3 if experts else None
        ),
        name="attend",
    )(q, k, v, u, gsend)


def first_kernel(
    capacity, experts, tok, gain, wq, wk, wv, route, cot, q_o, k_o, v_o, nl_o, gsend_o, slot_o, column_o, slot
):
    step = pl.program_id(0)
    slots = experts * capacity
    seq = route.shape[1]

    @pl.when(step == 0)
    def _():
        lane = lax.broadcasted_iota(jnp.int32, (8, seq), 1)
        hot = jnp.where(lax.broadcasted_iota(jnp.int32, (8, seq), 0) == route[...], 1.0, 0.0)
        count = hot
        shift = 1
        while shift < seq:
            count = count + jnp.where(lane >= shift, pltpu.roll(count, shift, 1), 0.0)
            shift *= 2
        position = jnp.sum(hot * (count - 1.0), axis=0, keepdims=True)
        place = route[...].astype(f32) * capacity + position
        slot[...] = jnp.where(position < capacity, place, float(slots))
        slot_o[...] = slot[...]
        column_o[...] = jnp.broadcast_to(slot[...], (128, seq)).T

    values = tok[...].astype(f32)
    scale = lax.rsqrt(jnp.mean(values * values, axis=-1, keepdims=True) + epsilon)
    normed = (values * scale * gain[...]).astype(bf16)
    nl_o[...] = normed
    for weight, out in ((wq, q_o), (wk, k_o), (wv, v_o)):
        out[...] = dot_f32(normed, weight[...]).astype(bf16)
    rows = gsend_o.shape[0]
    number = lax.broadcasted_iota(jnp.int32, (rows, seq), 0) + step * rows
    pick = jnp.where(number.astype(f32) == slot[...], 1.0, 0.0).astype(bf16)
    gsend_o[...] = dot_f32(pick, cot[...]).astype(bf16)


def first_pass(tokens, gain, wq, wk, wv, route, cotangent, capacity, experts):
    seq, width = tokens.shape
    slots = experts * capacity
    steps = 4
    rows = pl.BlockSpec((seq // steps, width), lambda i: (i, 0))
    fixed = lambda shape: pl.BlockSpec(shape, lambda i: (0, 0))
    return pl.pallas_call(
        functools.partial(first_kernel, capacity, experts),
        grid=(steps,),
        in_specs=[rows, fixed(gain.shape)] + [fixed(wq.shape)] * 3 + [fixed(route.shape), fixed(cotangent.shape)],
        out_specs=[rows] * 4 + [pl.BlockSpec((slots // steps, width), lambda i: (i, 0)), fixed(route.shape), fixed((seq, 128))],
        out_shape=[jax.ShapeDtypeStruct((seq, width), bf16)] * 4
        + [jax.ShapeDtypeStruct((slots, width), bf16), jax.ShapeDtypeStruct(route.shape, f32),
           jax.ShapeDtypeStruct((seq, 128), f32)],
        scratch_shapes=[pltpu.VMEM(route.shape, f32)],
        compiler_params=pltpu.CompilerParams(vmem_limit_bytes=62 << 20),
        cost_estimate=pl.CostEstimate(
            flops=6 * seq * width * width + 2 * slots * seq * width, bytes_accessed=20 * seq * width, transcendentals=seq
        ),
        name="first",
    )(tokens, gain, wq, wk, wv, route, cotangent)


def middle_kernel(experts, tok, ctx, wo, gain, rw, slot, column, hid_o, xs_o, meta_o, normed):
    seq, width = tok.shape
    span = 256

    def token_block(idx, carry):
        rows = pl.ds(pl.multiple_of(idx * span, span), span)
        hidden = tok[rows, :].astype(f32) + dot_f32(ctx[rows, :], wo[...])
        hid_o[rows, :] = hidden
        scale = lax.rsqrt(jnp.mean(hidden * hidden, axis=-1, keepdims=True) + epsilon)
        low = (hidden * scale * gain[...]).astype(bf16)
        normed[rows, :] = low
        lane = lax.broadcasted_iota(jnp.int32, (span, 128), 1)
        logits = jnp.where(lane < experts, dot_f32(low, rw[...]), -1e30)
        weights = jnp.exp(logits - jnp.max(logits, axis=-1, keepdims=True))
        place = column[rows, :]
        each = xs_o.shape[0] // experts
        first = lane.astype(f32) * each
        chosen = (place >= first) & (place < first + each) & (lane < experts)
        gate = jnp.sum(jnp.where(chosen, weights, 0.0), axis=-1, keepdims=True) / jnp.sum(
            weights, axis=-1, keepdims=True
        )
        meta_o[rows, :] = jnp.where(lane == 0, gate, place)
        return carry

    lax.fori_loop(0, seq // span, token_block, 0)

    def slot_block(idx, carry):
        rows = pl.ds(pl.multiple_of(idx * span, span), span)
        number = lax.broadcasted_iota(jnp.int32, (span, seq), 0) + idx * span
        pick = jnp.where(number.astype(f32) == slot[...], 1.0, 0.0).astype(bf16)
        xs_o[rows, :] = dot_f32(pick, normed[...]).astype(bf16)
        return carry

    lax.fori_loop(0, xs_o.shape[0] // span, slot_block, 0)


def middle_pass(tokens, ctx, wo, gain, rw, slot, column, slots, experts):
    seq, width = tokens.shape
    vmem = pl.BlockSpec(memory_space=pltpu.VMEM)
    return pl.pallas_call(
        functools.partial(middle_kernel, experts),
        in_specs=[vmem] * 7,
        out_specs=[vmem] * 3,
        out_shape=[
            jax.ShapeDtypeStruct((seq, width), f32),
            jax.ShapeDtypeStruct((slots, width), bf16),
            jax.ShapeDtypeStruct((seq, 128), f32),
        ],
        scratch_shapes=[pltpu.VMEM((seq, width), bf16)],
        compiler_params=pltpu.CompilerParams(vmem_limit_bytes=62 << 20),
        cost_estimate=pl.CostEstimate(
            flops=2 * seq * width * width + 2 * slots * seq * width, bytes_accessed=10 * seq * width, transcendentals=seq
        ),
        name="middle",
    )(tokens, ctx, wo, gain, rw, slot, column)


def combine_kernel(gback, hid, cot, gain, ctx, wo, meta, ghid_o, dwo_o, gctx_o, gain_o, low):
    seq, width = hid.shape
    slots = gback.shape[0]
    span = 256

    def token_block(idx, carry):
        rows = pl.ds(pl.multiple_of(idx * span, span), span)
        where = lax.broadcasted_iota(jnp.int32, (span, slots), 1).astype(f32)
        pick = jnp.where(meta[rows, 1:2] == where, 1.0, 0.0).astype(bf16)
        grad = dot_f32(pick, gback[...])
        values = hid[rows, :]
        scale = lax.rsqrt(jnp.mean(values * values, axis=-1, keepdims=True) + epsilon)
        weighted = grad * gain[...]
        inner = jnp.mean(weighted * values, axis=-1, keepdims=True)
        total = cot[rows, :].astype(f32) + scale * weighted - values * (scale * scale * scale * inner)
        ghid_o[rows, :] = total
        branch = total.astype(bf16)
        low[rows, :] = branch
        gctx_o[rows, :] = dot_nt(branch, wo[...]).astype(bf16)
        return carry + jnp.sum(grad * values * scale, axis=0, keepdims=True)

    gain_o[...] = lax.fori_loop(0, seq // span, token_block, jnp.zeros((1, width), f32))

    def weight_block(idx, carry):
        cols = pl.ds(pl.multiple_of(idx * span, span), span)
        dwo_o[cols, :] = dot_f32(ctx[:, cols].T, low[...]).astype(bf16)
        return carry

    lax.fori_loop(0, width // span, weight_block, 0)


def combine_pass(gback, hidden, cotangent, gain, ctx, wo, meta):
    seq, width = hidden.shape
    vmem = pl.BlockSpec(memory_space=pltpu.VMEM)
    return pl.pallas_call(
        combine_kernel,
        in_specs=[vmem] * 7,
        out_specs=[vmem] * 4,
        out_shape=[
            jax.ShapeDtypeStruct((seq, width), f32),
            jax.ShapeDtypeStruct((width, width), bf16),
            jax.ShapeDtypeStruct((seq, width), bf16),
            jax.ShapeDtypeStruct((1, width), f32),
        ],
        scratch_shapes=[pltpu.VMEM((seq, width), bf16)],
        compiler_params=pltpu.CompilerParams(vmem_limit_bytes=62 << 20),
        cost_estimate=pl.CostEstimate(
            flops=4 * seq * width * width + 2 * gback.shape[0] * seq * width,
            bytes_accessed=16 * seq * width, transcendentals=seq,
        ),
        name="combine",
    )(gback, hidden, cotangent, gain, ctx, wo, meta)


def split_rows(row):
    hi = row.astype(bf16).astype(f32)
    mid = (row - hi).astype(bf16).astype(f32)
    low = row - hi - mid
    idx = lax.broadcasted_iota(jnp.int32, (16, row.shape[1]), 0)
    return jnp.where(idx == 0, hi, jnp.where(idx == 1, mid, jnp.where(idx == 2, low, 0.0))).astype(bf16)


def attend_back_kernel(
    q_ref, k_ref, v_ref, g_ref, u_ref, ctxt_ref, lse_ref,
    dq_ref, dk_ref, dv_ref, diag_ref,
    base, acc, kaug, vaug, qaug, gaug, qz, gz, kt, dqt,
):
    seq = q_ref.shape[0]
    span = 256
    lane = lax.broadcasted_iota(jnp.int32, (seq, 128), 1)
    gt = g_ref[...].T
    qtv = q_ref[...].T
    kt[...] = k_ref[...].T
    gtf = gt.astype(f32)
    pad = jnp.zeros((48, seq), bf16)
    one = jnp.ones((seq, 128), bf16)
    nil = jnp.zeros((seq, 128), bf16)
    acc[...] = jnp.zeros_like(acc)
    for head in range(2):
        fill_toeplitz(base, head, u_ref[0, head : head + 1, :])
        own = (lane < 64) if head == 0 else (lane >= 64)
        origin = 64 if head == 0 else 0
        extra = jnp.where((lane >= origin) & (lane < origin + 3), one, nil)
        kaug[head] = jnp.where(own, k_ref[...], extra)
        vaug[head] = jnp.where(own, v_ref[...], extra)
        qz[head] = jnp.where(own, q_ref[...], nil)
        gz[head] = jnp.where(own, g_ref[...], nil)
        rows = slice(64 * head, 64 * head + 64)
        lse = split_rows(-lse_ref[0, head : head + 1, :])
        dsum = split_rows(-jnp.sum(gtf[rows] * ctxt_ref[rows, :], axis=0, keepdims=True))
        for dst, src, aug in ((qaug, qtv, lse), (gaug, gt, dsum)):
            dst[head, rows, :] = src[rows]
            dst[head, origin : origin + 16, :] = aug
            dst[head, origin + 16 : origin + 64, :] = pad

    dqt[...] = jnp.zeros_like(dqt)

    def step(idx, carry):
        rows = pl.ds(pl.multiple_of(idx * span, span), span)
        dv = None
        dk = None
        for head in range(2):
            s = dot_f32(kaug[head, rows, :], qaug[head])
            dp = dot_f32(vaug[head, rows, :], gaug[head])
            tops = []
            grads = []
            for part in range(2):
                offs = pl.ds(pl.multiple_of(seq - span * idx - 128 * part, 128), seq)
                p = jnp.exp(s[128 * part : 128 * part + 128] + base[head, :, offs])
                ds_ = p * dp[128 * part : 128 * part + 128]
                acc[head, :, offs] += ds_
                tops.append(p.astype(bf16))
                grads.append(ds_.astype(bf16))
            p = jnp.concatenate(tops, axis=0)
            ds_ = jnp.concatenate(grads, axis=0)
            now = dot_f32(p, gz[head])
            dv = now if dv is None else dv + now
            now = dot_f32(ds_, qz[head])
            dk = now if dk is None else dk + now
            dqt[64 * head : 64 * head + 64, :] += dot_f32(kt[64 * head : 64 * head + 64, rows], ds_)
        dv_ref[rows, :] = dv.astype(bf16)
        dk_ref[rows, :] = dk.astype(bf16)
        return carry

    lax.fori_loop(0, seq // span, step, 0)
    dq_ref[...] = dqt[...].T.astype(bf16)
    width = 2 * seq
    for head in range(2):
        total = acc[head, 0:8, :]
        for group in range(1, 16):
            total = total + pltpu.roll(acc[head, 8 * group : 8 * group + 8, :], width - 8 * group, 1)
        sub = lax.broadcasted_iota(jnp.int32, (8, width), 0)
        for bit in (1, 2, 4):
            total = jnp.where((sub & bit) != 0, pltpu.roll(total, width - bit, 1), total)
        diag_ref[0, head : head + 1, :] = jnp.sum(total, axis=0, keepdims=True)


def attend_back(q, k, v, g, u, ctxt, lse):
    seq, width = q.shape
    pairs = width // 128
    blk = pl.BlockSpec((seq, 128), lambda p: (0, p))
    return pl.pallas_call(
        attend_back_kernel,
        grid=(pairs,),
        in_specs=[
            blk, blk, blk, blk,
            pl.BlockSpec((1, 2, 2 * seq), lambda p: (p, 0, 0)),
            pl.BlockSpec((128, seq), lambda p: (p, 0)),
            pl.BlockSpec((1, 8, seq), lambda p: (p, 0, 0)),
        ],
        out_specs=[blk, blk, blk, pl.BlockSpec((1, 8, 2 * seq), lambda p: (p, 0, 0))],
        out_shape=[jax.ShapeDtypeStruct((seq, width), bf16)] * 3
        + [jax.ShapeDtypeStruct((pairs, 8, 2 * seq), f32)],
        scratch_shapes=[
            pltpu.VMEM((2, 128, 2 * seq), f32),
            pltpu.VMEM((2, 128, 2 * seq), f32),
            pltpu.VMEM((2, seq, 128), bf16),
            pltpu.VMEM((2, seq, 128), bf16),
            pltpu.VMEM((2, 128, seq), bf16),
            pltpu.VMEM((2, 128, seq), bf16),
            pltpu.VMEM((2, seq, 128), bf16),
            pltpu.VMEM((2, seq, 128), bf16),
            pltpu.VMEM((128, seq), bf16),
            pltpu.VMEM((128, seq), f32),
        ],
        compiler_params=pltpu.CompilerParams(vmem_limit_bytes=56 << 20),
        cost_estimate=pl.CostEstimate(
            flops=40 * seq * seq * width, bytes_accessed=20 * seq * width, transcendentals=seq * seq * 12
        ),
        name="attend_back",
    )(q, k, v, g, u, ctxt, lse)


def gelu_both(v):
    scale = 0.7978845608028654
    square = v * v
    t = jnp.tanh(scale * v * (1.0 + 0.044715 * square))
    half = 0.5 * (1.0 + t)
    slope = half + 0.5 * v * (1.0 - t * t) * (scale * (1.0 + 3 * 0.044715 * square))
    return v * half, slope


def expert_kernel(
    experts, capacity, tile,
    xs, gr_h, win_h, wout_h, rw,
    gback_o, prod_o, dwin_o, dwout_o, drw_o, shared_o,
    xall, gr, gp, win, wout, act, gpre, gback, gsend, prod, logit, acc_p, acc_g, xt, gpt, stage, dwt,
    send_x, recv_x, send_g, recv_g, local, out_sem, send_s, recv_s,
):
    me = lax.axis_index("expert")
    place = me // 2
    chips = experts // 2
    span = 2 * capacity
    width = xall.shape[1]
    hidden = win.shape[1]
    barrier = pltpu.get_barrier_semaphore()
    for k in range(1, experts):
        pl.semaphore_signal(barrier, inc=1, device_id={"expert": lax.rem(me + k, experts)})
    my_dp = lax.axis_index("dp")
    dp_x, dp_y = lax.rem(my_dp, 2), my_dp // 2
    peer_x, peer_y = my_dp + 1 - 2 * dp_x, my_dp + 2 - 4 * dp_y
    for peer in (peer_x, peer_y):
        pl.semaphore_signal(barrier, inc=1, device_id={"dp": peer})
    loads = [
        pltpu.make_async_copy(win_h, win, local.at[0]),
        pltpu.make_async_copy(wout_h, wout, local.at[1]),
        pltpu.make_async_copy(gr_h, gr, local.at[2]),
    ]
    rows_of = lambda who: pl.ds(pl.multiple_of(who * capacity, 16), capacity)
    own = pltpu.make_async_copy(xs.at[rows_of(me), :], xall.at[rows_of(me), :], local.at[3])
    own.start()
    for copy in loads:
        copy.start()
    pl.semaphore_wait(barrier, experts + 1)

    def partner(step):
        high, low = place // 2, lax.rem(place, 2)
        fhigh, flow = step // 2, lax.rem(step, 2)
        return 2 * (high + fhigh - 2 * high * fhigh) + low + flow - 2 * low * flow

    def send_rows(peer):
        return pltpu.make_async_remote_copy(
            src_ref=xs.at[rows_of(peer), :], dst_ref=xall.at[rows_of(me), :],
            send_sem=send_x.at[peer], recv_sem=recv_x.at[me], device_id={"expert": peer},
        )

    def got_rows(peer):
        return pltpu.make_async_remote_copy(
            src_ref=xs.at[rows_of(peer), :], dst_ref=xall.at[rows_of(peer), :],
            send_sem=send_x.at[peer], recv_sem=recv_x.at[peer], device_id={"expert": peer},
        )

    def send_back(peer):
        return pltpu.make_async_remote_copy(
            src_ref=gsend.at[rows_of(peer), :], dst_ref=gback.at[rows_of(me), :],
            send_sem=send_g.at[peer], recv_sem=recv_g.at[me], device_id={"expert": peer},
        )

    def got_back(peer):
        return pltpu.make_async_remote_copy(
            src_ref=gsend.at[rows_of(peer), :], dst_ref=gback.at[rows_of(peer), :],
            send_sem=send_g.at[peer], recv_sem=recv_g.at[peer], device_id={"expert": peer},
        )

    sibling = me + 1 - 2 * lax.rem(me, 2)
    send_rows(sibling).start()
    for step in range(1, chips):
        for core in range(2):
            send_rows(2 * partner(step) + lax.rem(me + core, 2)).start()
    for copy in loads:
        copy.wait()

    lanes = lax.broadcasted_iota(jnp.int32, (span, rw.shape[1]), 1)
    mine = jnp.where(lanes == me, 1.0, 0.0)

    def work(step, carry):
        where = partner(step)
        base = pl.multiple_of(where * span, 32)

        @pl.when(step == 0)
        def _():
            own.wait()
            got_rows(sibling).wait_recv()

        @pl.when(step > 0)
        def _():
            got_rows(2 * where).wait_recv()
            got_rows(2 * where + 1).wait_recv()

        rows = pl.ds(base, span)
        x = xall[rows, :]
        logits = jnp.where(lanes < experts, dot_f32(x, rw[...]), -1e30)
        weights = jnp.exp(logits - jnp.max(logits, axis=-1, keepdims=True))
        probs = weights / jnp.sum(weights, axis=-1, keepdims=True)
        gate = jnp.sum(probs * mine, axis=-1, keepdims=True)
        gp[rows, :] = (gr[rows, :].astype(f32) * gate).astype(bf16)
        acc_p[...] = jnp.zeros_like(acc_p)
        acc_g[...] = jnp.zeros_like(acc_g)

        def block(idx, carry):
            cols = pl.ds(pl.multiple_of(idx * tile, tile), tile)
            h = dot_f32(xall[rows, :], win[:, cols])
            grad = dot_nt(gp[rows, :], wout[cols, :])
            value, slope = gelu_both(h)
            value = value.astype(bf16)
            grad = (grad * slope).astype(bf16)
            act[rows, cols] = value
            gpre[rows, cols] = grad
            acc_p[...] += dot_f32(value, wout[cols, :])
            acc_g[...] += dot_nt(grad, win[:, cols])
            return carry

        lax.fori_loop(0, hidden // tile, block, 0)
        made = acc_p[...].astype(bf16)
        prod[rows, :] = made
        gate_grad = jnp.sum(gr[rows, :].astype(f32) * made.astype(f32), axis=-1, keepdims=True)
        low = (gate_grad * gate * (mine - probs)).astype(bf16)
        low = jnp.where(lanes < experts, low, jnp.zeros_like(low))
        logit[rows, :] = low
        gsend[rows, :] = (acc_g[...] + dot_nt(low, rw[...])).astype(bf16)

        @pl.when(step == 0)
        def _():
            send_back(sibling).start()

        @pl.when(step > 0)
        def _():
            send_back(2 * where).start()
            send_back(2 * where + 1).start()

        return carry

    lax.fori_loop(0, chips, work, 0)
    outs = [
        pltpu.make_async_copy(prod, prod_o, local.at[0]),
        pltpu.make_async_copy(gsend.at[rows_of(me), :], gback.at[rows_of(me), :], local.at[3]),
    ]
    for copy in outs:
        copy.start()
    xt[...] = xall[...].T
    gpt[...] = gp[...].T
    drw_o[...] = dot_f32(xt[...], logit[...])

    share = width // 4
    tiles = hidden // tile
    split = tiles // 2

    def left_copy(idx, block):
        cols = pl.ds(pl.multiple_of(idx * tile, tile), tile)
        rows = pl.ds(pl.multiple_of((1 - dp_x + 2 * block) * share, 16), share)
        return pltpu.make_async_remote_copy(
            src_ref=dwt.at[rows, cols], dst_ref=shared_o.at[pl.ds(block * share, share), cols],
            send_sem=send_s.at[block, idx], recv_sem=recv_s.at[block, idx], device_id={"dp": peer_x},
        )

    def right_copy(idx, block):
        cols = pl.ds(pl.multiple_of(idx * tile, tile), tile)
        rows = pl.ds(pl.multiple_of((2 - 2 * dp_y + block) * share, 16), share)
        dst_cols = pl.ds(pl.multiple_of((idx - split) * tile, tile), tile)
        return pltpu.make_async_remote_copy(
            src_ref=dwt.at[rows, cols], dst_ref=shared_o.at[pl.ds((2 + block) * share, share), dst_cols],
            send_sem=send_s.at[block, idx], recv_sem=recv_s.at[block, idx], device_id={"dp": peer_y},
        )

    def out_block(step, carry):
        idx = lax.rem(step, 2) * split + step // 2
        cols = pl.ds(pl.multiple_of(idx * tile, tile), tile)
        dwt[:, cols] = dot_f32(gpt[...], act[:, cols]).astype(bf16)

        @pl.when(idx < split)
        def _():
            for block in range(2):
                left_copy(idx, block).start()

        @pl.when(idx >= split)
        def _():
            for block in range(2):
                right_copy(idx, block).start()

        return carry

    lax.fori_loop(0, tiles, out_block, 0)
    whole = pltpu.make_async_copy(dwt, dwout_o, local.at[2])
    whole.start()

    def put(slot, cols):
        return pltpu.make_async_copy(stage.at[slot], dwin_o.at[:, cols], out_sem.at[slot])

    def in_block(idx, carry):
        cols = pl.ds(pl.multiple_of(idx * tile, tile), tile)
        slot = lax.rem(idx, 2)

        @pl.when(idx > 1)
        def _():
            put(slot, cols).wait()

        stage[slot] = dot_f32(xt[...], gpre[:, cols]).astype(bf16)
        put(slot, cols).start()
        return carry

    lax.fori_loop(0, tiles, in_block, 0)
    for slot in range(2):
        put(slot, pl.ds(0, tile)).wait()
    whole.wait()
    for copy in outs:
        copy.wait()
    for k in range(1, experts):
        peer = lax.rem(me + k, experts)
        got_rows(peer).wait_send()
        got_back(peer).wait_send()
        got_back(peer).wait_recv()
    back = pltpu.make_async_copy(gback, gback_o, local.at[1])
    back.start()
    for idx in range(tiles):
        for block in range(2):
            (left_copy if idx < split else right_copy)(idx, block).wait()
    back.wait()


def expert_pass(xs, gr, weight_in, weight_out, router_pad, experts, capacity):
    slots, width = xs.shape
    hidden = weight_in.shape[1]
    tile = 512
    span = 2 * capacity
    hbm = pl.BlockSpec(memory_space=pl.ANY)
    vmem = pl.BlockSpec(memory_space=pltpu.VMEM)
    return pl.pallas_call(
        functools.partial(expert_kernel, experts, capacity, tile),
        in_specs=[hbm, hbm, hbm, hbm, vmem],
        out_specs=[hbm, hbm, hbm, hbm, vmem, hbm],
        out_shape=[
            jax.ShapeDtypeStruct((slots, width), bf16),
            jax.ShapeDtypeStruct((slots, width), bf16),
            jax.ShapeDtypeStruct((width, hidden), bf16),
            jax.ShapeDtypeStruct((width, hidden), bf16),
            jax.ShapeDtypeStruct((width, router_pad.shape[1]), f32),
            jax.ShapeDtypeStruct((width, hidden // 2), bf16),
        ],
        scratch_shapes=[
            pltpu.VMEM((slots, width), bf16),
            pltpu.VMEM((slots, width), bf16),
            pltpu.VMEM((slots, width), bf16),
            pltpu.VMEM((width, hidden), bf16),
            pltpu.VMEM((hidden, width), bf16),
            pltpu.VMEM((slots, hidden), bf16),
            pltpu.VMEM((slots, hidden), bf16),
            pltpu.VMEM((slots, width), bf16),
            pltpu.VMEM((slots, width), bf16),
            pltpu.VMEM((slots, width), bf16),
            pltpu.VMEM((slots, router_pad.shape[1]), bf16),
            pltpu.VMEM((span, width), f32),
            pltpu.VMEM((span, width), f32),
            pltpu.VMEM((width, slots), bf16),
            pltpu.VMEM((width, slots), bf16),
            pltpu.VMEM((2, width, tile), bf16),
            pltpu.VMEM((width, hidden), bf16),
            pltpu.SemaphoreType.DMA((experts,)),
            pltpu.SemaphoreType.DMA((experts,)),
            pltpu.SemaphoreType.DMA((experts,)),
            pltpu.SemaphoreType.DMA((experts,)),
            pltpu.SemaphoreType.DMA((4,)),
            pltpu.SemaphoreType.DMA((2,)),
            pltpu.SemaphoreType.DMA((2, hidden // tile)),
            pltpu.SemaphoreType.DMA((2, hidden // tile)),
        ],
        compiler_params=pltpu.CompilerParams(
            vmem_limit_bytes=60 << 20, collective_id=1, has_side_effects=True
        ),
        cost_estimate=pl.CostEstimate(
            flops=12 * slots * width * hidden, bytes_accessed=8 * width * hidden, transcendentals=slots * hidden
        ),
        name="experts",
    )(xs, gr, weight_in, weight_out, router_pad)


def remote(src, dst, send_sem, recv_sem, axis, peer):
    return pltpu.make_async_remote_copy(
        src_ref=src, dst_ref=dst, send_sem=send_sem, recv_sem=recv_sem, device_id={axis: peer}
    )


def others(count, mine):
    return [lax.rem(mine + k, count) for k in range(1, count)]


PLAN = (
    (11, 16, 19, 22, 24),
    (12, 17, 20, 23, 25),
    (5, 13, 16, 19, 21),
    (9, 15, 18, 21, 23),
    (13, 18, 21, 24, 26),
    (17, 21, 24, 27, 29),
    (21, 24, 27, 29, 31),
)
OUTPUT_SLOT = 17
EXPERT_SLOTS = ((6, 2, 0), (14, 3, 0), (15, 2, 1), (22, 3, 1))


def back_kernel(
    groups, experts, pairs,
    q_ref, k_ref, v_ref, g_ref, ctxt_ref, wq, wk, wv, hot, gain, nl_h, tok_h, ghid_h, dwo_h, small_h,
    eout_h, shared_h, ein_h, p_h, prod_h, hid_h, meta,
    wsum_o, ing_o, small_o, esum_o, out_o,
    acc, vaug, gaug, qz, gz, kt, dqt, pbuf, pret, hbuf, obuf, dall, nt, tok,
    part, r1, r2, r3, full, sbuf, srecv, sone, stwo, keep, other, final,
    send1, recv1, send2, recv2, send3, recv3, send4, recv4, send5, recv5, send6, recv6, send7, recv7, local,
    send_a, recv_a, send_b, recv_b, out_sem, copy_sem, p_sem, send_p, recv_p, o_sem,
):
    seq = q_ref.shape[0]
    width = tok.shape[1]
    span = 256
    pair = pl.program_id(0)
    me = lax.axis_index("expert")
    my_dp = lax.axis_index("dp")
    core = lax.rem(me, 2)
    place = me // 2
    chips = experts // 2
    sibling = me + 1 - 2 * core
    half = width // 2
    piece = half // groups
    thick = part.shape[2]
    gain_rows = width // 128

    def half_rows(which):
        return pl.ds(pl.multiple_of(which * half, 16), half)

    def own_piece(which):
        return pl.ds(pl.multiple_of(core * half + which * piece, 16), piece)

    def copy1(c):
        return remote(part.at[c, half_rows(1 - core), :], r1.at[c], send1.at[c], recv1.at[c], "expert", sibling)

    def copy2(c, peer, slot):
        return remote(part.at[c, own_piece(peer), :], r2.at[c, slot], send2.at[c, peer], recv2.at[c, slot], "dp", peer)

    def copy3(c, peer, slot):
        return remote(
            r3.at[c, place], r3.at[c, slot], send3.at[c, peer], recv3.at[c, slot], "expert", 2 * peer + core
        )

    def copy4(c, peer, slot):
        return remote(
            full.at[c, own_piece(my_dp), :], full.at[c, own_piece(slot), :],
            send4.at[c, peer], recv4.at[c, slot], "dp", peer,
        )

    def copy5(c, which):
        return remote(
            full.at[c, half_rows(which), :], full.at[c, half_rows(which), :],
            send5.at[c], recv5.at[c], "expert", sibling,
        )

    def stage1(c):
        copy1(c).start()

    def stage2(c):
        copy1(c).wait_recv()
        part[c, half_rows(core), :] = (part[c, half_rows(core), :].astype(f32) + r1[c].astype(f32)).astype(bf16)
        for peer in others(groups, my_dp):
            copy2(c, peer, my_dp).start()

    def stage3(c):
        total = part[c, own_piece(my_dp), :].astype(f32)
        for peer in others(groups, my_dp):
            copy2(c, peer, peer).wait_recv()
            total = total + r2[c, peer].astype(f32)
        r3[c, place] = total.astype(bf16)
        for peer in others(chips, place):
            copy3(c, peer, place).start()

    def stage4(c):
        for peer in others(chips, place):
            copy3(c, peer, peer).wait_recv()
        total = r3[c, 0].astype(f32)
        for slot in range(1, chips):
            total = total + r3[c, slot].astype(f32)
        full[c, own_piece(my_dp), :] = total.astype(bf16)
        for peer in others(groups, my_dp):
            copy4(c, peer, my_dp).start()

    def stage5(c):
        for peer in others(groups, my_dp):
            copy4(c, peer, peer).wait_recv()
        copy5(c, core).start()

    def put_first(c):
        return pltpu.make_async_copy(full.at[c], wsum_o.at[0, :, thick * c : thick * c + thick], out_sem.at[c, 0])

    def put_pair(c, which):
        cols = pl.ds(128 * (c - 2) if isinstance(c, int) else pl.multiple_of(128 * (c - 2), 128), 128)
        return pltpu.make_async_copy(
            full.at[c, :, 128 * which : 128 * which + 128], wsum_o.at[1 + which, :, cols], out_sem.at[c, which]
        )

    def stage6(c):
        copy5(c, 1 - core).wait_recv()

        if c < 2:
            put_first(c).start()
        else:
            for which in range(3):
                put_pair(c, which).start()

    share = width // 4
    dp_x, dp_y = lax.rem(my_dp, 2), my_dp // 2
    peer_x, peer_y = my_dp + 1 - 2 * dp_x, my_dp + 2 - 4 * dp_y
    middle = keep.shape[1]
    left, right = pl.ds(0, middle), pl.ds(middle, middle)

    def share_rows(which):
        return pl.ds(pl.multiple_of(which * share, 16), share)

    def first_left(block):
        return remote(
            ein_h.at[share_rows(1 - dp_x + 2 * block), left], other.at[1, share_rows(block), :],
            send_a.at[0, block], recv_a.at[0, block], "dp", peer_x,
        )

    def first_right(block):
        return remote(
            ein_h.at[share_rows(2 - 2 * dp_y + block), right], other.at[1, share_rows(2 + block), :],
            send_a.at[1, block], recv_a.at[1, block], "dp", peer_y,
        )

    def second_left(which):
        return remote(
            keep.at[share_rows(1 - dp_y), :], final.at[which, :, left],
            send_b.at[which, 0], recv_b.at[which, 0], "dp", peer_y,
        )

    def second_right(which):
        return remote(
            keep.at[share_rows(2 + 1 - dp_x), :], final.at[which, :, right],
            send_b.at[which, 1], recv_b.at[which, 1], "dp", peer_x,
        )

    def own_loads(src):
        loads = []
        for block in range(2):
            loads.append(
                pltpu.make_async_copy(
                    src.at[share_rows(dp_x + 2 * block), left], keep.at[share_rows(block), :], copy_sem.at[block]
                )
            )
            loads.append(
                pltpu.make_async_copy(
                    src.at[share_rows(2 * dp_y + block), right], keep.at[share_rows(2 + block), :], copy_sem.at[2 + block]
                )
            )
        return loads

    def shared_load():
        return pltpu.make_async_copy(shared_h, other.at[0], copy_sem.at[4])

    def save(which):
        return pltpu.make_async_copy(final.at[which], esum_o.at[which], copy_sem.at[5])

    def experts_begin():
        for copy in own_loads(eout_h) + [shared_load()]:
            copy.start()
        for block in range(2):
            first_left(block).start()
            first_right(block).start()

    def experts_second(which):
        for copy in own_loads(eout_h if which == 0 else ein_h):
            copy.wait()
        if which == 0:
            shared_load().wait()
        else:
            for block in range(2):
                first_left(block).wait_recv()
                first_right(block).wait_recv()

        def block(idx, carry):
            rows = pl.ds(pl.multiple_of(idx * 64, 64), 64)
            keep[rows, :] = (keep[rows, :].astype(f32) + other[which, rows, :].astype(f32)).astype(bf16)
            return carry

        lax.fori_loop(0, width // 64, block, 0)
        second_left(which).start()
        second_right(which).start()

    def experts_last(which):
        second_left(which).wait()
        second_right(which).wait()

        def block(idx, carry):
            rows = pl.ds(pl.multiple_of(idx * 64, 64), 64)
            mine_left = pl.ds(pl.multiple_of(dp_y * share + idx * 64, 64), 64)
            mine_right = pl.ds(pl.multiple_of((2 + dp_x) * share + idx * 64, 64), 64)
            final[which, rows, left] = (final[which, rows, left].astype(f32) + keep[mine_left, :].astype(f32)).astype(bf16)
            final[which, rows, right] = (final[which, rows, right].astype(f32) + keep[mine_right, :].astype(f32)).astype(bf16)
            return carry

        lax.fori_loop(0, share // 64, block, 0)
        if which == 0:
            for copy in own_loads(ein_h):
                copy.start()
        else:
            save(0).wait()
        save(which).start()

    early = pl.ds(8 + hot.shape[0], sbuf.shape[0] - 8 - hot.shape[0])
    late = pl.ds(0, 8 + hot.shape[0])

    def copy6(part_idx, rows, peer, slot):
        return remote(
            sbuf.at[rows, :], srecv.at[slot, rows, :],
            send6.at[part_idx, peer], recv6.at[part_idx, slot], "expert", peer,
        )

    def copy7(part_idx, rows, peer, slot):
        return remote(
            sone.at[rows, :], stwo.at[slot, rows, :],
            send7.at[part_idx, peer], recv7.at[part_idx, slot], "dp", peer,
        )

    def small1(part_idx, rows):
        srecv[me, rows, :] = sbuf[rows, :]
        for peer in others(experts, me):
            copy6(part_idx, rows, peer, me).start()

    def small2(part_idx, rows):
        for peer in others(experts, me):
            copy6(part_idx, rows, peer, peer).wait_recv()
        total = srecv[0, rows, :]
        for slot in range(1, experts):
            total = total + srecv[slot, rows, :]
        sone[rows, :] = total
        stwo[my_dp, rows, :] = total
        for peer in others(groups, my_dp):
            copy7(part_idx, rows, peer, my_dp).start()

    def small3(part_idx, rows):
        for peer in others(groups, my_dp):
            copy7(part_idx, rows, peer, peer).wait_recv()
        total = stwo[0, rows, :]
        for slot in range(1, groups):
            total = total + stwo[slot, rows, :]
        small_o[rows, :] = total

    stages = (stage2, stage3, stage4, stage5, stage6)

    def advance(slot):
        for c, slots in enumerate(PLAN):
            for at, stage in reversed(list(zip(slots, stages))):
                if at < 4 * pairs:
                    pl.when(slot == at)(functools.partial(stage, c))

    def load_p(slot_idx, slot):
        rows = pl.ds(pl.multiple_of(lax.rem(slot_idx, 4) * span, span), span)
        return pltpu.make_async_copy(p_h.at[pl.ds(2 * (slot_idx // 4), 2), rows, :], pbuf.at[slot], p_sem.at[slot])

    slots_each = pret.shape[0] // experts

    def slot_rows(which):
        return pl.ds(pl.multiple_of(which * slots_each, 16), slots_each)

    def give_back(peer):
        return remote(
            prod_h.at[slot_rows(peer), :], pret.at[slot_rows(me), :], send_p.at[peer], recv_p.at[me], "expert", peer
        )

    def got_back(peer):
        return remote(
            prod_h.at[slot_rows(peer), :], pret.at[slot_rows(peer), :], send_p.at[peer], recv_p.at[peer], "expert", peer
        )

    def own_back():
        return pltpu.make_async_copy(prod_h.at[slot_rows(me), :], pret.at[slot_rows(me), :], o_sem.at[0])

    def out_rows(block):
        return pl.ds(block * span, span)

    def load_hidden(block):
        return pltpu.make_async_copy(hid_h.at[out_rows(block), :], hbuf, o_sem.at[1])

    def save_out(block):
        return pltpu.make_async_copy(obuf, out_o.at[out_rows(block), :], o_sem.at[2])

    def output_block(block):
        if block == 0:
            own_back().wait()
            for peer in others(experts, me):
                got_back(peer).wait_recv()
        load_hidden(block).wait()
        where = lax.broadcasted_iota(jnp.int32, (span, pret.shape[0]), 1).astype(f32)
        pick = jnp.where(meta[out_rows(block), 1:2] == where, 1.0, 0.0).astype(bf16)
        gathered = dot_f32(pick, pret[...])
        if block > 0:
            save_out(block - 1).wait()
        obuf[...] = (hbuf[...] + meta[out_rows(block), 0:1] * gathered).astype(bf16)
        save_out(block).start()
        if (block + 1) * span < seq:
            load_hidden(block + 1).start()

    loads = [
        pltpu.make_async_copy(nl_h, tok, local.at[0]),
        pltpu.make_async_copy(ghid_h, ing_o, local.at[2]),
        pltpu.make_async_copy(dwo_h.at[:, 0:thick], part.at[0], local.at[3]),
        pltpu.make_async_copy(dwo_h.at[:, thick : 2 * thick], part.at[1], local.at[4]),
        pltpu.make_async_copy(small_h, sbuf, local.at[5]),
    ]

    @pl.when(pair == 0)
    def _():
        barrier = pltpu.get_barrier_semaphore()
        for peer in others(experts, me):
            pl.semaphore_signal(barrier, inc=1, device_id={"expert": peer})
        for peer in others(groups, my_dp):
            pl.semaphore_signal(barrier, inc=1, device_id={"dp": peer})
        for copy in loads:
            copy.start()
        load_p(0, 0).start()
        own_back().start()
        load_hidden(0).start()
        for copy in loads:
            copy.wait()
        nt[...] = tok[...].T
        pl.semaphore_wait(barrier, experts + groups - 2)
        stage1(0)
        stage1(1)
        small1(0, early)
        experts_begin()
        for peer in others(experts, me):
            give_back(peer).start()

    mine = pl.ds(pl.multiple_of(128 * pair, 128), 128)
    lane = lax.broadcasted_iota(jnp.int32, (seq, 128), 1)
    gt = g_ref[...].T
    kt[...] = k_ref[...].T
    gtf = gt.astype(f32)
    pad = jnp.zeros((48, seq), bf16)
    one = jnp.ones((seq, 128), bf16)
    nil = jnp.zeros((seq, 128), bf16)
    acc[...] = jnp.zeros_like(acc)
    for head in range(2):
        own = (lane < 64) if head == 0 else (lane >= 64)
        origin = 64 if head == 0 else 0
        extra = jnp.where((lane >= origin) & (lane < origin + 3), one, nil)
        vaug[head] = jnp.where(own, v_ref[...], extra)
        qz[head] = jnp.where(own, q_ref[...], nil)
        gz[head] = jnp.where(own, g_ref[...], nil)
        rows = slice(64 * head, 64 * head + 64)
        gaug[head, rows, :] = gt[rows]
        gaug[head, origin : origin + 16, :] = split_rows(
            -jnp.sum(gtf[rows] * ctxt_ref[rows, :], axis=0, keepdims=True)
        )
        gaug[head, origin + 16 : origin + 64, :] = pad

    dqt[...] = jnp.zeros_like(dqt)

    def step(idx, carry):
        rows = pl.ds(pl.multiple_of(idx * span, span), span)
        dv = None
        dk = None
        slot = lax.rem(idx, 2)
        load_p(4 * pair + idx, slot).wait()

        @pl.when(4 * pair + idx + 1 < 4 * pairs)
        def _():
            load_p(4 * pair + idx + 1, 1 - slot).start()

        for head in range(2):
            dp = dot_f32(vaug[head, rows, :], gaug[head])
            grads = []
            for part_idx in range(2):
                offs = pl.ds(pl.multiple_of(seq - span * idx - 128 * part_idx, 128), seq)
                band = slice(128 * part_idx, 128 * part_idx + 128)
                ds_ = pbuf[slot, head, band, :].astype(f32) * dp[band]
                acc[head, :, offs] += ds_
                grads.append(ds_.astype(bf16))
            ds_ = jnp.concatenate(grads, axis=0)
            now = dot_f32(pbuf[slot, head], gz[head])
            dv = now if dv is None else dv + now
            now = dot_f32(ds_, qz[head])
            dk = now if dk is None else dk + now
            dqt[64 * head : 64 * head + 64, :] += dot_f32(kt[64 * head : 64 * head + 64, rows], ds_)
        dall[1, rows, mine] = dk.astype(bf16)
        dall[2, rows, mine] = dv.astype(bf16)
        advance(4 * pair + idx)

        for block in range(seq // span):
            @pl.when(4 * pair + idx == OUTPUT_SLOT + block)
            def _():
                output_block(block)

        for at, task, which in EXPERT_SLOTS:
            @pl.when(4 * pair + idx == at)
            def _():
                (experts_second if task == 2 else experts_last)(which)

        @pl.when(4 * pair + idx == 7)
        def _():
            small2(0, early)

        @pl.when(4 * pair + idx == 11)
        def _():
            small3(0, early)

        return carry

    lax.fori_loop(0, seq // span, step, 0)
    dall[0, :, mine] = dqt[...].T.astype(bf16)
    twice = 2 * seq
    sub = lax.broadcasted_iota(jnp.int32, (8, twice), 0)
    head_lane = lax.broadcasted_iota(jnp.int32, (hot.shape[0], 128), 1)
    rel_rows = slice(8, 8 + hot.shape[0])
    for head in range(2):
        total = acc[head, 0:8, :]
        for group in range(1, 16):
            total = total + pltpu.roll(acc[head, 8 * group : 8 * group + 8, :], twice - 8 * group, 1)
        for bit in (1, 2, 4):
            total = jnp.where((sub & bit) != 0, pltpu.roll(total, twice - bit, 1), total)
        diag = jnp.sum(total, axis=0, keepdims=True)
        sums = jnp.sum(hot[...] * diag, axis=1, keepdims=True)
        sbuf[rel_rows, :] = jnp.where(head_lane == 2 * pair + head, sums, sbuf[rel_rows, :])

    def weight_block(idx, carry):
        rows = pl.ds(pl.multiple_of(idx * 256, 256), 256)
        grads = jnp.concatenate([dall[which, :, mine] for which in range(3)], axis=1)
        part[pair + 2, rows, :] = dot_f32(nt[rows, :], grads).astype(bf16)
        return carry

    lax.fori_loop(0, width // 256, weight_block, 0)
    stage1(pair + 2)

    @pl.when(pair == pairs - 1)
    def _():
        def token_block(idx, carry):
            rows = pl.ds(pl.multiple_of(idx * 256, 256), 256)
            grad = (
                dot_nt(dall[0, rows, :], wq[...])
                + dot_nt(dall[1, rows, :], wk[...])
                + dot_nt(dall[2, rows, :], wv[...])
            )
            values = tok[rows, :].astype(f32)
            scale = lax.rsqrt(jnp.mean(values * values, axis=-1, keepdims=True) + epsilon)
            weighted = grad * gain[...]
            inner = jnp.mean(weighted * values, axis=-1, keepdims=True)
            ing_o[rows, :] += scale * weighted - values * (scale * scale * scale * inner)
            return carry + jnp.sum(grad * values * scale, axis=0, keepdims=True)

        reload = pltpu.make_async_copy(tok_h, tok, local.at[1])
        reload.start()
        last = pairs + 1
        first = 4 * pairs
        older = sorted(
            (at, c, stage)
            for c, slots in enumerate(PLAN)
            for stage, at in enumerate(slots)
            if at >= first
        )

        def drain(until):
            while older and older[0][0] < first + until:
                _, c, stage = older.pop(0)
                stages[stage](c)

        def tokens_done(lower, upper, gain_grad):
            return lax.fori_loop(lower, upper, token_block, gain_grad)

        drain(1)
        reload.wait()
        gain_grad = tokens_done(0, 1, jnp.zeros((1, width), f32))
        stage2(last)
        drain(2)
        gain_grad = tokens_done(1, seq // 512, gain_grad)
        drain(4)
        gain_grad = tokens_done(seq // 512, seq // 256, gain_grad)
        stage3(last)
        for row in range(gain_rows):
            sbuf[row : row + 1, :] = gain_grad[:, 128 * row : 128 * row + 128]
        small1(1, late)
        drain(8)
        small2(1, late)
        stage4(last)
        drain(99)
        small3(1, late)
        stage5(last)
        stage6(last)
        for c in range(2):
            put_first(c).wait()
        save(1).wait()
        save_out(seq // span - 1).wait()
        for peer in others(experts, me):
            give_back(peer).wait_send()
        for block in range(2):
            first_left(block).wait_send()
            first_right(block).wait_send()

        def finish(c, carry):
            copy1(c).wait_send()
            for peer in others(groups, my_dp):
                copy2(c, peer, my_dp).wait_send()
                copy4(c, peer, my_dp).wait_send()
            for peer in others(chips, place):
                copy3(c, peer, place).wait_send()
            copy5(c, core).wait_send()

            @pl.when(c >= 2)
            def _():
                for which in range(3):
                    put_pair(c, which).wait()

            return carry

        lax.fori_loop(0, pairs + 2, finish, 0)
        for part_idx, rows in ((0, early), (1, late)):
            for peer in others(experts, me):
                copy6(part_idx, rows, peer, me).wait_send()
            for peer in others(groups, my_dp):
                copy7(part_idx, rows, peer, my_dp).wait_send()


def back_pass(
    q, k, v, g, ctxt, wq, wk, wv, hot, gain, normed_low, tokens, grad_hidden, dwo, small,
    expert_out_grad, shared, expert_in_grad, weights, produced, hidden_rows, meta, groups, experts
):
    seq, width = q.shape
    pairs = width // 128
    chunks = pairs + 2
    hidden = expert_in_grad.shape[1]
    thick = width // 2
    half = width // 2
    piece = half // groups
    chips = experts // 2
    blk = pl.BlockSpec((seq, 128), lambda p: (0, p))
    hbm = pl.BlockSpec(memory_space=pl.ANY)
    fixed = lambda shape: pl.BlockSpec(shape, lambda p: (0,) * len(shape), pipeline_mode=pl.Buffered(1))
    dma = pltpu.SemaphoreType.DMA
    return pl.pallas_call(
        functools.partial(back_kernel, groups, experts, pairs),
        grid=(pairs,),
        in_specs=[
            blk, blk, blk, blk,
            pl.BlockSpec((128, seq), lambda p: (p, 0)),
            fixed((width, width)), fixed((width, width)), fixed((width, width)),
            fixed(hot.shape), fixed(gain.shape),
            hbm, hbm, hbm, hbm, hbm, hbm, hbm, hbm,
            hbm, hbm, hbm, fixed(meta.shape),
        ],
        out_specs=[hbm, fixed((seq, width)), fixed(small.shape), hbm, hbm],
        out_shape=[
            jax.ShapeDtypeStruct((4, width, width), bf16),
            jax.ShapeDtypeStruct((seq, width), f32),
            jax.ShapeDtypeStruct(small.shape, f32),
            jax.ShapeDtypeStruct((2, width // 4, hidden), bf16),
            jax.ShapeDtypeStruct((seq, width), bf16),
        ],
        scratch_shapes=[
            pltpu.VMEM((2, 128, 2 * seq), f32),
            pltpu.VMEM((2, seq, 128), bf16),
            pltpu.VMEM((2, 128, seq), bf16),
            pltpu.VMEM((2, seq, 128), bf16),
            pltpu.VMEM((2, seq, 128), bf16),
            pltpu.VMEM((128, seq), bf16),
            pltpu.VMEM((128, seq), f32),
            pltpu.VMEM((2, 2, 256, seq), bf16),
            pltpu.VMEM(produced.shape, bf16),
            pltpu.VMEM((256, width), f32),
            pltpu.VMEM((256, width), bf16),
            pltpu.VMEM((3, seq, width), bf16),
            pltpu.VMEM((width, seq), bf16),
            pltpu.VMEM((seq, width), bf16),
            pltpu.VMEM((chunks, width, thick), bf16),
            pltpu.VMEM((chunks, half, thick), bf16),
            pltpu.VMEM((chunks, groups, piece, thick), bf16),
            pltpu.VMEM((chunks, chips, piece, thick), bf16),
            pltpu.VMEM((chunks, width, thick), bf16),
            pltpu.VMEM(small.shape, f32),
            pltpu.VMEM((experts,) + small.shape, f32),
            pltpu.VMEM(small.shape, f32),
            pltpu.VMEM((groups,) + small.shape, f32),
            pltpu.VMEM((width, hidden // 2), bf16),
            pltpu.VMEM((2, width, hidden // 2), bf16),
            pltpu.VMEM((2, width // 4, hidden), bf16),
            dma((chunks,)), dma((chunks,)),
            dma((chunks, groups)), dma((chunks, groups)),
            dma((chunks, chips)), dma((chunks, chips)),
            dma((chunks, groups)), dma((chunks, groups)),
            dma((chunks,)), dma((chunks,)),
            dma((2, experts)), dma((2, experts)),
            dma((2, groups)), dma((2, groups)),
            dma((6,)),
            dma((2, 2)), dma((2, 2)),
            dma((2, 2)), dma((2, 2)),
            dma((chunks, 3)), dma((6,)),
            dma((2,)), dma((experts,)), dma((experts,)), dma((3,)),
        ],
        compiler_params=pltpu.CompilerParams(
            vmem_limit_bytes=62 << 20, collective_id=2, has_side_effects=True
        ),
        cost_estimate=pl.CostEstimate(
            flops=40 * seq * seq * width + 12 * seq * width * width,
            bytes_accessed=40 * seq * width, transcendentals=seq * seq * 12,
        ),
        name="attend_back",
    )(
        q, k, v, g, ctxt, wq, wk, wv, hot, gain, normed_low, tokens, grad_hidden, dwo, small,
        expert_out_grad, shared, expert_in_grad, weights, produced, hidden_rows, meta,
    )


def rms_backward(grad_norm, values, row_scale, gain_vec):
    weighted = grad_norm * gain_vec
    gain_grad = jnp.sum(grad_norm * values * row_scale, axis=0)
    grad_in = row_scale * weighted - values * row_scale**3 * jnp.mean(
        weighted * values, axis=-1, keepdims=True
    )
    return grad_in, gain_grad


def rms_forward(values, gain_vec):
    row_scale = lax.rsqrt(jnp.mean(values * values, axis=-1, keepdims=True) + epsilon)
    return values * row_scale * gain_vec, row_scale


def gelu_tanh(values):
    return jax.nn.gelu(values, approximate=True)


def contract(left, right, dims):
    return lax.dot_general(left, right, (((dims[0],), (dims[1],)), ((), ())), preferred_element_type=f32)


def exchange(rows, experts):
    slots, width = rows.shape
    rows = rows.reshape(experts, slots // experts, width)
    return lax.all_to_all(rows, "expert", split_axis=0, concat_axis=0, tiled=True).reshape(slots, width)


def expert_native(send, grad_recv, weight_in, weight_out, router_w, experts):
    received = exchange(send, experts)
    own = lax.axis_index("expert")
    own_hot = (jnp.arange(experts, dtype=jnp.int32) == own).astype(f32)[None, :]
    probs = jax.nn.softmax(contract(received, router_w, (1, 0)), axis=-1)
    gate = jnp.sum(probs * own_hot, axis=-1, keepdims=True)
    grad_recv_f = grad_recv.astype(f32)
    grad_produced = (grad_recv_f * gate).astype(bf16)
    preact = contract(received, weight_in, (1, 0))
    gelu_values, gelu_pullback = jax.vjp(gelu_tanh, preact)
    active = gelu_values.astype(bf16)
    produced = contract(active, weight_out, (1, 0)).astype(bf16)
    gate_grad = jnp.sum(grad_recv_f * produced.astype(f32), axis=-1, keepdims=True)
    logit_low = (gate_grad * gate * (own_hot - probs)).astype(bf16)
    grad_active = contract(grad_produced, weight_out, (1, 1))
    grad_preact = gelu_pullback(grad_active)[0].astype(bf16)
    grad_received = contract(grad_preact, weight_in, (1, 1)) + contract(logit_low, router_w, (1, 1))
    grad_rows = exchange(grad_received.astype(bf16), experts)
    in_grad = contract(received, grad_preact, (0, 0)).astype(bf16)
    out_grad_t = contract(grad_produced, active, (0, 0)).astype(bf16)
    router_grad = contract(received, logit_low, (0, 0))
    return grad_rows, produced, in_grad, out_grad_t, router_grad


def tail_native(tokens, gain, normed_low, dq, dk, dv, wq, wk, wv, grad_hidden, dwo, small):
    tokens_f = tokens.astype(f32)
    grads = jnp.stack([dwo.astype(f32)] + [contract(normed_low, d, (0, 0)) for d in (dq, dk, dv)])
    grad_normed = contract(dq, wq, (1, 1)) + contract(dk, wk, (1, 1)) + contract(dv, wv, (1, 1))
    _, scale = rms_forward(tokens_f, gain)
    grad_tokens, gain_grad = rms_backward(grad_normed, tokens_f, scale, gain)
    grads, gain_grad, small = lax.psum((grads, gain_grad, small), ("dp", "expert"))
    return grads, grad_hidden + grad_tokens, gain_grad, small


def on_device(
    tokens, gain_one, query_w, key_w, value_w, out_w, rel_table, gain_two, router_w,
    expert_in, expert_out, routes, buckets, cotangent,
):
    seq_len, width = tokens.shape
    heads = rel_table.shape[1]
    groups = lax.axis_size("dp")
    experts = lax.axis_size("expert")
    capacity = (5 * seq_len + 4 * experts - 1) // (4 * experts)
    slots = experts * capacity
    weight_in = expert_in[0]
    weight_out = expert_out[0]
    kernels = capacity % 16 == 0 and experts == 8 and groups == 4

    route_ids = routes[:, 0]
    route_hot = route_ids[:, None] == jnp.arange(experts, dtype=jnp.int32)[None, :]
    route_int = route_hot.astype(jnp.int32)
    route_float = route_hot.astype(f32)
    position = jnp.sum((jnp.cumsum(route_int, axis=0) - 1) * route_int, axis=1)
    slot_index = jnp.where(position < capacity, route_ids * capacity + position, slots)
    pick = (jnp.arange(slots, dtype=jnp.int32)[:, None] == slot_index[None, :]).astype(bf16)

    def scatter_rows(rows):
        return contract(pick, rows, (1, 0)).astype(bf16)

    def gather_rows(rows):
        return contract(pick, rows, (0, 0))

    tokens_f = tokens.astype(f32)
    if kernels:
        queries, key_rows, value_rows, normed_low, grad_send, slot_row, slot_column = first_pass(
            tokens, gain_one[None], query_w, key_w, value_w, routes.reshape(1, seq_len), cotangent, capacity, experts
        )
    else:
        grad_send = scatter_rows(cotangent)
        normed_low = rms_forward(tokens_f, gain_one)[0].astype(bf16)
        queries = contract(normed_low, query_w, (1, 0)).astype(bf16)
        key_rows = contract(normed_low, key_w, (1, 0)).astype(bf16)
        value_rows = contract(normed_low, value_w, (1, 0)).astype(bf16)
    reach = jnp.concatenate([buckets, jnp.full((1,), -1, jnp.int32)])[::-1]
    bucket_hot = (jnp.arange(rel_table.shape[0], dtype=jnp.int32)[:, None] == reach[None, :]).astype(f32)
    spread = jnp.einsum("bh,bx->hx", rel_table, bucket_hot, precision=highest)
    spread = spread.reshape(heads // 2, 2, 2 * seq_len)
    context, context_t, logsum, weights, grad_recv = attend(
        queries, key_rows, value_rows, spread, grad_send, experts if kernels else 0
    )
    if kernels:
        router_pad = jnp.pad(router_w, ((0, 0), (0, 128 - experts)))
        hidden, send, meta = middle_pass(
            tokens, context, out_w, gain_two[None], router_pad, slot_row, slot_column, slots, experts
        )
        grad_rows, produced, in_grad, out_grad_t, router_grad, shared = expert_pass(
            send, grad_recv, weight_in, weight_out, router_pad, experts, capacity
        )
        router_grad = router_grad[:, :experts]
        grad_hidden, out_w_grad, grad_context, gain_two_grad = combine_pass(
            grad_rows, hidden, cotangent, gain_two[None], context, out_w, meta
        )
    else:
        grad_recv = exchange(grad_send, experts)
        hidden = tokens_f + contract(context, out_w, (1, 0))
        normed_two, scale_two = rms_forward(hidden, gain_two)
        normed_two_low = normed_two.astype(bf16)
        grad_rows, produced, in_grad, out_grad_t, router_grad = expert_native(
            scatter_rows(normed_two_low), grad_recv, weight_in, weight_out, router_w, experts
        )
        router_probs = jax.nn.softmax(contract(normed_two_low, router_w, (1, 0)), axis=-1)
        gate_value = jnp.sum(router_probs * route_float, axis=-1, keepdims=True)
        grad_normed_two = gather_rows(grad_rows)
        grad_hidden_norm, gain_two_grad = rms_backward(grad_normed_two, hidden, scale_two, gain_two)
        grad_hidden = cotangent.astype(f32) + grad_hidden_norm
        branch_low = grad_hidden.astype(bf16)
        out_w_grad = contract(context, branch_low, (0, 0)).astype(bf16)
        grad_context = contract(branch_low, out_w, (1, 1)).astype(bf16)

    if kernels:
        small = jnp.concatenate(
            [
                jnp.zeros((8 + rel_table.shape[0], 128), f32),
                jnp.pad(gain_two_grad.reshape(-1, 128), ((0, 2), (0, 0))),
                router_grad.T.reshape(-1, 128),
            ]
        )
        grads, input_grad, small, shares, output = back_pass(
            queries, key_rows, value_rows, grad_context, context_t, query_w, key_w, value_w,
            bucket_hot, gain_one[None], normed_low, tokens, grad_hidden, out_w_grad, small,
            out_grad_t, shared, in_grad, weights, produced, hidden,
            meta, groups, experts,
        )
        tiles = width // 128
        first = 8 + rel_table.shape[0]
        gain_one_grad = small[:tiles].reshape(-1)
        rel_grad = small[8:first, :heads]
        gain_two_grad = small[first : first + tiles].reshape(-1)
        router_grad = small[first + 8 :].reshape(experts, width).T
        out_share, in_share = shares[0], shares[1]
    else:
        output = (hidden + gate_value * gather_rows(exchange(produced, experts))).astype(bf16)
        in_share = lax.psum_scatter(in_grad, "dp", scatter_dimension=0, tiled=True)
        out_share = lax.psum_scatter(out_grad_t, "dp", scatter_dimension=0, tiled=True)
        query_grad, key_grad, value_grad, diagonals = attend_back(
            queries, key_rows, value_rows, grad_context, spread, context_t, logsum
        )
        diagonals = diagonals[:, :2].reshape(heads, 2 * seq_len)
        rel_grad = jnp.einsum("bx,hx->bh", bucket_hot, diagonals, precision=highest)
        grads, input_grad, gain_one_grad, small = tail_native(
            tokens, gain_one, normed_low, query_grad, key_grad, value_grad,
            query_w, key_w, value_w, grad_hidden, out_w_grad, (rel_grad, gain_two_grad, router_grad),
        )
        rel_grad, gain_two_grad, router_grad = small
    grads = grads.astype(f32)
    return (
        output, input_grad, grads[1], grads[2], grads[3], grads[0], rel_grad,
        gain_one_grad, gain_two_grad, router_grad, in_share.astype(f32)[None], out_share.astype(f32).T[None],
    )


def solution(mesh):
    rows = P(("dp", "expert"), None)
    whole = P()
    split = P("expert", None, None)
    return jax.shard_map(
        on_device,
        mesh=mesh,
        in_specs=(
            rows, whole, whole, whole, whole, whole, whole, whole, whole, split, split, rows, whole, rows,
        ),
        out_specs=(
            rows, rows, whole, whole, whole, whole, whole, whole, whole, whole,
            P("expert", "dp", None), P("expert", None, "dp"),
        ),
        check_vma=False,
    )
```

```python
import functools

import jax
import jax.numpy as jnp
from jax import lax
from jax.experimental import pallas as pl
from jax.experimental.pallas import tpu as pltpu
from jax.sharding import PartitionSpec as P

bf16 = jnp.bfloat16
f32 = jnp.float32
epsilon = 1e-06
highest = lax.Precision.HIGHEST

def dot_f32(left, right):
    return lax.dot_general(left, right, (((1,), (0,)), ((), ())), preferred_element_type=f32)


def dot_nt(left, right):
    return lax.dot_general(left, right, (((1,), (1,)), ((), ())), preferred_element_type=f32)


def fill_toeplitz(base_ref, head, row):
    rows, width = base_ref.shape[1:]
    spread = jnp.broadcast_to(row, (8, width))
    eight = pltpu.roll(spread, 0, 1, stride=1, stride_axis=0)
    for group in range(rows // 8):
        base_ref[head, 8 * group : 8 * group + 8, :] = (
            eight if group == 0 else pltpu.roll(eight, 8 * group, 1)
        )


def attend_kernel(
    experts, q_ref, k_ref, v_ref, u_ref, gsend_h, ctx_ref, ctxt_ref, lse_ref, p_h, grecv_h,
    base, qt, vt, s_scr, p_scr, p_sem, send_g, recv_g, own_sem,
):
    seq = q_ref.shape[0]
    span = 256
    half = seq
    qt[...] = q_ref[...].T
    vt[...] = v_ref[...].T
    for head in range(2):
        fill_toeplitz(base, head, u_ref[0, head : head + 1, :])
    zeros = jnp.zeros((64, span), bf16)
    pair = pl.program_id(0)

    if experts:
        me = lax.axis_index("expert")
        count = grecv_h.shape[0] // experts
        rows_of = lambda who: pl.ds(pl.multiple_of(who * count, 16), count)
        peers = [lax.rem(me + k, experts) for k in range(1, experts)]
        barrier = pltpu.get_barrier_semaphore()
        own = pltpu.make_async_copy(gsend_h.at[rows_of(me), :], grecv_h.at[rows_of(me), :], own_sem)

        def give(peer, slot):
            return pltpu.make_async_remote_copy(
                src_ref=gsend_h.at[rows_of(peer), :], dst_ref=grecv_h.at[rows_of(slot), :],
                send_sem=send_g.at[peer], recv_sem=recv_g.at[slot], device_id={"expert": peer},
            )

        @pl.when(pair == 0)
        def _():
            for peer in peers:
                pl.semaphore_signal(barrier, inc=1, device_id={"expert": peer})
            own.start()

    def save(idx, slot):
        cols = pl.ds(pl.multiple_of(idx * span, span), span)
        return pltpu.make_async_copy(p_scr.at[slot], p_h.at[pl.ds(2 * pair, 2), :, cols], p_sem.at[slot])

    def step(idx, carry):
        slot = lax.rem(idx, 2)

        @pl.when((pair > 0) | (idx > 1))
        def _():
            save(idx, slot).wait()

        cols = pl.ds(pl.multiple_of(idx * span, span), span)
        outs = []
        for head in range(2):
            part = qt[64 * head : 64 * head + 64, cols]
            rhs = jnp.concatenate([part, zeros] if head == 0 else [zeros, part], axis=0)
            peak = None
            for kb in range(seq // 128):
                rows = slice(128 * kb, 128 * kb + 128)
                offs = pl.multiple_of(half + span * idx - 128 * kb, 128)
                s = dot_f32(k_ref[rows, :], rhs) + base[head, :, pl.ds(offs, span)]
                s_scr[head, rows, :] = s
                now = jnp.max(s.reshape(16, 8, span), axis=0)
                peak = now if peak is None else jnp.maximum(peak, now)
            peak = jnp.max(peak, axis=0, keepdims=True)
            total = None
            for kb in range(seq // 128):
                rows = slice(128 * kb, 128 * kb + 128)
                e = jnp.exp(s_scr[head, rows, :] - peak)
                s_scr[head, rows, :] = e
                now = jnp.sum(e.reshape(16, 8, span), axis=0)
                total = now if total is None else total + now
            total = jnp.sum(total, axis=0, keepdims=True)
            inv = 1.0 / total
            for kb in range(seq // 128):
                rows = slice(128 * kb, 128 * kb + 128)
                p_scr[slot, head, rows, :] = (s_scr[head, rows, :] * inv).astype(bf16)
            lse_ref[0, head : head + 1, cols] = peak + jnp.log(total)
            outs.append(dot_f32(vt[64 * head : 64 * head + 64, :], p_scr[slot, head]))
        save(idx, slot).start()
        both = jnp.concatenate(outs, axis=0)
        ctxt_ref[:, cols] = both
        ctx_ref[cols, :] = both.T.astype(bf16)
        return carry

    if experts:
        @pl.when(pair == 0)
        def _():
            pl.semaphore_wait(barrier, experts - 1)
            for peer in peers:
                give(peer, me).start()

    lax.fori_loop(0, seq // span, step, 0)

    @pl.when(pair == pl.num_programs(0) - 1)
    def _():
        for slot in range(2):
            save(slot, slot).wait()
        if experts:
            own.wait()
            for peer in peers:
                give(peer, me).wait_send()
                give(peer, peer).wait_recv()


def attend(q, k, v, u, gsend, experts=0):
    seq, width = q.shape
    pairs = width // 128
    blk = pl.BlockSpec((seq, 128), lambda p: (0, p))
    dma = pltpu.SemaphoreType.DMA
    return pl.pallas_call(
        functools.partial(attend_kernel, experts),
        grid=(pairs,),
        in_specs=[
            blk, blk, blk, pl.BlockSpec((1, 2, 2 * seq), lambda p: (p, 0, 0)), pl.BlockSpec(memory_space=pl.ANY),
        ],
        out_specs=[
            blk,
            pl.BlockSpec((128, seq), lambda p: (p, 0)),
            pl.BlockSpec((1, 8, seq), lambda p: (p, 0, 0)),
            pl.BlockSpec(memory_space=pl.ANY),
            pl.BlockSpec(memory_space=pl.ANY),
        ],
        out_shape=[
            jax.ShapeDtypeStruct((seq, width), bf16),
            jax.ShapeDtypeStruct((width, seq), f32),
            jax.ShapeDtypeStruct((pairs, 8, seq), f32),
            jax.ShapeDtypeStruct((2 * pairs, seq, seq), bf16),
            jax.ShapeDtypeStruct(gsend.shape, bf16),
        ],
        scratch_shapes=[
            pltpu.VMEM((2, 128, 2 * seq), f32),
            pltpu.VMEM((128, seq), bf16),
            pltpu.VMEM((128, seq), bf16),
            pltpu.VMEM((2, seq, 256), f32),
            pltpu.VMEM((2, 2, seq, 256), bf16),
            dma((2,)),
            dma((max(experts, 1),)), dma((max(experts, 1),)), dma(()),
        ],
        compiler_params=pltpu.CompilerParams(
            vmem_limit_bytes=62 << 20, has_side_effects=experts > 0, collective_id=3 if experts else None
        ),
        name="attend",
    )(q, k, v, u, gsend)


def first_kernel(
    capacity, experts, tok, gain, wq, wk, wv, route, cot, q_o, k_o, v_o, nl_o, gsend_o, slot_o, column_o, slot
):
    step = pl.program_id(0)
    slots = experts * capacity
    seq = route.shape[1]

    @pl.when(step == 0)
    def _():
        lane = lax.broadcasted_iota(jnp.int32, (8, seq), 1)
        hot = jnp.where(lax.broadcasted_iota(jnp.int32, (8, seq), 0) == route[...], 1.0, 0.0)
        count = hot
        shift = 1
        while shift < seq:
            count = count + jnp.where(lane >= shift, pltpu.roll(count, shift, 1), 0.0)
            shift *= 2
        position = jnp.sum(hot * (count - 1.0), axis=0, keepdims=True)
        place = route[...].astype(f32) * capacity + position
        slot[...] = jnp.where(position < capacity, place, float(slots))
        slot_o[...] = slot[...]
        column_o[...] = jnp.broadcast_to(slot[...], (128, seq)).T

    values = tok[...].astype(f32)
    scale = lax.rsqrt(jnp.mean(values * values, axis=-1, keepdims=True) + epsilon)
    normed = (values * scale * gain[0:1, :]).astype(bf16)
    nl_o[...] = normed
    for weight, out in ((wq, q_o), (wk, k_o), (wv, v_o)):
        out[...] = dot_f32(normed, weight[...]).astype(bf16)
    rows = gsend_o.shape[0]
    number = lax.broadcasted_iota(jnp.int32, (rows, seq), 0) + step * rows
    pick = jnp.where(number.astype(f32) == slot[...], 1.0, 0.0).astype(bf16)
    gsend_o[...] = dot_f32(pick, cot[...]).astype(bf16)


def first_pass(tokens, gain, wq, wk, wv, route, cotangent, capacity, experts):
    seq, width = tokens.shape
    slots = experts * capacity
    steps = 4
    rows = pl.BlockSpec((seq // steps, width), lambda i: (i, 0))
    fixed = lambda shape: pl.BlockSpec(shape, lambda i: (0, 0))
    return pl.pallas_call(
        functools.partial(first_kernel, capacity, experts),
        grid=(steps,),
        in_specs=[rows, fixed(gain.shape)] + [fixed(wq.shape)] * 3 + [fixed(route.shape), fixed(cotangent.shape)],
        out_specs=[rows] * 4 + [pl.BlockSpec((slots // steps, width), lambda i: (i, 0)), fixed(route.shape), fixed((seq, 128))],
        out_shape=[jax.ShapeDtypeStruct((seq, width), bf16)] * 4
        + [jax.ShapeDtypeStruct((slots, width), bf16), jax.ShapeDtypeStruct(route.shape, f32),
           jax.ShapeDtypeStruct((seq, 128), f32)],
        scratch_shapes=[pltpu.VMEM(route.shape, f32)],
        compiler_params=pltpu.CompilerParams(vmem_limit_bytes=62 << 20),
        cost_estimate=pl.CostEstimate(
            flops=6 * seq * width * width + 2 * slots * seq * width, bytes_accessed=20 * seq * width, transcendentals=seq
        ),
        name="first",
    )(tokens, gain, wq, wk, wv, route, cotangent)


def middle_kernel(experts, steps, tok, ctx, wo, gain, rw, slot, column, hid_o, xs_o, meta_o, normed):
    step = pl.program_id(0)
    span, width = tok.shape
    seq = normed.shape[0]

    @pl.when(step < steps)
    def _():
        hidden = tok[...].astype(f32) + dot_f32(ctx[...], wo[...])
        hid_o[...] = hidden
        scale = lax.rsqrt(jnp.mean(hidden * hidden, axis=-1, keepdims=True) + epsilon)
        low = (hidden * scale * gain[1:2, :]).astype(bf16)
        normed[pl.ds(pl.multiple_of(step * span, span), span), :] = low
        lane = lax.broadcasted_iota(jnp.int32, (span, 128), 1)
        logits = jnp.where(lane < experts, dot_f32(low, rw[...]), -1e30)
        weights = jnp.exp(logits - jnp.max(logits, axis=-1, keepdims=True))
        place = column[...]
        each = xs_o.shape[0] * (pl.num_programs(0) - steps) // experts
        first = (lane * each).astype(f32)
        chosen = (place >= first) & (place < first + each) & (lane < experts)
        gate = jnp.sum(jnp.where(chosen, weights, 0.0), axis=-1, keepdims=True) / jnp.sum(
            weights, axis=-1, keepdims=True
        )
        meta_o[...] = jnp.where(lane == 0, gate, place)

    @pl.when(step >= steps)
    def _():
        rows = xs_o.shape[0]
        number = lax.broadcasted_iota(jnp.int32, (rows, seq), 0) + (step - steps) * rows
        pick = jnp.where(number.astype(f32) == slot[...], 1.0, 0.0).astype(bf16)
        xs_o[...] = dot_f32(pick, normed[...]).astype(bf16)


def middle_pass(tokens, ctx, wo, gain, rw, slot, column, slots, experts):
    seq, width = tokens.shape
    steps = 4
    span = seq // steps
    each = slots // steps
    token_map = lambda i: (jnp.minimum(i, steps - 1), 0)
    fixed = lambda shape: pl.BlockSpec(shape, lambda i: (0, 0))
    return pl.pallas_call(
        functools.partial(middle_kernel, experts, steps),
        grid=(2 * steps,),
        in_specs=[
            pl.BlockSpec((span, width), token_map), pl.BlockSpec((span, width), token_map), fixed(wo.shape),
            fixed(gain.shape), fixed(rw.shape), fixed(slot.shape), pl.BlockSpec((span, 128), token_map),
        ],
        out_specs=[
            pl.BlockSpec((span, width), token_map),
            pl.BlockSpec((each, width), lambda i: (jnp.maximum(i - steps, 0), 0)),
            pl.BlockSpec((span, 128), token_map),
        ],
        out_shape=[
            jax.ShapeDtypeStruct((seq, width), f32),
            jax.ShapeDtypeStruct((slots, width), bf16),
            jax.ShapeDtypeStruct((seq, 128), f32),
        ],
        scratch_shapes=[pltpu.VMEM((seq, width), bf16)],
        compiler_params=pltpu.CompilerParams(vmem_limit_bytes=62 << 20),
        cost_estimate=pl.CostEstimate(
            flops=2 * seq * width * width + 2 * slots * seq * width, bytes_accessed=10 * seq * width, transcendentals=seq
        ),
        name="middle",
    )(tokens, ctx, wo, gain, rw, slot, column)


def combine_kernel(gback, hid, cot, gain, ctx, wo, meta, ghid_o, dwo_o, gctx_o, gain_o, total_w):
    step = pl.program_id(0)
    span = hid.shape[0]
    slots = gback.shape[0]
    where = lax.broadcasted_iota(jnp.int32, (span, slots), 1).astype(f32)
    pick = jnp.where(meta[:, 1:2] == where, 1.0, 0.0).astype(bf16)
    grad = dot_f32(pick, gback[...])
    values = hid[...]
    scale = lax.rsqrt(jnp.mean(values * values, axis=-1, keepdims=True) + epsilon)
    weighted = grad * gain[1:2, :]
    inner = jnp.mean(weighted * values, axis=-1, keepdims=True)
    total = cot[...].astype(f32) + scale * weighted - values * (scale * scale * scale * inner)
    ghid_o[...] = total
    branch = total.astype(bf16)
    gctx_o[...] = dot_nt(branch, wo[...]).astype(bf16)
    gains = jnp.sum(grad * values * scale, axis=0, keepdims=True)
    now = dot_f32(ctx[...].T, branch)

    @pl.when(step == 0)
    def _():
        total_w[...] = now
        gain_o[...] = gains

    @pl.when(step > 0)
    def _():
        total_w[...] += now
        gain_o[...] += gains

    @pl.when(step == pl.num_programs(0) - 1)
    def _():
        dwo_o[...] = total_w[...].astype(bf16)


def combine_pass(gback, hidden, cotangent, gain, ctx, wo, meta):
    seq, width = hidden.shape
    steps = 4
    rows = pl.BlockSpec((seq // steps, width), lambda i: (i, 0))
    fixed = lambda shape: pl.BlockSpec(shape, lambda i: (0, 0))
    return pl.pallas_call(
        combine_kernel,
        grid=(steps,),
        in_specs=[
            fixed(gback.shape), rows, rows, fixed(gain.shape), rows, fixed(wo.shape),
            pl.BlockSpec((seq // steps, 128), lambda i: (i, 0)),
        ],
        out_specs=[rows, fixed((width, width)), rows, fixed((1, width))],
        out_shape=[
            jax.ShapeDtypeStruct((seq, width), f32),
            jax.ShapeDtypeStruct((width, width), bf16),
            jax.ShapeDtypeStruct((seq, width), bf16),
            jax.ShapeDtypeStruct((1, width), f32),
        ],
        scratch_shapes=[pltpu.VMEM((width, width), f32)],
        compiler_params=pltpu.CompilerParams(vmem_limit_bytes=62 << 20),
        cost_estimate=pl.CostEstimate(
            flops=4 * seq * width * width + 2 * gback.shape[0] * seq * width,
            bytes_accessed=16 * seq * width, transcendentals=seq,
        ),
        name="combine",
    )(gback, hidden, cotangent, gain, ctx, wo, meta)


def split_rows(row):
    hi = row.astype(bf16).astype(f32)
    mid = (row - hi).astype(bf16).astype(f32)
    low = row - hi - mid
    idx = lax.broadcasted_iota(jnp.int32, (16, row.shape[1]), 0)
    return jnp.where(idx == 0, hi, jnp.where(idx == 1, mid, jnp.where(idx == 2, low, 0.0))).astype(bf16)


def attend_back_kernel(
    q_ref, k_ref, v_ref, g_ref, u_ref, ctxt_ref, lse_ref,
    dq_ref, dk_ref, dv_ref, diag_ref,
    base, acc, kaug, vaug, qaug, gaug, qz, gz, kt, dqt,
):
    seq = q_ref.shape[0]
    span = 256
    lane = lax.broadcasted_iota(jnp.int32, (seq, 128), 1)
    gt = g_ref[...].T
    qtv = q_ref[...].T
    kt[...] = k_ref[...].T
    gtf = gt.astype(f32)
    pad = jnp.zeros((48, seq), bf16)
    one = jnp.ones((seq, 128), bf16)
    nil = jnp.zeros((seq, 128), bf16)
    acc[...] = jnp.zeros_like(acc)
    for head in range(2):
        fill_toeplitz(base, head, u_ref[0, head : head + 1, :])
        own = (lane < 64) if head == 0 else (lane >= 64)
        origin = 64 if head == 0 else 0
        extra = jnp.where((lane >= origin) & (lane < origin + 3), one, nil)
        kaug[head] = jnp.where(own, k_ref[...], extra)
        vaug[head] = jnp.where(own, v_ref[...], extra)
        qz[head] = jnp.where(own, q_ref[...], nil)
        gz[head] = jnp.where(own, g_ref[...], nil)
        rows = slice(64 * head, 64 * head + 64)
        lse = split_rows(-lse_ref[0, head : head + 1, :])
        dsum = split_rows(-jnp.sum(gtf[rows] * ctxt_ref[rows, :], axis=0, keepdims=True))
        for dst, src, aug in ((qaug, qtv, lse), (gaug, gt, dsum)):
            dst[head, rows, :] = src[rows]
            dst[head, origin : origin + 16, :] = aug
            dst[head, origin + 16 : origin + 64, :] = pad

    dqt[...] = jnp.zeros_like(dqt)

    def step(idx, carry):
        rows = pl.ds(pl.multiple_of(idx * span, span), span)
        dv = None
        dk = None
        for head in range(2):
            s = dot_f32(kaug[head, rows, :], qaug[head])
            dp = dot_f32(vaug[head, rows, :], gaug[head])
            tops = []
            grads = []
            for part in range(2):
                offs = pl.ds(pl.multiple_of(seq - span * idx - 128 * part, 128), seq)
                p = jnp.exp(s[128 * part : 128 * part + 128] + base[head, :, offs])
                ds_ = p * dp[128 * part : 128 * part + 128]
                acc[head, :, offs] += ds_
                tops.append(p.astype(bf16))
                grads.append(ds_.astype(bf16))
            p = jnp.concatenate(tops, axis=0)
            ds_ = jnp.concatenate(grads, axis=0)
            now = dot_f32(p, gz[head])
            dv = now if dv is None else dv + now
            now = dot_f32(ds_, qz[head])
            dk = now if dk is None else dk + now
            dqt[64 * head : 64 * head + 64, :] += dot_f32(kt[64 * head : 64 * head + 64, rows], ds_)
        dv_ref[rows, :] = dv.astype(bf16)
        dk_ref[rows, :] = dk.astype(bf16)
        return carry

    lax.fori_loop(0, seq // span, step, 0)
    dq_ref[...] = dqt[...].T.astype(bf16)
    width = 2 * seq
    for head in range(2):
        total = acc[head, 0:8, :]
        for group in range(1, 16):
            total = total + pltpu.roll(acc[head, 8 * group : 8 * group + 8, :], width - 8 * group, 1)
        sub = lax.broadcasted_iota(jnp.int32, (8, width), 0)
        for bit in (1, 2, 4):
            total = jnp.where((sub & bit) != 0, pltpu.roll(total, width - bit, 1), total)
        diag_ref[0, head : head + 1, :] = jnp.sum(total, axis=0, keepdims=True)


def attend_back(q, k, v, g, u, ctxt, lse):
    seq, width = q.shape
    pairs = width // 128
    blk = pl.BlockSpec((seq, 128), lambda p: (0, p))
    return pl.pallas_call(
        attend_back_kernel,
        grid=(pairs,),
        in_specs=[
            blk, blk, blk, blk,
            pl.BlockSpec((1, 2, 2 * seq), lambda p: (p, 0, 0)),
            pl.BlockSpec((128, seq), lambda p: (p, 0)),
            pl.BlockSpec((1, 8, seq), lambda p: (p, 0, 0)),
        ],
        out_specs=[blk, blk, blk, pl.BlockSpec((1, 8, 2 * seq), lambda p: (p, 0, 0))],
        out_shape=[jax.ShapeDtypeStruct((seq, width), bf16)] * 3
        + [jax.ShapeDtypeStruct((pairs, 8, 2 * seq), f32)],
        scratch_shapes=[
            pltpu.VMEM((2, 128, 2 * seq), f32),
            pltpu.VMEM((2, 128, 2 * seq), f32),
            pltpu.VMEM((2, seq, 128), bf16),
            pltpu.VMEM((2, seq, 128), bf16),
            pltpu.VMEM((2, 128, seq), bf16),
            pltpu.VMEM((2, 128, seq), bf16),
            pltpu.VMEM((2, seq, 128), bf16),
            pltpu.VMEM((2, seq, 128), bf16),
            pltpu.VMEM((128, seq), bf16),
            pltpu.VMEM((128, seq), f32),
        ],
        compiler_params=pltpu.CompilerParams(vmem_limit_bytes=56 << 20),
        cost_estimate=pl.CostEstimate(
            flops=40 * seq * seq * width, bytes_accessed=20 * seq * width, transcendentals=seq * seq * 12
        ),
        name="attend_back",
    )(q, k, v, g, u, ctxt, lse)


def gelu_both(v):
    scale = 0.7978845608028654
    square = v * v
    t = jnp.tanh(scale * v * (1.0 + 0.044715 * square))
    half = 0.5 * (1.0 + t)
    slope = half + 0.5 * v * (1.0 - t * t) * (scale * (1.0 + 3 * 0.044715 * square))
    return v * half, slope


def expert_kernel(
    experts, capacity, tile,
    xs, gr_h, win_h, wout_h, rw,
    gback_o, prod_o, dwin_o, dwout_o, drw_o, shared_o,
    xall, gr, gp, win, wout, act, gpre, gback, gsend, prod, logit, acc_p, acc_g, xt, gpt, stage, dwt,
    send_x, recv_x, send_g, recv_g, local, out_sem, send_s, recv_s,
):
    me = lax.axis_index("expert")
    place = me // 2
    chips = experts // 2
    span = 2 * capacity
    width = xall.shape[1]
    hidden = win.shape[1]
    barrier = pltpu.get_barrier_semaphore()
    for k in range(1, experts):
        pl.semaphore_signal(barrier, inc=1, device_id={"expert": lax.rem(me + k, experts)})
    my_dp = lax.axis_index("dp")
    dp_x, dp_y = lax.rem(my_dp, 2), my_dp // 2
    peer_x, peer_y = my_dp + 1 - 2 * dp_x, my_dp + 2 - 4 * dp_y
    for peer in (peer_x, peer_y):
        pl.semaphore_signal(barrier, inc=1, device_id={"dp": peer})
    loads = [
        pltpu.make_async_copy(win_h, win, local.at[0]),
        pltpu.make_async_copy(wout_h, wout, local.at[1]),
        pltpu.make_async_copy(gr_h, gr, local.at[2]),
    ]
    rows_of = lambda who: pl.ds(pl.multiple_of(who * capacity, 16), capacity)
    own = pltpu.make_async_copy(xs.at[rows_of(me), :], xall.at[rows_of(me), :], local.at[3])
    own.start()
    for copy in loads:
        copy.start()
    pl.semaphore_wait(barrier, experts + 1)

    def partner(step):
        high, low = place // 2, lax.rem(place, 2)
        fhigh, flow = step // 2, lax.rem(step, 2)
        return 2 * (high + fhigh - 2 * high * fhigh) + low + flow - 2 * low * flow

    def send_rows(peer):
        return pltpu.make_async_remote_copy(
            src_ref=xs.at[rows_of(peer), :], dst_ref=xall.at[rows_of(me), :],
            send_sem=send_x.at[peer], recv_sem=recv_x.at[me], device_id={"expert": peer},
        )

    def got_rows(peer):
        return pltpu.make_async_remote_copy(
            src_ref=xs.at[rows_of(peer), :], dst_ref=xall.at[rows_of(peer), :],
            send_sem=send_x.at[peer], recv_sem=recv_x.at[peer], device_id={"expert": peer},
        )

    def send_back(peer):
        return pltpu.make_async_remote_copy(
            src_ref=gsend.at[rows_of(peer), :], dst_ref=gback.at[rows_of(me), :],
            send_sem=send_g.at[peer], recv_sem=recv_g.at[me], device_id={"expert": peer},
        )

    def got_back(peer):
        return pltpu.make_async_remote_copy(
            src_ref=gsend.at[rows_of(peer), :], dst_ref=gback.at[rows_of(peer), :],
            send_sem=send_g.at[peer], recv_sem=recv_g.at[peer], device_id={"expert": peer},
        )

    sibling = me + 1 - 2 * lax.rem(me, 2)
    send_rows(sibling).start()
    for step in range(1, chips):
        for core in range(2):
            send_rows(2 * partner(step) + lax.rem(me + core, 2)).start()
    for copy in loads:
        copy.wait()

    lanes = lax.broadcasted_iota(jnp.int32, (span, rw.shape[1]), 1)
    mine = jnp.where(lanes == me, 1.0, 0.0)

    def work(step, carry):
        where = partner(step)
        base = pl.multiple_of(where * span, 32)

        @pl.when(step == 0)
        def _():
            own.wait()
            got_rows(sibling).wait_recv()

        @pl.when(step > 0)
        def _():
            got_rows(2 * where).wait_recv()
            got_rows(2 * where + 1).wait_recv()

        rows = pl.ds(base, span)
        x = xall[rows, :]
        logits = jnp.where(lanes < experts, dot_f32(x, rw[...]), -1e30)
        weights = jnp.exp(logits - jnp.max(logits, axis=-1, keepdims=True))
        probs = weights / jnp.sum(weights, axis=-1, keepdims=True)
        gate = jnp.sum(probs * mine, axis=-1, keepdims=True)
        gp[rows, :] = (gr[rows, :].astype(f32) * gate).astype(bf16)
        acc_p[...] = jnp.zeros_like(acc_p)
        acc_g[...] = jnp.zeros_like(acc_g)

        def block(idx, carry):
            cols = pl.ds(pl.multiple_of(idx * tile, tile), tile)
            h = dot_f32(xall[rows, :], win[:, cols])
            grad = dot_nt(gp[rows, :], wout[cols, :])
            value, slope = gelu_both(h)
            value = value.astype(bf16)
            grad = (grad * slope).astype(bf16)
            act[rows, cols] = value
            gpre[rows, cols] = grad
            acc_p[...] += dot_f32(value, wout[cols, :])
            acc_g[...] += dot_nt(grad, win[:, cols])
            return carry

        lax.fori_loop(0, hidden // tile, block, 0)
        made = acc_p[...].astype(bf16)
        prod[rows, :] = made
        gate_grad = jnp.sum(gr[rows, :].astype(f32) * made.astype(f32), axis=-1, keepdims=True)
        low = (gate_grad * gate * (mine - probs)).astype(bf16)
        low = jnp.where(lanes < experts, low, jnp.zeros_like(low))
        logit[rows, :] = low
        gsend[rows, :] = (acc_g[...] + dot_nt(low, rw[...])).astype(bf16)

        @pl.when(step == 0)
        def _():
            send_back(sibling).start()

        @pl.when(step > 0)
        def _():
            send_back(2 * where).start()
            send_back(2 * where + 1).start()

        return carry

    lax.fori_loop(0, chips, work, 0)
    outs = [
        pltpu.make_async_copy(prod, prod_o, local.at[0]),
        pltpu.make_async_copy(gsend.at[rows_of(me), :], gback.at[rows_of(me), :], local.at[3]),
    ]
    for copy in outs:
        copy.start()
    xt[...] = xall[...].T
    gpt[...] = gp[...].T
    drw_o[...] = dot_f32(xt[...], logit[...])

    share = width // 4
    tiles = hidden // tile
    split = tiles // 2

    def left_copy(idx, block):
        cols = pl.ds(pl.multiple_of(idx * tile, tile), tile)
        rows = pl.ds(pl.multiple_of((1 - dp_x + 2 * block) * share, 16), share)
        return pltpu.make_async_remote_copy(
            src_ref=dwt.at[rows, cols], dst_ref=shared_o.at[pl.ds(block * share, share), cols],
            send_sem=send_s.at[block, idx], recv_sem=recv_s.at[block, idx], device_id={"dp": peer_x},
        )

    def right_copy(idx, block):
        cols = pl.ds(pl.multiple_of(idx * tile, tile), tile)
        rows = pl.ds(pl.multiple_of((2 - 2 * dp_y + block) * share, 16), share)
        dst_cols = pl.ds(pl.multiple_of((idx - split) * tile, tile), tile)
        return pltpu.make_async_remote_copy(
            src_ref=dwt.at[rows, cols], dst_ref=shared_o.at[pl.ds((2 + block) * share, share), dst_cols],
            send_sem=send_s.at[block, idx], recv_sem=recv_s.at[block, idx], device_id={"dp": peer_y},
        )

    def out_block(step, carry):
        idx = lax.rem(step, 2) * split + step // 2
        cols = pl.ds(pl.multiple_of(idx * tile, tile), tile)
        dwt[:, cols] = dot_f32(gpt[...], act[:, cols]).astype(bf16)

        @pl.when(idx < split)
        def _():
            for block in range(2):
                left_copy(idx, block).start()

        @pl.when(idx >= split)
        def _():
            for block in range(2):
                right_copy(idx, block).start()

        return carry

    lax.fori_loop(0, tiles, out_block, 0)
    whole = pltpu.make_async_copy(dwt, dwout_o, local.at[2])
    whole.start()

    def put(slot, cols):
        return pltpu.make_async_copy(stage.at[slot], dwin_o.at[:, cols], out_sem.at[slot])

    def in_block(idx, carry):
        cols = pl.ds(pl.multiple_of(idx * tile, tile), tile)
        slot = lax.rem(idx, 2)

        @pl.when(idx > 1)
        def _():
            put(slot, cols).wait()

        stage[slot] = dot_f32(xt[...], gpre[:, cols]).astype(bf16)
        put(slot, cols).start()
        return carry

    lax.fori_loop(0, tiles, in_block, 0)
    for slot in range(2):
        put(slot, pl.ds(0, tile)).wait()
    whole.wait()
    for copy in outs:
        copy.wait()
    for k in range(1, experts):
        peer = lax.rem(me + k, experts)
        got_rows(peer).wait_send()
        got_back(peer).wait_send()
        got_back(peer).wait_recv()
    back = pltpu.make_async_copy(gback, gback_o, local.at[1])
    back.start()
    for idx in range(tiles):
        for block in range(2):
            (left_copy if idx < split else right_copy)(idx, block).wait()
    back.wait()


def expert_pass(xs, gr, weight_in, weight_out, router_pad, experts, capacity):
    slots, width = xs.shape
    hidden = weight_in.shape[1]
    tile = 512
    span = 2 * capacity
    hbm = pl.BlockSpec(memory_space=pl.ANY)
    vmem = pl.BlockSpec(memory_space=pltpu.VMEM)
    return pl.pallas_call(
        functools.partial(expert_kernel, experts, capacity, tile),
        in_specs=[hbm, hbm, hbm, hbm, vmem],
        out_specs=[hbm, hbm, hbm, hbm, vmem, hbm],
        out_shape=[
            jax.ShapeDtypeStruct((slots, width), bf16),
            jax.ShapeDtypeStruct((slots, width), bf16),
            jax.ShapeDtypeStruct((width, hidden), bf16),
            jax.ShapeDtypeStruct((width, hidden), bf16),
            jax.ShapeDtypeStruct((width, router_pad.shape[1]), f32),
            jax.ShapeDtypeStruct((width, hidden // 2), bf16),
        ],
        scratch_shapes=[
            pltpu.VMEM((slots, width), bf16),
            pltpu.VMEM((slots, width), bf16),
            pltpu.VMEM((slots, width), bf16),
            pltpu.VMEM((width, hidden), bf16),
            pltpu.VMEM((hidden, width), bf16),
            pltpu.VMEM((slots, hidden), bf16),
            pltpu.VMEM((slots, hidden), bf16),
            pltpu.VMEM((slots, width), bf16),
            pltpu.VMEM((slots, width), bf16),
            pltpu.VMEM((slots, width), bf16),
            pltpu.VMEM((slots, router_pad.shape[1]), bf16),
            pltpu.VMEM((span, width), f32),
            pltpu.VMEM((span, width), f32),
            pltpu.VMEM((width, slots), bf16),
            pltpu.VMEM((width, slots), bf16),
            pltpu.VMEM((2, width, tile), bf16),
            pltpu.VMEM((width, hidden), bf16),
            pltpu.SemaphoreType.DMA((experts,)),
            pltpu.SemaphoreType.DMA((experts,)),
            pltpu.SemaphoreType.DMA((experts,)),
            pltpu.SemaphoreType.DMA((experts,)),
            pltpu.SemaphoreType.DMA((4,)),
            pltpu.SemaphoreType.DMA((2,)),
            pltpu.SemaphoreType.DMA((2, hidden // tile)),
            pltpu.SemaphoreType.DMA((2, hidden // tile)),
        ],
        compiler_params=pltpu.CompilerParams(
            vmem_limit_bytes=60 << 20, collective_id=1, has_side_effects=True
        ),
        cost_estimate=pl.CostEstimate(
            flops=12 * slots * width * hidden, bytes_accessed=8 * width * hidden, transcendentals=slots * hidden
        ),
        name="experts",
    )(xs, gr, weight_in, weight_out, router_pad)


def remote(src, dst, send_sem, recv_sem, axis, peer):
    return pltpu.make_async_remote_copy(
        src_ref=src, dst_ref=dst, send_sem=send_sem, recv_sem=recv_sem, device_id={axis: peer}
    )


def others(count, mine):
    return [lax.rem(mine + k, count) for k in range(1, count)]


PLAN = (
    (11, 16, 19, 22, 24),
    (12, 17, 20, 23, 25),
    (5, 13, 16, 19, 21),
    (9, 15, 18, 21, 23),
    (13, 18, 21, 24, 26),
    (17, 21, 24, 27, 29),
    (21, 24, 27, 29, 31),
)
OUTPUT_SLOT = 17
EXPERT_SLOTS = ((6, 2, 0), (14, 3, 0), (15, 2, 1), (22, 3, 1))


def back_kernel(
    groups, experts, pairs,
    q_ref, k_ref, v_ref, g_ref, ctxt_ref, wq, wk, wv, hot, gain, nl_h, tok_h, ghid_h, dwo_h, small_h,
    eout_h, shared_h, ein_h, p_h, prod_h, hid_h, meta,
    wsum_o, ing_o, small_o, esum_o, out_o,
    acc, vaug, gaug, qz, gz, kt, dqt, pbuf, pret, hbuf, obuf, dall, nt, tok,
    part, r1, r2, r3, full, sbuf, srecv, sone, stwo, keep, other, final,
    send1, recv1, send2, recv2, send3, recv3, send4, recv4, send5, recv5, send6, recv6, send7, recv7, local,
    send_a, recv_a, send_b, recv_b, out_sem, copy_sem, p_sem, send_p, recv_p, o_sem,
):
    seq = q_ref.shape[0]
    width = tok.shape[1]
    span = 256
    pair = pl.program_id(0)
    me = lax.axis_index("expert")
    my_dp = lax.axis_index("dp")
    core = lax.rem(me, 2)
    place = me // 2
    chips = experts // 2
    sibling = me + 1 - 2 * core
    half = width // 2
    piece = half // groups
    thick = part.shape[2]
    gain_rows = width // 128

    def half_rows(which):
        return pl.ds(pl.multiple_of(which * half, 16), half)

    def own_piece(which):
        return pl.ds(pl.multiple_of(core * half + which * piece, 16), piece)

    def copy1(c):
        return remote(part.at[c, half_rows(1 - core), :], r1.at[c], send1.at[c], recv1.at[c], "expert", sibling)

    def copy2(c, peer, slot):
        return remote(part.at[c, own_piece(peer), :], r2.at[c, slot], send2.at[c, peer], recv2.at[c, slot], "dp", peer)

    def copy3(c, peer, slot):
        return remote(
            r3.at[c, place], r3.at[c, slot], send3.at[c, peer], recv3.at[c, slot], "expert", 2 * peer + core
        )

    def copy4(c, peer, slot):
        return remote(
            full.at[c, own_piece(my_dp), :], full.at[c, own_piece(slot), :],
            send4.at[c, peer], recv4.at[c, slot], "dp", peer,
        )

    def copy5(c, which):
        return remote(
            full.at[c, half_rows(which), :], full.at[c, half_rows(which), :],
            send5.at[c], recv5.at[c], "expert", sibling,
        )

    def stage1(c):
        copy1(c).start()

    def stage2(c):
        copy1(c).wait_recv()
        part[c, half_rows(core), :] = (part[c, half_rows(core), :].astype(f32) + r1[c].astype(f32)).astype(bf16)
        for peer in others(groups, my_dp):
            copy2(c, peer, my_dp).start()

    def stage3(c):
        total = part[c, own_piece(my_dp), :].astype(f32)
        for peer in others(groups, my_dp):
            copy2(c, peer, peer).wait_recv()
            total = total + r2[c, peer].astype(f32)
        r3[c, place] = total.astype(bf16)
        for peer in others(chips, place):
            copy3(c, peer, place).start()

    def stage4(c):
        for peer in others(chips, place):
            copy3(c, peer, peer).wait_recv()
        total = r3[c, 0].astype(f32)
        for slot in range(1, chips):
            total = total + r3[c, slot].astype(f32)
        full[c, own_piece(my_dp), :] = total.astype(bf16)
        for peer in others(groups, my_dp):
            copy4(c, peer, my_dp).start()

    def stage5(c):
        for peer in others(groups, my_dp):
            copy4(c, peer, peer).wait_recv()
        copy5(c, core).start()

    def put_first(c):
        return pltpu.make_async_copy(full.at[c], wsum_o.at[0, :, thick * c : thick * c + thick], out_sem.at[c, 0])

    def put_pair(c, which):
        cols = pl.ds(128 * (c - 2) if isinstance(c, int) else pl.multiple_of(128 * (c - 2), 128), 128)
        return pltpu.make_async_copy(
            full.at[c, :, 128 * which : 128 * which + 128], wsum_o.at[1 + which, :, cols], out_sem.at[c, which]
        )

    def stage6(c):
        copy5(c, 1 - core).wait_recv()

        if c < 2:
            put_first(c).start()
        else:
            for which in range(3):
                put_pair(c, which).start()

    share = width // 4
    dp_x, dp_y = lax.rem(my_dp, 2), my_dp // 2
    peer_x, peer_y = my_dp + 1 - 2 * dp_x, my_dp + 2 - 4 * dp_y
    middle = keep.shape[1]
    left, right = pl.ds(0, middle), pl.ds(middle, middle)

    def share_rows(which):
        return pl.ds(pl.multiple_of(which * share, 16), share)

    def first_left(block):
        return remote(
            ein_h.at[share_rows(1 - dp_x + 2 * block), left], other.at[1, share_rows(block), :],
            send_a.at[0, block], recv_a.at[0, block], "dp", peer_x,
        )

    def first_right(block):
        return remote(
            ein_h.at[share_rows(2 - 2 * dp_y + block), right], other.at[1, share_rows(2 + block), :],
            send_a.at[1, block], recv_a.at[1, block], "dp", peer_y,
        )

    def second_left(which):
        return remote(
            keep.at[share_rows(1 - dp_y), :], final.at[which, :, left],
            send_b.at[which, 0], recv_b.at[which, 0], "dp", peer_y,
        )

    def second_right(which):
        return remote(
            keep.at[share_rows(2 + 1 - dp_x), :], final.at[which, :, right],
            send_b.at[which, 1], recv_b.at[which, 1], "dp", peer_x,
        )

    def own_loads(src):
        loads = []
        for block in range(2):
            loads.append(
                pltpu.make_async_copy(
                    src.at[share_rows(dp_x + 2 * block), left], keep.at[share_rows(block), :], copy_sem.at[block]
                )
            )
            loads.append(
                pltpu.make_async_copy(
                    src.at[share_rows(2 * dp_y + block), right], keep.at[share_rows(2 + block), :], copy_sem.at[2 + block]
                )
            )
        return loads

    def shared_load():
        return pltpu.make_async_copy(shared_h, other.at[0], copy_sem.at[4])

    def save(which):
        return pltpu.make_async_copy(final.at[which], esum_o.at[which], copy_sem.at[5])

    def experts_begin():
        for copy in own_loads(eout_h) + [shared_load()]:
            copy.start()
        for block in range(2):
            first_left(block).start()
            first_right(block).start()

    def experts_second(which):
        for copy in own_loads(eout_h if which == 0 else ein_h):
            copy.wait()
        if which == 0:
            shared_load().wait()
        else:
            for block in range(2):
                first_left(block).wait_recv()
                first_right(block).wait_recv()

        def block(idx, carry):
            rows = pl.ds(pl.multiple_of(idx * 64, 64), 64)
            keep[rows, :] = (keep[rows, :].astype(f32) + other[which, rows, :].astype(f32)).astype(bf16)
            return carry

        lax.fori_loop(0, width // 64, block, 0)
        second_left(which).start()
        second_right(which).start()

    def experts_last(which):
        second_left(which).wait()
        second_right(which).wait()

        def block(idx, carry):
            rows = pl.ds(pl.multiple_of(idx * 64, 64), 64)
            mine_left = pl.ds(pl.multiple_of(dp_y * share + idx * 64, 64), 64)
            mine_right = pl.ds(pl.multiple_of((2 + dp_x) * share + idx * 64, 64), 64)
            final[which, rows, left] = (final[which, rows, left].astype(f32) + keep[mine_left, :].astype(f32)).astype(bf16)
            final[which, rows, right] = (final[which, rows, right].astype(f32) + keep[mine_right, :].astype(f32)).astype(bf16)
            return carry

        lax.fori_loop(0, share // 64, block, 0)
        if which == 0:
            for copy in own_loads(ein_h):
                copy.start()
        else:
            save(0).wait()
        save(which).start()

    early = pl.ds(8 + hot.shape[0], sbuf.shape[0] - 8 - hot.shape[0])
    late = pl.ds(0, 8 + hot.shape[0])

    def copy6(part_idx, rows, peer, slot):
        return remote(
            sbuf.at[rows, :], srecv.at[slot, rows, :],
            send6.at[part_idx, peer], recv6.at[part_idx, slot], "expert", peer,
        )

    def copy7(part_idx, rows, peer, slot):
        return remote(
            sone.at[rows, :], stwo.at[slot, rows, :],
            send7.at[part_idx, peer], recv7.at[part_idx, slot], "dp", peer,
        )

    def small1(part_idx, rows):
        srecv[me, rows, :] = sbuf[rows, :]
        for peer in others(experts, me):
            copy6(part_idx, rows, peer, me).start()

    def small2(part_idx, rows):
        for peer in others(experts, me):
            copy6(part_idx, rows, peer, peer).wait_recv()
        total = srecv[0, rows, :]
        for slot in range(1, experts):
            total = total + srecv[slot, rows, :]
        sone[rows, :] = total
        stwo[my_dp, rows, :] = total
        for peer in others(groups, my_dp):
            copy7(part_idx, rows, peer, my_dp).start()

    def small3(part_idx, rows):
        for peer in others(groups, my_dp):
            copy7(part_idx, rows, peer, peer).wait_recv()
        total = stwo[0, rows, :]
        for slot in range(1, groups):
            total = total + stwo[slot, rows, :]
        small_o[rows, :] = total

    stages = (stage2, stage3, stage4, stage5, stage6)

    def advance(slot):
        for c, slots in enumerate(PLAN):
            for at, stage in reversed(list(zip(slots, stages))):
                if at < 4 * pairs:
                    pl.when(slot == at)(functools.partial(stage, c))

    def load_p(slot_idx, slot):
        rows = pl.ds(pl.multiple_of(lax.rem(slot_idx, 4) * span, span), span)
        return pltpu.make_async_copy(p_h.at[pl.ds(2 * (slot_idx // 4), 2), rows, :], pbuf.at[slot], p_sem.at[slot])

    slots_each = pret.shape[0] // experts

    def slot_rows(which):
        return pl.ds(pl.multiple_of(which * slots_each, 16), slots_each)

    def give_back(peer):
        return remote(
            prod_h.at[slot_rows(peer), :], pret.at[slot_rows(me), :], send_p.at[peer], recv_p.at[me], "expert", peer
        )

    def got_back(peer):
        return remote(
            prod_h.at[slot_rows(peer), :], pret.at[slot_rows(peer), :], send_p.at[peer], recv_p.at[peer], "expert", peer
        )

    def own_back():
        return pltpu.make_async_copy(prod_h.at[slot_rows(me), :], pret.at[slot_rows(me), :], o_sem.at[0])

    def out_rows(block):
        return pl.ds(block * span, span)

    def load_hidden(block):
        return pltpu.make_async_copy(hid_h.at[out_rows(block), :], hbuf, o_sem.at[1])

    def save_out(block):
        return pltpu.make_async_copy(obuf, out_o.at[out_rows(block), :], o_sem.at[2])

    def output_block(block):
        if block == 0:
            own_back().wait()
            for peer in others(experts, me):
                got_back(peer).wait_recv()
        load_hidden(block).wait()
        where = lax.broadcasted_iota(jnp.int32, (span, pret.shape[0]), 1).astype(f32)
        pick = jnp.where(meta[out_rows(block), 1:2] == where, 1.0, 0.0).astype(bf16)
        gathered = dot_f32(pick, pret[...])
        if block > 0:
            save_out(block - 1).wait()
        obuf[...] = (hbuf[...] + meta[out_rows(block), 0:1] * gathered).astype(bf16)
        save_out(block).start()
        if (block + 1) * span < seq:
            load_hidden(block + 1).start()

    loads = [
        pltpu.make_async_copy(nl_h, tok, local.at[0]),
        pltpu.make_async_copy(ghid_h, ing_o, local.at[2]),
        pltpu.make_async_copy(dwo_h.at[:, 0:thick], part.at[0], local.at[3]),
        pltpu.make_async_copy(dwo_h.at[:, thick : 2 * thick], part.at[1], local.at[4]),
        pltpu.make_async_copy(small_h, sbuf, local.at[5]),
    ]

    @pl.when(pair == 0)
    def _():
        barrier = pltpu.get_barrier_semaphore()
        for peer in others(experts, me):
            pl.semaphore_signal(barrier, inc=1, device_id={"expert": peer})
        for peer in others(groups, my_dp):
            pl.semaphore_signal(barrier, inc=1, device_id={"dp": peer})
        for copy in loads:
            copy.start()
        load_p(0, 0).start()
        own_back().start()
        load_hidden(0).start()
        for copy in loads:
            copy.wait()
        nt[...] = tok[...].T
        pl.semaphore_wait(barrier, experts + groups - 2)
        stage1(0)
        stage1(1)
        small1(0, early)
        experts_begin()
        for peer in others(experts, me):
            give_back(peer).start()

    mine = pl.ds(pl.multiple_of(128 * pair, 128), 128)
    lane = lax.broadcasted_iota(jnp.int32, (seq, 128), 1)
    gt = g_ref[...].T
    kt[...] = k_ref[...].T
    gtf = gt.astype(f32)
    pad = jnp.zeros((48, seq), bf16)
    one = jnp.ones((seq, 128), bf16)
    nil = jnp.zeros((seq, 128), bf16)
    acc[...] = jnp.zeros_like(acc)
    for head in range(2):
        own = (lane < 64) if head == 0 else (lane >= 64)
        origin = 64 if head == 0 else 0
        extra = jnp.where((lane >= origin) & (lane < origin + 3), one, nil)
        vaug[head] = jnp.where(own, v_ref[...], extra)
        qz[head] = jnp.where(own, q_ref[...], nil)
        gz[head] = jnp.where(own, g_ref[...], nil)
        rows = slice(64 * head, 64 * head + 64)
        gaug[head, rows, :] = gt[rows]
        gaug[head, origin : origin + 16, :] = split_rows(
            -jnp.sum(gtf[rows] * ctxt_ref[rows, :], axis=0, keepdims=True)
        )
        gaug[head, origin + 16 : origin + 64, :] = pad

    dqt[...] = jnp.zeros_like(dqt)

    def step(idx, carry):
        rows = pl.ds(pl.multiple_of(idx * span, span), span)
        dv = None
        dk = None
        slot = lax.rem(idx, 2)
        load_p(4 * pair + idx, slot).wait()

        @pl.when(4 * pair + idx + 1 < 4 * pairs)
        def _():
            load_p(4 * pair + idx + 1, 1 - slot).start()

        for head in range(2):
            dp = dot_f32(vaug[head, rows, :], gaug[head])
            grads = []
            for part_idx in range(2):
                offs = pl.ds(pl.multiple_of(seq - span * idx - 128 * part_idx, 128), seq)
                band = slice(128 * part_idx, 128 * part_idx + 128)
                ds_ = pbuf[slot, head, band, :].astype(f32) * dp[band]
                acc[head, :, offs] += ds_
                grads.append(ds_.astype(bf16))
            ds_ = jnp.concatenate(grads, axis=0)
            now = dot_f32(pbuf[slot, head], gz[head])
            dv = now if dv is None else dv + now
            now = dot_f32(ds_, qz[head])
            dk = now if dk is None else dk + now
            dqt[64 * head : 64 * head + 64, :] += dot_f32(kt[64 * head : 64 * head + 64, rows], ds_)
        dall[1, rows, mine] = dk.astype(bf16)
        dall[2, rows, mine] = dv.astype(bf16)
        advance(4 * pair + idx)

        for block in range(seq // span):
            @pl.when(4 * pair + idx == OUTPUT_SLOT + block)
            def _():
                output_block(block)

        for at, task, which in EXPERT_SLOTS:
            @pl.when(4 * pair + idx == at)
            def _():
                (experts_second if task == 2 else experts_last)(which)

        @pl.when(4 * pair + idx == 7)
        def _():
            small2(0, early)

        @pl.when(4 * pair + idx == 11)
        def _():
            small3(0, early)

        return carry

    lax.fori_loop(0, seq // span, step, 0)
    dall[0, :, mine] = dqt[...].T.astype(bf16)
    twice = 2 * seq
    sub = lax.broadcasted_iota(jnp.int32, (8, twice), 0)
    head_lane = lax.broadcasted_iota(jnp.int32, (hot.shape[0], 128), 1)
    rel_rows = slice(8, 8 + hot.shape[0])
    for head in range(2):
        total = acc[head, 0:8, :]
        for group in range(1, 16):
            total = total + pltpu.roll(acc[head, 8 * group : 8 * group + 8, :], twice - 8 * group, 1)
        for bit in (1, 2, 4):
            total = jnp.where((sub & bit) != 0, pltpu.roll(total, twice - bit, 1), total)
        diag = jnp.sum(total, axis=0, keepdims=True)
        sums = jnp.sum(hot[...] * diag, axis=1, keepdims=True)
        sbuf[rel_rows, :] = jnp.where(head_lane == 2 * pair + head, sums, sbuf[rel_rows, :])

    def weight_block(idx, carry):
        rows = pl.ds(pl.multiple_of(idx * 256, 256), 256)
        grads = jnp.concatenate([dall[which, :, mine] for which in range(3)], axis=1)
        part[pair + 2, rows, :] = dot_f32(nt[rows, :], grads).astype(bf16)
        return carry

    lax.fori_loop(0, width // 256, weight_block, 0)
    stage1(pair + 2)

    @pl.when(pair == pairs - 1)
    def _():
        def token_block(idx, carry):
            rows = pl.ds(pl.multiple_of(idx * 256, 256), 256)
            grad = (
                dot_nt(dall[0, rows, :], wq[...])
                + dot_nt(dall[1, rows, :], wk[...])
                + dot_nt(dall[2, rows, :], wv[...])
            )
            values = tok[rows, :].astype(f32)
            scale = lax.rsqrt(jnp.mean(values * values, axis=-1, keepdims=True) + epsilon)
            weighted = grad * gain[0:1, :]
            inner = jnp.mean(weighted * values, axis=-1, keepdims=True)
            ing_o[rows, :] += scale * weighted - values * (scale * scale * scale * inner)
            return carry + jnp.sum(grad * values * scale, axis=0, keepdims=True)

        reload = pltpu.make_async_copy(tok_h, tok, local.at[1])
        reload.start()
        last = pairs + 1
        first = 4 * pairs
        older = sorted(
            (at, c, stage)
            for c, slots in enumerate(PLAN)
            for stage, at in enumerate(slots)
            if at >= first
        )

        def drain(until):
            while older and older[0][0] < first + until:
                _, c, stage = older.pop(0)
                stages[stage](c)

        def tokens_done(lower, upper, gain_grad):
            return lax.fori_loop(lower, upper, token_block, gain_grad)

        drain(1)
        reload.wait()
        gain_grad = tokens_done(0, 1, jnp.zeros((1, width), f32))
        stage2(last)
        drain(2)
        gain_grad = tokens_done(1, seq // 512, gain_grad)
        drain(4)
        gain_grad = tokens_done(seq // 512, seq // 256, gain_grad)
        stage3(last)
        for row in range(gain_rows):
            sbuf[row : row + 1, :] = gain_grad[:, 128 * row : 128 * row + 128]
        small1(1, late)
        drain(8)
        small2(1, late)
        stage4(last)
        drain(99)
        small3(1, late)
        stage5(last)
        stage6(last)
        for c in range(2):
            put_first(c).wait()
        save(1).wait()
        save_out(seq // span - 1).wait()
        for peer in others(experts, me):
            give_back(peer).wait_send()
        for block in range(2):
            first_left(block).wait_send()
            first_right(block).wait_send()

        def finish(c, carry):
            copy1(c).wait_send()
            for peer in others(groups, my_dp):
                copy2(c, peer, my_dp).wait_send()
                copy4(c, peer, my_dp).wait_send()
            for peer in others(chips, place):
                copy3(c, peer, place).wait_send()
            copy5(c, core).wait_send()

            @pl.when(c >= 2)
            def _():
                for which in range(3):
                    put_pair(c, which).wait()

            return carry

        lax.fori_loop(0, pairs + 2, finish, 0)
        for part_idx, rows in ((0, early), (1, late)):
            for peer in others(experts, me):
                copy6(part_idx, rows, peer, me).wait_send()
            for peer in others(groups, my_dp):
                copy7(part_idx, rows, peer, my_dp).wait_send()


def back_pass(
    q, k, v, g, ctxt, wq, wk, wv, hot, gain, normed_low, tokens, grad_hidden, dwo, small,
    expert_out_grad, shared, expert_in_grad, weights, produced, hidden_rows, meta, groups, experts
):
    seq, width = q.shape
    pairs = width // 128
    chunks = pairs + 2
    hidden = expert_in_grad.shape[1]
    thick = width // 2
    half = width // 2
    piece = half // groups
    chips = experts // 2
    blk = pl.BlockSpec((seq, 128), lambda p: (0, p))
    hbm = pl.BlockSpec(memory_space=pl.ANY)
    fixed = lambda shape: pl.BlockSpec(shape, lambda p: (0,) * len(shape), pipeline_mode=pl.Buffered(1))
    dma = pltpu.SemaphoreType.DMA
    return pl.pallas_call(
        functools.partial(back_kernel, groups, experts, pairs),
        grid=(pairs,),
        in_specs=[
            blk, blk, blk, blk,
            pl.BlockSpec((128, seq), lambda p: (p, 0)),
            fixed((width, width)), fixed((width, width)), fixed((width, width)),
            fixed(hot.shape), fixed(gain.shape),
            hbm, hbm, hbm, hbm, hbm, hbm, hbm, hbm,
            hbm, hbm, hbm, fixed(meta.shape),
        ],
        out_specs=[hbm, fixed((seq, width)), fixed(small.shape), hbm, hbm],
        out_shape=[
            jax.ShapeDtypeStruct((4, width, width), bf16),
            jax.ShapeDtypeStruct((seq, width), f32),
            jax.ShapeDtypeStruct(small.shape, f32),
            jax.ShapeDtypeStruct((2, width // 4, hidden), bf16),
            jax.ShapeDtypeStruct((seq, width), bf16),
        ],
        scratch_shapes=[
            pltpu.VMEM((2, 128, 2 * seq), f32),
            pltpu.VMEM((2, seq, 128), bf16),
            pltpu.VMEM((2, 128, seq), bf16),
            pltpu.VMEM((2, seq, 128), bf16),
            pltpu.VMEM((2, seq, 128), bf16),
            pltpu.VMEM((128, seq), bf16),
            pltpu.VMEM((128, seq), f32),
            pltpu.VMEM((2, 2, 256, seq), bf16),
            pltpu.VMEM(produced.shape, bf16),
            pltpu.VMEM((256, width), f32),
            pltpu.VMEM((256, width), bf16),
            pltpu.VMEM((3, seq, width), bf16),
            pltpu.VMEM((width, seq), bf16),
            pltpu.VMEM((seq, width), bf16),
            pltpu.VMEM((chunks, width, thick), bf16),
            pltpu.VMEM((chunks, half, thick), bf16),
            pltpu.VMEM((chunks, groups, piece, thick), bf16),
            pltpu.VMEM((chunks, chips, piece, thick), bf16),
            pltpu.VMEM((chunks, width, thick), bf16),
            pltpu.VMEM(small.shape, f32),
            pltpu.VMEM((experts,) + small.shape, f32),
            pltpu.VMEM(small.shape, f32),
            pltpu.VMEM((groups,) + small.shape, f32),
            pltpu.VMEM((width, hidden // 2), bf16),
            pltpu.VMEM((2, width, hidden // 2), bf16),
            pltpu.VMEM((2, width // 4, hidden), bf16),
            dma((chunks,)), dma((chunks,)),
            dma((chunks, groups)), dma((chunks, groups)),
            dma((chunks, chips)), dma((chunks, chips)),
            dma((chunks, groups)), dma((chunks, groups)),
            dma((chunks,)), dma((chunks,)),
            dma((2, experts)), dma((2, experts)),
            dma((2, groups)), dma((2, groups)),
            dma((6,)),
            dma((2, 2)), dma((2, 2)),
            dma((2, 2)), dma((2, 2)),
            dma((chunks, 3)), dma((6,)),
            dma((2,)), dma((experts,)), dma((experts,)), dma((3,)),
        ],
        compiler_params=pltpu.CompilerParams(
            vmem_limit_bytes=62 << 20, collective_id=2, has_side_effects=True
        ),
        cost_estimate=pl.CostEstimate(
            flops=40 * seq * seq * width + 12 * seq * width * width,
            bytes_accessed=40 * seq * width, transcendentals=seq * seq * 12,
        ),
        name="attend_back",
    )(
        q, k, v, g, ctxt, wq, wk, wv, hot, gain, normed_low, tokens, grad_hidden, dwo, small,
        expert_out_grad, shared, expert_in_grad, weights, produced, hidden_rows, meta,
    )


def rms_backward(grad_norm, values, row_scale, gain_vec):
    weighted = grad_norm * gain_vec
    gain_grad = jnp.sum(grad_norm * values * row_scale, axis=0)
    grad_in = row_scale * weighted - values * row_scale**3 * jnp.mean(
        weighted * values, axis=-1, keepdims=True
    )
    return grad_in, gain_grad


def rms_forward(values, gain_vec):
    row_scale = lax.rsqrt(jnp.mean(values * values, axis=-1, keepdims=True) + epsilon)
    return values * row_scale * gain_vec, row_scale


def gelu_tanh(values):
    return jax.nn.gelu(values, approximate=True)


def contract(left, right, dims):
    return lax.dot_general(left, right, (((dims[0],), (dims[1],)), ((), ())), preferred_element_type=f32)


def exchange(rows, experts):
    slots, width = rows.shape
    rows = rows.reshape(experts, slots // experts, width)
    return lax.all_to_all(rows, "expert", split_axis=0, concat_axis=0, tiled=True).reshape(slots, width)


def expert_native(send, grad_recv, weight_in, weight_out, router_w, experts):
    received = exchange(send, experts)
    own = lax.axis_index("expert")
    own_hot = (jnp.arange(experts, dtype=jnp.int32) == own).astype(f32)[None, :]
    probs = jax.nn.softmax(contract(received, router_w, (1, 0)), axis=-1)
    gate = jnp.sum(probs * own_hot, axis=-1, keepdims=True)
    grad_recv_f = grad_recv.astype(f32)
    grad_produced = (grad_recv_f * gate).astype(bf16)
    preact = contract(received, weight_in, (1, 0))
    gelu_values, gelu_pullback = jax.vjp(gelu_tanh, preact)
    active = gelu_values.astype(bf16)
    produced = contract(active, weight_out, (1, 0)).astype(bf16)
    gate_grad = jnp.sum(grad_recv_f * produced.astype(f32), axis=-1, keepdims=True)
    logit_low = (gate_grad * gate * (own_hot - probs)).astype(bf16)
    grad_active = contract(grad_produced, weight_out, (1, 1))
    grad_preact = gelu_pullback(grad_active)[0].astype(bf16)
    grad_received = contract(grad_preact, weight_in, (1, 1)) + contract(logit_low, router_w, (1, 1))
    grad_rows = exchange(grad_received.astype(bf16), experts)
    in_grad = contract(received, grad_preact, (0, 0)).astype(bf16)
    out_grad_t = contract(grad_produced, active, (0, 0)).astype(bf16)
    router_grad = contract(received, logit_low, (0, 0))
    return grad_rows, produced, in_grad, out_grad_t, router_grad


def tail_native(tokens, gain, normed_low, dq, dk, dv, wq, wk, wv, grad_hidden, dwo, small):
    tokens_f = tokens.astype(f32)
    grads = jnp.stack([dwo.astype(f32)] + [contract(normed_low, d, (0, 0)) for d in (dq, dk, dv)])
    grad_normed = contract(dq, wq, (1, 1)) + contract(dk, wk, (1, 1)) + contract(dv, wv, (1, 1))
    _, scale = rms_forward(tokens_f, gain)
    grad_tokens, gain_grad = rms_backward(grad_normed, tokens_f, scale, gain)
    grads, gain_grad, small = lax.psum((grads, gain_grad, small), ("dp", "expert"))
    return grads, grad_hidden + grad_tokens, gain_grad, small


def on_device(
    tokens, gain_one, query_w, key_w, value_w, out_w, rel_table, gain_two, router_w,
    expert_in, expert_out, routes, buckets, cotangent,
):
    seq_len, width = tokens.shape
    heads = rel_table.shape[1]
    groups = lax.axis_size("dp")
    experts = lax.axis_size("expert")
    capacity = (5 * seq_len + 4 * experts - 1) // (4 * experts)
    slots = experts * capacity
    weight_in = expert_in[0]
    weight_out = expert_out[0]
    kernels = capacity % 16 == 0 and experts == 8 and groups == 4

    route_ids = routes[:, 0]
    route_hot = route_ids[:, None] == jnp.arange(experts, dtype=jnp.int32)[None, :]
    route_int = route_hot.astype(jnp.int32)
    route_float = route_hot.astype(f32)
    position = jnp.sum((jnp.cumsum(route_int, axis=0) - 1) * route_int, axis=1)
    slot_index = jnp.where(position < capacity, route_ids * capacity + position, slots)
    pick = (jnp.arange(slots, dtype=jnp.int32)[:, None] == slot_index[None, :]).astype(bf16)

    def scatter_rows(rows):
        return contract(pick, rows, (1, 0)).astype(bf16)

    def gather_rows(rows):
        return contract(pick, rows, (0, 0))

    tokens_f = tokens.astype(f32)
    gains = jnp.stack([gain_one, gain_two])
    if kernels:
        queries, key_rows, value_rows, normed_low, grad_send, slot_row, slot_column = first_pass(
            tokens, gains, query_w, key_w, value_w, routes.reshape(1, seq_len), cotangent, capacity, experts
        )
    else:
        grad_send = scatter_rows(cotangent)
        normed_low = rms_forward(tokens_f, gain_one)[0].astype(bf16)
        queries = contract(normed_low, query_w, (1, 0)).astype(bf16)
        key_rows = contract(normed_low, key_w, (1, 0)).astype(bf16)
        value_rows = contract(normed_low, value_w, (1, 0)).astype(bf16)
    reach = jnp.concatenate([buckets, jnp.full((1,), -1, jnp.int32)])[::-1]
    bucket_hot = (jnp.arange(rel_table.shape[0], dtype=jnp.int32)[:, None] == reach[None, :]).astype(f32)
    spread = jnp.einsum("bh,bx->hx", rel_table, bucket_hot, precision=highest)
    spread = spread.reshape(heads // 2, 2, 2 * seq_len)
    context, context_t, logsum, weights, grad_recv = attend(
        queries, key_rows, value_rows, spread, grad_send, experts if kernels else 0
    )
    if kernels:
        router_pad = jnp.pad(router_w, ((0, 0), (0, 128 - experts)))
        hidden, send, meta = middle_pass(
            tokens, context, out_w, gains, router_pad, slot_row, slot_column, slots, experts
        )
        grad_rows, produced, in_grad, out_grad_t, router_grad, shared = expert_pass(
            send, grad_recv, weight_in, weight_out, router_pad, experts, capacity
        )
        router_grad = router_grad[:, :experts]
        grad_hidden, out_w_grad, grad_context, gain_two_grad = combine_pass(
            grad_rows, hidden, cotangent, gains, context, out_w, meta
        )
    else:
        grad_recv = exchange(grad_send, experts)
        hidden = tokens_f + contract(context, out_w, (1, 0))
        normed_two, scale_two = rms_forward(hidden, gain_two)
        normed_two_low = normed_two.astype(bf16)
        grad_rows, produced, in_grad, out_grad_t, router_grad = expert_native(
            scatter_rows(normed_two_low), grad_recv, weight_in, weight_out, router_w, experts
        )
        router_probs = jax.nn.softmax(contract(normed_two_low, router_w, (1, 0)), axis=-1)
        gate_value = jnp.sum(router_probs * route_float, axis=-1, keepdims=True)
        grad_normed_two = gather_rows(grad_rows)
        grad_hidden_norm, gain_two_grad = rms_backward(grad_normed_two, hidden, scale_two, gain_two)
        grad_hidden = cotangent.astype(f32) + grad_hidden_norm
        branch_low = grad_hidden.astype(bf16)
        out_w_grad = contract(context, branch_low, (0, 0)).astype(bf16)
        grad_context = contract(branch_low, out_w, (1, 1)).astype(bf16)

    if kernels:
        small = jnp.concatenate(
            [
                jnp.zeros((8 + rel_table.shape[0], 128), f32),
                jnp.pad(gain_two_grad.reshape(-1, 128), ((0, 2), (0, 0))),
                router_grad.T.reshape(-1, 128),
            ]
        )
        grads, input_grad, small, shares, output = back_pass(
            queries, key_rows, value_rows, grad_context, context_t, query_w, key_w, value_w,
            bucket_hot, gains, normed_low, tokens, grad_hidden, out_w_grad, small,
            out_grad_t, shared, in_grad, weights, produced, hidden,
            meta, groups, experts,
        )
        tiles = width // 128
        first = 8 + rel_table.shape[0]
        gain_one_grad = small[:tiles].reshape(-1)
        rel_grad = small[8:first, :heads]
        gain_two_grad = small[first : first + tiles].reshape(-1)
        router_grad = small[first + 8 :].reshape(experts, width).T
        out_share, in_share = shares[0], shares[1]
    else:
        output = (hidden + gate_value * gather_rows(exchange(produced, experts))).astype(bf16)
        in_share = lax.psum_scatter(in_grad, "dp", scatter_dimension=0, tiled=True)
        out_share = lax.psum_scatter(out_grad_t, "dp", scatter_dimension=0, tiled=True)
        query_grad, key_grad, value_grad, diagonals = attend_back(
            queries, key_rows, value_rows, grad_context, spread, context_t, logsum
        )
        diagonals = diagonals[:, :2].reshape(heads, 2 * seq_len)
        rel_grad = jnp.einsum("bx,hx->bh", bucket_hot, diagonals, precision=highest)
        grads, input_grad, gain_one_grad, small = tail_native(
            tokens, gain_one, normed_low, query_grad, key_grad, value_grad,
            query_w, key_w, value_w, grad_hidden, out_w_grad, (rel_grad, gain_two_grad, router_grad),
        )
        rel_grad, gain_two_grad, router_grad = small
    grads = grads.astype(f32)
    return (
        output, input_grad, grads[1], grads[2], grads[3], grads[0], rel_grad,
        gain_one_grad, gain_two_grad, router_grad, in_share.astype(f32)[None], out_share.astype(f32).T[None],
    )


def solution(mesh):
    rows = P(("dp", "expert"), None)
    whole = P()
    split = P("expert", None, None)
    return jax.shard_map(
        on_device,
        mesh=mesh,
        in_specs=(
            rows, whole, whole, whole, whole, whole, whole, whole, whole, split, split, rows, whole, rows,
        ),
        out_specs=(
            rows, rows, whole, whole, whole, whole, whole, whole, whole, whole,
            P("expert", "dp", None), P("expert", None, "dp"),
        ),
        check_vma=False,
    )
```

```python
import functools

import jax
import jax.numpy as jnp
from jax import lax
from jax.experimental import pallas as pl
from jax.experimental.pallas import tpu as pltpu
from jax.sharding import PartitionSpec as P

bf16 = jnp.bfloat16
f32 = jnp.float32
epsilon = 1e-06
highest = lax.Precision.HIGHEST

def dot_f32(left, right):
    return lax.dot_general(left, right, (((1,), (0,)), ((), ())), preferred_element_type=f32)


def dot_nt(left, right):
    return lax.dot_general(left, right, (((1,), (1,)), ((), ())), preferred_element_type=f32)


def fill_toeplitz(base_ref, head, row):
    rows, width = base_ref.shape[1:]
    spread = jnp.broadcast_to(row, (8, width))
    eight = pltpu.roll(spread, 0, 1, stride=1, stride_axis=0)
    for group in range(rows // 8):
        base_ref[head, 8 * group : 8 * group + 8, :] = (
            eight if group == 0 else pltpu.roll(eight, 8 * group, 1)
        )


def attend_kernel(
    experts, q_ref, k_ref, v_ref, u_ref, gsend_h, ctx_ref, ctxt_ref, lse_ref, p_h, grecv_h,
    base, qt, vt, s_scr, p_scr, p_sem, send_g, recv_g, own_sem,
):
    seq = q_ref.shape[0]
    span = 256
    half = seq
    qt[...] = q_ref[...].T
    vt[...] = v_ref[...].T
    for head in range(2):
        fill_toeplitz(base, head, u_ref[0, head : head + 1, :])
    zeros = jnp.zeros((64, span), bf16)
    pair = pl.program_id(0)

    if experts:
        me = lax.axis_index("expert")
        count = grecv_h.shape[0] // experts
        rows_of = lambda who: pl.ds(pl.multiple_of(who * count, 16), count)
        peers = [lax.rem(me + k, experts) for k in range(1, experts)]
        barrier = pltpu.get_barrier_semaphore()
        own = pltpu.make_async_copy(gsend_h.at[rows_of(me), :], grecv_h.at[rows_of(me), :], own_sem)

        def give(peer, slot):
            return pltpu.make_async_remote_copy(
                src_ref=gsend_h.at[rows_of(peer), :], dst_ref=grecv_h.at[rows_of(slot), :],
                send_sem=send_g.at[peer], recv_sem=recv_g.at[slot], device_id={"expert": peer},
            )

        @pl.when(pair == 0)
        def _():
            for peer in peers:
                pl.semaphore_signal(barrier, inc=1, device_id={"expert": peer})
            own.start()

    def save(idx, slot):
        cols = pl.ds(pl.multiple_of(idx * span, span), span)
        return pltpu.make_async_copy(p_scr.at[slot], p_h.at[pl.ds(2 * pair, 2), :, cols], p_sem.at[slot])

    def step(idx, carry):
        slot = lax.rem(idx, 2)

        @pl.when((pair > 0) | (idx > 1))
        def _():
            save(idx, slot).wait()

        cols = pl.ds(pl.multiple_of(idx * span, span), span)
        outs = []
        for head in range(2):
            part = qt[64 * head : 64 * head + 64, cols]
            rhs = jnp.concatenate([part, zeros] if head == 0 else [zeros, part], axis=0)
            peak = None
            for kb in range(seq // 128):
                rows = slice(128 * kb, 128 * kb + 128)
                offs = pl.multiple_of(half + span * idx - 128 * kb, 128)
                s = dot_f32(k_ref[rows, :], rhs) + base[head, :, pl.ds(offs, span)]
                s_scr[head, rows, :] = s
                now = jnp.max(s.reshape(16, 8, span), axis=0)
                peak = now if peak is None else jnp.maximum(peak, now)
            peak = jnp.max(peak, axis=0, keepdims=True)
            total = None
            for kb in range(seq // 128):
                rows = slice(128 * kb, 128 * kb + 128)
                e = jnp.exp(s_scr[head, rows, :] - peak)
                s_scr[head, rows, :] = e
                now = jnp.sum(e.reshape(16, 8, span), axis=0)
                total = now if total is None else total + now
            total = jnp.sum(total, axis=0, keepdims=True)
            inv = 1.0 / total
            for kb in range(seq // 128):
                rows = slice(128 * kb, 128 * kb + 128)
                p_scr[slot, head, rows, :] = (s_scr[head, rows, :] * inv).astype(bf16)
            lse_ref[0, head : head + 1, cols] = peak + jnp.log(total)
            outs.append(dot_f32(vt[64 * head : 64 * head + 64, :], p_scr[slot, head]))
        save(idx, slot).start()
        both = jnp.concatenate(outs, axis=0)
        ctxt_ref[:, cols] = both
        ctx_ref[cols, :] = both.T.astype(bf16)
        return carry

    if experts:
        @pl.when(pair == 0)
        def _():
            pl.semaphore_wait(barrier, experts - 1)
            for peer in peers:
                give(peer, me).start()

    lax.fori_loop(0, seq // span, step, 0)

    @pl.when(pair == pl.num_programs(0) - 1)
    def _():
        for slot in range(2):
            save(slot, slot).wait()
        if experts:
            own.wait()
            for peer in peers:
                give(peer, me).wait_send()
                give(peer, peer).wait_recv()


def attend(q, k, v, u, gsend, experts=0):
    seq, width = q.shape
    pairs = width // 128
    blk = pl.BlockSpec((seq, 128), lambda p: (0, p))
    dma = pltpu.SemaphoreType.DMA
    return pl.pallas_call(
        functools.partial(attend_kernel, experts),
        grid=(pairs,),
        in_specs=[
            blk, blk, blk, pl.BlockSpec((1, 2, 2 * seq), lambda p: (p, 0, 0)), pl.BlockSpec(memory_space=pl.ANY),
        ],
        out_specs=[
            blk,
            pl.BlockSpec((128, seq), lambda p: (p, 0)),
            pl.BlockSpec((1, 8, seq), lambda p: (p, 0, 0)),
            pl.BlockSpec(memory_space=pl.ANY),
            pl.BlockSpec(memory_space=pl.ANY),
        ],
        out_shape=[
            jax.ShapeDtypeStruct((seq, width), bf16),
            jax.ShapeDtypeStruct((width, seq), f32),
            jax.ShapeDtypeStruct((pairs, 8, seq), f32),
            jax.ShapeDtypeStruct((2 * pairs, seq, seq), bf16),
            jax.ShapeDtypeStruct(gsend.shape, bf16),
        ],
        scratch_shapes=[
            pltpu.VMEM((2, 128, 2 * seq), f32),
            pltpu.VMEM((128, seq), bf16),
            pltpu.VMEM((128, seq), bf16),
            pltpu.VMEM((2, seq, 256), f32),
            pltpu.VMEM((2, 2, seq, 256), bf16),
            dma((2,)),
            dma((max(experts, 1),)), dma((max(experts, 1),)), dma(()),
        ],
        compiler_params=pltpu.CompilerParams(
            vmem_limit_bytes=62 << 20, has_side_effects=experts > 0, collective_id=3 if experts else None
        ),
        name="attend",
    )(q, k, v, u, gsend)


def first_kernel(
    capacity, experts, tok, gain, wq, wk, wv, route, cot, q_o, k_o, v_o, nl_o, gsend_o, slot_o, column_o, slot
):
    step = pl.program_id(0)
    slots = experts * capacity
    seq = route.shape[1]

    @pl.when(step == 0)
    def _():
        lane = lax.broadcasted_iota(jnp.int32, (8, seq), 1)
        hot = jnp.where(lax.broadcasted_iota(jnp.int32, (8, seq), 0) == route[...], 1.0, 0.0)
        count = hot
        shift = 1
        while shift < seq:
            count = count + jnp.where(lane >= shift, pltpu.roll(count, shift, 1), 0.0)
            shift *= 2
        position = jnp.sum(hot * (count - 1.0), axis=0, keepdims=True)
        place = route[...].astype(f32) * capacity + position
        slot[...] = jnp.where(position < capacity, place, float(slots))
        slot_o[...] = slot[...]
        column_o[...] = jnp.broadcast_to(slot[...], (128, seq)).T

    values = tok[...].astype(f32)
    scale = lax.rsqrt(jnp.mean(values * values, axis=-1, keepdims=True) + epsilon)
    normed = (values * scale * gain[0:1, :]).astype(bf16)
    nl_o[...] = normed
    for weight, out in ((wq, q_o), (wk, k_o), (wv, v_o)):
        out[...] = dot_f32(normed, weight[...]).astype(bf16)
    rows = gsend_o.shape[0]
    number = lax.broadcasted_iota(jnp.int32, (rows, seq), 0) + step * rows
    pick = jnp.where(number.astype(f32) == slot[...], 1.0, 0.0).astype(bf16)
    gsend_o[...] = dot_f32(pick, cot[...]).astype(bf16)


def first_pass(tokens, gain, wq, wk, wv, route, cotangent, capacity, experts):
    seq, width = tokens.shape
    slots = experts * capacity
    steps = 4
    rows = pl.BlockSpec((seq // steps, width), lambda i: (i, 0))
    fixed = lambda shape: pl.BlockSpec(shape, lambda i: (0, 0))
    return pl.pallas_call(
        functools.partial(first_kernel, capacity, experts),
        grid=(steps,),
        in_specs=[rows, fixed(gain.shape)] + [fixed(wq.shape)] * 3 + [fixed(route.shape), fixed(cotangent.shape)],
        out_specs=[rows] * 4 + [pl.BlockSpec((slots // steps, width), lambda i: (i, 0)), fixed(route.shape), fixed((seq, 128))],
        out_shape=[jax.ShapeDtypeStruct((seq, width), bf16)] * 4
        + [jax.ShapeDtypeStruct((slots, width), bf16), jax.ShapeDtypeStruct(route.shape, f32),
           jax.ShapeDtypeStruct((seq, 128), f32)],
        scratch_shapes=[pltpu.VMEM(route.shape, f32)],
        compiler_params=pltpu.CompilerParams(vmem_limit_bytes=62 << 20),
        cost_estimate=pl.CostEstimate(
            flops=6 * seq * width * width + 2 * slots * seq * width, bytes_accessed=20 * seq * width, transcendentals=seq
        ),
        name="first",
    )(tokens, gain, wq, wk, wv, route, cotangent)


def middle_kernel(experts, steps, tok, ctx, wo, gain, rw, slot, column, hid_o, xs_o, meta_o, normed):
    step = pl.program_id(0)
    span, width = tok.shape
    seq = normed.shape[0]

    @pl.when(step < steps)
    def _():
        hidden = tok[...].astype(f32) + dot_f32(ctx[...], wo[...])
        hid_o[...] = hidden
        scale = lax.rsqrt(jnp.mean(hidden * hidden, axis=-1, keepdims=True) + epsilon)
        low = (hidden * scale * gain[1:2, :]).astype(bf16)
        normed[pl.ds(pl.multiple_of(step * span, span), span), :] = low
        lane = lax.broadcasted_iota(jnp.int32, (span, 128), 1)
        logits = jnp.where(lane < experts, dot_f32(low, rw[...]), -1e30)
        weights = jnp.exp(logits - jnp.max(logits, axis=-1, keepdims=True))
        place = column[...]
        each = xs_o.shape[0] * (pl.num_programs(0) - steps) // experts
        first = (lane * each).astype(f32)
        chosen = (place >= first) & (place < first + each) & (lane < experts)
        gate = jnp.sum(jnp.where(chosen, weights, 0.0), axis=-1, keepdims=True) / jnp.sum(
            weights, axis=-1, keepdims=True
        )
        meta_o[...] = jnp.where(lane == 0, gate, place)

    @pl.when(step >= steps)
    def _():
        rows = xs_o.shape[0]
        number = lax.broadcasted_iota(jnp.int32, (rows, seq), 0) + (step - steps) * rows
        pick = jnp.where(number.astype(f32) == slot[...], 1.0, 0.0).astype(bf16)
        xs_o[...] = dot_f32(pick, normed[...]).astype(bf16)


def middle_pass(tokens, ctx, wo, gain, rw, slot, column, slots, experts):
    seq, width = tokens.shape
    steps = 4
    span = seq // steps
    each = slots // steps
    token_map = lambda i: (jnp.minimum(i, steps - 1), 0)
    fixed = lambda shape: pl.BlockSpec(shape, lambda i: (0, 0))
    return pl.pallas_call(
        functools.partial(middle_kernel, experts, steps),
        grid=(2 * steps,),
        in_specs=[
            pl.BlockSpec((span, width), token_map), pl.BlockSpec((span, width), token_map), fixed(wo.shape),
            fixed(gain.shape), fixed(rw.shape), fixed(slot.shape), pl.BlockSpec((span, 128), token_map),
        ],
        out_specs=[
            pl.BlockSpec((span, width), token_map),
            pl.BlockSpec((each, width), lambda i: (jnp.maximum(i - steps, 0), 0)),
            pl.BlockSpec((span, 128), token_map),
        ],
        out_shape=[
            jax.ShapeDtypeStruct((seq, width), f32),
            jax.ShapeDtypeStruct((slots, width), bf16),
            jax.ShapeDtypeStruct((seq, 128), f32),
        ],
        scratch_shapes=[pltpu.VMEM((seq, width), bf16)],
        compiler_params=pltpu.CompilerParams(vmem_limit_bytes=62 << 20),
        cost_estimate=pl.CostEstimate(
            flops=2 * seq * width * width + 2 * slots * seq * width, bytes_accessed=10 * seq * width, transcendentals=seq
        ),
        name="middle",
    )(tokens, ctx, wo, gain, rw, slot, column)


def combine_kernel(gback, hid, cot, gain, ctx, wo, meta, ghid_o, dwo_o, gctx_o, gain_o, total_w):
    step = pl.program_id(0)
    span = hid.shape[0]
    slots = gback.shape[0]
    where = lax.broadcasted_iota(jnp.int32, (span, slots), 1).astype(f32)
    pick = jnp.where(meta[:, 1:2] == where, 1.0, 0.0).astype(bf16)
    grad = dot_f32(pick, gback[...])
    values = hid[...]
    scale = lax.rsqrt(jnp.mean(values * values, axis=-1, keepdims=True) + epsilon)
    weighted = grad * gain[1:2, :]
    inner = jnp.mean(weighted * values, axis=-1, keepdims=True)
    total = cot[...].astype(f32) + scale * weighted - values * (scale * scale * scale * inner)
    ghid_o[...] = total
    branch = total.astype(bf16)
    gctx_o[...] = dot_nt(branch, wo[...]).astype(bf16)
    gains = jnp.sum(grad * values * scale, axis=0, keepdims=True)
    now = dot_f32(ctx[...].T, branch)

    @pl.when(step == 0)
    def _():
        total_w[...] = now
        gain_o[...] = gains

    @pl.when(step > 0)
    def _():
        total_w[...] += now
        gain_o[...] += gains

    @pl.when(step == pl.num_programs(0) - 1)
    def _():
        dwo_o[...] = total_w[...].astype(bf16)


def combine_pass(gback, hidden, cotangent, gain, ctx, wo, meta):
    seq, width = hidden.shape
    steps = 4
    rows = pl.BlockSpec((seq // steps, width), lambda i: (i, 0))
    fixed = lambda shape: pl.BlockSpec(shape, lambda i: (0, 0))
    return pl.pallas_call(
        combine_kernel,
        grid=(steps,),
        in_specs=[
            fixed(gback.shape), rows, rows, fixed(gain.shape), rows, fixed(wo.shape),
            pl.BlockSpec((seq // steps, 128), lambda i: (i, 0)),
        ],
        out_specs=[rows, fixed((width, width)), rows, fixed((1, width))],
        out_shape=[
            jax.ShapeDtypeStruct((seq, width), f32),
            jax.ShapeDtypeStruct((width, width), bf16),
            jax.ShapeDtypeStruct((seq, width), bf16),
            jax.ShapeDtypeStruct((1, width), f32),
        ],
        scratch_shapes=[pltpu.VMEM((width, width), f32)],
        compiler_params=pltpu.CompilerParams(vmem_limit_bytes=62 << 20),
        cost_estimate=pl.CostEstimate(
            flops=4 * seq * width * width + 2 * gback.shape[0] * seq * width,
            bytes_accessed=16 * seq * width, transcendentals=seq,
        ),
        name="combine",
    )(gback, hidden, cotangent, gain, ctx, wo, meta)


def split_rows(row):
    hi = row.astype(bf16).astype(f32)
    mid = (row - hi).astype(bf16).astype(f32)
    low = row - hi - mid
    idx = lax.broadcasted_iota(jnp.int32, (16, row.shape[1]), 0)
    return jnp.where(idx == 0, hi, jnp.where(idx == 1, mid, jnp.where(idx == 2, low, 0.0))).astype(bf16)


def attend_back_kernel(
    q_ref, k_ref, v_ref, g_ref, u_ref, ctxt_ref, lse_ref,
    dq_ref, dk_ref, dv_ref, diag_ref,
    base, acc, kaug, vaug, qaug, gaug, qz, gz, kt, dqt,
):
    seq = q_ref.shape[0]
    span = 256
    lane = lax.broadcasted_iota(jnp.int32, (seq, 128), 1)
    gt = g_ref[...].T
    qtv = q_ref[...].T
    kt[...] = k_ref[...].T
    gtf = gt.astype(f32)
    pad = jnp.zeros((48, seq), bf16)
    one = jnp.ones((seq, 128), bf16)
    nil = jnp.zeros((seq, 128), bf16)
    acc[...] = jnp.zeros_like(acc)
    for head in range(2):
        fill_toeplitz(base, head, u_ref[0, head : head + 1, :])
        own = (lane < 64) if head == 0 else (lane >= 64)
        origin = 64 if head == 0 else 0
        extra = jnp.where((lane >= origin) & (lane < origin + 3), one, nil)
        kaug[head] = jnp.where(own, k_ref[...], extra)
        vaug[head] = jnp.where(own, v_ref[...], extra)
        qz[head] = jnp.where(own, q_ref[...], nil)
        gz[head] = jnp.where(own, g_ref[...], nil)
        rows = slice(64 * head, 64 * head + 64)
        lse = split_rows(-lse_ref[0, head : head + 1, :])
        dsum = split_rows(-jnp.sum(gtf[rows] * ctxt_ref[rows, :], axis=0, keepdims=True))
        for dst, src, aug in ((qaug, qtv, lse), (gaug, gt, dsum)):
            dst[head, rows, :] = src[rows]
            dst[head, origin : origin + 16, :] = aug
            dst[head, origin + 16 : origin + 64, :] = pad

    dqt[...] = jnp.zeros_like(dqt)

    def step(idx, carry):
        rows = pl.ds(pl.multiple_of(idx * span, span), span)
        dv = None
        dk = None
        for head in range(2):
            s = dot_f32(kaug[head, rows, :], qaug[head])
            dp = dot_f32(vaug[head, rows, :], gaug[head])
            tops = []
            grads = []
            for part in range(2):
                offs = pl.ds(pl.multiple_of(seq - span * idx - 128 * part, 128), seq)
                p = jnp.exp(s[128 * part : 128 * part + 128] + base[head, :, offs])
                ds_ = p * dp[128 * part : 128 * part + 128]
                acc[head, :, offs] += ds_
                tops.append(p.astype(bf16))
                grads.append(ds_.astype(bf16))
            p = jnp.concatenate(tops, axis=0)
            ds_ = jnp.concatenate(grads, axis=0)
            now = dot_f32(p, gz[head])
            dv = now if dv is None else dv + now
            now = dot_f32(ds_, qz[head])
            dk = now if dk is None else dk + now
            dqt[64 * head : 64 * head + 64, :] += dot_f32(kt[64 * head : 64 * head + 64, rows], ds_)
        dv_ref[rows, :] = dv.astype(bf16)
        dk_ref[rows, :] = dk.astype(bf16)
        return carry

    lax.fori_loop(0, seq // span, step, 0)
    dq_ref[...] = dqt[...].T.astype(bf16)
    width = 2 * seq
    for head in range(2):
        total = acc[head, 0:8, :]
        for group in range(1, 16):
            total = total + pltpu.roll(acc[head, 8 * group : 8 * group + 8, :], width - 8 * group, 1)
        sub = lax.broadcasted_iota(jnp.int32, (8, width), 0)
        for bit in (1, 2, 4):
            total = jnp.where((sub & bit) != 0, pltpu.roll(total, width - bit, 1), total)
        diag_ref[0, head : head + 1, :] = jnp.sum(total, axis=0, keepdims=True)


def attend_back(q, k, v, g, u, ctxt, lse):
    seq, width = q.shape
    pairs = width // 128
    blk = pl.BlockSpec((seq, 128), lambda p: (0, p))
    return pl.pallas_call(
        attend_back_kernel,
        grid=(pairs,),
        in_specs=[
            blk, blk, blk, blk,
            pl.BlockSpec((1, 2, 2 * seq), lambda p: (p, 0, 0)),
            pl.BlockSpec((128, seq), lambda p: (p, 0)),
            pl.BlockSpec((1, 8, seq), lambda p: (p, 0, 0)),
        ],
        out_specs=[blk, blk, blk, pl.BlockSpec((1, 8, 2 * seq), lambda p: (p, 0, 0))],
        out_shape=[jax.ShapeDtypeStruct((seq, width), bf16)] * 3
        + [jax.ShapeDtypeStruct((pairs, 8, 2 * seq), f32)],
        scratch_shapes=[
            pltpu.VMEM((2, 128, 2 * seq), f32),
            pltpu.VMEM((2, 128, 2 * seq), f32),
            pltpu.VMEM((2, seq, 128), bf16),
            pltpu.VMEM((2, seq, 128), bf16),
            pltpu.VMEM((2, 128, seq), bf16),
            pltpu.VMEM((2, 128, seq), bf16),
            pltpu.VMEM((2, seq, 128), bf16),
            pltpu.VMEM((2, seq, 128), bf16),
            pltpu.VMEM((128, seq), bf16),
            pltpu.VMEM((128, seq), f32),
        ],
        compiler_params=pltpu.CompilerParams(vmem_limit_bytes=56 << 20),
        cost_estimate=pl.CostEstimate(
            flops=40 * seq * seq * width, bytes_accessed=20 * seq * width, transcendentals=seq * seq * 12
        ),
        name="attend_back",
    )(q, k, v, g, u, ctxt, lse)


def gelu_both(v):
    scale = 0.7978845608028654
    square = v * v
    t = jnp.tanh(scale * v * (1.0 + 0.044715 * square))
    half = 0.5 * (1.0 + t)
    slope = half + 0.5 * v * (1.0 - t * t) * (scale * (1.0 + 3 * 0.044715 * square))
    return v * half, slope


def expert_kernel(
    experts, capacity, tile,
    xs, gr_h, win_h, wout_h, rw,
    gback_o, prod_o, dwin_o, dwout_o, drw_o, shared_o,
    xall, gr, gp, win, wout, act, gpre, gback, gsend, prod, logit, acc_p, acc_g, xt, gpt, stage, dwt,
    send_x, recv_x, send_g, recv_g, local, out_sem, send_s, recv_s,
):
    me = lax.axis_index("expert")
    place = me // 2
    chips = experts // 2
    span = 2 * capacity
    width = xall.shape[1]
    hidden = win.shape[1]
    barrier = pltpu.get_barrier_semaphore()
    for k in range(1, experts):
        pl.semaphore_signal(barrier, inc=1, device_id={"expert": lax.rem(me + k, experts)})
    my_dp = lax.axis_index("dp")
    dp_x, dp_y = lax.rem(my_dp, 2), my_dp // 2
    peer_x, peer_y = my_dp + 1 - 2 * dp_x, my_dp + 2 - 4 * dp_y
    for peer in (peer_x, peer_y):
        pl.semaphore_signal(barrier, inc=1, device_id={"dp": peer})
    loads = [
        pltpu.make_async_copy(win_h, win, local.at[0]),
        pltpu.make_async_copy(wout_h, wout, local.at[1]),
        pltpu.make_async_copy(gr_h, gr, local.at[2]),
    ]
    rows_of = lambda who: pl.ds(pl.multiple_of(who * capacity, 16), capacity)
    own = pltpu.make_async_copy(xs.at[rows_of(me), :], xall.at[rows_of(me), :], local.at[3])
    own.start()
    for copy in loads:
        copy.start()
    pl.semaphore_wait(barrier, experts + 1)

    def partner(step):
        high, low = place // 2, lax.rem(place, 2)
        fhigh, flow = step // 2, lax.rem(step, 2)
        return 2 * (high + fhigh - 2 * high * fhigh) + low + flow - 2 * low * flow

    def send_rows(peer):
        return pltpu.make_async_remote_copy(
            src_ref=xs.at[rows_of(peer), :], dst_ref=xall.at[rows_of(me), :],
            send_sem=send_x.at[peer], recv_sem=recv_x.at[me], device_id={"expert": peer},
        )

    def got_rows(peer):
        return pltpu.make_async_remote_copy(
            src_ref=xs.at[rows_of(peer), :], dst_ref=xall.at[rows_of(peer), :],
            send_sem=send_x.at[peer], recv_sem=recv_x.at[peer], device_id={"expert": peer},
        )

    def send_back(peer):
        return pltpu.make_async_remote_copy(
            src_ref=gsend.at[rows_of(peer), :], dst_ref=gback.at[rows_of(me), :],
            send_sem=send_g.at[peer], recv_sem=recv_g.at[me], device_id={"expert": peer},
        )

    def got_back(peer):
        return pltpu.make_async_remote_copy(
            src_ref=gsend.at[rows_of(peer), :], dst_ref=gback.at[rows_of(peer), :],
            send_sem=send_g.at[peer], recv_sem=recv_g.at[peer], device_id={"expert": peer},
        )

    sibling = me + 1 - 2 * lax.rem(me, 2)
    send_rows(sibling).start()
    for step in range(1, chips):
        for core in range(2):
            send_rows(2 * partner(step) + lax.rem(me + core, 2)).start()
    for copy in loads:
        copy.wait()

    lanes = lax.broadcasted_iota(jnp.int32, (span, rw.shape[1]), 1)
    mine = jnp.where(lanes == me, 1.0, 0.0)

    def work(step, carry):
        where = partner(step)
        base = pl.multiple_of(where * span, 32)

        @pl.when(step == 0)
        def _():
            own.wait()
            got_rows(sibling).wait_recv()

        @pl.when(step > 0)
        def _():
            got_rows(2 * where).wait_recv()
            got_rows(2 * where + 1).wait_recv()

        rows = pl.ds(base, span)
        x = xall[rows, :]
        logits = jnp.where(lanes < experts, dot_f32(x, rw[...]), -1e30)
        weights = jnp.exp(logits - jnp.max(logits, axis=-1, keepdims=True))
        probs = weights / jnp.sum(weights, axis=-1, keepdims=True)
        gate = jnp.sum(probs * mine, axis=-1, keepdims=True)
        gp[rows, :] = (gr[rows, :].astype(f32) * gate).astype(bf16)
        acc_p[...] = jnp.zeros_like(acc_p)
        acc_g[...] = jnp.zeros_like(acc_g)

        def block(idx, carry):
            cols = pl.ds(pl.multiple_of(idx * tile, tile), tile)
            h = dot_f32(xall[rows, :], win[:, cols])
            grad = dot_nt(gp[rows, :], wout[cols, :])
            value, slope = gelu_both(h)
            value = value.astype(bf16)
            grad = (grad * slope).astype(bf16)
            act[rows, cols] = value
            gpre[rows, cols] = grad
            acc_p[...] += dot_f32(value, wout[cols, :])
            acc_g[...] += dot_nt(grad, win[:, cols])
            return carry

        lax.fori_loop(0, hidden // tile, block, 0)
        made = acc_p[...].astype(bf16)
        prod[rows, :] = made
        gate_grad = jnp.sum(gr[rows, :].astype(f32) * made.astype(f32), axis=-1, keepdims=True)
        low = (gate_grad * gate * (mine - probs)).astype(bf16)
        low = jnp.where(lanes < experts, low, jnp.zeros_like(low))
        logit[rows, :] = low
        gsend[rows, :] = (acc_g[...] + dot_nt(low, rw[...])).astype(bf16)

        @pl.when(step == 0)
        def _():
            send_back(sibling).start()

        @pl.when(step > 0)
        def _():
            send_back(2 * where).start()
            send_back(2 * where + 1).start()

        return carry

    lax.fori_loop(0, chips, work, 0)
    outs = [
        pltpu.make_async_copy(prod, prod_o, local.at[0]),
        pltpu.make_async_copy(gsend.at[rows_of(me), :], gback.at[rows_of(me), :], local.at[3]),
    ]
    for copy in outs:
        copy.start()
    xt[...] = xall[...].T
    gpt[...] = gp[...].T
    drw_o[...] = dot_f32(xt[...], logit[...])

    share = width // 4
    tiles = hidden // tile
    split = tiles // 2

    def left_copy(idx, block):
        cols = pl.ds(pl.multiple_of(idx * tile, tile), tile)
        rows = pl.ds(pl.multiple_of((1 - dp_x + 2 * block) * share, 16), share)
        return pltpu.make_async_remote_copy(
            src_ref=dwt.at[rows, cols], dst_ref=shared_o.at[pl.ds(block * share, share), cols],
            send_sem=send_s.at[block, idx], recv_sem=recv_s.at[block, idx], device_id={"dp": peer_x},
        )

    def right_copy(idx, block):
        cols = pl.ds(pl.multiple_of(idx * tile, tile), tile)
        rows = pl.ds(pl.multiple_of((2 - 2 * dp_y + block) * share, 16), share)
        dst_cols = pl.ds(pl.multiple_of((idx - split) * tile, tile), tile)
        return pltpu.make_async_remote_copy(
            src_ref=dwt.at[rows, cols], dst_ref=shared_o.at[pl.ds((2 + block) * share, share), dst_cols],
            send_sem=send_s.at[block, idx], recv_sem=recv_s.at[block, idx], device_id={"dp": peer_y},
        )

    def out_block(step, carry):
        idx = lax.rem(step, 2) * split + step // 2
        cols = pl.ds(pl.multiple_of(idx * tile, tile), tile)
        dwt[:, cols] = dot_f32(gpt[...], act[:, cols]).astype(bf16)

        @pl.when(idx < split)
        def _():
            for block in range(2):
                left_copy(idx, block).start()

        @pl.when(idx >= split)
        def _():
            for block in range(2):
                right_copy(idx, block).start()

        return carry

    lax.fori_loop(0, tiles, out_block, 0)
    whole = pltpu.make_async_copy(dwt, dwout_o, local.at[2])
    whole.start()

    def put(slot, cols):
        return pltpu.make_async_copy(stage.at[slot], dwin_o.at[:, cols], out_sem.at[slot])

    def in_block(idx, carry):
        cols = pl.ds(pl.multiple_of(idx * tile, tile), tile)
        slot = lax.rem(idx, 2)

        @pl.when(idx > 1)
        def _():
            put(slot, cols).wait()

        stage[slot] = dot_f32(xt[...], gpre[:, cols]).astype(bf16)
        put(slot, cols).start()
        return carry

    lax.fori_loop(0, tiles, in_block, 0)
    for slot in range(2):
        put(slot, pl.ds(0, tile)).wait()
    whole.wait()
    for copy in outs:
        copy.wait()
    for k in range(1, experts):
        peer = lax.rem(me + k, experts)
        got_rows(peer).wait_send()
        got_back(peer).wait_send()
        got_back(peer).wait_recv()
    back = pltpu.make_async_copy(gback, gback_o, local.at[1])
    back.start()
    for idx in range(tiles):
        for block in range(2):
            (left_copy if idx < split else right_copy)(idx, block).wait()
    back.wait()


def expert_pass(xs, gr, weight_in, weight_out, router_pad, experts, capacity):
    slots, width = xs.shape
    hidden = weight_in.shape[1]
    tile = 512
    span = 2 * capacity
    hbm = pl.BlockSpec(memory_space=pl.ANY)
    vmem = pl.BlockSpec(memory_space=pltpu.VMEM)
    return pl.pallas_call(
        functools.partial(expert_kernel, experts, capacity, tile),
        in_specs=[hbm, hbm, hbm, hbm, vmem],
        out_specs=[hbm, hbm, hbm, hbm, vmem, hbm],
        out_shape=[
            jax.ShapeDtypeStruct((slots, width), bf16),
            jax.ShapeDtypeStruct((slots, width), bf16),
            jax.ShapeDtypeStruct((width, hidden), bf16),
            jax.ShapeDtypeStruct((width, hidden), bf16),
            jax.ShapeDtypeStruct((width, router_pad.shape[1]), f32),
            jax.ShapeDtypeStruct((width, hidden // 2), bf16),
        ],
        scratch_shapes=[
            pltpu.VMEM((slots, width), bf16),
            pltpu.VMEM((slots, width), bf16),
            pltpu.VMEM((slots, width), bf16),
            pltpu.VMEM((width, hidden), bf16),
            pltpu.VMEM((hidden, width), bf16),
            pltpu.VMEM((slots, hidden), bf16),
            pltpu.VMEM((slots, hidden), bf16),
            pltpu.VMEM((slots, width), bf16),
            pltpu.VMEM((slots, width), bf16),
            pltpu.VMEM((slots, width), bf16),
            pltpu.VMEM((slots, router_pad.shape[1]), bf16),
            pltpu.VMEM((span, width), f32),
            pltpu.VMEM((span, width), f32),
            pltpu.VMEM((width, slots), bf16),
            pltpu.VMEM((width, slots), bf16),
            pltpu.VMEM((2, width, tile), bf16),
            pltpu.VMEM((width, hidden), bf16),
            pltpu.SemaphoreType.DMA((experts,)),
            pltpu.SemaphoreType.DMA((experts,)),
            pltpu.SemaphoreType.DMA((experts,)),
            pltpu.SemaphoreType.DMA((experts,)),
            pltpu.SemaphoreType.DMA((4,)),
            pltpu.SemaphoreType.DMA((2,)),
            pltpu.SemaphoreType.DMA((2, hidden // tile)),
            pltpu.SemaphoreType.DMA((2, hidden // tile)),
        ],
        compiler_params=pltpu.CompilerParams(
            vmem_limit_bytes=60 << 20, collective_id=1, has_side_effects=True
        ),
        cost_estimate=pl.CostEstimate(
            flops=12 * slots * width * hidden, bytes_accessed=8 * width * hidden, transcendentals=slots * hidden
        ),
        name="experts",
    )(xs, gr, weight_in, weight_out, router_pad)


def remote(src, dst, send_sem, recv_sem, axis, peer):
    return pltpu.make_async_remote_copy(
        src_ref=src, dst_ref=dst, send_sem=send_sem, recv_sem=recv_sem, device_id={axis: peer}
    )


def others(count, mine):
    return [lax.rem(mine + k, count) for k in range(1, count)]


PLAN = (
    (11, 16, 19, 22, 24),
    (12, 17, 20, 23, 25),
    (5, 13, 16, 19, 21),
    (9, 15, 18, 21, 23),
    (13, 18, 21, 24, 26),
    (17, 21, 24, 27, 29),
    (21, 24, 27, 29, 31),
)
OUTPUT_SLOT = 17
EXPERT_SLOTS = ((6, 2, 0), (14, 3, 0), (15, 2, 1), (22, 3, 1))


def back_kernel(
    groups, experts, pairs,
    q_ref, k_ref, v_ref, g_ref, ctxt_ref, wq, wk, wv, hot, gain, nl_h, tok_h, ghid_h, dwo_h, gain_two, router,
    eout_h, shared_h, ein_h, p_h, prod_h, hid_h, meta,
    wsum_o, ing_o, small_o, esum_o, out_o, eflip_o,
    acc, vaug, gaug, qz, gz, kt, dqt, pbuf, pret, hbuf, obuf, dall, nt, tok,
    part, r1, r2, r3, full, sbuf, srecv, sone, stwo, keep, other, final, flip,
    send1, recv1, send2, recv2, send3, recv3, send4, recv4, send5, recv5, send6, recv6, send7, recv7, local,
    send_a, recv_a, send_b, recv_b, out_sem, copy_sem, p_sem, send_p, recv_p, o_sem,
):
    seq = q_ref.shape[0]
    width = tok.shape[1]
    span = 256
    pair = pl.program_id(0)
    me = lax.axis_index("expert")
    my_dp = lax.axis_index("dp")
    core = lax.rem(me, 2)
    place = me // 2
    chips = experts // 2
    sibling = me + 1 - 2 * core
    half = width // 2
    piece = half // groups
    thick = part.shape[2]
    gain_rows = width // 128

    def half_rows(which):
        return pl.ds(pl.multiple_of(which * half, 16), half)

    def own_piece(which):
        return pl.ds(pl.multiple_of(core * half + which * piece, 16), piece)

    def copy1(c):
        return remote(part.at[c, half_rows(1 - core), :], r1.at[c], send1.at[c], recv1.at[c], "expert", sibling)

    def copy2(c, peer, slot):
        return remote(part.at[c, own_piece(peer), :], r2.at[c, slot], send2.at[c, peer], recv2.at[c, slot], "dp", peer)

    def copy3(c, peer, slot):
        return remote(
            r3.at[c, place], r3.at[c, slot], send3.at[c, peer], recv3.at[c, slot], "expert", 2 * peer + core
        )

    def copy4(c, peer, slot):
        return remote(
            full.at[c, own_piece(my_dp), :], full.at[c, own_piece(slot), :],
            send4.at[c, peer], recv4.at[c, slot], "dp", peer,
        )

    def copy5(c, which):
        return remote(
            full.at[c, half_rows(which), :], full.at[c, half_rows(which), :],
            send5.at[c], recv5.at[c], "expert", sibling,
        )

    def stage1(c):
        copy1(c).start()

    def stage2(c):
        copy1(c).wait_recv()
        part[c, half_rows(core), :] = (part[c, half_rows(core), :].astype(f32) + r1[c].astype(f32)).astype(bf16)
        for peer in others(groups, my_dp):
            copy2(c, peer, my_dp).start()

    def stage3(c):
        total = part[c, own_piece(my_dp), :].astype(f32)
        for peer in others(groups, my_dp):
            copy2(c, peer, peer).wait_recv()
            total = total + r2[c, peer].astype(f32)
        r3[c, place] = total.astype(bf16)
        for peer in others(chips, place):
            copy3(c, peer, place).start()

    def stage4(c):
        for peer in others(chips, place):
            copy3(c, peer, peer).wait_recv()
        total = r3[c, 0].astype(f32)
        for slot in range(1, chips):
            total = total + r3[c, slot].astype(f32)
        full[c, own_piece(my_dp), :] = total.astype(bf16)
        for peer in others(groups, my_dp):
            copy4(c, peer, my_dp).start()

    def stage5(c):
        for peer in others(groups, my_dp):
            copy4(c, peer, peer).wait_recv()
        copy5(c, core).start()

    def put_first(c):
        return pltpu.make_async_copy(full.at[c], wsum_o.at[0, :, thick * c : thick * c + thick], out_sem.at[c, 0])

    def put_pair(c, which):
        cols = pl.ds(128 * (c - 2) if isinstance(c, int) else pl.multiple_of(128 * (c - 2), 128), 128)
        return pltpu.make_async_copy(
            full.at[c, :, 128 * which : 128 * which + 128], wsum_o.at[1 + which, :, cols], out_sem.at[c, which]
        )

    def stage6(c):
        copy5(c, 1 - core).wait_recv()

        if c < 2:
            put_first(c).start()
        else:
            for which in range(3):
                put_pair(c, which).start()

    share = width // 4
    dp_x, dp_y = lax.rem(my_dp, 2), my_dp // 2
    peer_x, peer_y = my_dp + 1 - 2 * dp_x, my_dp + 2 - 4 * dp_y
    middle = keep.shape[1]
    left, right = pl.ds(0, middle), pl.ds(middle, middle)

    def share_rows(which):
        return pl.ds(pl.multiple_of(which * share, 16), share)

    def first_left(block):
        return remote(
            ein_h.at[share_rows(1 - dp_x + 2 * block), left], other.at[1, share_rows(block), :],
            send_a.at[0, block], recv_a.at[0, block], "dp", peer_x,
        )

    def first_right(block):
        return remote(
            ein_h.at[share_rows(2 - 2 * dp_y + block), right], other.at[1, share_rows(2 + block), :],
            send_a.at[1, block], recv_a.at[1, block], "dp", peer_y,
        )

    def second_left(which):
        return remote(
            keep.at[share_rows(1 - dp_y), :], final.at[which, :, left],
            send_b.at[which, 0], recv_b.at[which, 0], "dp", peer_y,
        )

    def second_right(which):
        return remote(
            keep.at[share_rows(2 + 1 - dp_x), :], final.at[which, :, right],
            send_b.at[which, 1], recv_b.at[which, 1], "dp", peer_x,
        )

    def own_loads(src):
        loads = []
        for block in range(2):
            loads.append(
                pltpu.make_async_copy(
                    src.at[share_rows(dp_x + 2 * block), left], keep.at[share_rows(block), :], copy_sem.at[block]
                )
            )
            loads.append(
                pltpu.make_async_copy(
                    src.at[share_rows(2 * dp_y + block), right], keep.at[share_rows(2 + block), :], copy_sem.at[2 + block]
                )
            )
        return loads

    def shared_load():
        return pltpu.make_async_copy(shared_h, other.at[0], copy_sem.at[4])

    def save(which):
        if which == 0:
            return pltpu.make_async_copy(flip, eflip_o, copy_sem.at[5])
        return pltpu.make_async_copy(final.at[1], esum_o, copy_sem.at[5])

    def experts_begin():
        for copy in own_loads(eout_h) + [shared_load()]:
            copy.start()
        for block in range(2):
            first_left(block).start()
            first_right(block).start()

    def experts_second(which):
        for copy in own_loads(eout_h if which == 0 else ein_h):
            copy.wait()
        if which == 0:
            shared_load().wait()
        else:
            for block in range(2):
                first_left(block).wait_recv()
                first_right(block).wait_recv()

        def block(idx, carry):
            rows = pl.ds(pl.multiple_of(idx * 64, 64), 64)
            keep[rows, :] = (keep[rows, :].astype(f32) + other[which, rows, :].astype(f32)).astype(bf16)
            return carry

        lax.fori_loop(0, width // 64, block, 0)
        second_left(which).start()
        second_right(which).start()

    def experts_last(which):
        second_left(which).wait()
        second_right(which).wait()

        def block(idx, carry):
            rows = pl.ds(pl.multiple_of(idx * 64, 64), 64)
            mine_left = pl.ds(pl.multiple_of(dp_y * share + idx * 64, 64), 64)
            mine_right = pl.ds(pl.multiple_of((2 + dp_x) * share + idx * 64, 64), 64)
            final[which, rows, left] = (final[which, rows, left].astype(f32) + keep[mine_left, :].astype(f32)).astype(bf16)
            final[which, rows, right] = (final[which, rows, right].astype(f32) + keep[mine_right, :].astype(f32)).astype(bf16)
            return carry

        lax.fori_loop(0, share // 64, block, 0)
        if which == 0:
            for side in range(2):
                cols = slice(middle * side, middle * side + middle)
                tall = jnp.concatenate([final[0, :, cols], jnp.zeros((256 - share, middle), bf16)], axis=0)
                flip[cols, :] = tall.T[:, :share]
            for copy in own_loads(ein_h):
                copy.start()
        else:
            save(0).wait()
        save(which).start()

    early = pl.ds(8 + hot.shape[0], sbuf.shape[0] - 8 - hot.shape[0])
    late = pl.ds(0, 8 + hot.shape[0])

    def copy6(part_idx, rows, peer, slot):
        return remote(
            sbuf.at[rows, :], srecv.at[slot, rows, :],
            send6.at[part_idx, peer], recv6.at[part_idx, slot], "expert", peer,
        )

    def copy7(part_idx, rows, peer, slot):
        return remote(
            sone.at[rows, :], stwo.at[slot, rows, :],
            send7.at[part_idx, peer], recv7.at[part_idx, slot], "dp", peer,
        )

    def small1(part_idx, rows):
        srecv[me, rows, :] = sbuf[rows, :]
        for peer in others(experts, me):
            copy6(part_idx, rows, peer, me).start()

    def small2(part_idx, rows):
        for peer in others(experts, me):
            copy6(part_idx, rows, peer, peer).wait_recv()
        total = srecv[0, rows, :]
        for slot in range(1, experts):
            total = total + srecv[slot, rows, :]
        sone[rows, :] = total
        stwo[my_dp, rows, :] = total
        for peer in others(groups, my_dp):
            copy7(part_idx, rows, peer, my_dp).start()

    def small3(part_idx, rows):
        for peer in others(groups, my_dp):
            copy7(part_idx, rows, peer, peer).wait_recv()
        total = stwo[0, rows, :]
        for slot in range(1, groups):
            total = total + stwo[slot, rows, :]
        small_o[rows, :] = total

    stages = (stage2, stage3, stage4, stage5, stage6)

    def advance(slot):
        for c, slots in enumerate(PLAN):
            for at, stage in reversed(list(zip(slots, stages))):
                if at < 4 * pairs:
                    pl.when(slot == at)(functools.partial(stage, c))

    def load_p(slot_idx, slot):
        rows = pl.ds(pl.multiple_of(lax.rem(slot_idx, 4) * span, span), span)
        return pltpu.make_async_copy(p_h.at[pl.ds(2 * (slot_idx // 4), 2), rows, :], pbuf.at[slot], p_sem.at[slot])

    slots_each = pret.shape[0] // experts

    def slot_rows(which):
        return pl.ds(pl.multiple_of(which * slots_each, 16), slots_each)

    def give_back(peer):
        return remote(
            prod_h.at[slot_rows(peer), :], pret.at[slot_rows(me), :], send_p.at[peer], recv_p.at[me], "expert", peer
        )

    def got_back(peer):
        return remote(
            prod_h.at[slot_rows(peer), :], pret.at[slot_rows(peer), :], send_p.at[peer], recv_p.at[peer], "expert", peer
        )

    def own_back():
        return pltpu.make_async_copy(prod_h.at[slot_rows(me), :], pret.at[slot_rows(me), :], o_sem.at[0])

    def out_rows(block):
        return pl.ds(block * span, span)

    def load_hidden(block):
        return pltpu.make_async_copy(hid_h.at[out_rows(block), :], hbuf, o_sem.at[1])

    def save_out(block):
        return pltpu.make_async_copy(obuf, out_o.at[out_rows(block), :], o_sem.at[2])

    def output_block(block):
        if block == 0:
            own_back().wait()
            for peer in others(experts, me):
                got_back(peer).wait_recv()
        load_hidden(block).wait()
        where = lax.broadcasted_iota(jnp.int32, (span, pret.shape[0]), 1).astype(f32)
        pick = jnp.where(meta[out_rows(block), 1:2] == where, 1.0, 0.0).astype(bf16)
        gathered = dot_f32(pick, pret[...])
        if block > 0:
            save_out(block - 1).wait()
        obuf[...] = (hbuf[...] + meta[out_rows(block), 0:1] * gathered).astype(bf16)
        save_out(block).start()
        if (block + 1) * span < seq:
            load_hidden(block + 1).start()

    loads = [
        pltpu.make_async_copy(nl_h, tok, local.at[0]),
        pltpu.make_async_copy(ghid_h, ing_o, local.at[2]),
        pltpu.make_async_copy(dwo_h.at[:, 0:thick], part.at[0], local.at[3]),
        pltpu.make_async_copy(dwo_h.at[:, thick : 2 * thick], part.at[1], local.at[4]),
    ]

    @pl.when(pair == 0)
    def _():
        barrier = pltpu.get_barrier_semaphore()
        for peer in others(experts, me):
            pl.semaphore_signal(barrier, inc=1, device_id={"expert": peer})
        for peer in others(groups, my_dp):
            pl.semaphore_signal(barrier, inc=1, device_id={"dp": peer})
        for copy in loads:
            copy.start()
        load_p(0, 0).start()
        own_back().start()
        load_hidden(0).start()
        sbuf[...] = jnp.zeros_like(sbuf)
        first_row = 8 + hot.shape[0]
        by_expert = router[...].T
        for tile in range(gain_rows):
            lanes = slice(128 * tile, 128 * tile + 128)
            sbuf[first_row + tile : first_row + tile + 1, :] = gain_two[:, lanes]
            for which in range(experts):
                row = first_row + 8 + gain_rows * which + tile
                sbuf[row : row + 1, :] = by_expert[which : which + 1, lanes]
        for copy in loads:
            copy.wait()
        nt[...] = tok[...].T
        pl.semaphore_wait(barrier, experts + groups - 2)
        stage1(0)
        stage1(1)
        small1(0, early)
        experts_begin()
        for peer in others(experts, me):
            give_back(peer).start()

    mine = pl.ds(pl.multiple_of(128 * pair, 128), 128)
    lane = lax.broadcasted_iota(jnp.int32, (seq, 128), 1)
    gt = g_ref[...].T
    kt[...] = k_ref[...].T
    gtf = gt.astype(f32)
    pad = jnp.zeros((48, seq), bf16)
    one = jnp.ones((seq, 128), bf16)
    nil = jnp.zeros((seq, 128), bf16)
    acc[...] = jnp.zeros_like(acc)
    for head in range(2):
        own = (lane < 64) if head == 0 else (lane >= 64)
        origin = 64 if head == 0 else 0
        extra = jnp.where((lane >= origin) & (lane < origin + 3), one, nil)
        vaug[head] = jnp.where(own, v_ref[...], extra)
        qz[head] = jnp.where(own, q_ref[...], nil)
        gz[head] = jnp.where(own, g_ref[...], nil)
        rows = slice(64 * head, 64 * head + 64)
        gaug[head, rows, :] = gt[rows]
        gaug[head, origin : origin + 16, :] = split_rows(
            -jnp.sum(gtf[rows] * ctxt_ref[rows, :], axis=0, keepdims=True)
        )
        gaug[head, origin + 16 : origin + 64, :] = pad

    dqt[...] = jnp.zeros_like(dqt)

    def step(idx, carry):
        rows = pl.ds(pl.multiple_of(idx * span, span), span)
        dv = None
        dk = None
        slot = lax.rem(idx, 2)
        load_p(4 * pair + idx, slot).wait()

        @pl.when(4 * pair + idx + 1 < 4 * pairs)
        def _():
            load_p(4 * pair + idx + 1, 1 - slot).start()

        for head in range(2):
            dp = dot_f32(vaug[head, rows, :], gaug[head])
            grads = []
            for part_idx in range(2):
                offs = pl.ds(pl.multiple_of(seq - span * idx - 128 * part_idx, 128), seq)
                band = slice(128 * part_idx, 128 * part_idx + 128)
                ds_ = pbuf[slot, head, band, :].astype(f32) * dp[band]
                acc[head, :, offs] += ds_
                grads.append(ds_.astype(bf16))
            ds_ = jnp.concatenate(grads, axis=0)
            now = dot_f32(pbuf[slot, head], gz[head])
            dv = now if dv is None else dv + now
            now = dot_f32(ds_, qz[head])
            dk = now if dk is None else dk + now
            dqt[64 * head : 64 * head + 64, :] += dot_f32(kt[64 * head : 64 * head + 64, rows], ds_)
        dall[1, rows, mine] = dk.astype(bf16)
        dall[2, rows, mine] = dv.astype(bf16)
        advance(4 * pair + idx)

        for block in range(seq // span):
            @pl.when(4 * pair + idx == OUTPUT_SLOT + block)
            def _():
                output_block(block)

        for at, task, which in EXPERT_SLOTS:
            @pl.when(4 * pair + idx == at)
            def _():
                (experts_second if task == 2 else experts_last)(which)

        @pl.when(4 * pair + idx == 7)
        def _():
            small2(0, early)

        @pl.when(4 * pair + idx == 11)
        def _():
            small3(0, early)

        return carry

    lax.fori_loop(0, seq // span, step, 0)
    dall[0, :, mine] = dqt[...].T.astype(bf16)
    twice = 2 * seq
    sub = lax.broadcasted_iota(jnp.int32, (8, twice), 0)
    head_lane = lax.broadcasted_iota(jnp.int32, (hot.shape[0], 128), 1)
    rel_rows = slice(8, 8 + hot.shape[0])
    for head in range(2):
        total = acc[head, 0:8, :]
        for group in range(1, 16):
            total = total + pltpu.roll(acc[head, 8 * group : 8 * group + 8, :], twice - 8 * group, 1)
        for bit in (1, 2, 4):
            total = jnp.where((sub & bit) != 0, pltpu.roll(total, twice - bit, 1), total)
        diag = jnp.sum(total, axis=0, keepdims=True)
        sums = jnp.sum(hot[...] * diag, axis=1, keepdims=True)
        sbuf[rel_rows, :] = jnp.where(head_lane == 2 * pair + head, sums, sbuf[rel_rows, :])

    def weight_block(idx, carry):
        rows = pl.ds(pl.multiple_of(idx * 256, 256), 256)
        grads = jnp.concatenate([dall[which, :, mine] for which in range(3)], axis=1)
        part[pair + 2, rows, :] = dot_f32(nt[rows, :], grads).astype(bf16)
        return carry

    lax.fori_loop(0, width // 256, weight_block, 0)
    stage1(pair + 2)

    @pl.when(pair == pairs - 1)
    def _():
        def token_block(idx, carry):
            rows = pl.ds(pl.multiple_of(idx * 256, 256), 256)
            grad = (
                dot_nt(dall[0, rows, :], wq[...])
                + dot_nt(dall[1, rows, :], wk[...])
                + dot_nt(dall[2, rows, :], wv[...])
            )
            values = tok[rows, :].astype(f32)
            scale = lax.rsqrt(jnp.mean(values * values, axis=-1, keepdims=True) + epsilon)
            weighted = grad * gain[0:1, :]
            inner = jnp.mean(weighted * values, axis=-1, keepdims=True)
            ing_o[rows, :] += scale * weighted - values * (scale * scale * scale * inner)
            return carry + jnp.sum(grad * values * scale, axis=0, keepdims=True)

        reload = pltpu.make_async_copy(tok_h, tok, local.at[1])
        reload.start()
        last = pairs + 1
        first = 4 * pairs
        older = sorted(
            (at, c, stage)
            for c, slots in enumerate(PLAN)
            for stage, at in enumerate(slots)
            if at >= first
        )

        def drain(until):
            while older and older[0][0] < first + until:
                _, c, stage = older.pop(0)
                stages[stage](c)

        def tokens_done(lower, upper, gain_grad):
            return lax.fori_loop(lower, upper, token_block, gain_grad)

        drain(1)
        reload.wait()
        gain_grad = tokens_done(0, 1, jnp.zeros((1, width), f32))
        stage2(last)
        drain(2)
        gain_grad = tokens_done(1, seq // 512, gain_grad)
        drain(4)
        gain_grad = tokens_done(seq // 512, seq // 256, gain_grad)
        stage3(last)
        for row in range(gain_rows):
            sbuf[row : row + 1, :] = gain_grad[:, 128 * row : 128 * row + 128]
        small1(1, late)
        drain(8)
        small2(1, late)
        stage4(last)
        drain(99)
        small3(1, late)
        stage5(last)
        stage6(last)
        for c in range(2):
            put_first(c).wait()
        save(1).wait()
        save_out(seq // span - 1).wait()
        for peer in others(experts, me):
            give_back(peer).wait_send()
        for block in range(2):
            first_left(block).wait_send()
            first_right(block).wait_send()

        def finish(c, carry):
            copy1(c).wait_send()
            for peer in others(groups, my_dp):
                copy2(c, peer, my_dp).wait_send()
                copy4(c, peer, my_dp).wait_send()
            for peer in others(chips, place):
                copy3(c, peer, place).wait_send()
            copy5(c, core).wait_send()

            @pl.when(c >= 2)
            def _():
                for which in range(3):
                    put_pair(c, which).wait()

            return carry

        lax.fori_loop(0, pairs + 2, finish, 0)
        for part_idx, rows in ((0, early), (1, late)):
            for peer in others(experts, me):
                copy6(part_idx, rows, peer, me).wait_send()
            for peer in others(groups, my_dp):
                copy7(part_idx, rows, peer, my_dp).wait_send()


def back_pass(
    q, k, v, g, ctxt, wq, wk, wv, hot, gain, normed_low, tokens, grad_hidden, dwo, gain_two, router,
    expert_out_grad, shared, expert_in_grad, weights, produced, hidden_rows, meta, groups, experts
):
    seq, width = q.shape
    pairs = width // 128
    chunks = pairs + 2
    small_shape = (8 + hot.shape[0] + 8 + width // 128 * experts, 128)
    hidden = expert_in_grad.shape[1]
    thick = width // 2
    half = width // 2
    piece = half // groups
    chips = experts // 2
    blk = pl.BlockSpec((seq, 128), lambda p: (0, p))
    hbm = pl.BlockSpec(memory_space=pl.ANY)
    fixed = lambda shape: pl.BlockSpec(shape, lambda p: (0,) * len(shape), pipeline_mode=pl.Buffered(1))
    dma = pltpu.SemaphoreType.DMA
    return pl.pallas_call(
        functools.partial(back_kernel, groups, experts, pairs),
        grid=(pairs,),
        in_specs=[
            blk, blk, blk, blk,
            pl.BlockSpec((128, seq), lambda p: (p, 0)),
            fixed((width, width)), fixed((width, width)), fixed((width, width)),
            fixed(hot.shape), fixed(gain.shape),
            hbm, hbm, hbm, hbm, fixed(gain_two.shape), fixed(router.shape), hbm, hbm, hbm,
            hbm, hbm, hbm, fixed(meta.shape),
        ],
        out_specs=[hbm, fixed((seq, width)), fixed(small_shape), hbm, hbm, hbm],
        out_shape=[
            jax.ShapeDtypeStruct((4, width, width), bf16),
            jax.ShapeDtypeStruct((seq, width), f32),
            jax.ShapeDtypeStruct(small_shape, f32),
            jax.ShapeDtypeStruct((width // 4, hidden), bf16),
            jax.ShapeDtypeStruct((seq, width), bf16),
            jax.ShapeDtypeStruct((hidden, width // 4), bf16),
        ],
        scratch_shapes=[
            pltpu.VMEM((2, 128, 2 * seq), f32),
            pltpu.VMEM((2, seq, 128), bf16),
            pltpu.VMEM((2, 128, seq), bf16),
            pltpu.VMEM((2, seq, 128), bf16),
            pltpu.VMEM((2, seq, 128), bf16),
            pltpu.VMEM((128, seq), bf16),
            pltpu.VMEM((128, seq), f32),
            pltpu.VMEM((2, 2, 256, seq), bf16),
            pltpu.VMEM(produced.shape, bf16),
            pltpu.VMEM((256, width), f32),
            pltpu.VMEM((256, width), bf16),
            pltpu.VMEM((3, seq, width), bf16),
            pltpu.VMEM((width, seq), bf16),
            pltpu.VMEM((seq, width), bf16),
            pltpu.VMEM((chunks, width, thick), bf16),
            pltpu.VMEM((chunks, half, thick), bf16),
            pltpu.VMEM((chunks, groups, piece, thick), bf16),
            pltpu.VMEM((chunks, chips, piece, thick), bf16),
            pltpu.VMEM((chunks, width, thick), bf16),
            pltpu.VMEM(small_shape, f32),
            pltpu.VMEM((experts,) + small_shape, f32),
            pltpu.VMEM(small_shape, f32),
            pltpu.VMEM((groups,) + small_shape, f32),
            pltpu.VMEM((width, hidden // 2), bf16),
            pltpu.VMEM((2, width, hidden // 2), bf16),
            pltpu.VMEM((2, width // 4, hidden), bf16),
            pltpu.VMEM((hidden, width // 4), bf16),
            dma((chunks,)), dma((chunks,)),
            dma((chunks, groups)), dma((chunks, groups)),
            dma((chunks, chips)), dma((chunks, chips)),
            dma((chunks, groups)), dma((chunks, groups)),
            dma((chunks,)), dma((chunks,)),
            dma((2, experts)), dma((2, experts)),
            dma((2, groups)), dma((2, groups)),
            dma((6,)),
            dma((2, 2)), dma((2, 2)),
            dma((2, 2)), dma((2, 2)),
            dma((chunks, 3)), dma((6,)),
            dma((2,)), dma((experts,)), dma((experts,)), dma((3,)),
        ],
        compiler_params=pltpu.CompilerParams(
            vmem_limit_bytes=62 << 20, collective_id=2, has_side_effects=True
        ),
        cost_estimate=pl.CostEstimate(
            flops=40 * seq * seq * width + 12 * seq * width * width,
            bytes_accessed=40 * seq * width, transcendentals=seq * seq * 12,
        ),
        name="attend_back",
    )(
        q, k, v, g, ctxt, wq, wk, wv, hot, gain, normed_low, tokens, grad_hidden, dwo, gain_two, router,
        expert_out_grad, shared, expert_in_grad, weights, produced, hidden_rows, meta,
    )


def rms_backward(grad_norm, values, row_scale, gain_vec):
    weighted = grad_norm * gain_vec
    gain_grad = jnp.sum(grad_norm * values * row_scale, axis=0)
    grad_in = row_scale * weighted - values * row_scale**3 * jnp.mean(
        weighted * values, axis=-1, keepdims=True
    )
    return grad_in, gain_grad


def rms_forward(values, gain_vec):
    row_scale = lax.rsqrt(jnp.mean(values * values, axis=-1, keepdims=True) + epsilon)
    return values * row_scale * gain_vec, row_scale


def gelu_tanh(values):
    return jax.nn.gelu(values, approximate=True)


def contract(left, right, dims):
    return lax.dot_general(left, right, (((dims[0],), (dims[1],)), ((), ())), preferred_element_type=f32)


def exchange(rows, experts):
    slots, width = rows.shape
    rows = rows.reshape(experts, slots // experts, width)
    return lax.all_to_all(rows, "expert", split_axis=0, concat_axis=0, tiled=True).reshape(slots, width)


def expert_native(send, grad_recv, weight_in, weight_out, router_w, experts):
    received = exchange(send, experts)
    own = lax.axis_index("expert")
    own_hot = (jnp.arange(experts, dtype=jnp.int32) == own).astype(f32)[None, :]
    probs = jax.nn.softmax(contract(received, router_w, (1, 0)), axis=-1)
    gate = jnp.sum(probs * own_hot, axis=-1, keepdims=True)
    grad_recv_f = grad_recv.astype(f32)
    grad_produced = (grad_recv_f * gate).astype(bf16)
    preact = contract(received, weight_in, (1, 0))
    gelu_values, gelu_pullback = jax.vjp(gelu_tanh, preact)
    active = gelu_values.astype(bf16)
    produced = contract(active, weight_out, (1, 0)).astype(bf16)
    gate_grad = jnp.sum(grad_recv_f * produced.astype(f32), axis=-1, keepdims=True)
    logit_low = (gate_grad * gate * (own_hot - probs)).astype(bf16)
    grad_active = contract(grad_produced, weight_out, (1, 1))
    grad_preact = gelu_pullback(grad_active)[0].astype(bf16)
    grad_received = contract(grad_preact, weight_in, (1, 1)) + contract(logit_low, router_w, (1, 1))
    grad_rows = exchange(grad_received.astype(bf16), experts)
    in_grad = contract(received, grad_preact, (0, 0)).astype(bf16)
    out_grad_t = contract(grad_produced, active, (0, 0)).astype(bf16)
    router_grad = contract(received, logit_low, (0, 0))
    return grad_rows, produced, in_grad, out_grad_t, router_grad


def tail_native(tokens, gain, normed_low, dq, dk, dv, wq, wk, wv, grad_hidden, dwo, small):
    tokens_f = tokens.astype(f32)
    grads = jnp.stack([dwo.astype(f32)] + [contract(normed_low, d, (0, 0)) for d in (dq, dk, dv)])
    grad_normed = contract(dq, wq, (1, 1)) + contract(dk, wk, (1, 1)) + contract(dv, wv, (1, 1))
    _, scale = rms_forward(tokens_f, gain)
    grad_tokens, gain_grad = rms_backward(grad_normed, tokens_f, scale, gain)
    grads, gain_grad, small = lax.psum((grads, gain_grad, small), ("dp", "expert"))
    return grads, grad_hidden + grad_tokens, gain_grad, small


def on_device(
    tokens, gain_one, query_w, key_w, value_w, out_w, rel_table, gain_two, router_w,
    expert_in, expert_out, routes, buckets, cotangent,
):
    seq_len, width = tokens.shape
    heads = rel_table.shape[1]
    groups = lax.axis_size("dp")
    experts = lax.axis_size("expert")
    capacity = (5 * seq_len + 4 * experts - 1) // (4 * experts)
    slots = experts * capacity
    weight_in = expert_in[0]
    weight_out = expert_out[0]
    kernels = capacity % 16 == 0 and experts == 8 and groups == 4

    route_ids = routes[:, 0]
    route_hot = route_ids[:, None] == jnp.arange(experts, dtype=jnp.int32)[None, :]
    route_int = route_hot.astype(jnp.int32)
    route_float = route_hot.astype(f32)
    position = jnp.sum((jnp.cumsum(route_int, axis=0) - 1) * route_int, axis=1)
    slot_index = jnp.where(position < capacity, route_ids * capacity + position, slots)
    pick = (jnp.arange(slots, dtype=jnp.int32)[:, None] == slot_index[None, :]).astype(bf16)

    def scatter_rows(rows):
        return contract(pick, rows, (1, 0)).astype(bf16)

    def gather_rows(rows):
        return contract(pick, rows, (0, 0))

    tokens_f = tokens.astype(f32)
    gains = jnp.stack([gain_one, gain_two])
    if kernels:
        queries, key_rows, value_rows, normed_low, grad_send, slot_row, slot_column = first_pass(
            tokens, gains, query_w, key_w, value_w, routes.reshape(1, seq_len), cotangent, capacity, experts
        )
    else:
        grad_send = scatter_rows(cotangent)
        normed_low = rms_forward(tokens_f, gain_one)[0].astype(bf16)
        queries = contract(normed_low, query_w, (1, 0)).astype(bf16)
        key_rows = contract(normed_low, key_w, (1, 0)).astype(bf16)
        value_rows = contract(normed_low, value_w, (1, 0)).astype(bf16)
    reach = jnp.concatenate([buckets, jnp.full((1,), -1, jnp.int32)])[::-1]
    bucket_hot = (jnp.arange(rel_table.shape[0], dtype=jnp.int32)[:, None] == reach[None, :]).astype(f32)
    spread = jnp.einsum("bh,bx->hx", rel_table, bucket_hot, precision=highest)
    spread = spread.reshape(heads // 2, 2, 2 * seq_len)
    context, context_t, logsum, weights, grad_recv = attend(
        queries, key_rows, value_rows, spread, grad_send, experts if kernels else 0
    )
    if kernels:
        router_pad = jnp.pad(router_w, ((0, 0), (0, 128 - experts)))
        hidden, send, meta = middle_pass(
            tokens, context, out_w, gains, router_pad, slot_row, slot_column, slots, experts
        )
        grad_rows, produced, in_grad, out_grad_t, router_grad, shared = expert_pass(
            send, grad_recv, weight_in, weight_out, router_pad, experts, capacity
        )
        grad_hidden, out_w_grad, grad_context, gain_two_grad = combine_pass(
            grad_rows, hidden, cotangent, gains, context, out_w, meta
        )
    else:
        grad_recv = exchange(grad_send, experts)
        hidden = tokens_f + contract(context, out_w, (1, 0))
        normed_two, scale_two = rms_forward(hidden, gain_two)
        normed_two_low = normed_two.astype(bf16)
        grad_rows, produced, in_grad, out_grad_t, router_grad = expert_native(
            scatter_rows(normed_two_low), grad_recv, weight_in, weight_out, router_w, experts
        )
        router_probs = jax.nn.softmax(contract(normed_two_low, router_w, (1, 0)), axis=-1)
        gate_value = jnp.sum(router_probs * route_float, axis=-1, keepdims=True)
        grad_normed_two = gather_rows(grad_rows)
        grad_hidden_norm, gain_two_grad = rms_backward(grad_normed_two, hidden, scale_two, gain_two)
        grad_hidden = cotangent.astype(f32) + grad_hidden_norm
        branch_low = grad_hidden.astype(bf16)
        out_w_grad = contract(context, branch_low, (0, 0)).astype(bf16)
        grad_context = contract(branch_low, out_w, (1, 1)).astype(bf16)

    if kernels:
        grads, input_grad, small, in_share, output, out_share = back_pass(
            queries, key_rows, value_rows, grad_context, context_t, query_w, key_w, value_w,
            bucket_hot, gains, normed_low, tokens, grad_hidden, out_w_grad,
            gain_two_grad, router_grad,
            out_grad_t, shared, in_grad, weights, produced, hidden,
            meta, groups, experts,
        )
        tiles = width // 128
        first = 8 + rel_table.shape[0]
        gain_one_grad = small[:tiles].reshape(-1)
        rel_grad = small[8:first, :heads]
        gain_two_grad = small[first : first + tiles].reshape(-1)
        router_grad = small[first + 8 :].reshape(experts, width).T
    else:
        output = (hidden + gate_value * gather_rows(exchange(produced, experts))).astype(bf16)
        in_share = lax.psum_scatter(in_grad, "dp", scatter_dimension=0, tiled=True)
        out_share = lax.psum_scatter(out_grad_t, "dp", scatter_dimension=0, tiled=True).T
        query_grad, key_grad, value_grad, diagonals = attend_back(
            queries, key_rows, value_rows, grad_context, spread, context_t, logsum
        )
        diagonals = diagonals[:, :2].reshape(heads, 2 * seq_len)
        rel_grad = jnp.einsum("bx,hx->bh", bucket_hot, diagonals, precision=highest)
        grads, input_grad, gain_one_grad, small = tail_native(
            tokens, gain_one, normed_low, query_grad, key_grad, value_grad,
            query_w, key_w, value_w, grad_hidden, out_w_grad, (rel_grad, gain_two_grad, router_grad),
        )
        rel_grad, gain_two_grad, router_grad = small
    grads = grads.astype(f32)
    return (
        output, input_grad, grads[1], grads[2], grads[3], grads[0], rel_grad,
        gain_one_grad, gain_two_grad, router_grad, in_share.astype(f32)[None], out_share.astype(f32)[None],
    )


def solution(mesh):
    rows = P(("dp", "expert"), None)
    whole = P()
    split = P("expert", None, None)
    return jax.shard_map(
        on_device,
        mesh=mesh,
        in_specs=(
            rows, whole, whole, whole, whole, whole, whole, whole, whole, split, split, rows, whole, rows,
        ),
        out_specs=(
            rows, rows, whole, whole, whole, whole, whole, whole, whole, whole,
            P("expert", "dp", None), P("expert", None, "dp"),
        ),
        check_vma=False,
    )
```

```python
import functools

import jax
import jax.numpy as jnp
from jax import lax
from jax.experimental import pallas as pl
from jax.experimental.pallas import tpu as pltpu
from jax.sharding import PartitionSpec as P

bf16 = jnp.bfloat16
f32 = jnp.float32
epsilon = 1e-06
highest = lax.Precision.HIGHEST

def dot_f32(left, right):
    return lax.dot_general(left, right, (((1,), (0,)), ((), ())), preferred_element_type=f32)


def dot_nt(left, right):
    return lax.dot_general(left, right, (((1,), (1,)), ((), ())), preferred_element_type=f32)


def fill_toeplitz(base_ref, head, row):
    rows, width = base_ref.shape[1:]
    spread = jnp.broadcast_to(row, (8, width))
    eight = pltpu.roll(spread, 0, 1, stride=1, stride_axis=0)
    for group in range(rows // 8):
        base_ref[head, 8 * group : 8 * group + 8, :] = (
            eight if group == 0 else pltpu.roll(eight, 8 * group, 1)
        )


def attend_kernel(
    experts, q_ref, k_ref, v_ref, u_ref, gsend_h, ctx_ref, ctxt_ref, lse_ref, p_h, grecv_h,
    base, qt, vt, s_scr, p_scr, p_sem, send_g, recv_g, own_sem,
):
    seq = q_ref.shape[0]
    span = 256
    half = seq
    qt[...] = q_ref[...].T
    vt[...] = v_ref[...].T
    for head in range(2):
        fill_toeplitz(base, head, u_ref[0, head : head + 1, :])
    zeros = jnp.zeros((64, span), bf16)
    pair = pl.program_id(0)

    if experts:
        me = lax.axis_index("expert")
        count = grecv_h.shape[0] // experts
        rows_of = lambda who: pl.ds(pl.multiple_of(who * count, 16), count)
        peers = [lax.rem(me + k, experts) for k in range(1, experts)]
        barrier = pltpu.get_barrier_semaphore()
        own = pltpu.make_async_copy(gsend_h.at[rows_of(me), :], grecv_h.at[rows_of(me), :], own_sem)

        def give(peer, slot):
            return pltpu.make_async_remote_copy(
                src_ref=gsend_h.at[rows_of(peer), :], dst_ref=grecv_h.at[rows_of(slot), :],
                send_sem=send_g.at[peer], recv_sem=recv_g.at[slot], device_id={"expert": peer},
            )

        @pl.when(pair == 0)
        def _():
            for peer in peers:
                pl.semaphore_signal(barrier, inc=1, device_id={"expert": peer})
            own.start()

    def save(idx, slot):
        cols = pl.ds(pl.multiple_of(idx * span, span), span)
        return pltpu.make_async_copy(p_scr.at[slot], p_h.at[pl.ds(2 * pair, 2), :, cols], p_sem.at[slot])

    def step(idx, carry):
        slot = lax.rem(idx, 2)

        @pl.when((pair > 0) | (idx > 1))
        def _():
            save(idx, slot).wait()

        cols = pl.ds(pl.multiple_of(idx * span, span), span)
        outs = []
        for head in range(2):
            part = qt[64 * head : 64 * head + 64, cols]
            rhs = jnp.concatenate([part, zeros] if head == 0 else [zeros, part], axis=0)
            peak = None
            for kb in range(seq // 128):
                rows = slice(128 * kb, 128 * kb + 128)
                offs = pl.multiple_of(half + span * idx - 128 * kb, 128)
                s = dot_f32(k_ref[rows, :], rhs) + base[head, :, pl.ds(offs, span)]
                s_scr[head, rows, :] = s
                now = jnp.max(s.reshape(16, 8, span), axis=0)
                peak = now if peak is None else jnp.maximum(peak, now)
            peak = jnp.max(peak, axis=0, keepdims=True)
            total = None
            for kb in range(seq // 128):
                rows = slice(128 * kb, 128 * kb + 128)
                e = jnp.exp(s_scr[head, rows, :] - peak)
                s_scr[head, rows, :] = e
                now = jnp.sum(e.reshape(16, 8, span), axis=0)
                total = now if total is None else total + now
            total = jnp.sum(total, axis=0, keepdims=True)
            inv = 1.0 / total
            for kb in range(seq // 128):
                rows = slice(128 * kb, 128 * kb + 128)
                p_scr[slot, head, rows, :] = (s_scr[head, rows, :] * inv).astype(bf16)
            lse_ref[0, head : head + 1, cols] = peak + jnp.log(total)
            outs.append(dot_f32(vt[64 * head : 64 * head + 64, :], p_scr[slot, head]))
        save(idx, slot).start()
        both = jnp.concatenate(outs, axis=0)
        ctxt_ref[:, cols] = both
        ctx_ref[cols, :] = both.T.astype(bf16)
        return carry

    if experts:
        @pl.when(pair == 0)
        def _():
            pl.semaphore_wait(barrier, experts - 1)
            for peer in peers:
                give(peer, me).start()

    lax.fori_loop(0, seq // span, step, 0)

    @pl.when(pair == pl.num_programs(0) - 1)
    def _():
        for slot in range(2):
            save(slot, slot).wait()
        if experts:
            own.wait()
            for peer in peers:
                give(peer, me).wait_send()
                give(peer, peer).wait_recv()


def attend(q, k, v, u, gsend, experts=0):
    seq, width = q.shape
    pairs = width // 128
    blk = pl.BlockSpec((seq, 128), lambda p: (0, p))
    dma = pltpu.SemaphoreType.DMA
    return pl.pallas_call(
        functools.partial(attend_kernel, experts),
        grid=(pairs,),
        in_specs=[
            blk, blk, blk, pl.BlockSpec((1, 2, 2 * seq), lambda p: (p, 0, 0)), pl.BlockSpec(memory_space=pl.ANY),
        ],
        out_specs=[
            blk,
            pl.BlockSpec((128, seq), lambda p: (p, 0)),
            pl.BlockSpec((1, 8, seq), lambda p: (p, 0, 0)),
            pl.BlockSpec(memory_space=pl.ANY),
            pl.BlockSpec(memory_space=pl.ANY),
        ],
        out_shape=[
            jax.ShapeDtypeStruct((seq, width), bf16),
            jax.ShapeDtypeStruct((width, seq), f32),
            jax.ShapeDtypeStruct((pairs, 8, seq), f32),
            jax.ShapeDtypeStruct((2 * pairs, seq, seq), bf16),
            jax.ShapeDtypeStruct(gsend.shape, bf16),
        ],
        scratch_shapes=[
            pltpu.VMEM((2, 128, 2 * seq), f32),
            pltpu.VMEM((128, seq), bf16),
            pltpu.VMEM((128, seq), bf16),
            pltpu.VMEM((2, seq, 256), f32),
            pltpu.VMEM((2, 2, seq, 256), bf16),
            dma((2,)),
            dma((max(experts, 1),)), dma((max(experts, 1),)), dma(()),
        ],
        compiler_params=pltpu.CompilerParams(
            vmem_limit_bytes=62 << 20, has_side_effects=experts > 0, collective_id=3 if experts else None
        ),
        name="attend",
    )(q, k, v, u, gsend)


def first_kernel(
    capacity, experts, tok, gain, wq, wk, wv, route, cot, q_o, k_o, v_o, nl_o, gsend_o, slot_o, column_o, slot
):
    step = pl.program_id(0)
    slots = experts * capacity
    seq = route.shape[1]

    @pl.when(step == 0)
    def _():
        lane = lax.broadcasted_iota(jnp.int32, (8, seq), 1)
        hot = jnp.where(lax.broadcasted_iota(jnp.int32, (8, seq), 0) == route[...], 1.0, 0.0)
        count = hot
        shift = 1
        while shift < seq:
            count = count + jnp.where(lane >= shift, pltpu.roll(count, shift, 1), 0.0)
            shift *= 2
        position = jnp.sum(hot * (count - 1.0), axis=0, keepdims=True)
        place = route[...].astype(f32) * capacity + position
        slot[...] = jnp.where(position < capacity, place, float(slots))
        slot_o[...] = slot[...]
        column_o[...] = jnp.broadcast_to(slot[...], (128, seq)).T

    values = tok[...].astype(f32)
    scale = lax.rsqrt(jnp.mean(values * values, axis=-1, keepdims=True) + epsilon)
    normed = (values * scale * gain[0:1, :]).astype(bf16)
    nl_o[...] = normed
    for weight, out in ((wq, q_o), (wk, k_o), (wv, v_o)):
        out[...] = dot_f32(normed, weight[...]).astype(bf16)
    rows = gsend_o.shape[0]
    number = lax.broadcasted_iota(jnp.int32, (rows, seq), 0) + step * rows
    pick = jnp.where(number.astype(f32) == slot[...], 1.0, 0.0).astype(bf16)
    gsend_o[...] = dot_f32(pick, cot[...]).astype(bf16)


def first_pass(tokens, gain, wq, wk, wv, route, cotangent, capacity, experts):
    seq, width = tokens.shape
    slots = experts * capacity
    steps = 4
    rows = pl.BlockSpec((seq // steps, width), lambda i: (i, 0))
    fixed = lambda shape: pl.BlockSpec(shape, lambda i: (0, 0))
    return pl.pallas_call(
        functools.partial(first_kernel, capacity, experts),
        grid=(steps,),
        in_specs=[rows, fixed(gain.shape)] + [fixed(wq.shape)] * 3 + [fixed(route.shape), fixed(cotangent.shape)],
        out_specs=[rows] * 4 + [pl.BlockSpec((slots // steps, width), lambda i: (i, 0)), fixed(route.shape), fixed((seq, 128))],
        out_shape=[jax.ShapeDtypeStruct((seq, width), bf16)] * 4
        + [jax.ShapeDtypeStruct((slots, width), bf16), jax.ShapeDtypeStruct(route.shape, f32),
           jax.ShapeDtypeStruct((seq, 128), f32)],
        scratch_shapes=[pltpu.VMEM(route.shape, f32)],
        compiler_params=pltpu.CompilerParams(vmem_limit_bytes=62 << 20),
        cost_estimate=pl.CostEstimate(
            flops=6 * seq * width * width + 2 * slots * seq * width, bytes_accessed=20 * seq * width, transcendentals=seq
        ),
        name="first",
    )(tokens, gain, wq, wk, wv, route, cotangent)


def middle_kernel(experts, steps, tok, ctx, wo, gain, rw, slot, column, hid_o, xs_o, meta_o, normed):
    step = pl.program_id(0)
    span, width = tok.shape
    seq = normed.shape[0]

    @pl.when(step < steps)
    def _():
        hidden = tok[...].astype(f32) + dot_f32(ctx[...], wo[...])
        hid_o[...] = hidden
        scale = lax.rsqrt(jnp.mean(hidden * hidden, axis=-1, keepdims=True) + epsilon)
        low = (hidden * scale * gain[1:2, :]).astype(bf16)
        normed[pl.ds(pl.multiple_of(step * span, span), span), :] = low
        lane = lax.broadcasted_iota(jnp.int32, (span, 128), 1)
        logits = jnp.where(lane < experts, dot_f32(low, rw[...]), -1e30)
        weights = jnp.exp(logits - jnp.max(logits, axis=-1, keepdims=True))
        place = column[...]
        each = xs_o.shape[0] * (pl.num_programs(0) - steps) // experts
        first = (lane * each).astype(f32)
        chosen = (place >= first) & (place < first + each) & (lane < experts)
        gate = jnp.sum(jnp.where(chosen, weights, 0.0), axis=-1, keepdims=True) / jnp.sum(
            weights, axis=-1, keepdims=True
        )
        meta_o[...] = jnp.where(lane == 0, gate, place)

    @pl.when(step >= steps)
    def _():
        rows = xs_o.shape[0]
        number = lax.broadcasted_iota(jnp.int32, (rows, seq), 0) + (step - steps) * rows
        pick = jnp.where(number.astype(f32) == slot[...], 1.0, 0.0).astype(bf16)
        xs_o[...] = dot_f32(pick, normed[...]).astype(bf16)


def middle_pass(tokens, ctx, wo, gain, rw, slot, column, slots, experts):
    seq, width = tokens.shape
    steps = 4
    span = seq // steps
    each = slots // steps
    token_map = lambda i: (jnp.minimum(i, steps - 1), 0)
    fixed = lambda shape: pl.BlockSpec(shape, lambda i: (0, 0))
    return pl.pallas_call(
        functools.partial(middle_kernel, experts, steps),
        grid=(2 * steps,),
        in_specs=[
            pl.BlockSpec((span, width), token_map), pl.BlockSpec((span, width), token_map), fixed(wo.shape),
            fixed(gain.shape), fixed(rw.shape), fixed(slot.shape), pl.BlockSpec((span, 128), token_map),
        ],
        out_specs=[
            pl.BlockSpec((span, width), token_map),
            pl.BlockSpec((each, width), lambda i: (jnp.maximum(i - steps, 0), 0)),
            pl.BlockSpec((span, 128), token_map),
        ],
        out_shape=[
            jax.ShapeDtypeStruct((seq, width), f32),
            jax.ShapeDtypeStruct((slots, width), bf16),
            jax.ShapeDtypeStruct((seq, 128), f32),
        ],
        scratch_shapes=[pltpu.VMEM((seq, width), bf16)],
        compiler_params=pltpu.CompilerParams(vmem_limit_bytes=62 << 20),
        cost_estimate=pl.CostEstimate(
            flops=2 * seq * width * width + 2 * slots * seq * width, bytes_accessed=10 * seq * width, transcendentals=seq
        ),
        name="middle",
    )(tokens, ctx, wo, gain, rw, slot, column)


def combine_kernel(gback, hid, cot, gain, ctx, wo, meta, ghid_o, dwo_o, gctx_o, gain_o, total_w):
    step = pl.program_id(0)
    span = hid.shape[0]
    slots = gback.shape[0]
    where = lax.broadcasted_iota(jnp.int32, (span, slots), 1).astype(f32)
    pick = jnp.where(meta[:, 1:2] == where, 1.0, 0.0).astype(bf16)
    grad = dot_f32(pick, gback[...])
    values = hid[...]
    scale = lax.rsqrt(jnp.mean(values * values, axis=-1, keepdims=True) + epsilon)
    weighted = grad * gain[1:2, :]
    inner = jnp.mean(weighted * values, axis=-1, keepdims=True)
    total = cot[...].astype(f32) + scale * weighted - values * (scale * scale * scale * inner)
    ghid_o[...] = total
    branch = total.astype(bf16)
    gctx_o[...] = dot_nt(branch, wo[...]).astype(bf16)
    gains = jnp.sum(grad * values * scale, axis=0, keepdims=True)
    now = dot_f32(ctx[...].T, branch)

    @pl.when(step == 0)
    def _():
        total_w[...] = now
        gain_o[...] = gains

    @pl.when(step > 0)
    def _():
        total_w[...] += now
        gain_o[...] += gains

    @pl.when(step == pl.num_programs(0) - 1)
    def _():
        dwo_o[...] = total_w[...].astype(bf16)


def combine_pass(gback, hidden, cotangent, gain, ctx, wo, meta):
    seq, width = hidden.shape
    steps = 4
    rows = pl.BlockSpec((seq // steps, width), lambda i: (i, 0))
    fixed = lambda shape: pl.BlockSpec(shape, lambda i: (0, 0))
    return pl.pallas_call(
        combine_kernel,
        grid=(steps,),
        in_specs=[
            fixed(gback.shape), rows, rows, fixed(gain.shape), rows, fixed(wo.shape),
            pl.BlockSpec((seq // steps, 128), lambda i: (i, 0)),
        ],
        out_specs=[rows, fixed((width, width)), rows, fixed((1, width))],
        out_shape=[
            jax.ShapeDtypeStruct((seq, width), f32),
            jax.ShapeDtypeStruct((width, width), bf16),
            jax.ShapeDtypeStruct((seq, width), bf16),
            jax.ShapeDtypeStruct((1, width), f32),
        ],
        scratch_shapes=[pltpu.VMEM((width, width), f32)],
        compiler_params=pltpu.CompilerParams(vmem_limit_bytes=62 << 20),
        cost_estimate=pl.CostEstimate(
            flops=4 * seq * width * width + 2 * gback.shape[0] * seq * width,
            bytes_accessed=16 * seq * width, transcendentals=seq,
        ),
        name="combine",
    )(gback, hidden, cotangent, gain, ctx, wo, meta)


def split_rows(row):
    hi = row.astype(bf16).astype(f32)
    mid = (row - hi).astype(bf16).astype(f32)
    low = row - hi - mid
    idx = lax.broadcasted_iota(jnp.int32, (16, row.shape[1]), 0)
    return jnp.where(idx == 0, hi, jnp.where(idx == 1, mid, jnp.where(idx == 2, low, 0.0))).astype(bf16)


def attend_back_kernel(
    q_ref, k_ref, v_ref, g_ref, u_ref, ctxt_ref, lse_ref,
    dq_ref, dk_ref, dv_ref, diag_ref,
    base, acc, kaug, vaug, qaug, gaug, qz, gz, kt, dqt,
):
    seq = q_ref.shape[0]
    span = 256
    lane = lax.broadcasted_iota(jnp.int32, (seq, 128), 1)
    gt = g_ref[...].T
    qtv = q_ref[...].T
    kt[...] = k_ref[...].T
    gtf = gt.astype(f32)
    pad = jnp.zeros((48, seq), bf16)
    one = jnp.ones((seq, 128), bf16)
    nil = jnp.zeros((seq, 128), bf16)
    acc[...] = jnp.zeros_like(acc)
    for head in range(2):
        fill_toeplitz(base, head, u_ref[0, head : head + 1, :])
        own = (lane < 64) if head == 0 else (lane >= 64)
        origin = 64 if head == 0 else 0
        extra = jnp.where((lane >= origin) & (lane < origin + 3), one, nil)
        kaug[head] = jnp.where(own, k_ref[...], extra)
        vaug[head] = jnp.where(own, v_ref[...], extra)
        qz[head] = jnp.where(own, q_ref[...], nil)
        gz[head] = jnp.where(own, g_ref[...], nil)
        rows = slice(64 * head, 64 * head + 64)
        lse = split_rows(-lse_ref[0, head : head + 1, :])
        dsum = split_rows(-jnp.sum(gtf[rows] * ctxt_ref[rows, :], axis=0, keepdims=True))
        for dst, src, aug in ((qaug, qtv, lse), (gaug, gt, dsum)):
            dst[head, rows, :] = src[rows]
            dst[head, origin : origin + 16, :] = aug
            dst[head, origin + 16 : origin + 64, :] = pad

    dqt[...] = jnp.zeros_like(dqt)

    def step(idx, carry):
        rows = pl.ds(pl.multiple_of(idx * span, span), span)
        dv = None
        dk = None
        for head in range(2):
            s = dot_f32(kaug[head, rows, :], qaug[head])
            dp = dot_f32(vaug[head, rows, :], gaug[head])
            tops = []
            grads = []
            for part in range(2):
                offs = pl.ds(pl.multiple_of(seq - span * idx - 128 * part, 128), seq)
                p = jnp.exp(s[128 * part : 128 * part + 128] + base[head, :, offs])
                ds_ = p * dp[128 * part : 128 * part + 128]
                acc[head, :, offs] += ds_
                tops.append(p.astype(bf16))
                grads.append(ds_.astype(bf16))
            p = jnp.concatenate(tops, axis=0)
            ds_ = jnp.concatenate(grads, axis=0)
            now = dot_f32(p, gz[head])
            dv = now if dv is None else dv + now
            now = dot_f32(ds_, qz[head])
            dk = now if dk is None else dk + now
            dqt[64 * head : 64 * head + 64, :] += dot_f32(kt[64 * head : 64 * head + 64, rows], ds_)
        dv_ref[rows, :] = dv.astype(bf16)
        dk_ref[rows, :] = dk.astype(bf16)
        return carry

    lax.fori_loop(0, seq // span, step, 0)
    dq_ref[...] = dqt[...].T.astype(bf16)
    width = 2 * seq
    for head in range(2):
        total = acc[head, 0:8, :]
        for group in range(1, 16):
            total = total + pltpu.roll(acc[head, 8 * group : 8 * group + 8, :], width - 8 * group, 1)
        sub = lax.broadcasted_iota(jnp.int32, (8, width), 0)
        for bit in (1, 2, 4):
            total = jnp.where((sub & bit) != 0, pltpu.roll(total, width - bit, 1), total)
        diag_ref[0, head : head + 1, :] = jnp.sum(total, axis=0, keepdims=True)


def attend_back(q, k, v, g, u, ctxt, lse):
    seq, width = q.shape
    pairs = width // 128
    blk = pl.BlockSpec((seq, 128), lambda p: (0, p))
    return pl.pallas_call(
        attend_back_kernel,
        grid=(pairs,),
        in_specs=[
            blk, blk, blk, blk,
            pl.BlockSpec((1, 2, 2 * seq), lambda p: (p, 0, 0)),
            pl.BlockSpec((128, seq), lambda p: (p, 0)),
            pl.BlockSpec((1, 8, seq), lambda p: (p, 0, 0)),
        ],
        out_specs=[blk, blk, blk, pl.BlockSpec((1, 8, 2 * seq), lambda p: (p, 0, 0))],
        out_shape=[jax.ShapeDtypeStruct((seq, width), bf16)] * 3
        + [jax.ShapeDtypeStruct((pairs, 8, 2 * seq), f32)],
        scratch_shapes=[
            pltpu.VMEM((2, 128, 2 * seq), f32),
            pltpu.VMEM((2, 128, 2 * seq), f32),
            pltpu.VMEM((2, seq, 128), bf16),
            pltpu.VMEM((2, seq, 128), bf16),
            pltpu.VMEM((2, 128, seq), bf16),
            pltpu.VMEM((2, 128, seq), bf16),
            pltpu.VMEM((2, seq, 128), bf16),
            pltpu.VMEM((2, seq, 128), bf16),
            pltpu.VMEM((128, seq), bf16),
            pltpu.VMEM((128, seq), f32),
        ],
        compiler_params=pltpu.CompilerParams(vmem_limit_bytes=56 << 20),
        cost_estimate=pl.CostEstimate(
            flops=40 * seq * seq * width, bytes_accessed=20 * seq * width, transcendentals=seq * seq * 12
        ),
        name="attend_back",
    )(q, k, v, g, u, ctxt, lse)


def gelu_both(v):
    scale = 0.7978845608028654
    square = v * v
    t = jnp.tanh(scale * v * (1.0 + 0.044715 * square))
    half = 0.5 * (1.0 + t)
    slope = half + 0.5 * v * (1.0 - t * t) * (scale * (1.0 + 3 * 0.044715 * square))
    return v * half, slope


def expert_kernel(
    experts, capacity, tile,
    xs, gr_h, win_h, wout_h, rw,
    gback_o, prod_o, dwin_o, dwout_o, drw_o, shared_o,
    xall, gr, gp, win, wout, act, gpre, gback, gsend, prod, logit, acc_p, acc_g, xt, gpt, stage, dwt,
    send_x, recv_x, send_g, recv_g, local, out_sem, send_s, recv_s,
):
    me = lax.axis_index("expert")
    place = me // 2
    chips = experts // 2
    span = 2 * capacity
    width = xall.shape[1]
    hidden = win.shape[1]
    barrier = pltpu.get_barrier_semaphore()
    for k in range(1, experts):
        pl.semaphore_signal(barrier, inc=1, device_id={"expert": lax.rem(me + k, experts)})
    my_dp = lax.axis_index("dp")
    dp_x, dp_y = lax.rem(my_dp, 2), my_dp // 2
    peer_x, peer_y = my_dp + 1 - 2 * dp_x, my_dp + 2 - 4 * dp_y
    for peer in (peer_x, peer_y):
        pl.semaphore_signal(barrier, inc=1, device_id={"dp": peer})
    loads = [
        pltpu.make_async_copy(win_h, win, local.at[0]),
        pltpu.make_async_copy(wout_h, wout, local.at[1]),
        pltpu.make_async_copy(gr_h, gr, local.at[2]),
    ]
    rows_of = lambda who: pl.ds(pl.multiple_of(who * capacity, 16), capacity)
    own = pltpu.make_async_copy(xs.at[rows_of(me), :], xall.at[rows_of(me), :], local.at[3])
    own.start()
    for copy in loads:
        copy.start()
    pl.semaphore_wait(barrier, experts + 1)

    def partner(step):
        high, low = place // 2, lax.rem(place, 2)
        fhigh, flow = step // 2, lax.rem(step, 2)
        return 2 * (high + fhigh - 2 * high * fhigh) + low + flow - 2 * low * flow

    def send_rows(peer):
        return pltpu.make_async_remote_copy(
            src_ref=xs.at[rows_of(peer), :], dst_ref=xall.at[rows_of(me), :],
            send_sem=send_x.at[peer], recv_sem=recv_x.at[me], device_id={"expert": peer},
        )

    def got_rows(peer):
        return pltpu.make_async_remote_copy(
            src_ref=xs.at[rows_of(peer), :], dst_ref=xall.at[rows_of(peer), :],
            send_sem=send_x.at[peer], recv_sem=recv_x.at[peer], device_id={"expert": peer},
        )

    def send_back(peer):
        return pltpu.make_async_remote_copy(
            src_ref=gsend.at[rows_of(peer), :], dst_ref=gback.at[rows_of(me), :],
            send_sem=send_g.at[peer], recv_sem=recv_g.at[me], device_id={"expert": peer},
        )

    def got_back(peer):
        return pltpu.make_async_remote_copy(
            src_ref=gsend.at[rows_of(peer), :], dst_ref=gback.at[rows_of(peer), :],
            send_sem=send_g.at[peer], recv_sem=recv_g.at[peer], device_id={"expert": peer},
        )

    sibling = me + 1 - 2 * lax.rem(me, 2)
    send_rows(sibling).start()
    for step in range(1, chips):
        for core in range(2):
            send_rows(2 * partner(step) + lax.rem(me + core, 2)).start()
    for copy in loads:
        copy.wait()

    lanes = lax.broadcasted_iota(jnp.int32, (span, rw.shape[1]), 1)
    mine = jnp.where(lanes == me, 1.0, 0.0)

    def work(step, carry):
        where = partner(step)
        base = pl.multiple_of(where * span, 32)

        @pl.when(step == 0)
        def _():
            own.wait()
            got_rows(sibling).wait_recv()

        @pl.when(step > 0)
        def _():
            got_rows(2 * where).wait_recv()
            got_rows(2 * where + 1).wait_recv()

        rows = pl.ds(base, span)
        x = xall[rows, :]
        logits = jnp.where(lanes < experts, dot_f32(x, rw[...]), -1e30)
        weights = jnp.exp(logits - jnp.max(logits, axis=-1, keepdims=True))
        probs = weights / jnp.sum(weights, axis=-1, keepdims=True)
        gate = jnp.sum(probs * mine, axis=-1, keepdims=True)
        gp[rows, :] = (gr[rows, :].astype(f32) * gate).astype(bf16)
        acc_p[...] = jnp.zeros_like(acc_p)
        acc_g[...] = jnp.zeros_like(acc_g)

        def block(idx, carry):
            cols = pl.ds(pl.multiple_of(idx * tile, tile), tile)
            h = dot_f32(xall[rows, :], win[:, cols])
            grad = dot_nt(gp[rows, :], wout[cols, :])
            value, slope = gelu_both(h)
            value = value.astype(bf16)
            grad = (grad * slope).astype(bf16)
            act[rows, cols] = value
            gpre[rows, cols] = grad
            acc_p[...] += dot_f32(value, wout[cols, :])
            acc_g[...] += dot_nt(grad, win[:, cols])
            return carry

        lax.fori_loop(0, hidden // tile, block, 0)
        made = acc_p[...].astype(bf16)
        prod[rows, :] = made
        gate_grad = jnp.sum(gr[rows, :].astype(f32) * made.astype(f32), axis=-1, keepdims=True)
        low = (gate_grad * gate * (mine - probs)).astype(bf16)
        low = jnp.where(lanes < experts, low, jnp.zeros_like(low))
        logit[rows, :] = low
        gsend[rows, :] = (acc_g[...] + dot_nt(low, rw[...])).astype(bf16)

        @pl.when(step == 0)
        def _():
            send_back(sibling).start()

        @pl.when(step > 0)
        def _():
            send_back(2 * where).start()
            send_back(2 * where + 1).start()

        return carry

    lax.fori_loop(0, chips, work, 0)
    outs = [
        pltpu.make_async_copy(prod, prod_o, local.at[0]),
        pltpu.make_async_copy(gsend.at[rows_of(me), :], gback.at[rows_of(me), :], local.at[3]),
    ]
    for copy in outs:
        copy.start()
    xt[...] = xall[...].T
    gpt[...] = gp[...].T
    drw_o[...] = dot_f32(xt[...], logit[...])

    share = width // 4
    tiles = hidden // tile
    split = tiles // 2

    def left_copy(idx, block):
        cols = pl.ds(pl.multiple_of(idx * tile, tile), tile)
        rows = pl.ds(pl.multiple_of((1 - dp_x + 2 * block) * share, 16), share)
        return pltpu.make_async_remote_copy(
            src_ref=dwt.at[rows, cols], dst_ref=shared_o.at[pl.ds(block * share, share), cols],
            send_sem=send_s.at[block, idx], recv_sem=recv_s.at[block, idx], device_id={"dp": peer_x},
        )

    def right_copy(idx, block):
        cols = pl.ds(pl.multiple_of(idx * tile, tile), tile)
        rows = pl.ds(pl.multiple_of((2 - 2 * dp_y + block) * share, 16), share)
        dst_cols = pl.ds(pl.multiple_of((idx - split) * tile, tile), tile)
        return pltpu.make_async_remote_copy(
            src_ref=dwt.at[rows, cols], dst_ref=shared_o.at[pl.ds((2 + block) * share, share), dst_cols],
            send_sem=send_s.at[block, idx], recv_sem=recv_s.at[block, idx], device_id={"dp": peer_y},
        )

    def out_block(step, carry):
        idx = lax.rem(step, 2) * split + step // 2
        cols = pl.ds(pl.multiple_of(idx * tile, tile), tile)
        dwt[:, cols] = dot_f32(gpt[...], act[:, cols]).astype(bf16)

        @pl.when(idx < split)
        def _():
            for block in range(2):
                left_copy(idx, block).start()

        @pl.when(idx >= split)
        def _():
            for block in range(2):
                right_copy(idx, block).start()

        return carry

    lax.fori_loop(0, tiles, out_block, 0)
    whole = pltpu.make_async_copy(dwt, dwout_o, local.at[2])
    whole.start()

    def put(slot, cols):
        return pltpu.make_async_copy(stage.at[slot], dwin_o.at[:, cols], out_sem.at[slot])

    def in_block(idx, carry):
        cols = pl.ds(pl.multiple_of(idx * tile, tile), tile)
        slot = lax.rem(idx, 2)

        @pl.when(idx > 1)
        def _():
            put(slot, cols).wait()

        stage[slot] = dot_f32(xt[...], gpre[:, cols]).astype(bf16)
        put(slot, cols).start()
        return carry

    lax.fori_loop(0, tiles, in_block, 0)
    for slot in range(2):
        put(slot, pl.ds(0, tile)).wait()
    whole.wait()
    for copy in outs:
        copy.wait()
    for k in range(1, experts):
        peer = lax.rem(me + k, experts)
        got_rows(peer).wait_send()
        got_back(peer).wait_send()
        got_back(peer).wait_recv()
    back = pltpu.make_async_copy(gback, gback_o, local.at[1])
    back.start()
    for idx in range(tiles):
        for block in range(2):
            (left_copy if idx < split else right_copy)(idx, block).wait()
    back.wait()


def expert_pass(xs, gr, weight_in, weight_out, router_pad, experts, capacity):
    slots, width = xs.shape
    hidden = weight_in.shape[1]
    tile = 512
    span = 2 * capacity
    hbm = pl.BlockSpec(memory_space=pl.ANY)
    vmem = pl.BlockSpec(memory_space=pltpu.VMEM)
    return pl.pallas_call(
        functools.partial(expert_kernel, experts, capacity, tile),
        in_specs=[hbm, hbm, hbm, hbm, vmem],
        out_specs=[hbm, hbm, hbm, hbm, vmem, hbm],
        out_shape=[
            jax.ShapeDtypeStruct((slots, width), bf16),
            jax.ShapeDtypeStruct((slots, width), bf16),
            jax.ShapeDtypeStruct((width, hidden), bf16),
            jax.ShapeDtypeStruct((width, hidden), bf16),
            jax.ShapeDtypeStruct((width, router_pad.shape[1]), f32),
            jax.ShapeDtypeStruct((width, hidden // 2), bf16),
        ],
        scratch_shapes=[
            pltpu.VMEM((slots, width), bf16),
            pltpu.VMEM((slots, width), bf16),
            pltpu.VMEM((slots, width), bf16),
            pltpu.VMEM((width, hidden), bf16),
            pltpu.VMEM((hidden, width), bf16),
            pltpu.VMEM((slots, hidden), bf16),
            pltpu.VMEM((slots, hidden), bf16),
            pltpu.VMEM((slots, width), bf16),
            pltpu.VMEM((slots, width), bf16),
            pltpu.VMEM((slots, width), bf16),
            pltpu.VMEM((slots, router_pad.shape[1]), bf16),
            pltpu.VMEM((span, width), f32),
            pltpu.VMEM((span, width), f32),
            pltpu.VMEM((width, slots), bf16),
            pltpu.VMEM((width, slots), bf16),
            pltpu.VMEM((2, width, tile), bf16),
            pltpu.VMEM((width, hidden), bf16),
            pltpu.SemaphoreType.DMA((experts,)),
            pltpu.SemaphoreType.DMA((experts,)),
            pltpu.SemaphoreType.DMA((experts,)),
            pltpu.SemaphoreType.DMA((experts,)),
            pltpu.SemaphoreType.DMA((4,)),
            pltpu.SemaphoreType.DMA((2,)),
            pltpu.SemaphoreType.DMA((2, hidden // tile)),
            pltpu.SemaphoreType.DMA((2, hidden // tile)),
        ],
        compiler_params=pltpu.CompilerParams(
            vmem_limit_bytes=60 << 20, collective_id=1, has_side_effects=True
        ),
        cost_estimate=pl.CostEstimate(
            flops=12 * slots * width * hidden, bytes_accessed=8 * width * hidden, transcendentals=slots * hidden
        ),
        name="experts",
    )(xs, gr, weight_in, weight_out, router_pad)


def remote(src, dst, send_sem, recv_sem, axis, peer):
    return pltpu.make_async_remote_copy(
        src_ref=src, dst_ref=dst, send_sem=send_sem, recv_sem=recv_sem, device_id={axis: peer}
    )


def others(count, mine):
    return [lax.rem(mine + k, count) for k in range(1, count)]


PLAN = (
    (11, 16, 19, 22, 24),
    (12, 17, 20, 23, 25),
    (5, 13, 16, 19, 21),
    (9, 15, 18, 21, 23),
    (13, 18, 21, 24, 26),
    (17, 21, 24, 27, 29),
    (21, 24, 27, 29, 31),
)
OUTPUT_SLOT = 17
EXPERT_SLOTS = ((6, 2, 0), (14, 3, 0), (15, 2, 1), (22, 3, 1))


def back_kernel(
    groups, experts, pairs,
    q_ref, k_ref, v_ref, g_ref, ctxt_ref, wq, wk, wv, hot, gain, nl_h, tok_h, ghid_h, dwo_h, gain_two, router,
    eout_h, shared_h, ein_h, p_h, prod_h, hid_h, meta,
    wsum_o, ing_o, small_o, esum_o, out_o,
    acc, vaug, gaug, qz, gz, kt, dqt, pbuf, pret, hbuf, obuf, dall, nt, tok,
    part, r1, r2, r3, full, sbuf, srecv, sone, stwo, keep, other, final,
    send1, recv1, send2, recv2, send3, recv3, send4, recv4, send5, recv5, send6, recv6, send7, recv7, local,
    send_a, recv_a, send_b, recv_b, out_sem, copy_sem, p_sem, send_p, recv_p, o_sem,
):
    seq = q_ref.shape[0]
    width = tok.shape[1]
    span = 256
    pair = pl.program_id(0)
    me = lax.axis_index("expert")
    my_dp = lax.axis_index("dp")
    core = lax.rem(me, 2)
    place = me // 2
    chips = experts // 2
    sibling = me + 1 - 2 * core
    half = width // 2
    piece = half // groups
    thick = part.shape[2]
    gain_rows = width // 128

    def half_rows(which):
        return pl.ds(pl.multiple_of(which * half, 16), half)

    def own_piece(which):
        return pl.ds(pl.multiple_of(core * half + which * piece, 16), piece)

    def copy1(c):
        return remote(part.at[c, half_rows(1 - core), :], r1.at[c], send1.at[c], recv1.at[c], "expert", sibling)

    def copy2(c, peer, slot):
        return remote(part.at[c, own_piece(peer), :], r2.at[c, slot], send2.at[c, peer], recv2.at[c, slot], "dp", peer)

    def copy3(c, peer, slot):
        return remote(
            r3.at[c, place], r3.at[c, slot], send3.at[c, peer], recv3.at[c, slot], "expert", 2 * peer + core
        )

    def copy4(c, peer, slot):
        return remote(
            full.at[c, own_piece(my_dp), :], full.at[c, own_piece(slot), :],
            send4.at[c, peer], recv4.at[c, slot], "dp", peer,
        )

    def copy5(c, which):
        return remote(
            full.at[c, half_rows(which), :], full.at[c, half_rows(which), :],
            send5.at[c], recv5.at[c], "expert", sibling,
        )

    def stage1(c):
        copy1(c).start()

    def stage2(c):
        copy1(c).wait_recv()
        part[c, half_rows(core), :] = (part[c, half_rows(core), :].astype(f32) + r1[c].astype(f32)).astype(bf16)
        for peer in others(groups, my_dp):
            copy2(c, peer, my_dp).start()

    def stage3(c):
        total = part[c, own_piece(my_dp), :].astype(f32)
        for peer in others(groups, my_dp):
            copy2(c, peer, peer).wait_recv()
            total = total + r2[c, peer].astype(f32)
        r3[c, place] = total.astype(bf16)
        for peer in others(chips, place):
            copy3(c, peer, place).start()

    def stage4(c):
        for peer in others(chips, place):
            copy3(c, peer, peer).wait_recv()
        total = r3[c, 0].astype(f32)
        for slot in range(1, chips):
            total = total + r3[c, slot].astype(f32)
        full[c, own_piece(my_dp), :] = total.astype(bf16)
        for peer in others(groups, my_dp):
            copy4(c, peer, my_dp).start()

    def stage5(c):
        for peer in others(groups, my_dp):
            copy4(c, peer, peer).wait_recv()
        copy5(c, core).start()

    def put_first(c):
        return pltpu.make_async_copy(full.at[c], wsum_o.at[0, :, thick * c : thick * c + thick], out_sem.at[c, 0])

    def put_pair(c, which):
        cols = pl.ds(128 * (c - 2) if isinstance(c, int) else pl.multiple_of(128 * (c - 2), 128), 128)
        return pltpu.make_async_copy(
            full.at[c, :, 128 * which : 128 * which + 128], wsum_o.at[1 + which, :, cols], out_sem.at[c, which]
        )

    def stage6(c):
        copy5(c, 1 - core).wait_recv()

        if c < 2:
            put_first(c).start()
        else:
            for which in range(3):
                put_pair(c, which).start()

    share = width // 4
    dp_x, dp_y = lax.rem(my_dp, 2), my_dp // 2
    peer_x, peer_y = my_dp + 1 - 2 * dp_x, my_dp + 2 - 4 * dp_y
    middle = keep.shape[1]
    left, right = pl.ds(0, middle), pl.ds(middle, middle)

    def share_rows(which):
        return pl.ds(pl.multiple_of(which * share, 16), share)

    def first_left(block):
        return remote(
            ein_h.at[share_rows(1 - dp_x + 2 * block), left], other.at[1, share_rows(block), :],
            send_a.at[0, block], recv_a.at[0, block], "dp", peer_x,
        )

    def first_right(block):
        return remote(
            ein_h.at[share_rows(2 - 2 * dp_y + block), right], other.at[1, share_rows(2 + block), :],
            send_a.at[1, block], recv_a.at[1, block], "dp", peer_y,
        )

    def second_left(which):
        return remote(
            keep.at[share_rows(1 - dp_y), :], final.at[which, :, left],
            send_b.at[which, 0], recv_b.at[which, 0], "dp", peer_y,
        )

    def second_right(which):
        return remote(
            keep.at[share_rows(2 + 1 - dp_x), :], final.at[which, :, right],
            send_b.at[which, 1], recv_b.at[which, 1], "dp", peer_x,
        )

    def own_loads(src):
        loads = []
        for block in range(2):
            loads.append(
                pltpu.make_async_copy(
                    src.at[share_rows(dp_x + 2 * block), left], keep.at[share_rows(block), :], copy_sem.at[block]
                )
            )
            loads.append(
                pltpu.make_async_copy(
                    src.at[share_rows(2 * dp_y + block), right], keep.at[share_rows(2 + block), :], copy_sem.at[2 + block]
                )
            )
        return loads

    def shared_load():
        return pltpu.make_async_copy(shared_h, other.at[0], copy_sem.at[4])

    def save(which):
        return pltpu.make_async_copy(final.at[which], esum_o.at[which], copy_sem.at[5])

    def experts_begin():
        for copy in own_loads(eout_h) + [shared_load()]:
            copy.start()
        for block in range(2):
            first_left(block).start()
            first_right(block).start()

    def experts_second(which):
        for copy in own_loads(eout_h if which == 0 else ein_h):
            copy.wait()
        if which == 0:
            shared_load().wait()
        else:
            for block in range(2):
                first_left(block).wait_recv()
                first_right(block).wait_recv()

        def block(idx, carry):
            rows = pl.ds(pl.multiple_of(idx * 64, 64), 64)
            keep[rows, :] = (keep[rows, :].astype(f32) + other[which, rows, :].astype(f32)).astype(bf16)
            return carry

        lax.fori_loop(0, width // 64, block, 0)
        second_left(which).start()
        second_right(which).start()

    def experts_last(which):
        second_left(which).wait()
        second_right(which).wait()

        def block(idx, carry):
            rows = pl.ds(pl.multiple_of(idx * 64, 64), 64)
            mine_left = pl.ds(pl.multiple_of(dp_y * share + idx * 64, 64), 64)
            mine_right = pl.ds(pl.multiple_of((2 + dp_x) * share + idx * 64, 64), 64)
            final[which, rows, left] = (final[which, rows, left].astype(f32) + keep[mine_left, :].astype(f32)).astype(bf16)
            final[which, rows, right] = (final[which, rows, right].astype(f32) + keep[mine_right, :].astype(f32)).astype(bf16)
            return carry

        lax.fori_loop(0, share // 64, block, 0)
        if which == 0:
            for copy in own_loads(ein_h):
                copy.start()
        else:
            save(0).wait()
        save(which).start()

    early = pl.ds(8 + hot.shape[0], sbuf.shape[0] - 8 - hot.shape[0])
    late = pl.ds(0, 8 + hot.shape[0])

    def copy6(part_idx, rows, peer, slot):
        return remote(
            sbuf.at[rows, :], srecv.at[slot, rows, :],
            send6.at[part_idx, peer], recv6.at[part_idx, slot], "expert", peer,
        )

    def copy7(part_idx, rows, peer, slot):
        return remote(
            sone.at[rows, :], stwo.at[slot, rows, :],
            send7.at[part_idx, peer], recv7.at[part_idx, slot], "dp", peer,
        )

    def small1(part_idx, rows):
        srecv[me, rows, :] = sbuf[rows, :]
        for peer in others(experts, me):
            copy6(part_idx, rows, peer, me).start()

    def small2(part_idx, rows):
        for peer in others(experts, me):
            copy6(part_idx, rows, peer, peer).wait_recv()
        total = srecv[0, rows, :]
        for slot in range(1, experts):
            total = total + srecv[slot, rows, :]
        sone[rows, :] = total
        stwo[my_dp, rows, :] = total
        for peer in others(groups, my_dp):
            copy7(part_idx, rows, peer, my_dp).start()

    def small3(part_idx, rows):
        for peer in others(groups, my_dp):
            copy7(part_idx, rows, peer, peer).wait_recv()
        total = stwo[0, rows, :]
        for slot in range(1, groups):
            total = total + stwo[slot, rows, :]
        small_o[rows, :] = total

    stages = (stage2, stage3, stage4, stage5, stage6)

    def advance(slot):
        for c, slots in enumerate(PLAN):
            for at, stage in reversed(list(zip(slots, stages))):
                if at < 4 * pairs:
                    pl.when(slot == at)(functools.partial(stage, c))

    def load_p(slot_idx, slot):
        rows = pl.ds(pl.multiple_of(lax.rem(slot_idx, 4) * span, span), span)
        return pltpu.make_async_copy(p_h.at[pl.ds(2 * (slot_idx // 4), 2), rows, :], pbuf.at[slot], p_sem.at[slot])

    slots_each = pret.shape[0] // experts

    def slot_rows(which):
        return pl.ds(pl.multiple_of(which * slots_each, 16), slots_each)

    def give_back(peer):
        return remote(
            prod_h.at[slot_rows(peer), :], pret.at[slot_rows(me), :], send_p.at[peer], recv_p.at[me], "expert", peer
        )

    def got_back(peer):
        return remote(
            prod_h.at[slot_rows(peer), :], pret.at[slot_rows(peer), :], send_p.at[peer], recv_p.at[peer], "expert", peer
        )

    def own_back():
        return pltpu.make_async_copy(prod_h.at[slot_rows(me), :], pret.at[slot_rows(me), :], o_sem.at[0])

    def out_rows(block):
        return pl.ds(block * span, span)

    def load_hidden(block):
        return pltpu.make_async_copy(hid_h.at[out_rows(block), :], hbuf, o_sem.at[1])

    def save_out(block):
        return pltpu.make_async_copy(obuf, out_o.at[out_rows(block), :], o_sem.at[2])

    def output_block(block):
        if block == 0:
            own_back().wait()
            for peer in others(experts, me):
                got_back(peer).wait_recv()
        load_hidden(block).wait()
        where = lax.broadcasted_iota(jnp.int32, (span, pret.shape[0]), 1).astype(f32)
        pick = jnp.where(meta[out_rows(block), 1:2] == where, 1.0, 0.0).astype(bf16)
        gathered = dot_f32(pick, pret[...])
        if block > 0:
            save_out(block - 1).wait()
        obuf[...] = (hbuf[...] + meta[out_rows(block), 0:1] * gathered).astype(bf16)
        save_out(block).start()
        if (block + 1) * span < seq:
            load_hidden(block + 1).start()

    loads = [
        pltpu.make_async_copy(nl_h, tok, local.at[0]),
        pltpu.make_async_copy(ghid_h, ing_o, local.at[2]),
        pltpu.make_async_copy(dwo_h.at[:, 0:thick], part.at[0], local.at[3]),
        pltpu.make_async_copy(dwo_h.at[:, thick : 2 * thick], part.at[1], local.at[4]),
    ]

    @pl.when(pair == 0)
    def _():
        barrier = pltpu.get_barrier_semaphore()
        for peer in others(experts, me):
            pl.semaphore_signal(barrier, inc=1, device_id={"expert": peer})
        for peer in others(groups, my_dp):
            pl.semaphore_signal(barrier, inc=1, device_id={"dp": peer})
        for copy in loads:
            copy.start()
        load_p(0, 0).start()
        own_back().start()
        load_hidden(0).start()
        sbuf[...] = jnp.zeros_like(sbuf)
        first_row = 8 + hot.shape[0]
        by_expert = router[...].T
        for tile in range(gain_rows):
            lanes = slice(128 * tile, 128 * tile + 128)
            sbuf[first_row + tile : first_row + tile + 1, :] = gain_two[:, lanes]
            for which in range(experts):
                row = first_row + 8 + gain_rows * which + tile
                sbuf[row : row + 1, :] = by_expert[which : which + 1, lanes]
        for copy in loads:
            copy.wait()
        nt[...] = tok[...].T
        pl.semaphore_wait(barrier, experts + groups - 2)
        stage1(0)
        stage1(1)
        small1(0, early)
        experts_begin()
        for peer in others(experts, me):
            give_back(peer).start()

    mine = pl.ds(pl.multiple_of(128 * pair, 128), 128)
    lane = lax.broadcasted_iota(jnp.int32, (seq, 128), 1)
    gt = g_ref[...].T
    kt[...] = k_ref[...].T
    gtf = gt.astype(f32)
    pad = jnp.zeros((48, seq), bf16)
    one = jnp.ones((seq, 128), bf16)
    nil = jnp.zeros((seq, 128), bf16)
    acc[...] = jnp.zeros_like(acc)
    for head in range(2):
        own = (lane < 64) if head == 0 else (lane >= 64)
        origin = 64 if head == 0 else 0
        extra = jnp.where((lane >= origin) & (lane < origin + 3), one, nil)
        vaug[head] = jnp.where(own, v_ref[...], extra)
        qz[head] = jnp.where(own, q_ref[...], nil)
        gz[head] = jnp.where(own, g_ref[...], nil)
        rows = slice(64 * head, 64 * head + 64)
        gaug[head, rows, :] = gt[rows]
        gaug[head, origin : origin + 16, :] = split_rows(
            -jnp.sum(gtf[rows] * ctxt_ref[rows, :], axis=0, keepdims=True)
        )
        gaug[head, origin + 16 : origin + 64, :] = pad

    dqt[...] = jnp.zeros_like(dqt)

    def step(idx, carry):
        rows = pl.ds(pl.multiple_of(idx * span, span), span)
        dv = None
        dk = None
        slot = lax.rem(idx, 2)
        load_p(4 * pair + idx, slot).wait()

        @pl.when(4 * pair + idx + 1 < 4 * pairs)
        def _():
            load_p(4 * pair + idx + 1, 1 - slot).start()

        for head in range(2):
            dp = dot_f32(vaug[head, rows, :], gaug[head])
            grads = []
            for part_idx in range(2):
                offs = pl.ds(pl.multiple_of(seq - span * idx - 128 * part_idx, 128), seq)
                band = slice(128 * part_idx, 128 * part_idx + 128)
                ds_ = pbuf[slot, head, band, :].astype(f32) * dp[band]
                acc[head, :, offs] += ds_
                grads.append(ds_.astype(bf16))
            ds_ = jnp.concatenate(grads, axis=0)
            now = dot_f32(pbuf[slot, head], gz[head])
            dv = now if dv is None else dv + now
            now = dot_f32(ds_, qz[head])
            dk = now if dk is None else dk + now
            dqt[64 * head : 64 * head + 64, :] += dot_f32(kt[64 * head : 64 * head + 64, rows], ds_)
        dall[1, rows, mine] = dk.astype(bf16)
        dall[2, rows, mine] = dv.astype(bf16)
        advance(4 * pair + idx)

        for block in range(seq // span):
            @pl.when(4 * pair + idx == OUTPUT_SLOT + block)
            def _():
                output_block(block)

        for at, task, which in EXPERT_SLOTS:
            @pl.when(4 * pair + idx == at)
            def _():
                (experts_second if task == 2 else experts_last)(which)

        @pl.when(4 * pair + idx == 7)
        def _():
            small2(0, early)

        @pl.when(4 * pair + idx == 11)
        def _():
            small3(0, early)

        return carry

    lax.fori_loop(0, seq // span, step, 0)
    dall[0, :, mine] = dqt[...].T.astype(bf16)
    twice = 2 * seq
    sub = lax.broadcasted_iota(jnp.int32, (8, twice), 0)
    head_lane = lax.broadcasted_iota(jnp.int32, (hot.shape[0], 128), 1)
    rel_rows = slice(8, 8 + hot.shape[0])
    for head in range(2):
        total = acc[head, 0:8, :]
        for group in range(1, 16):
            total = total + pltpu.roll(acc[head, 8 * group : 8 * group + 8, :], twice - 8 * group, 1)
        for bit in (1, 2, 4):
            total = jnp.where((sub & bit) != 0, pltpu.roll(total, twice - bit, 1), total)
        diag = jnp.sum(total, axis=0, keepdims=True)
        sums = jnp.sum(hot[...] * diag, axis=1, keepdims=True)
        sbuf[rel_rows, :] = jnp.where(head_lane == 2 * pair + head, sums, sbuf[rel_rows, :])

    def weight_block(idx, carry):
        rows = pl.ds(pl.multiple_of(idx * 256, 256), 256)
        grads = jnp.concatenate([dall[which, :, mine] for which in range(3)], axis=1)
        part[pair + 2, rows, :] = dot_f32(nt[rows, :], grads).astype(bf16)
        return carry

    lax.fori_loop(0, width // 256, weight_block, 0)
    stage1(pair + 2)

    @pl.when(pair == pairs - 1)
    def _():
        def token_block(idx, carry):
            rows = pl.ds(pl.multiple_of(idx * 256, 256), 256)
            grad = (
                dot_nt(dall[0, rows, :], wq[...])
                + dot_nt(dall[1, rows, :], wk[...])
                + dot_nt(dall[2, rows, :], wv[...])
            )
            values = tok[rows, :].astype(f32)
            scale = lax.rsqrt(jnp.mean(values * values, axis=-1, keepdims=True) + epsilon)
            weighted = grad * gain[0:1, :]
            inner = jnp.mean(weighted * values, axis=-1, keepdims=True)
            ing_o[rows, :] += scale * weighted - values * (scale * scale * scale * inner)
            return carry + jnp.sum(grad * values * scale, axis=0, keepdims=True)

        reload = pltpu.make_async_copy(tok_h, tok, local.at[1])
        reload.start()
        last = pairs + 1
        first = 4 * pairs
        older = sorted(
            (at, c, stage)
            for c, slots in enumerate(PLAN)
            for stage, at in enumerate(slots)
            if at >= first
        )

        def drain(until):
            while older and older[0][0] < first + until:
                _, c, stage = older.pop(0)
                stages[stage](c)

        def tokens_done(lower, upper, gain_grad):
            return lax.fori_loop(lower, upper, token_block, gain_grad)

        drain(1)
        reload.wait()
        gain_grad = tokens_done(0, 1, jnp.zeros((1, width), f32))
        stage2(last)
        drain(2)
        gain_grad = tokens_done(1, seq // 512, gain_grad)
        drain(4)
        gain_grad = tokens_done(seq // 512, seq // 256, gain_grad)
        stage3(last)
        for row in range(gain_rows):
            sbuf[row : row + 1, :] = gain_grad[:, 128 * row : 128 * row + 128]
        small1(1, late)
        drain(8)
        small2(1, late)
        stage4(last)
        drain(99)
        small3(1, late)
        stage5(last)
        stage6(last)
        for c in range(2):
            put_first(c).wait()
        save(1).wait()
        save_out(seq // span - 1).wait()
        for peer in others(experts, me):
            give_back(peer).wait_send()
        for block in range(2):
            first_left(block).wait_send()
            first_right(block).wait_send()

        def finish(c, carry):
            copy1(c).wait_send()
            for peer in others(groups, my_dp):
                copy2(c, peer, my_dp).wait_send()
                copy4(c, peer, my_dp).wait_send()
            for peer in others(chips, place):
                copy3(c, peer, place).wait_send()
            copy5(c, core).wait_send()

            @pl.when(c >= 2)
            def _():
                for which in range(3):
                    put_pair(c, which).wait()

            return carry

        lax.fori_loop(0, pairs + 2, finish, 0)
        for part_idx, rows in ((0, early), (1, late)):
            for peer in others(experts, me):
                copy6(part_idx, rows, peer, me).wait_send()
            for peer in others(groups, my_dp):
                copy7(part_idx, rows, peer, my_dp).wait_send()


def back_pass(
    q, k, v, g, ctxt, wq, wk, wv, hot, gain, normed_low, tokens, grad_hidden, dwo, gain_two, router,
    expert_out_grad, shared, expert_in_grad, weights, produced, hidden_rows, meta, groups, experts
):
    seq, width = q.shape
    pairs = width // 128
    chunks = pairs + 2
    small_shape = (8 + hot.shape[0] + 8 + width // 128 * experts, 128)
    hidden = expert_in_grad.shape[1]
    thick = width // 2
    half = width // 2
    piece = half // groups
    chips = experts // 2
    blk = pl.BlockSpec((seq, 128), lambda p: (0, p))
    hbm = pl.BlockSpec(memory_space=pl.ANY)
    fixed = lambda shape: pl.BlockSpec(shape, lambda p: (0,) * len(shape), pipeline_mode=pl.Buffered(1))
    dma = pltpu.SemaphoreType.DMA
    return pl.pallas_call(
        functools.partial(back_kernel, groups, experts, pairs),
        grid=(pairs,),
        in_specs=[
            blk, blk, blk, blk,
            pl.BlockSpec((128, seq), lambda p: (p, 0)),
            fixed((width, width)), fixed((width, width)), fixed((width, width)),
            fixed(hot.shape), fixed(gain.shape),
            hbm, hbm, hbm, hbm, fixed(gain_two.shape), fixed(router.shape), hbm, hbm, hbm,
            hbm, hbm, hbm, fixed(meta.shape),
        ],
        out_specs=[hbm, fixed((seq, width)), fixed(small_shape), hbm, hbm],
        out_shape=[
            jax.ShapeDtypeStruct((4, width, width), bf16),
            jax.ShapeDtypeStruct((seq, width), f32),
            jax.ShapeDtypeStruct(small_shape, f32),
            jax.ShapeDtypeStruct((2, width // 4, hidden), bf16),
            jax.ShapeDtypeStruct((seq, width), bf16),
        ],
        scratch_shapes=[
            pltpu.VMEM((2, 128, 2 * seq), f32),
            pltpu.VMEM((2, seq, 128), bf16),
            pltpu.VMEM((2, 128, seq), bf16),
            pltpu.VMEM((2, seq, 128), bf16),
            pltpu.VMEM((2, seq, 128), bf16),
            pltpu.VMEM((128, seq), bf16),
            pltpu.VMEM((128, seq), f32),
            pltpu.VMEM((2, 2, 256, seq), bf16),
            pltpu.VMEM(produced.shape, bf16),
            pltpu.VMEM((256, width), f32),
            pltpu.VMEM((256, width), bf16),
            pltpu.VMEM((3, seq, width), bf16),
            pltpu.VMEM((width, seq), bf16),
            pltpu.VMEM((seq, width), bf16),
            pltpu.VMEM((chunks, width, thick), bf16),
            pltpu.VMEM((chunks, half, thick), bf16),
            pltpu.VMEM((chunks, groups, piece, thick), bf16),
            pltpu.VMEM((chunks, chips, piece, thick), bf16),
            pltpu.VMEM((chunks, width, thick), bf16),
            pltpu.VMEM(small_shape, f32),
            pltpu.VMEM((experts,) + small_shape, f32),
            pltpu.VMEM(small_shape, f32),
            pltpu.VMEM((groups,) + small_shape, f32),
            pltpu.VMEM((width, hidden // 2), bf16),
            pltpu.VMEM((2, width, hidden // 2), bf16),
            pltpu.VMEM((2, width // 4, hidden), bf16),
            dma((chunks,)), dma((chunks,)),
            dma((chunks, groups)), dma((chunks, groups)),
            dma((chunks, chips)), dma((chunks, chips)),
            dma((chunks, groups)), dma((chunks, groups)),
            dma((chunks,)), dma((chunks,)),
            dma((2, experts)), dma((2, experts)),
            dma((2, groups)), dma((2, groups)),
            dma((6,)),
            dma((2, 2)), dma((2, 2)),
            dma((2, 2)), dma((2, 2)),
            dma((chunks, 3)), dma((6,)),
            dma((2,)), dma((experts,)), dma((experts,)), dma((3,)),
        ],
        compiler_params=pltpu.CompilerParams(
            vmem_limit_bytes=62 << 20, collective_id=2, has_side_effects=True
        ),
        cost_estimate=pl.CostEstimate(
            flops=40 * seq * seq * width + 12 * seq * width * width,
            bytes_accessed=40 * seq * width, transcendentals=seq * seq * 12,
        ),
        name="attend_back",
    )(
        q, k, v, g, ctxt, wq, wk, wv, hot, gain, normed_low, tokens, grad_hidden, dwo, gain_two, router,
        expert_out_grad, shared, expert_in_grad, weights, produced, hidden_rows, meta,
    )


def rms_backward(grad_norm, values, row_scale, gain_vec):
    weighted = grad_norm * gain_vec
    gain_grad = jnp.sum(grad_norm * values * row_scale, axis=0)
    grad_in = row_scale * weighted - values * row_scale**3 * jnp.mean(
        weighted * values, axis=-1, keepdims=True
    )
    return grad_in, gain_grad


def rms_forward(values, gain_vec):
    row_scale = lax.rsqrt(jnp.mean(values * values, axis=-1, keepdims=True) + epsilon)
    return values * row_scale * gain_vec, row_scale


def gelu_tanh(values):
    return jax.nn.gelu(values, approximate=True)


def contract(left, right, dims):
    return lax.dot_general(left, right, (((dims[0],), (dims[1],)), ((), ())), preferred_element_type=f32)


def exchange(rows, experts):
    slots, width = rows.shape
    rows = rows.reshape(experts, slots // experts, width)
    return lax.all_to_all(rows, "expert", split_axis=0, concat_axis=0, tiled=True).reshape(slots, width)


def expert_native(send, grad_recv, weight_in, weight_out, router_w, experts):
    received = exchange(send, experts)
    own = lax.axis_index("expert")
    own_hot = (jnp.arange(experts, dtype=jnp.int32) == own).astype(f32)[None, :]
    probs = jax.nn.softmax(contract(received, router_w, (1, 0)), axis=-1)
    gate = jnp.sum(probs * own_hot, axis=-1, keepdims=True)
    grad_recv_f = grad_recv.astype(f32)
    grad_produced = (grad_recv_f * gate).astype(bf16)
    preact = contract(received, weight_in, (1, 0))
    gelu_values, gelu_pullback = jax.vjp(gelu_tanh, preact)
    active = gelu_values.astype(bf16)
    produced = contract(active, weight_out, (1, 0)).astype(bf16)
    gate_grad = jnp.sum(grad_recv_f * produced.astype(f32), axis=-1, keepdims=True)
    logit_low = (gate_grad * gate * (own_hot - probs)).astype(bf16)
    grad_active = contract(grad_produced, weight_out, (1, 1))
    grad_preact = gelu_pullback(grad_active)[0].astype(bf16)
    grad_received = contract(grad_preact, weight_in, (1, 1)) + contract(logit_low, router_w, (1, 1))
    grad_rows = exchange(grad_received.astype(bf16), experts)
    in_grad = contract(received, grad_preact, (0, 0)).astype(bf16)
    out_grad_t = contract(grad_produced, active, (0, 0)).astype(bf16)
    router_grad = contract(received, logit_low, (0, 0))
    return grad_rows, produced, in_grad, out_grad_t, router_grad


def tail_native(tokens, gain, normed_low, dq, dk, dv, wq, wk, wv, grad_hidden, dwo, small):
    tokens_f = tokens.astype(f32)
    grads = jnp.stack([dwo.astype(f32)] + [contract(normed_low, d, (0, 0)) for d in (dq, dk, dv)])
    grad_normed = contract(dq, wq, (1, 1)) + contract(dk, wk, (1, 1)) + contract(dv, wv, (1, 1))
    _, scale = rms_forward(tokens_f, gain)
    grad_tokens, gain_grad = rms_backward(grad_normed, tokens_f, scale, gain)
    grads, gain_grad, small = lax.psum((grads, gain_grad, small), ("dp", "expert"))
    return grads, grad_hidden + grad_tokens, gain_grad, small


def on_device(
    tokens, gain_one, query_w, key_w, value_w, out_w, rel_table, gain_two, router_w,
    expert_in, expert_out, routes, buckets, cotangent,
):
    seq_len, width = tokens.shape
    heads = rel_table.shape[1]
    groups = lax.axis_size("dp")
    experts = lax.axis_size("expert")
    capacity = (5 * seq_len + 4 * experts - 1) // (4 * experts)
    slots = experts * capacity
    weight_in = expert_in[0]
    weight_out = expert_out[0]
    kernels = capacity % 16 == 0 and experts == 8 and groups == 4

    route_ids = routes[:, 0]
    route_hot = route_ids[:, None] == jnp.arange(experts, dtype=jnp.int32)[None, :]
    route_int = route_hot.astype(jnp.int32)
    route_float = route_hot.astype(f32)
    position = jnp.sum((jnp.cumsum(route_int, axis=0) - 1) * route_int, axis=1)
    slot_index = jnp.where(position < capacity, route_ids * capacity + position, slots)
    pick = (jnp.arange(slots, dtype=jnp.int32)[:, None] == slot_index[None, :]).astype(bf16)

    def scatter_rows(rows):
        return contract(pick, rows, (1, 0)).astype(bf16)

    def gather_rows(rows):
        return contract(pick, rows, (0, 0))

    tokens_f = tokens.astype(f32)
    gains = jnp.stack([gain_one, gain_two])
    if kernels:
        queries, key_rows, value_rows, normed_low, grad_send, slot_row, slot_column = first_pass(
            tokens, gains, query_w, key_w, value_w, routes.reshape(1, seq_len), cotangent, capacity, experts
        )
    else:
        grad_send = scatter_rows(cotangent)
        normed_low = rms_forward(tokens_f, gain_one)[0].astype(bf16)
        queries = contract(normed_low, query_w, (1, 0)).astype(bf16)
        key_rows = contract(normed_low, key_w, (1, 0)).astype(bf16)
        value_rows = contract(normed_low, value_w, (1, 0)).astype(bf16)
    reach = jnp.concatenate([buckets, jnp.full((1,), -1, jnp.int32)])[::-1]
    bucket_hot = (jnp.arange(rel_table.shape[0], dtype=jnp.int32)[:, None] == reach[None, :]).astype(f32)
    spread = jnp.einsum("bh,bx->hx", rel_table, bucket_hot, precision=highest)
    spread = spread.reshape(heads // 2, 2, 2 * seq_len)
    context, context_t, logsum, weights, grad_recv = attend(
        queries, key_rows, value_rows, spread, grad_send, experts if kernels else 0
    )
    if kernels:
        router_pad = jnp.pad(router_w, ((0, 0), (0, 128 - experts)))
        hidden, send, meta = middle_pass(
            tokens, context, out_w, gains, router_pad, slot_row, slot_column, slots, experts
        )
        grad_rows, produced, in_grad, out_grad_t, router_grad, shared = expert_pass(
            send, grad_recv, weight_in, weight_out, router_pad, experts, capacity
        )
        grad_hidden, out_w_grad, grad_context, gain_two_grad = combine_pass(
            grad_rows, hidden, cotangent, gains, context, out_w, meta
        )
    else:
        grad_recv = exchange(grad_send, experts)
        hidden = tokens_f + contract(context, out_w, (1, 0))
        normed_two, scale_two = rms_forward(hidden, gain_two)
        normed_two_low = normed_two.astype(bf16)
        grad_rows, produced, in_grad, out_grad_t, router_grad = expert_native(
            scatter_rows(normed_two_low), grad_recv, weight_in, weight_out, router_w, experts
        )
        router_probs = jax.nn.softmax(contract(normed_two_low, router_w, (1, 0)), axis=-1)
        gate_value = jnp.sum(router_probs * route_float, axis=-1, keepdims=True)
        grad_normed_two = gather_rows(grad_rows)
        grad_hidden_norm, gain_two_grad = rms_backward(grad_normed_two, hidden, scale_two, gain_two)
        grad_hidden = cotangent.astype(f32) + grad_hidden_norm
        branch_low = grad_hidden.astype(bf16)
        out_w_grad = contract(context, branch_low, (0, 0)).astype(bf16)
        grad_context = contract(branch_low, out_w, (1, 1)).astype(bf16)

    if kernels:
        grads, input_grad, small, shares, output = back_pass(
            queries, key_rows, value_rows, grad_context, context_t, query_w, key_w, value_w,
            bucket_hot, gains, normed_low, tokens, grad_hidden, out_w_grad,
            gain_two_grad, router_grad,
            out_grad_t, shared, in_grad, weights, produced, hidden,
            meta, groups, experts,
        )
        tiles = width // 128
        first = 8 + rel_table.shape[0]
        gain_one_grad = small[:tiles].reshape(-1)
        rel_grad = small[8:first, :heads]
        gain_two_grad = small[first : first + tiles].reshape(-1)
        router_grad = small[first + 8 :].reshape(experts, width).T
        out_share, in_share = shares[0], shares[1]
    else:
        output = (hidden + gate_value * gather_rows(exchange(produced, experts))).astype(bf16)
        in_share = lax.psum_scatter(in_grad, "dp", scatter_dimension=0, tiled=True)
        out_share = lax.psum_scatter(out_grad_t, "dp", scatter_dimension=0, tiled=True)
        query_grad, key_grad, value_grad, diagonals = attend_back(
            queries, key_rows, value_rows, grad_context, spread, context_t, logsum
        )
        diagonals = diagonals[:, :2].reshape(heads, 2 * seq_len)
        rel_grad = jnp.einsum("bx,hx->bh", bucket_hot, diagonals, precision=highest)
        grads, input_grad, gain_one_grad, small = tail_native(
            tokens, gain_one, normed_low, query_grad, key_grad, value_grad,
            query_w, key_w, value_w, grad_hidden, out_w_grad, (rel_grad, gain_two_grad, router_grad),
        )
        rel_grad, gain_two_grad, router_grad = small
    grads = grads.astype(f32)
    return (
        output, input_grad, grads[1], grads[2], grads[3], grads[0], rel_grad,
        gain_one_grad, gain_two_grad, router_grad, in_share.astype(f32)[None], out_share.astype(f32).T[None],
    )


def solution(mesh):
    rows = P(("dp", "expert"), None)
    whole = P()
    split = P("expert", None, None)
    return jax.shard_map(
        on_device,
        mesh=mesh,
        in_specs=(
            rows, whole, whole, whole, whole, whole, whole, whole, whole, split, split, rows, whole, rows,
        ),
        out_specs=(
            rows, rows, whole, whole, whole, whole, whole, whole, whole, whole,
            P("expert", "dp", None), P("expert", None, "dp"),
        ),
        check_vma=False,
    )
```

```python
import functools

import jax
import jax.numpy as jnp
from jax import lax
from jax.experimental import pallas as pl
from jax.experimental.pallas import tpu as pltpu
from jax.sharding import PartitionSpec as P

bf16 = jnp.bfloat16
f32 = jnp.float32
epsilon = 1e-06
highest = lax.Precision.HIGHEST

def dot_f32(left, right):
    return lax.dot_general(left, right, (((1,), (0,)), ((), ())), preferred_element_type=f32)


def dot_nt(left, right):
    return lax.dot_general(left, right, (((1,), (1,)), ((), ())), preferred_element_type=f32)


def fill_toeplitz(base_ref, head, row):
    rows, width = base_ref.shape[1:]
    spread = jnp.broadcast_to(row, (8, width))
    eight = pltpu.roll(spread, 0, 1, stride=1, stride_axis=0)
    for group in range(rows // 8):
        base_ref[head, 8 * group : 8 * group + 8, :] = (
            eight if group == 0 else pltpu.roll(eight, 8 * group, 1)
        )


def attend_kernel(
    experts, q_ref, k_ref, v_ref, u_ref, gsend_h, ctx_ref, ctxt_ref, lse_ref, p_h, grecv_h,
    base, qt, vt, s_scr, p_scr, p_sem, send_g, recv_g, own_sem,
):
    seq = q_ref.shape[0]
    span = 256
    half = seq
    qt[...] = q_ref[...].T
    vt[...] = v_ref[...].T
    for head in range(2):
        fill_toeplitz(base, head, u_ref[0, head : head + 1, :])
    zeros = jnp.zeros((64, span), bf16)
    pair = pl.program_id(0)

    if experts:
        me = lax.axis_index("expert")
        count = grecv_h.shape[0] // experts
        rows_of = lambda who: pl.ds(pl.multiple_of(who * count, 16), count)
        peers = [lax.rem(me + k, experts) for k in range(1, experts)]
        barrier = pltpu.get_barrier_semaphore()
        own = pltpu.make_async_copy(gsend_h.at[rows_of(me), :], grecv_h.at[rows_of(me), :], own_sem)

        def give(peer, slot):
            return pltpu.make_async_remote_copy(
                src_ref=gsend_h.at[rows_of(peer), :], dst_ref=grecv_h.at[rows_of(slot), :],
                send_sem=send_g.at[peer], recv_sem=recv_g.at[slot], device_id={"expert": peer},
            )

        @pl.when(pair == 0)
        def _():
            for peer in peers:
                pl.semaphore_signal(barrier, inc=1, device_id={"expert": peer})
            own.start()

    def save(idx, slot):
        cols = pl.ds(pl.multiple_of(idx * span, span), span)
        return pltpu.make_async_copy(p_scr.at[slot], p_h.at[pl.ds(2 * pair, 2), :, cols], p_sem.at[slot])

    def step(idx, carry):
        slot = lax.rem(idx, 2)

        @pl.when((pair > 0) | (idx > 1))
        def _():
            save(idx, slot).wait()

        cols = pl.ds(pl.multiple_of(idx * span, span), span)
        outs = []
        for head in range(2):
            part = qt[64 * head : 64 * head + 64, cols]
            rhs = jnp.concatenate([part, zeros] if head == 0 else [zeros, part], axis=0)
            peak = None
            for kb in range(seq // 128):
                rows = slice(128 * kb, 128 * kb + 128)
                offs = pl.multiple_of(half + span * idx - 128 * kb, 128)
                s = dot_f32(k_ref[rows, :], rhs) + base[head, :, pl.ds(offs, span)]
                s_scr[head, rows, :] = s
                now = jnp.max(s.reshape(16, 8, span), axis=0)
                peak = now if peak is None else jnp.maximum(peak, now)
            peak = jnp.max(peak, axis=0, keepdims=True)
            total = None
            for kb in range(seq // 128):
                rows = slice(128 * kb, 128 * kb + 128)
                e = jnp.exp(s_scr[head, rows, :] - peak)
                s_scr[head, rows, :] = e
                now = jnp.sum(e.reshape(16, 8, span), axis=0)
                total = now if total is None else total + now
            total = jnp.sum(total, axis=0, keepdims=True)
            inv = 1.0 / total
            for kb in range(seq // 128):
                rows = slice(128 * kb, 128 * kb + 128)
                p_scr[slot, head, rows, :] = (s_scr[head, rows, :] * inv).astype(bf16)
            lse_ref[0, head : head + 1, cols] = peak + jnp.log(total)
            outs.append(dot_f32(vt[64 * head : 64 * head + 64, :], p_scr[slot, head]))
        save(idx, slot).start()
        both = jnp.concatenate(outs, axis=0)
        ctxt_ref[:, cols] = both
        ctx_ref[cols, :] = both.T.astype(bf16)
        return carry

    if experts:
        @pl.when(pair == 0)
        def _():
            pl.semaphore_wait(barrier, experts - 1)
            for peer in peers:
                give(peer, me).start()

    lax.fori_loop(0, seq // span, step, 0)

    @pl.when(pair == pl.num_programs(0) - 1)
    def _():
        for slot in range(2):
            save(slot, slot).wait()
        if experts:
            own.wait()
            for peer in peers:
                give(peer, me).wait_send()
                give(peer, peer).wait_recv()


def attend(q, k, v, u, gsend, experts=0):
    seq, width = q.shape
    pairs = width // 128
    blk = pl.BlockSpec((seq, 128), lambda p: (0, p))
    dma = pltpu.SemaphoreType.DMA
    return pl.pallas_call(
        functools.partial(attend_kernel, experts),
        grid=(pairs,),
        in_specs=[
            blk, blk, blk, pl.BlockSpec((1, 2, 2 * seq), lambda p: (p, 0, 0)), pl.BlockSpec(memory_space=pl.ANY),
        ],
        out_specs=[
            blk,
            pl.BlockSpec((128, seq), lambda p: (p, 0)),
            pl.BlockSpec((1, 8, seq), lambda p: (p, 0, 0)),
            pl.BlockSpec(memory_space=pl.ANY),
            pl.BlockSpec(memory_space=pl.ANY),
        ],
        out_shape=[
            jax.ShapeDtypeStruct((seq, width), bf16),
            jax.ShapeDtypeStruct((width, seq), f32),
            jax.ShapeDtypeStruct((pairs, 8, seq), f32),
            jax.ShapeDtypeStruct((2 * pairs, seq, seq), bf16),
            jax.ShapeDtypeStruct(gsend.shape, bf16),
        ],
        scratch_shapes=[
            pltpu.VMEM((2, 128, 2 * seq), f32),
            pltpu.VMEM((128, seq), bf16),
            pltpu.VMEM((128, seq), bf16),
            pltpu.VMEM((2, seq, 256), f32),
            pltpu.VMEM((2, 2, seq, 256), bf16),
            dma((2,)),
            dma((max(experts, 1),)), dma((max(experts, 1),)), dma(()),
        ],
        compiler_params=pltpu.CompilerParams(
            vmem_limit_bytes=62 << 20, has_side_effects=experts > 0, collective_id=3 if experts else None
        ),
        name="attend",
    )(q, k, v, u, gsend)


def first_kernel(
    capacity, experts, tok, gain, wq, wk, wv, route, cot, q_o, k_o, v_o, nl_o, gsend_o, slot_o, column_o, slot
):
    step = pl.program_id(0)
    slots = experts * capacity
    seq = route.shape[1]

    @pl.when(step == 0)
    def _():
        lane = lax.broadcasted_iota(jnp.int32, (8, seq), 1)
        hot = jnp.where(lax.broadcasted_iota(jnp.int32, (8, seq), 0) == route[...], 1.0, 0.0)
        count = hot
        shift = 1
        while shift < seq:
            count = count + jnp.where(lane >= shift, pltpu.roll(count, shift, 1), 0.0)
            shift *= 2
        position = jnp.sum(hot * (count - 1.0), axis=0, keepdims=True)
        place = route[...].astype(f32) * capacity + position
        slot[...] = jnp.where(position < capacity, place, float(slots))
        slot_o[...] = slot[...]
        column_o[...] = jnp.broadcast_to(slot[...], (128, seq)).T

    values = tok[...].astype(f32)
    scale = lax.rsqrt(jnp.mean(values * values, axis=-1, keepdims=True) + epsilon)
    normed = (values * scale * gain[0:1, :]).astype(bf16)
    nl_o[...] = normed
    for weight, out in ((wq, q_o), (wk, k_o), (wv, v_o)):
        out[...] = dot_f32(normed, weight[...]).astype(bf16)
    rows = gsend_o.shape[0]
    number = lax.broadcasted_iota(jnp.int32, (rows, seq), 0) + step * rows
    pick = jnp.where(number.astype(f32) == slot[...], 1.0, 0.0).astype(bf16)
    gsend_o[...] = dot_f32(pick, cot[...]).astype(bf16)


def first_pass(tokens, gain, wq, wk, wv, route, cotangent, capacity, experts):
    seq, width = tokens.shape
    slots = experts * capacity
    steps = 4
    rows = pl.BlockSpec((seq // steps, width), lambda i: (i, 0))
    fixed = lambda shape: pl.BlockSpec(shape, lambda i: (0, 0))
    return pl.pallas_call(
        functools.partial(first_kernel, capacity, experts),
        grid=(steps,),
        in_specs=[rows, fixed(gain.shape)] + [fixed(wq.shape)] * 3 + [fixed(route.shape), fixed(cotangent.shape)],
        out_specs=[rows] * 4 + [pl.BlockSpec((slots // steps, width), lambda i: (i, 0)), fixed(route.shape), fixed((seq, 128))],
        out_shape=[jax.ShapeDtypeStruct((seq, width), bf16)] * 4
        + [jax.ShapeDtypeStruct((slots, width), bf16), jax.ShapeDtypeStruct(route.shape, f32),
           jax.ShapeDtypeStruct((seq, 128), f32)],
        scratch_shapes=[pltpu.VMEM(route.shape, f32)],
        compiler_params=pltpu.CompilerParams(vmem_limit_bytes=62 << 20),
        cost_estimate=pl.CostEstimate(
            flops=6 * seq * width * width + 2 * slots * seq * width, bytes_accessed=20 * seq * width, transcendentals=seq
        ),
        name="first",
    )(tokens, gain, wq, wk, wv, route, cotangent)


def middle_kernel(experts, steps, tok, ctx, wo, gain, rw, slot, column, hid_o, xs_o, meta_o, normed):
    step = pl.program_id(0)
    span, width = tok.shape
    seq = normed.shape[0]

    @pl.when(step < steps)
    def _():
        hidden = tok[...].astype(f32) + dot_f32(ctx[...], wo[...])
        hid_o[...] = hidden
        scale = lax.rsqrt(jnp.mean(hidden * hidden, axis=-1, keepdims=True) + epsilon)
        low = (hidden * scale * gain[1:2, :]).astype(bf16)
        normed[pl.ds(pl.multiple_of(step * span, span), span), :] = low
        lane = lax.broadcasted_iota(jnp.int32, (span, 128), 1)
        logits = jnp.where(lane < experts, dot_f32(low, rw[...]), -1e30)
        weights = jnp.exp(logits - jnp.max(logits, axis=-1, keepdims=True))
        place = column[...]
        each = xs_o.shape[0] * (pl.num_programs(0) - steps) // experts
        first = (lane * each).astype(f32)
        chosen = (place >= first) & (place < first + each) & (lane < experts)
        gate = jnp.sum(jnp.where(chosen, weights, 0.0), axis=-1, keepdims=True) / jnp.sum(
            weights, axis=-1, keepdims=True
        )
        meta_o[...] = jnp.where(lane == 0, gate, place)

    @pl.when(step >= steps)
    def _():
        rows = xs_o.shape[0]
        number = lax.broadcasted_iota(jnp.int32, (rows, seq), 0) + (step - steps) * rows
        pick = jnp.where(number.astype(f32) == slot[...], 1.0, 0.0).astype(bf16)
        xs_o[...] = dot_f32(pick, normed[...]).astype(bf16)


def middle_pass(tokens, ctx, wo, gain, rw, slot, column, slots, experts):
    seq, width = tokens.shape
    steps = 4
    span = seq // steps
    each = slots // steps
    token_map = lambda i: (jnp.minimum(i, steps - 1), 0)
    fixed = lambda shape: pl.BlockSpec(shape, lambda i: (0, 0))
    return pl.pallas_call(
        functools.partial(middle_kernel, experts, steps),
        grid=(2 * steps,),
        in_specs=[
            pl.BlockSpec((span, width), token_map), pl.BlockSpec((span, width), token_map), fixed(wo.shape),
            fixed(gain.shape), fixed(rw.shape), fixed(slot.shape), pl.BlockSpec((span, 128), token_map),
        ],
        out_specs=[
            pl.BlockSpec((span, width), token_map),
            pl.BlockSpec((each, width), lambda i: (jnp.maximum(i - steps, 0), 0)),
            pl.BlockSpec((span, 128), token_map),
        ],
        out_shape=[
            jax.ShapeDtypeStruct((seq, width), f32),
            jax.ShapeDtypeStruct((slots, width), bf16),
            jax.ShapeDtypeStruct((seq, 128), f32),
        ],
        scratch_shapes=[pltpu.VMEM((seq, width), bf16)],
        compiler_params=pltpu.CompilerParams(vmem_limit_bytes=62 << 20),
        cost_estimate=pl.CostEstimate(
            flops=2 * seq * width * width + 2 * slots * seq * width, bytes_accessed=10 * seq * width, transcendentals=seq
        ),
        name="middle",
    )(tokens, ctx, wo, gain, rw, slot, column)


def combine_kernel(gback, hid, cot, gain, ctx, wo, meta, ghid_o, dwo_o, gctx_o, gain_o, total_w):
    step = pl.program_id(0)
    span = hid.shape[0]
    slots = gback.shape[0]
    where = lax.broadcasted_iota(jnp.int32, (span, slots), 1).astype(f32)
    pick = jnp.where(meta[:, 1:2] == where, 1.0, 0.0).astype(bf16)
    grad = dot_f32(pick, gback[...])
    values = hid[...]
    scale = lax.rsqrt(jnp.mean(values * values, axis=-1, keepdims=True) + epsilon)
    weighted = grad * gain[1:2, :]
    inner = jnp.mean(weighted * values, axis=-1, keepdims=True)
    total = cot[...].astype(f32) + scale * weighted - values * (scale * scale * scale * inner)
    ghid_o[...] = total
    branch = total.astype(bf16)
    gctx_o[...] = dot_nt(branch, wo[...]).astype(bf16)
    gains = jnp.sum(grad * values * scale, axis=0, keepdims=True)
    now = dot_f32(ctx[...].T, branch)

    @pl.when(step == 0)
    def _():
        total_w[...] = now
        gain_o[...] = gains

    @pl.when(step > 0)
    def _():
        total_w[...] += now
        gain_o[...] += gains

    @pl.when(step == pl.num_programs(0) - 1)
    def _():
        dwo_o[...] = total_w[...].astype(bf16)


def combine_pass(gback, hidden, cotangent, gain, ctx, wo, meta):
    seq, width = hidden.shape
    steps = 4
    rows = pl.BlockSpec((seq // steps, width), lambda i: (i, 0))
    fixed = lambda shape: pl.BlockSpec(shape, lambda i: (0, 0))
    return pl.pallas_call(
        combine_kernel,
        grid=(steps,),
        in_specs=[
            fixed(gback.shape), rows, rows, fixed(gain.shape), rows, fixed(wo.shape),
            pl.BlockSpec((seq // steps, 128), lambda i: (i, 0)),
        ],
        out_specs=[rows, fixed((width, width)), rows, fixed((1, width))],
        out_shape=[
            jax.ShapeDtypeStruct((seq, width), f32),
            jax.ShapeDtypeStruct((width, width), bf16),
            jax.ShapeDtypeStruct((seq, width), bf16),
            jax.ShapeDtypeStruct((1, width), f32),
        ],
        scratch_shapes=[pltpu.VMEM((width, width), f32)],
        compiler_params=pltpu.CompilerParams(vmem_limit_bytes=62 << 20),
        cost_estimate=pl.CostEstimate(
            flops=4 * seq * width * width + 2 * gback.shape[0] * seq * width,
            bytes_accessed=16 * seq * width, transcendentals=seq,
        ),
        name="combine",
    )(gback, hidden, cotangent, gain, ctx, wo, meta)


def split_rows(row):
    hi = row.astype(bf16).astype(f32)
    mid = (row - hi).astype(bf16).astype(f32)
    low = row - hi - mid
    idx = lax.broadcasted_iota(jnp.int32, (16, row.shape[1]), 0)
    return jnp.where(idx == 0, hi, jnp.where(idx == 1, mid, jnp.where(idx == 2, low, 0.0))).astype(bf16)


def attend_back_kernel(
    q_ref, k_ref, v_ref, g_ref, u_ref, ctxt_ref, lse_ref,
    dq_ref, dk_ref, dv_ref, diag_ref,
    base, acc, kaug, vaug, qaug, gaug, qz, gz, kt, dqt,
):
    seq = q_ref.shape[0]
    span = 256
    lane = lax.broadcasted_iota(jnp.int32, (seq, 128), 1)
    gt = g_ref[...].T
    qtv = q_ref[...].T
    kt[...] = k_ref[...].T
    gtf = gt.astype(f32)
    pad = jnp.zeros((48, seq), bf16)
    one = jnp.ones((seq, 128), bf16)
    nil = jnp.zeros((seq, 128), bf16)
    acc[...] = jnp.zeros_like(acc)
    for head in range(2):
        fill_toeplitz(base, head, u_ref[0, head : head + 1, :])
        own = (lane < 64) if head == 0 else (lane >= 64)
        origin = 64 if head == 0 else 0
        extra = jnp.where((lane >= origin) & (lane < origin + 3), one, nil)
        kaug[head] = jnp.where(own, k_ref[...], extra)
        vaug[head] = jnp.where(own, v_ref[...], extra)
        qz[head] = jnp.where(own, q_ref[...], nil)
        gz[head] = jnp.where(own, g_ref[...], nil)
        rows = slice(64 * head, 64 * head + 64)
        lse = split_rows(-lse_ref[0, head : head + 1, :])
        dsum = split_rows(-jnp.sum(gtf[rows] * ctxt_ref[rows, :], axis=0, keepdims=True))
        for dst, src, aug in ((qaug, qtv, lse), (gaug, gt, dsum)):
            dst[head, rows, :] = src[rows]
            dst[head, origin : origin + 16, :] = aug
            dst[head, origin + 16 : origin + 64, :] = pad

    dqt[...] = jnp.zeros_like(dqt)

    def step(idx, carry):
        rows = pl.ds(pl.multiple_of(idx * span, span), span)
        dv = None
        dk = None
        for head in range(2):
            s = dot_f32(kaug[head, rows, :], qaug[head])
            dp = dot_f32(vaug[head, rows, :], gaug[head])
            tops = []
            grads = []
            for part in range(2):
                offs = pl.ds(pl.multiple_of(seq - span * idx - 128 * part, 128), seq)
                p = jnp.exp(s[128 * part : 128 * part + 128] + base[head, :, offs])
                ds_ = p * dp[128 * part : 128 * part + 128]
                acc[head, :, offs] += ds_
                tops.append(p.astype(bf16))
                grads.append(ds_.astype(bf16))
            p = jnp.concatenate(tops, axis=0)
            ds_ = jnp.concatenate(grads, axis=0)
            now = dot_f32(p, gz[head])
            dv = now if dv is None else dv + now
            now = dot_f32(ds_, qz[head])
            dk = now if dk is None else dk + now
            dqt[64 * head : 64 * head + 64, :] += dot_f32(kt[64 * head : 64 * head + 64, rows], ds_)
        dv_ref[rows, :] = dv.astype(bf16)
        dk_ref[rows, :] = dk.astype(bf16)
        return carry

    lax.fori_loop(0, seq // span, step, 0)
    dq_ref[...] = dqt[...].T.astype(bf16)
    width = 2 * seq
    for head in range(2):
        total = acc[head, 0:8, :]
        for group in range(1, 16):
            total = total + pltpu.roll(acc[head, 8 * group : 8 * group + 8, :], width - 8 * group, 1)
        sub = lax.broadcasted_iota(jnp.int32, (8, width), 0)
        for bit in (1, 2, 4):
            total = jnp.where((sub & bit) != 0, pltpu.roll(total, width - bit, 1), total)
        diag_ref[0, head : head + 1, :] = jnp.sum(total, axis=0, keepdims=True)


def attend_back(q, k, v, g, u, ctxt, lse):
    seq, width = q.shape
    pairs = width // 128
    blk = pl.BlockSpec((seq, 128), lambda p: (0, p))
    return pl.pallas_call(
        attend_back_kernel,
        grid=(pairs,),
        in_specs=[
            blk, blk, blk, blk,
            pl.BlockSpec((1, 2, 2 * seq), lambda p: (p, 0, 0)),
            pl.BlockSpec((128, seq), lambda p: (p, 0)),
            pl.BlockSpec((1, 8, seq), lambda p: (p, 0, 0)),
        ],
        out_specs=[blk, blk, blk, pl.BlockSpec((1, 8, 2 * seq), lambda p: (p, 0, 0))],
        out_shape=[jax.ShapeDtypeStruct((seq, width), bf16)] * 3
        + [jax.ShapeDtypeStruct((pairs, 8, 2 * seq), f32)],
        scratch_shapes=[
            pltpu.VMEM((2, 128, 2 * seq), f32),
            pltpu.VMEM((2, 128, 2 * seq), f32),
            pltpu.VMEM((2, seq, 128), bf16),
            pltpu.VMEM((2, seq, 128), bf16),
            pltpu.VMEM((2, 128, seq), bf16),
            pltpu.VMEM((2, 128, seq), bf16),
            pltpu.VMEM((2, seq, 128), bf16),
            pltpu.VMEM((2, seq, 128), bf16),
            pltpu.VMEM((128, seq), bf16),
            pltpu.VMEM((128, seq), f32),
        ],
        compiler_params=pltpu.CompilerParams(vmem_limit_bytes=56 << 20),
        cost_estimate=pl.CostEstimate(
            flops=40 * seq * seq * width, bytes_accessed=20 * seq * width, transcendentals=seq * seq * 12
        ),
        name="attend_back",
    )(q, k, v, g, u, ctxt, lse)


def gelu_both(v):
    scale = 0.7978845608028654
    square = v * v
    t = jnp.tanh(scale * v * (1.0 + 0.044715 * square))
    half = 0.5 * (1.0 + t)
    slope = half + 0.5 * v * (1.0 - t * t) * (scale * (1.0 + 3 * 0.044715 * square))
    return v * half, slope


def expert_kernel(
    experts, capacity, tile,
    xs, gr_h, win_h, wout_h, rw,
    gback_o, prod_o, dwin_o, dwout_o, drw_o, shared_o,
    xall, gr, gp, win, wout, act, gpre, gback, gsend, prod, logit, acc_p, acc_g, xt, gpt, stage, dwt,
    send_x, recv_x, send_g, recv_g, local, out_sem, send_s, recv_s,
):
    me = lax.axis_index("expert")
    place = me // 2
    chips = experts // 2
    span = 2 * capacity
    width = xall.shape[1]
    hidden = win.shape[1]
    barrier = pltpu.get_barrier_semaphore()
    for k in range(1, experts):
        pl.semaphore_signal(barrier, inc=1, device_id={"expert": lax.rem(me + k, experts)})
    my_dp = lax.axis_index("dp")
    dp_x, dp_y = lax.rem(my_dp, 2), my_dp // 2
    peer_x, peer_y = my_dp + 1 - 2 * dp_x, my_dp + 2 - 4 * dp_y
    for peer in (peer_x, peer_y):
        pl.semaphore_signal(barrier, inc=1, device_id={"dp": peer})
    loads = [
        pltpu.make_async_copy(win_h, win, local.at[0]),
        pltpu.make_async_copy(wout_h, wout, local.at[1]),
        pltpu.make_async_copy(gr_h, gr, local.at[2]),
    ]
    rows_of = lambda who: pl.ds(pl.multiple_of(who * capacity, 16), capacity)
    own = pltpu.make_async_copy(xs.at[rows_of(me), :], xall.at[rows_of(me), :], local.at[3])
    own.start()
    for copy in loads:
        copy.start()
    pl.semaphore_wait(barrier, experts + 1)

    def partner(step):
        high, low = place // 2, lax.rem(place, 2)
        fhigh, flow = step // 2, lax.rem(step, 2)
        return 2 * (high + fhigh - 2 * high * fhigh) + low + flow - 2 * low * flow

    def send_rows(peer):
        return pltpu.make_async_remote_copy(
            src_ref=xs.at[rows_of(peer), :], dst_ref=xall.at[rows_of(me), :],
            send_sem=send_x.at[peer], recv_sem=recv_x.at[me], device_id={"expert": peer},
        )

    def got_rows(peer):
        return pltpu.make_async_remote_copy(
            src_ref=xs.at[rows_of(peer), :], dst_ref=xall.at[rows_of(peer), :],
            send_sem=send_x.at[peer], recv_sem=recv_x.at[peer], device_id={"expert": peer},
        )

    def send_back(peer):
        return pltpu.make_async_remote_copy(
            src_ref=gsend.at[rows_of(peer), :], dst_ref=gback.at[rows_of(me), :],
            send_sem=send_g.at[peer], recv_sem=recv_g.at[me], device_id={"expert": peer},
        )

    def got_back(peer):
        return pltpu.make_async_remote_copy(
            src_ref=gsend.at[rows_of(peer), :], dst_ref=gback.at[rows_of(peer), :],
            send_sem=send_g.at[peer], recv_sem=recv_g.at[peer], device_id={"expert": peer},
        )

    sibling = me + 1 - 2 * lax.rem(me, 2)
    send_rows(sibling).start()
    for step in range(1, chips):
        for core in range(2):
            send_rows(2 * partner(step) + lax.rem(me + core, 2)).start()
    for copy in loads:
        copy.wait()

    lanes = lax.broadcasted_iota(jnp.int32, (span, rw.shape[1]), 1)
    mine = jnp.where(lanes == me, 1.0, 0.0)

    def work(step, carry):
        where = partner(step)
        base = pl.multiple_of(where * span, 32)

        @pl.when(step == 0)
        def _():
            own.wait()
            got_rows(sibling).wait_recv()

        @pl.when(step > 0)
        def _():
            got_rows(2 * where).wait_recv()
            got_rows(2 * where + 1).wait_recv()

        rows = pl.ds(base, span)
        x = xall[rows, :]
        logits = jnp.where(lanes < experts, dot_f32(x, rw[...]), -1e30)
        weights = jnp.exp(logits - jnp.max(logits, axis=-1, keepdims=True))
        probs = weights / jnp.sum(weights, axis=-1, keepdims=True)
        gate = jnp.sum(probs * mine, axis=-1, keepdims=True)
        gp[rows, :] = (gr[rows, :].astype(f32) * gate).astype(bf16)
        acc_p[...] = jnp.zeros_like(acc_p)
        acc_g[...] = jnp.zeros_like(acc_g)

        def block(idx, carry):
            cols = pl.ds(pl.multiple_of(idx * tile, tile), tile)
            h = dot_f32(xall[rows, :], win[:, cols])
            grad = dot_nt(gp[rows, :], wout[cols, :])
            value, slope = gelu_both(h)
            value = value.astype(bf16)
            grad = (grad * slope).astype(bf16)
            act[rows, cols] = value
            gpre[rows, cols] = grad
            acc_p[...] += dot_f32(value, wout[cols, :])
            acc_g[...] += dot_nt(grad, win[:, cols])
            return carry

        lax.fori_loop(0, hidden // tile, block, 0)
        made = acc_p[...].astype(bf16)
        prod[rows, :] = made
        gate_grad = jnp.sum(gr[rows, :].astype(f32) * made.astype(f32), axis=-1, keepdims=True)
        low = (gate_grad * gate * (mine - probs)).astype(bf16)
        low = jnp.where(lanes < experts, low, jnp.zeros_like(low))
        logit[rows, :] = low
        gsend[rows, :] = (acc_g[...] + dot_nt(low, rw[...])).astype(bf16)

        @pl.when(step == 0)
        def _():
            send_back(sibling).start()

        @pl.when(step > 0)
        def _():
            send_back(2 * where).start()
            send_back(2 * where + 1).start()

        return carry

    lax.fori_loop(0, chips, work, 0)
    outs = [
        pltpu.make_async_copy(prod, prod_o, local.at[0]),
        pltpu.make_async_copy(gsend.at[rows_of(me), :], gback.at[rows_of(me), :], local.at[3]),
    ]
    for copy in outs:
        copy.start()
    gpt[...] = gp[...].T

    share = width // 4
    tiles = hidden // tile
    split = tiles // 2

    def left_copy(idx, block):
        cols = pl.ds(pl.multiple_of(idx * tile, tile), tile)
        rows = pl.ds(pl.multiple_of((1 - dp_x + 2 * block) * share, 16), share)
        return pltpu.make_async_remote_copy(
            src_ref=dwt.at[rows, cols], dst_ref=shared_o.at[pl.ds(block * share, share), cols],
            send_sem=send_s.at[block, idx], recv_sem=recv_s.at[block, idx], device_id={"dp": peer_x},
        )

    def right_copy(idx, block):
        cols = pl.ds(pl.multiple_of(idx * tile, tile), tile)
        rows = pl.ds(pl.multiple_of((2 - 2 * dp_y + block) * share, 16), share)
        dst_cols = pl.ds(pl.multiple_of((idx - split) * tile, tile), tile)
        return pltpu.make_async_remote_copy(
            src_ref=dwt.at[rows, cols], dst_ref=shared_o.at[pl.ds((2 + block) * share, share), dst_cols],
            send_sem=send_s.at[block, idx], recv_sem=recv_s.at[block, idx], device_id={"dp": peer_y},
        )

    def out_block(step, carry):
        idx = lax.rem(step, 2) * split + step // 2
        cols = pl.ds(pl.multiple_of(idx * tile, tile), tile)
        dwt[:, cols] = dot_f32(gpt[...], act[:, cols]).astype(bf16)

        @pl.when(idx < split)
        def _():
            for block in range(2):
                left_copy(idx, block).start()

        @pl.when(idx >= split)
        def _():
            for block in range(2):
                right_copy(idx, block).start()

        return carry

    lax.fori_loop(0, tiles, out_block, 0)
    whole = pltpu.make_async_copy(dwt, dwout_o, local.at[2])
    whole.start()
    xt[...] = xall[...].T
    drw_o[...] = dot_f32(xt[...], logit[...])

    def put(slot, cols):
        return pltpu.make_async_copy(stage.at[slot], dwin_o.at[:, cols], out_sem.at[slot])

    def in_block(idx, carry):
        cols = pl.ds(pl.multiple_of(idx * tile, tile), tile)
        slot = lax.rem(idx, 2)

        @pl.when(idx > 1)
        def _():
            put(slot, cols).wait()

        stage[slot] = dot_f32(xt[...], gpre[:, cols]).astype(bf16)
        put(slot, cols).start()
        return carry

    lax.fori_loop(0, tiles, in_block, 0)
    for slot in range(2):
        put(slot, pl.ds(0, tile)).wait()
    whole.wait()
    for copy in outs:
        copy.wait()
    for k in range(1, experts):
        peer = lax.rem(me + k, experts)
        got_rows(peer).wait_send()
        got_back(peer).wait_send()
        got_back(peer).wait_recv()
    back = pltpu.make_async_copy(gback, gback_o, local.at[1])
    back.start()
    for idx in range(tiles):
        for block in range(2):
            (left_copy if idx < split else right_copy)(idx, block).wait()
    back.wait()


def expert_pass(xs, gr, weight_in, weight_out, router_pad, experts, capacity):
    slots, width = xs.shape
    hidden = weight_in.shape[1]
    tile = 512
    span = 2 * capacity
    hbm = pl.BlockSpec(memory_space=pl.ANY)
    vmem = pl.BlockSpec(memory_space=pltpu.VMEM)
    return pl.pallas_call(
        functools.partial(expert_kernel, experts, capacity, tile),
        in_specs=[hbm, hbm, hbm, hbm, vmem],
        out_specs=[hbm, hbm, hbm, hbm, vmem, hbm],
        out_shape=[
            jax.ShapeDtypeStruct((slots, width), bf16),
            jax.ShapeDtypeStruct((slots, width), bf16),
            jax.ShapeDtypeStruct((width, hidden), bf16),
            jax.ShapeDtypeStruct((width, hidden), bf16),
            jax.ShapeDtypeStruct((width, router_pad.shape[1]), f32),
            jax.ShapeDtypeStruct((width, hidden // 2), bf16),
        ],
        scratch_shapes=[
            pltpu.VMEM((slots, width), bf16),
            pltpu.VMEM((slots, width), bf16),
            pltpu.VMEM((slots, width), bf16),
            pltpu.VMEM((width, hidden), bf16),
            pltpu.VMEM((hidden, width), bf16),
            pltpu.VMEM((slots, hidden), bf16),
            pltpu.VMEM((slots, hidden), bf16),
            pltpu.VMEM((slots, width), bf16),
            pltpu.VMEM((slots, width), bf16),
            pltpu.VMEM((slots, width), bf16),
            pltpu.VMEM((slots, router_pad.shape[1]), bf16),
            pltpu.VMEM((span, width), f32),
            pltpu.VMEM((span, width), f32),
            pltpu.VMEM((width, slots), bf16),
            pltpu.VMEM((width, slots), bf16),
            pltpu.VMEM((2, width, tile), bf16),
            pltpu.VMEM((width, hidden), bf16),
            pltpu.SemaphoreType.DMA((experts,)),
            pltpu.SemaphoreType.DMA((experts,)),
            pltpu.SemaphoreType.DMA((experts,)),
            pltpu.SemaphoreType.DMA((experts,)),
            pltpu.SemaphoreType.DMA((4,)),
            pltpu.SemaphoreType.DMA((2,)),
            pltpu.SemaphoreType.DMA((2, hidden // tile)),
            pltpu.SemaphoreType.DMA((2, hidden // tile)),
        ],
        compiler_params=pltpu.CompilerParams(
            vmem_limit_bytes=60 << 20, collective_id=1, has_side_effects=True
        ),
        cost_estimate=pl.CostEstimate(
            flops=12 * slots * width * hidden, bytes_accessed=8 * width * hidden, transcendentals=slots * hidden
        ),
        name="experts",
    )(xs, gr, weight_in, weight_out, router_pad)


def remote(src, dst, send_sem, recv_sem, axis, peer):
    return pltpu.make_async_remote_copy(
        src_ref=src, dst_ref=dst, send_sem=send_sem, recv_sem=recv_sem, device_id={axis: peer}
    )


def others(count, mine):
    return [lax.rem(mine + k, count) for k in range(1, count)]


PLAN = (
    (11, 16, 19, 22, 24),
    (12, 17, 20, 23, 25),
    (5, 13, 16, 19, 21),
    (9, 15, 18, 21, 23),
    (13, 18, 21, 24, 26),
    (17, 21, 24, 27, 29),
    (21, 24, 27, 29, 31),
)
OUTPUT_SLOT = 17
EXPERT_SLOTS = ((6, 2, 0), (14, 3, 0), (15, 2, 1), (22, 3, 1))


def back_kernel(
    groups, experts, pairs,
    q_ref, k_ref, v_ref, g_ref, ctxt_ref, wq, wk, wv, hot, gain, nl_h, tok_h, ghid_h, dwo_h, gain_two, router,
    eout_h, shared_h, ein_h, p_h, prod_h, hid_h, meta,
    wsum_o, ing_o, small_o, esum_o, out_o,
    acc, vaug, gaug, qz, gz, kt, dqt, pbuf, pret, hbuf, obuf, dall, nt, tok,
    part, r1, r2, r3, full, sbuf, srecv, sone, stwo, keep, other, final,
    send1, recv1, send2, recv2, send3, recv3, send4, recv4, send5, recv5, send6, recv6, send7, recv7, local,
    send_a, recv_a, send_b, recv_b, out_sem, copy_sem, p_sem, send_p, recv_p, o_sem,
):
    seq = q_ref.shape[0]
    width = tok.shape[1]
    span = 256
    pair = pl.program_id(0)
    me = lax.axis_index("expert")
    my_dp = lax.axis_index("dp")
    core = lax.rem(me, 2)
    place = me // 2
    chips = experts // 2
    sibling = me + 1 - 2 * core
    half = width // 2
    piece = half // groups
    thick = part.shape[2]
    gain_rows = width // 128

    def half_rows(which):
        return pl.ds(pl.multiple_of(which * half, 16), half)

    def own_piece(which):
        return pl.ds(pl.multiple_of(core * half + which * piece, 16), piece)

    def copy1(c):
        return remote(part.at[c, half_rows(1 - core), :], r1.at[c], send1.at[c], recv1.at[c], "expert", sibling)

    def copy2(c, peer, slot):
        return remote(part.at[c, own_piece(peer), :], r2.at[c, slot], send2.at[c, peer], recv2.at[c, slot], "dp", peer)

    def copy3(c, peer, slot):
        return remote(
            r3.at[c, place], r3.at[c, slot], send3.at[c, peer], recv3.at[c, slot], "expert", 2 * peer + core
        )

    def copy4(c, peer, slot):
        return remote(
            full.at[c, own_piece(my_dp), :], full.at[c, own_piece(slot), :],
            send4.at[c, peer], recv4.at[c, slot], "dp", peer,
        )

    def copy5(c, which):
        return remote(
            full.at[c, half_rows(which), :], full.at[c, half_rows(which), :],
            send5.at[c], recv5.at[c], "expert", sibling,
        )

    def stage1(c):
        copy1(c).start()

    def stage2(c):
        copy1(c).wait_recv()
        part[c, half_rows(core), :] = (part[c, half_rows(core), :].astype(f32) + r1[c].astype(f32)).astype(bf16)
        for peer in others(groups, my_dp):
            copy2(c, peer, my_dp).start()

    def stage3(c):
        total = part[c, own_piece(my_dp), :].astype(f32)
        for peer in others(groups, my_dp):
            copy2(c, peer, peer).wait_recv()
            total = total + r2[c, peer].astype(f32)
        r3[c, place] = total.astype(bf16)
        for peer in others(chips, place):
            copy3(c, peer, place).start()

    def stage4(c):
        for peer in others(chips, place):
            copy3(c, peer, peer).wait_recv()
        total = r3[c, 0].astype(f32)
        for slot in range(1, chips):
            total = total + r3[c, slot].astype(f32)
        full[c, own_piece(my_dp), :] = total.astype(bf16)
        for peer in others(groups, my_dp):
            copy4(c, peer, my_dp).start()

    def stage5(c):
        for peer in others(groups, my_dp):
            copy4(c, peer, peer).wait_recv()
        copy5(c, core).start()

    def put_first(c):
        return pltpu.make_async_copy(full.at[c], wsum_o.at[0, :, thick * c : thick * c + thick], out_sem.at[c, 0])

    def put_pair(c, which):
        cols = pl.ds(128 * (c - 2) if isinstance(c, int) else pl.multiple_of(128 * (c - 2), 128), 128)
        return pltpu.make_async_copy(
            full.at[c, :, 128 * which : 128 * which + 128], wsum_o.at[1 + which, :, cols], out_sem.at[c, which]
        )

    def stage6(c):
        copy5(c, 1 - core).wait_recv()

        if c < 2:
            put_first(c).start()
        else:
            for which in range(3):
                put_pair(c, which).start()

    share = width // 4
    dp_x, dp_y = lax.rem(my_dp, 2), my_dp // 2
    peer_x, peer_y = my_dp + 1 - 2 * dp_x, my_dp + 2 - 4 * dp_y
    middle = keep.shape[1]
    left, right = pl.ds(0, middle), pl.ds(middle, middle)

    def share_rows(which):
        return pl.ds(pl.multiple_of(which * share, 16), share)

    def first_left(block):
        return remote(
            ein_h.at[share_rows(1 - dp_x + 2 * block), left], other.at[1, share_rows(block), :],
            send_a.at[0, block], recv_a.at[0, block], "dp", peer_x,
        )

    def first_right(block):
        return remote(
            ein_h.at[share_rows(2 - 2 * dp_y + block), right], other.at[1, share_rows(2 + block), :],
            send_a.at[1, block], recv_a.at[1, block], "dp", peer_y,
        )

    def second_left(which):
        return remote(
            keep.at[share_rows(1 - dp_y), :], final.at[which, :, left],
            send_b.at[which, 0], recv_b.at[which, 0], "dp", peer_y,
        )

    def second_right(which):
        return remote(
            keep.at[share_rows(2 + 1 - dp_x), :], final.at[which, :, right],
            send_b.at[which, 1], recv_b.at[which, 1], "dp", peer_x,
        )

    def own_loads(src):
        loads = []
        for block in range(2):
            loads.append(
                pltpu.make_async_copy(
                    src.at[share_rows(dp_x + 2 * block), left], keep.at[share_rows(block), :], copy_sem.at[block]
                )
            )
            loads.append(
                pltpu.make_async_copy(
                    src.at[share_rows(2 * dp_y + block), right], keep.at[share_rows(2 + block), :], copy_sem.at[2 + block]
                )
            )
        return loads

    def shared_load():
        return pltpu.make_async_copy(shared_h, other.at[0], copy_sem.at[4])

    def save(which):
        return pltpu.make_async_copy(final.at[which], esum_o.at[which], copy_sem.at[5])

    def experts_begin():
        for copy in own_loads(eout_h) + [shared_load()]:
            copy.start()
        for block in range(2):
            first_left(block).start()
            first_right(block).start()

    def experts_second(which):
        for copy in own_loads(eout_h if which == 0 else ein_h):
            copy.wait()
        if which == 0:
            shared_load().wait()
        else:
            for block in range(2):
                first_left(block).wait_recv()
                first_right(block).wait_recv()

        def block(idx, carry):
            rows = pl.ds(pl.multiple_of(idx * 64, 64), 64)
            keep[rows, :] = (keep[rows, :].astype(f32) + other[which, rows, :].astype(f32)).astype(bf16)
            return carry

        lax.fori_loop(0, width // 64, block, 0)
        second_left(which).start()
        second_right(which).start()

    def experts_last(which):
        second_left(which).wait()
        second_right(which).wait()

        def block(idx, carry):
            rows = pl.ds(pl.multiple_of(idx * 64, 64), 64)
            mine_left = pl.ds(pl.multiple_of(dp_y * share + idx * 64, 64), 64)
            mine_right = pl.ds(pl.multiple_of((2 + dp_x) * share + idx * 64, 64), 64)
            final[which, rows, left] = (final[which, rows, left].astype(f32) + keep[mine_left, :].astype(f32)).astype(bf16)
            final[which, rows, right] = (final[which, rows, right].astype(f32) + keep[mine_right, :].astype(f32)).astype(bf16)
            return carry

        lax.fori_loop(0, share // 64, block, 0)
        if which == 0:
            for copy in own_loads(ein_h):
                copy.start()
        else:
            save(0).wait()
        save(which).start()

    early = pl.ds(8 + hot.shape[0], sbuf.shape[0] - 8 - hot.shape[0])
    late = pl.ds(0, 8 + hot.shape[0])

    def copy6(part_idx, rows, peer, slot):
        return remote(
            sbuf.at[rows, :], srecv.at[slot, rows, :],
            send6.at[part_idx, peer], recv6.at[part_idx, slot], "expert", peer,
        )

    def copy7(part_idx, rows, peer, slot):
        return remote(
            sone.at[rows, :], stwo.at[slot, rows, :],
            send7.at[part_idx, peer], recv7.at[part_idx, slot], "dp", peer,
        )

    def small1(part_idx, rows):
        srecv[me, rows, :] = sbuf[rows, :]
        for peer in others(experts, me):
            copy6(part_idx, rows, peer, me).start()

    def small2(part_idx, rows):
        for peer in others(experts, me):
            copy6(part_idx, rows, peer, peer).wait_recv()
        total = srecv[0, rows, :]
        for slot in range(1, experts):
            total = total + srecv[slot, rows, :]
        sone[rows, :] = total
        stwo[my_dp, rows, :] = total
        for peer in others(groups, my_dp):
            copy7(part_idx, rows, peer, my_dp).start()

    def small3(part_idx, rows):
        for peer in others(groups, my_dp):
            copy7(part_idx, rows, peer, peer).wait_recv()
        total = stwo[0, rows, :]
        for slot in range(1, groups):
            total = total + stwo[slot, rows, :]
        small_o[rows, :] = total

    stages = (stage2, stage3, stage4, stage5, stage6)

    def advance(slot):
        for c, slots in enumerate(PLAN):
            for at, stage in reversed(list(zip(slots, stages))):
                if at < 4 * pairs:
                    pl.when(slot == at)(functools.partial(stage, c))

    def load_p(slot_idx, slot):
        rows = pl.ds(pl.multiple_of(lax.rem(slot_idx, 4) * span, span), span)
        return pltpu.make_async_copy(p_h.at[pl.ds(2 * (slot_idx // 4), 2), rows, :], pbuf.at[slot], p_sem.at[slot])

    slots_each = pret.shape[0] // experts

    def slot_rows(which):
        return pl.ds(pl.multiple_of(which * slots_each, 16), slots_each)

    def give_back(peer):
        return remote(
            prod_h.at[slot_rows(peer), :], pret.at[slot_rows(me), :], send_p.at[peer], recv_p.at[me], "expert", peer
        )

    def got_back(peer):
        return remote(
            prod_h.at[slot_rows(peer), :], pret.at[slot_rows(peer), :], send_p.at[peer], recv_p.at[peer], "expert", peer
        )

    def own_back():
        return pltpu.make_async_copy(prod_h.at[slot_rows(me), :], pret.at[slot_rows(me), :], o_sem.at[0])

    def out_rows(block):
        return pl.ds(block * span, span)

    def load_hidden(block):
        return pltpu.make_async_copy(hid_h.at[out_rows(block), :], hbuf, o_sem.at[1])

    def save_out(block):
        return pltpu.make_async_copy(obuf, out_o.at[out_rows(block), :], o_sem.at[2])

    def output_block(block):
        if block == 0:
            own_back().wait()
            for peer in others(experts, me):
                got_back(peer).wait_recv()
        load_hidden(block).wait()
        where = lax.broadcasted_iota(jnp.int32, (span, pret.shape[0]), 1).astype(f32)
        pick = jnp.where(meta[out_rows(block), 1:2] == where, 1.0, 0.0).astype(bf16)
        gathered = dot_f32(pick, pret[...])
        if block > 0:
            save_out(block - 1).wait()
        obuf[...] = (hbuf[...] + meta[out_rows(block), 0:1] * gathered).astype(bf16)
        save_out(block).start()
        if (block + 1) * span < seq:
            load_hidden(block + 1).start()

    loads = [
        pltpu.make_async_copy(nl_h, tok, local.at[0]),
        pltpu.make_async_copy(ghid_h, ing_o, local.at[2]),
        pltpu.make_async_copy(dwo_h.at[:, 0:thick], part.at[0], local.at[3]),
        pltpu.make_async_copy(dwo_h.at[:, thick : 2 * thick], part.at[1], local.at[4]),
    ]

    @pl.when(pair == 0)
    def _():
        barrier = pltpu.get_barrier_semaphore()
        for peer in others(experts, me):
            pl.semaphore_signal(barrier, inc=1, device_id={"expert": peer})
        for peer in others(groups, my_dp):
            pl.semaphore_signal(barrier, inc=1, device_id={"dp": peer})
        for copy in loads:
            copy.start()
        load_p(0, 0).start()
        own_back().start()
        load_hidden(0).start()
        sbuf[...] = jnp.zeros_like(sbuf)
        first_row = 8 + hot.shape[0]
        by_expert = router[...].T
        for tile in range(gain_rows):
            lanes = slice(128 * tile, 128 * tile + 128)
            sbuf[first_row + tile : first_row + tile + 1, :] = gain_two[:, lanes]
            for which in range(experts):
                row = first_row + 8 + gain_rows * which + tile
                sbuf[row : row + 1, :] = by_expert[which : which + 1, lanes]
        for copy in loads:
            copy.wait()
        nt[...] = tok[...].T
        pl.semaphore_wait(barrier, experts + groups - 2)
        stage1(0)
        stage1(1)
        small1(0, early)
        experts_begin()
        for peer in others(experts, me):
            give_back(peer).start()

    mine = pl.ds(pl.multiple_of(128 * pair, 128), 128)
    lane = lax.broadcasted_iota(jnp.int32, (seq, 128), 1)
    gt = g_ref[...].T
    kt[...] = k_ref[...].T
    gtf = gt.astype(f32)
    pad = jnp.zeros((48, seq), bf16)
    one = jnp.ones((seq, 128), bf16)
    nil = jnp.zeros((seq, 128), bf16)
    acc[...] = jnp.zeros_like(acc)
    for head in range(2):
        own = (lane < 64) if head == 0 else (lane >= 64)
        origin = 64 if head == 0 else 0
        extra = jnp.where((lane >= origin) & (lane < origin + 3), one, nil)
        vaug[head] = jnp.where(own, v_ref[...], extra)
        qz[head] = jnp.where(own, q_ref[...], nil)
        gz[head] = jnp.where(own, g_ref[...], nil)
        rows = slice(64 * head, 64 * head + 64)
        gaug[head, rows, :] = gt[rows]
        gaug[head, origin : origin + 16, :] = split_rows(
            -jnp.sum(gtf[rows] * ctxt_ref[rows, :], axis=0, keepdims=True)
        )
        gaug[head, origin + 16 : origin + 64, :] = pad

    dqt[...] = jnp.zeros_like(dqt)

    def step(idx, carry):
        rows = pl.ds(pl.multiple_of(idx * span, span), span)
        dv = None
        dk = None
        slot = lax.rem(idx, 2)
        load_p(4 * pair + idx, slot).wait()

        @pl.when(4 * pair + idx + 1 < 4 * pairs)
        def _():
            load_p(4 * pair + idx + 1, 1 - slot).start()

        for head in range(2):
            dp = dot_f32(vaug[head, rows, :], gaug[head])
            grads = []
            for part_idx in range(2):
                offs = pl.ds(pl.multiple_of(seq - span * idx - 128 * part_idx, 128), seq)
                band = slice(128 * part_idx, 128 * part_idx + 128)
                ds_ = pbuf[slot, head, band, :].astype(f32) * dp[band]
                acc[head, :, offs] += ds_
                grads.append(ds_.astype(bf16))
            ds_ = jnp.concatenate(grads, axis=0)
            now = dot_f32(pbuf[slot, head], gz[head])
            dv = now if dv is None else dv + now
            now = dot_f32(ds_, qz[head])
            dk = now if dk is None else dk + now
            dqt[64 * head : 64 * head + 64, :] += dot_f32(kt[64 * head : 64 * head + 64, rows], ds_)
        dall[1, rows, mine] = dk.astype(bf16)
        dall[2, rows, mine] = dv.astype(bf16)
        advance(4 * pair + idx)

        for block in range(seq // span):
            @pl.when(4 * pair + idx == OUTPUT_SLOT + block)
            def _():
                output_block(block)

        for at, task, which in EXPERT_SLOTS:
            @pl.when(4 * pair + idx == at)
            def _():
                (experts_second if task == 2 else experts_last)(which)

        @pl.when(4 * pair + idx == 7)
        def _():
            small2(0, early)

        @pl.when(4 * pair + idx == 11)
        def _():
            small3(0, early)

        return carry

    lax.fori_loop(0, seq // span, step, 0)
    dall[0, :, mine] = dqt[...].T.astype(bf16)
    twice = 2 * seq
    sub = lax.broadcasted_iota(jnp.int32, (8, twice), 0)
    head_lane = lax.broadcasted_iota(jnp.int32, (hot.shape[0], 128), 1)
    rel_rows = slice(8, 8 + hot.shape[0])
    for head in range(2):
        total = acc[head, 0:8, :]
        for group in range(1, 16):
            total = total + pltpu.roll(acc[head, 8 * group : 8 * group + 8, :], twice - 8 * group, 1)
        for bit in (1, 2, 4):
            total = jnp.where((sub & bit) != 0, pltpu.roll(total, twice - bit, 1), total)
        diag = jnp.sum(total, axis=0, keepdims=True)
        sums = jnp.sum(hot[...] * diag, axis=1, keepdims=True)
        sbuf[rel_rows, :] = jnp.where(head_lane == 2 * pair + head, sums, sbuf[rel_rows, :])

    def weight_block(idx, carry):
        rows = pl.ds(pl.multiple_of(idx * 256, 256), 256)
        grads = jnp.concatenate([dall[which, :, mine] for which in range(3)], axis=1)
        part[pair + 2, rows, :] = dot_f32(nt[rows, :], grads).astype(bf16)
        return carry

    lax.fori_loop(0, width // 256, weight_block, 0)
    stage1(pair + 2)

    @pl.when(pair == pairs - 1)
    def _():
        def token_block(idx, carry):
            rows = pl.ds(pl.multiple_of(idx * 256, 256), 256)
            grad = (
                dot_nt(dall[0, rows, :], wq[...])
                + dot_nt(dall[1, rows, :], wk[...])
                + dot_nt(dall[2, rows, :], wv[...])
            )
            values = tok[rows, :].astype(f32)
            scale = lax.rsqrt(jnp.mean(values * values, axis=-1, keepdims=True) + epsilon)
            weighted = grad * gain[0:1, :]
            inner = jnp.mean(weighted * values, axis=-1, keepdims=True)
            ing_o[rows, :] += scale * weighted - values * (scale * scale * scale * inner)
            return carry + jnp.sum(grad * values * scale, axis=0, keepdims=True)

        reload = pltpu.make_async_copy(tok_h, tok, local.at[1])
        reload.start()
        last = pairs + 1
        first = 4 * pairs
        older = sorted(
            (at, c, stage)
            for c, slots in enumerate(PLAN)
            for stage, at in enumerate(slots)
            if at >= first
        )

        def drain(until):
            while older and older[0][0] < first + until:
                _, c, stage = older.pop(0)
                stages[stage](c)

        def tokens_done(lower, upper, gain_grad):
            return lax.fori_loop(lower, upper, token_block, gain_grad)

        drain(1)
        reload.wait()
        gain_grad = tokens_done(0, 1, jnp.zeros((1, width), f32))
        stage2(last)
        drain(2)
        gain_grad = tokens_done(1, seq // 512, gain_grad)
        drain(4)
        gain_grad = tokens_done(seq // 512, seq // 256, gain_grad)
        stage3(last)
        for row in range(gain_rows):
            sbuf[row : row + 1, :] = gain_grad[:, 128 * row : 128 * row + 128]
        small1(1, late)
        drain(8)
        small2(1, late)
        stage4(last)
        drain(99)
        small3(1, late)
        stage5(last)
        stage6(last)
        for c in range(2):
            put_first(c).wait()
        save(1).wait()
        save_out(seq // span - 1).wait()
        for peer in others(experts, me):
            give_back(peer).wait_send()
        for block in range(2):
            first_left(block).wait_send()
            first_right(block).wait_send()

        def finish(c, carry):
            copy1(c).wait_send()
            for peer in others(groups, my_dp):
                copy2(c, peer, my_dp).wait_send()
                copy4(c, peer, my_dp).wait_send()
            for peer in others(chips, place):
                copy3(c, peer, place).wait_send()
            copy5(c, core).wait_send()

            @pl.when(c >= 2)
            def _():
                for which in range(3):
                    put_pair(c, which).wait()

            return carry

        lax.fori_loop(0, pairs + 2, finish, 0)
        for part_idx, rows in ((0, early), (1, late)):
            for peer in others(experts, me):
                copy6(part_idx, rows, peer, me).wait_send()
            for peer in others(groups, my_dp):
                copy7(part_idx, rows, peer, my_dp).wait_send()


def back_pass(
    q, k, v, g, ctxt, wq, wk, wv, hot, gain, normed_low, tokens, grad_hidden, dwo, gain_two, router,
    expert_out_grad, shared, expert_in_grad, weights, produced, hidden_rows, meta, groups, experts
):
    seq, width = q.shape
    pairs = width // 128
    chunks = pairs + 2
    small_shape = (8 + hot.shape[0] + 8 + width // 128 * experts, 128)
    hidden = expert_in_grad.shape[1]
    thick = width // 2
    half = width // 2
    piece = half // groups
    chips = experts // 2
    blk = pl.BlockSpec((seq, 128), lambda p: (0, p))
    hbm = pl.BlockSpec(memory_space=pl.ANY)
    fixed = lambda shape: pl.BlockSpec(shape, lambda p: (0,) * len(shape), pipeline_mode=pl.Buffered(1))
    dma = pltpu.SemaphoreType.DMA
    return pl.pallas_call(
        functools.partial(back_kernel, groups, experts, pairs),
        grid=(pairs,),
        in_specs=[
            blk, blk, blk, blk,
            pl.BlockSpec((128, seq), lambda p: (p, 0)),
            fixed((width, width)), fixed((width, width)), fixed((width, width)),
            fixed(hot.shape), fixed(gain.shape),
            hbm, hbm, hbm, hbm, fixed(gain_two.shape), fixed(router.shape), hbm, hbm, hbm,
            hbm, hbm, hbm, fixed(meta.shape),
        ],
        out_specs=[hbm, fixed((seq, width)), fixed(small_shape), hbm, hbm],
        out_shape=[
            jax.ShapeDtypeStruct((4, width, width), bf16),
            jax.ShapeDtypeStruct((seq, width), f32),
            jax.ShapeDtypeStruct(small_shape, f32),
            jax.ShapeDtypeStruct((2, width // 4, hidden), bf16),
            jax.ShapeDtypeStruct((seq, width), bf16),
        ],
        scratch_shapes=[
            pltpu.VMEM((2, 128, 2 * seq), f32),
            pltpu.VMEM((2, seq, 128), bf16),
            pltpu.VMEM((2, 128, seq), bf16),
            pltpu.VMEM((2, seq, 128), bf16),
            pltpu.VMEM((2, seq, 128), bf16),
            pltpu.VMEM((128, seq), bf16),
            pltpu.VMEM((128, seq), f32),
            pltpu.VMEM((2, 2, 256, seq), bf16),
            pltpu.VMEM(produced.shape, bf16),
            pltpu.VMEM((256, width), f32),
            pltpu.VMEM((256, width), bf16),
            pltpu.VMEM((3, seq, width), bf16),
            pltpu.VMEM((width, seq), bf16),
            pltpu.VMEM((seq, width), bf16),
            pltpu.VMEM((chunks, width, thick), bf16),
            pltpu.VMEM((chunks, half, thick), bf16),
            pltpu.VMEM((chunks, groups, piece, thick), bf16),
            pltpu.VMEM((chunks, chips, piece, thick), bf16),
            pltpu.VMEM((chunks, width, thick), bf16),
            pltpu.VMEM(small_shape, f32),
            pltpu.VMEM((experts,) + small_shape, f32),
            pltpu.VMEM(small_shape, f32),
            pltpu.VMEM((groups,) + small_shape, f32),
            pltpu.VMEM((width, hidden // 2), bf16),
            pltpu.VMEM((2, width, hidden // 2), bf16),
            pltpu.VMEM((2, width // 4, hidden), bf16),
            dma((chunks,)), dma((chunks,)),
            dma((chunks, groups)), dma((chunks, groups)),
            dma((chunks, chips)), dma((chunks, chips)),
            dma((chunks, groups)), dma((chunks, groups)),
            dma((chunks,)), dma((chunks,)),
            dma((2, experts)), dma((2, experts)),
            dma((2, groups)), dma((2, groups)),
            dma((6,)),
            dma((2, 2)), dma((2, 2)),
            dma((2, 2)), dma((2, 2)),
            dma((chunks, 3)), dma((6,)),
            dma((2,)), dma((experts,)), dma((experts,)), dma((3,)),
        ],
        compiler_params=pltpu.CompilerParams(
            vmem_limit_bytes=62 << 20, collective_id=2, has_side_effects=True
        ),
        cost_estimate=pl.CostEstimate(
            flops=40 * seq * seq * width + 12 * seq * width * width,
            bytes_accessed=40 * seq * width, transcendentals=seq * seq * 12,
        ),
        name="attend_back",
    )(
        q, k, v, g, ctxt, wq, wk, wv, hot, gain, normed_low, tokens, grad_hidden, dwo, gain_two, router,
        expert_out_grad, shared, expert_in_grad, weights, produced, hidden_rows, meta,
    )


def rms_backward(grad_norm, values, row_scale, gain_vec):
    weighted = grad_norm * gain_vec
    gain_grad = jnp.sum(grad_norm * values * row_scale, axis=0)
    grad_in = row_scale * weighted - values * row_scale**3 * jnp.mean(
        weighted * values, axis=-1, keepdims=True
    )
    return grad_in, gain_grad


def rms_forward(values, gain_vec):
    row_scale = lax.rsqrt(jnp.mean(values * values, axis=-1, keepdims=True) + epsilon)
    return values * row_scale * gain_vec, row_scale


def gelu_tanh(values):
    return jax.nn.gelu(values, approximate=True)


def contract(left, right, dims):
    return lax.dot_general(left, right, (((dims[0],), (dims[1],)), ((), ())), preferred_element_type=f32)


def exchange(rows, experts):
    slots, width = rows.shape
    rows = rows.reshape(experts, slots // experts, width)
    return lax.all_to_all(rows, "expert", split_axis=0, concat_axis=0, tiled=True).reshape(slots, width)


def expert_native(send, grad_recv, weight_in, weight_out, router_w, experts):
    received = exchange(send, experts)
    own = lax.axis_index("expert")
    own_hot = (jnp.arange(experts, dtype=jnp.int32) == own).astype(f32)[None, :]
    probs = jax.nn.softmax(contract(received, router_w, (1, 0)), axis=-1)
    gate = jnp.sum(probs * own_hot, axis=-1, keepdims=True)
    grad_recv_f = grad_recv.astype(f32)
    grad_produced = (grad_recv_f * gate).astype(bf16)
    preact = contract(received, weight_in, (1, 0))
    gelu_values, gelu_pullback = jax.vjp(gelu_tanh, preact)
    active = gelu_values.astype(bf16)
    produced = contract(active, weight_out, (1, 0)).astype(bf16)
    gate_grad = jnp.sum(grad_recv_f * produced.astype(f32), axis=-1, keepdims=True)
    logit_low = (gate_grad * gate * (own_hot - probs)).astype(bf16)
    grad_active = contract(grad_produced, weight_out, (1, 1))
    grad_preact = gelu_pullback(grad_active)[0].astype(bf16)
    grad_received = contract(grad_preact, weight_in, (1, 1)) + contract(logit_low, router_w, (1, 1))
    grad_rows = exchange(grad_received.astype(bf16), experts)
    in_grad = contract(received, grad_preact, (0, 0)).astype(bf16)
    out_grad_t = contract(grad_produced, active, (0, 0)).astype(bf16)
    router_grad = contract(received, logit_low, (0, 0))
    return grad_rows, produced, in_grad, out_grad_t, router_grad


def tail_native(tokens, gain, normed_low, dq, dk, dv, wq, wk, wv, grad_hidden, dwo, small):
    tokens_f = tokens.astype(f32)
    grads = jnp.stack([dwo.astype(f32)] + [contract(normed_low, d, (0, 0)) for d in (dq, dk, dv)])
    grad_normed = contract(dq, wq, (1, 1)) + contract(dk, wk, (1, 1)) + contract(dv, wv, (1, 1))
    _, scale = rms_forward(tokens_f, gain)
    grad_tokens, gain_grad = rms_backward(grad_normed, tokens_f, scale, gain)
    grads, gain_grad, small = lax.psum((grads, gain_grad, small), ("dp", "expert"))
    return grads, grad_hidden + grad_tokens, gain_grad, small


def on_device(
    tokens, gain_one, query_w, key_w, value_w, out_w, rel_table, gain_two, router_w,
    expert_in, expert_out, routes, buckets, cotangent,
):
    seq_len, width = tokens.shape
    heads = rel_table.shape[1]
    groups = lax.axis_size("dp")
    experts = lax.axis_size("expert")
    capacity = (5 * seq_len + 4 * experts - 1) // (4 * experts)
    slots = experts * capacity
    weight_in = expert_in[0]
    weight_out = expert_out[0]
    kernels = capacity % 16 == 0 and experts == 8 and groups == 4

    route_ids = routes[:, 0]
    route_hot = route_ids[:, None] == jnp.arange(experts, dtype=jnp.int32)[None, :]
    route_int = route_hot.astype(jnp.int32)
    route_float = route_hot.astype(f32)
    position = jnp.sum((jnp.cumsum(route_int, axis=0) - 1) * route_int, axis=1)
    slot_index = jnp.where(position < capacity, route_ids * capacity + position, slots)
    pick = (jnp.arange(slots, dtype=jnp.int32)[:, None] == slot_index[None, :]).astype(bf16)

    def scatter_rows(rows):
        return contract(pick, rows, (1, 0)).astype(bf16)

    def gather_rows(rows):
        return contract(pick, rows, (0, 0))

    tokens_f = tokens.astype(f32)
    gains = jnp.stack([gain_one, gain_two])
    if kernels:
        queries, key_rows, value_rows, normed_low, grad_send, slot_row, slot_column = first_pass(
            tokens, gains, query_w, key_w, value_w, routes.reshape(1, seq_len), cotangent, capacity, experts
        )
    else:
        grad_send = scatter_rows(cotangent)
        normed_low = rms_forward(tokens_f, gain_one)[0].astype(bf16)
        queries = contract(normed_low, query_w, (1, 0)).astype(bf16)
        key_rows = contract(normed_low, key_w, (1, 0)).astype(bf16)
        value_rows = contract(normed_low, value_w, (1, 0)).astype(bf16)
    reach = jnp.concatenate([buckets, jnp.full((1,), -1, jnp.int32)])[::-1]
    bucket_hot = (jnp.arange(rel_table.shape[0], dtype=jnp.int32)[:, None] == reach[None, :]).astype(f32)
    spread = jnp.einsum("bh,bx->hx", rel_table, bucket_hot, precision=highest)
    spread = spread.reshape(heads // 2, 2, 2 * seq_len)
    context, context_t, logsum, weights, grad_recv = attend(
        queries, key_rows, value_rows, spread, grad_send, experts if kernels else 0
    )
    if kernels:
        router_pad = jnp.pad(router_w, ((0, 0), (0, 128 - experts)))
        hidden, send, meta = middle_pass(
            tokens, context, out_w, gains, router_pad, slot_row, slot_column, slots, experts
        )
        grad_rows, produced, in_grad, out_grad_t, router_grad, shared = expert_pass(
            send, grad_recv, weight_in, weight_out, router_pad, experts, capacity
        )
        grad_hidden, out_w_grad, grad_context, gain_two_grad = combine_pass(
            grad_rows, hidden, cotangent, gains, context, out_w, meta
        )
    else:
        grad_recv = exchange(grad_send, experts)
        hidden = tokens_f + contract(context, out_w, (1, 0))
        normed_two, scale_two = rms_forward(hidden, gain_two)
        normed_two_low = normed_two.astype(bf16)
        grad_rows, produced, in_grad, out_grad_t, router_grad = expert_native(
            scatter_rows(normed_two_low), grad_recv, weight_in, weight_out, router_w, experts
        )
        router_probs = jax.nn.softmax(contract(normed_two_low, router_w, (1, 0)), axis=-1)
        gate_value = jnp.sum(router_probs * route_float, axis=-1, keepdims=True)
        grad_normed_two = gather_rows(grad_rows)
        grad_hidden_norm, gain_two_grad = rms_backward(grad_normed_two, hidden, scale_two, gain_two)
        grad_hidden = cotangent.astype(f32) + grad_hidden_norm
        branch_low = grad_hidden.astype(bf16)
        out_w_grad = contract(context, branch_low, (0, 0)).astype(bf16)
        grad_context = contract(branch_low, out_w, (1, 1)).astype(bf16)

    if kernels:
        grads, input_grad, small, shares, output = back_pass(
            queries, key_rows, value_rows, grad_context, context_t, query_w, key_w, value_w,
            bucket_hot, gains, normed_low, tokens, grad_hidden, out_w_grad,
            gain_two_grad, router_grad,
            out_grad_t, shared, in_grad, weights, produced, hidden,
            meta, groups, experts,
        )
        tiles = width // 128
        first = 8 + rel_table.shape[0]
        gain_one_grad = small[:tiles].reshape(-1)
        rel_grad = small[8:first, :heads]
        gain_two_grad = small[first : first + tiles].reshape(-1)
        router_grad = small[first + 8 :].reshape(experts, width).T
        out_share, in_share = shares[0], shares[1]
    else:
        output = (hidden + gate_value * gather_rows(exchange(produced, experts))).astype(bf16)
        in_share = lax.psum_scatter(in_grad, "dp", scatter_dimension=0, tiled=True)
        out_share = lax.psum_scatter(out_grad_t, "dp", scatter_dimension=0, tiled=True)
        query_grad, key_grad, value_grad, diagonals = attend_back(
            queries, key_rows, value_rows, grad_context, spread, context_t, logsum
        )
        diagonals = diagonals[:, :2].reshape(heads, 2 * seq_len)
        rel_grad = jnp.einsum("bx,hx->bh", bucket_hot, diagonals, precision=highest)
        grads, input_grad, gain_one_grad, small = tail_native(
            tokens, gain_one, normed_low, query_grad, key_grad, value_grad,
            query_w, key_w, value_w, grad_hidden, out_w_grad, (rel_grad, gain_two_grad, router_grad),
        )
        rel_grad, gain_two_grad, router_grad = small
    grads = grads.astype(f32)
    return (
        output, input_grad, grads[1], grads[2], grads[3], grads[0], rel_grad,
        gain_one_grad, gain_two_grad, router_grad, in_share.astype(f32)[None], out_share.astype(f32).T[None],
    )


def solution(mesh):
    rows = P(("dp", "expert"), None)
    whole = P()
    split = P("expert", None, None)
    return jax.shard_map(
        on_device,
        mesh=mesh,
        in_specs=(
            rows, whole, whole, whole, whole, whole, whole, whole, whole, split, split, rows, whole, rows,
        ),
        out_specs=(
            rows, rows, whole, whole, whole, whole, whole, whole, whole, whole,
            P("expert", "dp", None), P("expert", None, "dp"),
        ),
        check_vma=False,
    )
```
